32 devices in a mesh: dp: 8 (over z, x), tensor: 4 (over y, core).
Axes of the slice: x: 2, y: 2, z: 4, core: 2. Of those that a mesh axis runs over, the one named last changes fastest.
Arguments:
- layer_input: bfloat16 [32768, 1024], P(('dp', 'tensor')), may hold values from -6 to 6
- row_ids: int32 [32768], P('dp'), may hold values from 0 to 1, as said below
- input_gain: bfloat16 [1024], replicated, may hold values from 0.5 to 1.5
- input_shift: bfloat16 [1024], replicated, may hold values from -1.796875 to 1.796875
- query_weight: bfloat16 [1024, 1024], P(None, 'tensor'), may hold values from -0.1875 to 0.1875
- query_bias: bfloat16 [1024], P('tensor'), may hold values from -1.796875 to 1.796875
- key_weight: bfloat16 [1024, 1024], P(None, 'tensor'), may hold values from -0.1875 to 0.1875
- value_weight: bfloat16 [1024, 1024], P(None, 'tensor'), may hold values from -0.1875 to 0.1875
- value_bias: bfloat16 [1024], P('tensor'), may hold values from -1.796875 to 1.796875
- dense_weight: bfloat16 [1024, 1024], P('tensor'), may hold values from -0.75 to 0.75
- dense_bias: bfloat16 [1024], replicated, may hold values from -1.796875 to 1.796875
- post_gain: bfloat16 [1024], replicated, may hold values from 0.5 to 1.5
- post_shift: bfloat16 [1024], replicated, may hold values from -1.796875 to 1.796875
- up_weight: bfloat16 [1024, 4096], P(None, 'tensor'), may hold values from -0.1875 to 0.1875
- up_bias: bfloat16 [4096], P('tensor'), may hold values from -1.796875 to 1.796875
- down_weight: bfloat16 [4096, 1024], P('tensor'), may hold values from -0.1875 to 0.1875
- down_bias: bfloat16 [1024], replicated, may hold values from -1.796875 to 1.796875
- cotangent: bfloat16 [32768, 1024], P(('dp', 'tensor')), may hold values from -6 to 6
Outputs:
- layer_output: bfloat16 [32768, 1024], P(('dp', 'tensor'))
- input_grad: float32 [32768, 1024], P(('dp', 'tensor'))
- input_gain_grad: float32 [1024], replicated
- input_shift_grad: float32 [1024], replicated
- query_weight_grad: float32 [1024, 1024], P(None, 'tensor')
- query_bias_grad: float32 [1024], P('tensor')
- key_weight_grad: float32 [1024, 1024], P(None, 'tensor')
- value_weight_grad: float32 [1024, 1024], P(None, 'tensor')
- value_bias_grad: float32 [1024], P('tensor')
- dense_weight_grad: float32 [1024, 1024], P('tensor')
- dense_bias_grad: float32 [1024], replicated
- post_gain_grad: float32 [1024], replicated
- post_shift_grad: float32 [1024], replicated
- up_weight_grad: float32 [1024, 4096], P(None, 'tensor')
- up_bias_grad: float32 [4096], P('tensor')
- down_weight_grad: float32 [4096, 1024], P('tensor')
- down_bias_grad: float32 [1024], replicated
The draws below stay inside these ranges and needn't reach their ends.
Inputs may be any that keep to these rules, and one draw needn't show every extreme that they name: `row_ids`: within each data group of 4096 consecutive tokens, the tokens form rows of 2048 or 4096 consecutive tokens, each row starting at a multiple of its own length within the group; every token of a row carries the index, within its group, of the row's last block of 2048 tokens, so ids never fall within a group and two rows of a group never share an id.
All inputs are finite; a program needn't handle non-finite values.
Results may differ from the reference program's by a relative error of at most 0.013.
Values may be sent and summed in bfloat16 or wider, within the bound.
A program may use at most 576 MiB of HBM per device.

```python
import jax
import jax.numpy as jnp
from jax import lax

D = 1024
HEADS = 16
HD = 64
FF = 4096
SHORT = 2048
GROUP_TOK = 4096
TOKENS = 32768


def draw_row_ids(key, part):
    unit_count = GROUP_TOK // SHORT
    pair_count = unit_count // 2
    group_count = TOKENS // GROUP_TOK
    flip_key, pick_key = jax.random.split(jax.random.fold_in(key, 17))
    merged = jax.random.randint(flip_key, (group_count, pair_count), 0, 2)
    chosen = jax.random.randint(pick_key, (), 0, group_count)
    forced = (jnp.arange(group_count) == chosen).astype(jnp.int32)[:, None]
    merged = jnp.maximum(merged, forced)
    unit_index = jnp.arange(unit_count)
    pair_of = unit_index // 2
    last_unit = jnp.where(merged[:, pair_of] == 1, 2 * pair_of[None, :] + 1, unit_index[None, :])
    token_ids = jnp.repeat(last_unit, SHORT, axis=1)
    return token_ids.reshape(group_count * GROUP_TOK).astype(jnp.int32)


def block_levels(stream_key, shape, pieces, least, largest):
    loudness, own = 1.0, jax.random.fold_in(stream_key, 6)
    for dim, blocks in pieces:
        steps = jnp.exp(jax.random.uniform(jax.random.fold_in(own, dim), (blocks,), jnp.float32, least / len(pieces), largest / len(pieces)))
        loudness = loudness * jnp.repeat(steps, shape[dim] // blocks).reshape([-1 if axis == dim else 1 for axis in range(len(shape))])
    return loudness


def normal_values(own_key, shape, scale, reach, cuts=(), kind=jnp.bfloat16):
    gain = block_levels(own_key, shape, cuts, -0.22, 0.18) if cuts else 1.0
    drawn = jax.random.normal(own_key, shape, jnp.float32) * scale * gain
    return jnp.minimum(jnp.maximum(drawn, -reach), reach).astype(kind)


def setup_inputs(seed: int = 0) -> dict:
    keys = jax.random.split(jax.random.key(seed), 19)
    layer_input = normal_values(keys[0], (TOKENS, D), 1.0, 6.0, ((0, 32),))
    row_ids = draw_row_ids(jax.random.fold_in(keys[18], 71), 0)
    input_gain = jnp.clip(1.0 + 0.1 * jax.random.normal(keys[2], (D,), jnp.float32), 0.5, 1.5).astype(jnp.bfloat16)
    input_shift = normal_values(keys[3], (D,), 0.3, 1.796875)
    query_weight = normal_values(keys[4], (D, D), D ** -0.5, 0.1875, ((1, 4),))
    query_bias = normal_values(keys[5], (D,), 0.3, 1.796875, ((0, 4),))
    key_weight = normal_values(keys[6], (D, D), D ** -0.5, 0.1875, ((1, 4),))
    value_weight = normal_values(keys[7], (D, D), D ** -0.5, 0.1875, ((1, 4),))
    value_bias = normal_values(keys[8], (D,), 0.3, 1.796875, ((0, 4),))
    dense_weight = normal_values(keys[9], (D, D), HD ** -0.5, 0.75, ((0, 4),))
    dense_bias = normal_values(keys[10], (D,), 0.3, 1.796875)
    post_gain = jnp.clip(1.0 + 0.1 * jax.random.normal(keys[11], (D,), jnp.float32), 0.5, 1.5).astype(jnp.bfloat16)
    post_shift = normal_values(keys[12], (D,), 0.3, 1.796875)
    up_weight = normal_values(keys[13], (D, FF), D ** -0.5, 0.1875, ((1, 4),))
    up_bias = normal_values(keys[14], (FF,), 0.3, 1.796875, ((0, 4),))
    down_weight = normal_values(keys[15], (FF, D), (FF // 4) ** -0.5, 0.1875, ((0, 4),))
    down_bias = normal_values(keys[16], (D,), 0.3, 1.796875)
    cotangent = normal_values(keys[17], (TOKENS, D), 1.0, 6.0, ((0, 32),))
    return {"layer_input": layer_input, "row_ids": row_ids, "input_gain": input_gain, "input_shift": input_shift, "query_weight": query_weight, "query_bias": query_bias, "key_weight": key_weight, "value_weight": value_weight, "value_bias": value_bias, "dense_weight": dense_weight, "dense_bias": dense_bias, "post_gain": post_gain, "post_shift": post_shift, "up_weight": up_weight, "up_bias": up_bias, "down_weight": down_weight, "down_bias": down_bias, "cotangent": cotangent}


@jax.custom_vjp
def low(v):
    return lax.optimization_barrier(v.astype(jnp.bfloat16)).astype(jnp.float32)

@jax.custom_vjp
def low_back(v):
    return v

def low_keep(v):
    return (low(v), None)

def low_pass(kept, grad):
    return (grad,)

def back_keep(v):
    return (v, None)

def back_low(kept, grad):
    return (low(grad),)
low.defvjp(low_keep, low_pass)
low_back.defvjp(back_keep, back_low)
EPSILON = 1e-05
HIGHEST = lax.Precision.HIGHEST

def layer_norm(inputs, gain_vec, shift_vec):
    center = lax.optimization_barrier(jnp.mean(inputs, axis=-1, keepdims=True))
    centered = inputs - center
    spread = lax.optimization_barrier(jnp.mean(centered * centered, axis=-1, keepdims=True))
    return centered * lax.rsqrt(spread + EPSILON) * gain_vec + shift_vec

def head_attention(operands):
    queries, key_rows, values, head_slope, window_ids = operands
    products = jnp.dot(queries, key_rows.T, precision=HIGHEST)
    positions = jnp.arange(queries.shape[0])
    offsets = (positions[None, :] - positions[:, None]).astype(queries.dtype)
    scores = low_back(products * HD ** (-0.5) + head_slope * offsets)
    allowed = (window_ids[None, :] == window_ids[:, None]) & (offsets <= 0)
    masked = jnp.where(allowed, scores, -1e+30)
    log_total = jax.nn.logsumexp(masked, axis=-1, keepdims=True)
    prob_low = low(jnp.where(allowed, jnp.exp(masked - log_total), 0.0))
    return jnp.dot(prob_low, values, precision=HIGHEST)

def forward(window_in, param_set, window_ids):
    input_gain, input_shift, query_weight, query_bias, key_weight, value_weight, value_bias, dense_weight, dense_bias, post_gain, post_shift, up_weight, up_bias, down_weight, down_bias = param_set
    length = window_in.shape[0]
    normed = low(layer_norm(window_in, input_gain, input_shift))
    queries = low(low_back(jnp.dot(normed, query_weight, precision=HIGHEST) + query_bias))
    key_rows = low(low_back(jnp.dot(normed, key_weight, precision=HIGHEST)))
    values = low(low_back(jnp.dot(normed, value_weight, precision=HIGHEST) + value_bias))

    def split_heads(matrix):
        return matrix.reshape(length, HEADS, HD).transpose(1, 0, 2)
    slopes = jnp.exp2(-8.0 * (jnp.arange(HEADS) + 1).astype(window_in.dtype) / HEADS)
    head_ids = jnp.broadcast_to(window_ids, (HEADS, length))
    heads_out = lax.map(jax.checkpoint(head_attention), (split_heads(queries), split_heads(key_rows), split_heads(values), slopes, head_ids))
    mixed_heads = low(low_back(heads_out.transpose(1, 0, 2).reshape(length, D)))
    attended = low_back(jnp.dot(mixed_heads, dense_weight, precision=HIGHEST))
    residual = window_in + attended + dense_bias
    post_rows = low(layer_norm(residual, post_gain, post_shift))
    hidden = low_back(jnp.dot(post_rows, up_weight, precision=HIGHEST) + up_bias)
    active = low(jax.nn.gelu(hidden, approximate=True))
    ffn_out = low_back(jnp.dot(active, down_weight, precision=HIGHEST))
    return residual + ffn_out + down_bias

def reference(layer_input, row_ids, input_gain, input_shift, query_weight, query_bias, key_weight, value_weight, value_bias, dense_weight, dense_bias, post_gain, post_shift, up_weight, up_bias, down_weight, down_bias, cotangent):
    window_len = 2 * SHORT
    window_count = TOKENS // window_len
    param_set = tuple((param_item.astype(jnp.float32) for param_item in (input_gain, input_shift, query_weight, query_bias, key_weight, value_weight, value_bias, dense_weight, dense_bias, post_gain, post_shift, up_weight, up_bias, down_weight, down_bias)))
    inputs = layer_input.astype(jnp.float32).reshape(window_count, window_len, D)
    grads_in = cotangent.astype(jnp.float32).reshape(window_count, window_len, D)
    window_ids = row_ids.reshape(window_count, window_len)

    def window_step(running, operands):
        window_rows, rows_ids, rows_grad = operands
        output, pullback = jax.vjp(lambda window_in, params_now: forward(window_in, params_now, rows_ids), window_rows, param_set)
        input_grad, param_grads = pullback(rows_grad)
        running = tuple((earlier + addend for earlier, addend in zip(running, param_grads)))
        return (running, (output.astype(jnp.bfloat16), input_grad))
    zero_grads = tuple((jnp.zeros(param_item.shape, jnp.float32) for param_item in param_set))
    totals, (outputs, input_grads) = lax.scan(window_step, zero_grads, (inputs, window_ids, grads_in))
    return (outputs.reshape(TOKENS, D), input_grads.reshape(TOKENS, D), totals[0], totals[1], totals[2], totals[3], totals[4], totals[5], totals[6], totals[7], totals[8], totals[9], totals[10], totals[11], totals[12], totals[13], totals[14])
```

```python
import functools
import math

import jax
import jax.numpy as jnp
from jax import lax
from jax.experimental import pallas as pl
from jax.experimental.pallas import tpu as pltpu
from jax.sharding import PartitionSpec as P

HD=64; HEADS=16; SHORT=2048
LOG2E=math.log2(math.e)
f32=jnp.float32; bf=jnp.bfloat16
NT=(((1,),(1,)),((),()))
NN=(((1,),(0,)),((),()))
def dot(a,b,d): return lax.dot_general(a,b,d,preferred_element_type=f32)
def split3(x):
    h=x.astype(bf); r=x-h.astype(f32); m=r.astype(bf); l=(r-m.astype(f32)).astype(bf)
    return h,m,l
def lane(n): return lax.broadcasted_iota(jnp.int32,(n,128),1)
def row(n): return lax.broadcasted_iota(jnp.int32,(n,128),0)
def key_cols(x, base, n):
    ln=lane(n); pos=row(n)+base
    coarse=((pos>>6)<<6).astype(f32); fine=(pos&63).astype(f32)
    c=jnp.where(ln<67,coarse,jnp.where(ln<70,fine,jnp.where(ln<73,-1.0,jnp.where(ln==73,jnp.where(pos<SHORT,-1e30,0.0),0.0))))
    pad=jnp.concatenate([x.astype(f32),jnp.zeros((n,64),f32)],axis=1)
    return jnp.where(ln<64,pad,c).astype(bf)
def query_cols(x, base, n, slope2, apart, lse=None):
    ln=lane(n); pos=row(n)+base
    sh=slope2.astype(bf).astype(f32); r=slope2-sh; sm=r.astype(bf).astype(f32); sl=r-sm
    k3=jnp.where(ln<67,ln-64,ln-67)
    c=jnp.where(k3==0,sh,jnp.where(k3==1,sm,sl))
    c=jnp.where(ln<70,c,0.0)
    if lse is not None:
        h,m,l=split3(lse)
        c=jnp.where(ln==70,h.astype(f32),jnp.where(ln==71,m.astype(f32),jnp.where(ln==72,l.astype(f32),c)))
    c=jnp.where(ln==73,jnp.where(pos>=SHORT,apart,0.0),c)
    pad=jnp.concatenate([x.astype(f32),jnp.zeros((n,64),f32)],axis=1)
    return jnp.where(ln<64,pad,c).astype(bf)
def ones_cols(x,n,at,cnt):
    ln=lane(n)
    pad=jnp.concatenate([x.astype(f32),jnp.zeros((n,64),f32)],axis=1)
    return jnp.where(ln<64,pad,jnp.where((ln>=at)&(ln<at+cnt),1.0,0.0)).astype(bf)

def fwd_kernel(apart_ref, slope_ref, q_ref,k_ref,v_ref,o_ref,lse_ref,qa,ka,va,*,T,pair,bq,bk,form):
    g=pl.program_id(0)
    apart=apart_ref[0].astype(f32)
    nq=T//bq
    for s in range(pair):
        slope2=slope_ref[g*pair+s]
        C=512
        @pl.loop(0,T//C)
        def _(c):
            o=pl.multiple_of(c*C,C); sl=pl.ds(o,C)
            cs=slice(s*64,s*64+64)
            qa[s,sl,:]=query_cols(q_ref[sl,cs],o,C,slope2,apart)
            ka[s,sl,:]=key_cols(k_ref[sl,cs],o,C)
            if form=="A":
                va[s,sl,:]=ones_cols(v_ref[sl,cs],C,64,1)
            else:
                va[s,:,sl]=ones_cols(v_ref[sl,cs],C,64,1).astype(f32).T.astype(bf)
    tri=lax.broadcasted_iota(jnp.int32,(bq,bq),1)<=lax.broadcasted_iota(jnp.int32,(bq,bq),0)
    triT=lax.broadcasted_iota(jnp.int32,(bq,bq),0)<=lax.broadcasted_iota(jnp.int32,(bq,bq),1)
    def q_body(qi,_):
        qo=pl.multiple_of(qi*bq,bq)
        if form=="A":
            qs=[qa[s,pl.ds(qo,bq),:] for s in range(pair)]
            def step(ko,carry,diag,w):
                out=[]
                for s in range(pair):
                    m,acc=carry[s]
                    kk=ka[s,pl.ds(ko,w),:]
                    sc=dot(qs[s],kk,NT)
                    if diag: sc=jnp.where(tri,sc,-1e30)
                    mn=jnp.maximum(m,jnp.max(sc,axis=1,keepdims=True))
                    p=jnp.exp2(sc-mn).astype(bf)
                    acc=acc*jnp.exp2(m-mn)+dot(p,va[s,pl.ds(ko,w),:],NN)
                    out.append((mn,acc))
                return tuple(out)
            init=tuple((jnp.full((bq,1),-1e38,f32),jnp.zeros((bq,128),f32)) for _ in range(pair))
            carry=step(qo,init,True,bq)
            carry=lax.fori_loop(0,qo//bk,lambda t,c:step(pl.multiple_of(t*bk,bk),c,False,bk),carry)
            rem=(qo%bk)//bq
            if bk>bq:
                carry=lax.fori_loop(0,rem,lambda t,c:step(pl.multiple_of(qo-(t+1)*bq,bq),c,False,bq),carry)
            outs=[]
            for s in range(pair):
                m,acc=carry[s]
                l=acc[:,64:65]
                outs.append(acc[:,:64]*(1.0/l))
                lse_ref[s,0,pl.ds(qo,bq)]=(m+jnp.log2(l))[:,0]
            o_ref[pl.ds(qo,bq),:]=jnp.concatenate(outs,axis=1).astype(o_ref.dtype)
        else:
            qs=[qa[s,pl.ds(qo,bq),:] for s in range(pair)]
            def step(ko,carry,diag,w):
                out=[]
                for s in range(pair):
                    m,acc=carry[s]
                    kk=ka[s,pl.ds(ko,w),:]
                    sc=dot(kk,qs[s],NT)
                    if diag: sc=jnp.where(triT,sc,-1e30)
                    mn=jnp.maximum(m,jnp.max(sc,axis=0,keepdims=True))
                    p=jnp.exp2(sc-mn).astype(bf)
                    acc=acc*jnp.exp2(m-mn)+dot(va[s,:,pl.ds(ko,w)],p,NN)
                    out.append((mn,acc))
                return tuple(out)
            init=tuple((jnp.full((1,bq),-1e38,f32),jnp.zeros((va.shape[1],bq),f32)) for _ in range(pair))
            carry=step(qo,init,True,bq)
            carry=lax.fori_loop(0,qo//bk,lambda t,c:step(pl.multiple_of(t*bk,bk),c,False,bk),carry)
            rem=(qo%bk)//bq
            if bk>bq:
                carry=lax.fori_loop(0,rem,lambda t,c:step(pl.multiple_of(qo-(t+1)*bq,bq),c,False,bq),carry)
            outs=[]
            for s in range(pair):
                m,acc=carry[s]
                l=acc[64:65,:]
                outs.append(acc[:64,:]*(1.0/l))
                lse_ref[s,:,pl.ds(qo,bq)]=m+jnp.log2(l)
            o_ref[pl.ds(qo,bq),:]=jnp.concatenate(outs,axis=0).T.astype(o_ref.dtype)
        return 0
    lax.fori_loop(0,nq,q_body,0)

def attn_fwd(q,k,v,slopes2,apart,*,bq=512,bk=512,form="A"):
    T,W=q.shape; H=W//HD; pair=min(2,H)
    spec=pl.BlockSpec((T,pair*HD),lambda g:(0,g))
    return pl.pallas_call(
        functools.partial(fwd_kernel,T=T,pair=pair,bq=bq,bk=bk,form=form),
        grid=(H//pair,),
        in_specs=[pl.BlockSpec(memory_space=pltpu.SMEM),pl.BlockSpec(memory_space=pltpu.SMEM),spec,spec,spec],
        out_specs=[spec,pl.BlockSpec((pair,1,T),lambda g:(g,0,0))],
        out_shape=[jax.ShapeDtypeStruct((T,W),bf),jax.ShapeDtypeStruct((H,1,T),f32)],
        scratch_shapes=[pltpu.VMEM((pair,T,128),bf),pltpu.VMEM((pair,T,128),bf),pltpu.VMEM((pair,T,128) if form=="A" else (pair,128,T),bf)],
        compiler_params=pltpu.CompilerParams(vmem_limit_bytes=56<<20),
        name="attn_fwd_"+form+f"{bq}_{bk}",
    )(apart,slopes2,q,k,v)

def bwd_kernel(apart_ref, slope_ref, q_ref,k_ref,v_ref,do_ref,o_ref,lse_ref,dq_ref,dk_ref,dv_ref,qa,ka,va,da,kt_s,dq_s,*,T,pair,bq,bk):
    g=pl.program_id(0)
    apart=apart_ref[0].astype(f32)
    C=512
    for s in range(pair):
        slope2=slope_ref[g*pair+s]
        cs=slice(s*64,s*64+64)
        @pl.loop(0,T//C)
        def _(c):
            o=pl.multiple_of(c*C,C); sl=pl.ds(o,C)
            lse=lse_ref[s,:,sl].T
            qa[s,sl,:]=query_cols(q_ref[sl,cs],o,C,slope2,apart,lse)
            kc=key_cols(k_ref[sl,cs],o,C)
            ka[s,sl,:]=kc
            kt_s[s,:,sl]=kc.astype(f32).T.astype(bf)
            va[s,sl,:]=ones_cols(v_ref[sl,cs],C,64,3)
            do=do_ref[sl,cs].astype(f32)
            dl=jnp.sum(do*o_ref[sl,cs].astype(f32),axis=1,keepdims=True)
            h,m,l=split3(-dl)
            ln=lane(C)
            pad=jnp.concatenate([do,jnp.zeros((C,64),f32)],axis=1)
            da[s,sl,:]=jnp.where(ln<64,pad,jnp.where(ln==64,h.astype(f32),jnp.where(ln==65,m.astype(f32),jnp.where(ln==66,l.astype(f32),0.0)))).astype(bf)
            dq_s[s,:,sl]=jnp.zeros((128,C),f32)
    triT=lax.broadcasted_iota(jnp.int32,(bk,bk),0)<=lax.broadcasted_iota(jnp.int32,(bk,bk),1)
    nk=T//bk
    def k_body(ki,_):
        ko=pl.multiple_of(ki*bk,bk)
        kk=[ka[s,pl.ds(ko,bk),:] for s in range(pair)]
        vv=[va[s,pl.ds(ko,bk),:] for s in range(pair)]
        def step(qo,carry,diag,w):
            out=[]
            for s in range(pair):
                dk,dv=carry[s]
                qq=qa[s,pl.ds(qo,w),:]; dd=da[s,pl.ds(qo,w),:]
                p=jnp.exp2(dot(kk[s],qq,NT))
                if diag: p=jnp.where(triT,p,0.0)
                dv=dv+dot(p.astype(bf),dd,NN)
                ds=(p*dot(vv[s],dd,NT)).astype(bf)
                dk=dk+dot(ds,qq,NN)
                dq_s[s,:,pl.ds(qo,w)]+=dot(kt_s[s,:,pl.ds(ko,bk)],ds,NN)
                out.append((dk,dv))
            return tuple(out)
        z=jnp.zeros((bk,128),f32)
        carry=step(ko,tuple((z,z) for _ in range(pair)),True,bk)
        start=ko+bk
        r=jnp.minimum((-start)%bq, T-start)//bk
        if bq>bk:
            carry=lax.fori_loop(0,r,lambda t,c:step(pl.multiple_of(start+t*bk,bk),c,False,bk),carry)
            start=start+r*bk
        carry=lax.fori_loop(0,(T-start)//bq,lambda t,c:step(pl.multiple_of(start+t*bq,min(bq,bk)),c,False,bq),carry)
        dk_ref[pl.ds(ko,bk),:]=jnp.concatenate([carry[s][0][:,:64]*(1.0/LOG2E) for s in range(pair)],axis=1).astype(bf)
        dv_ref[pl.ds(ko,bk),:]=jnp.concatenate([carry[s][1][:,:64] for s in range(pair)],axis=1).astype(bf)
        return 0
    lax.fori_loop(0,nk,k_body,0)
    @pl.loop(0,T//C)
    def _(c):
        o=pl.multiple_of(c*C,C); sl=pl.ds(o,C)
        dq_ref[sl,:]=(jnp.concatenate([dq_s[s,:64,sl] for s in range(pair)],axis=0).T*(HD**-0.5)).astype(bf)

def attn_bwd(q,k,v,do,o,lse,slopes2,apart,*,bq=512,bk=512):
    T,W=q.shape; H=W//HD; pair=min(2,H)
    spec=pl.BlockSpec((T,pair*HD),lambda g:(0,g))
    return pl.pallas_call(
        functools.partial(bwd_kernel,T=T,pair=pair,bq=bq,bk=bk),
        grid=(H//pair,),
        in_specs=[pl.BlockSpec(memory_space=pltpu.SMEM),pl.BlockSpec(memory_space=pltpu.SMEM)]+[spec]*5+[pl.BlockSpec((pair,1,T),lambda g:(g,0,0))],
        out_specs=[spec]*3,
        out_shape=[jax.ShapeDtypeStruct((T,W),bf)]*3,
        scratch_shapes=[pltpu.VMEM((pair,T,128),bf)]*4+[pltpu.VMEM((pair,128,T),bf),pltpu.VMEM((pair,128,T),f32)],
        compiler_params=pltpu.CompilerParams(vmem_limit_bytes=60<<20),
        name=f"attn_bwd{bq}_{bk}",
    )(apart,slopes2,q,k,v,do,o,lse)


EPSILON = 1e-05


def layer_norm(inputs, gain_vec, shift_vec):
    center = jnp.mean(inputs, axis=-1, keepdims=True)
    centered = inputs - center
    spread = jnp.mean(centered * centered, axis=-1, keepdims=True)
    return centered * lax.rsqrt(spread + EPSILON) * gain_vec + shift_vec


def gelu_tanh(inputs):
    return jax.nn.gelu(inputs, approximate=True)


def shards(
    layer_input,
    row_ids,
    input_gain,
    input_shift,
    query_weight,
    query_bias,
    key_weight,
    value_weight,
    value_bias,
    dense_weight,
    dense_bias,
    post_gain,
    post_shift,
    up_weight,
    up_bias,
    down_weight,
    down_bias,
    cotangent,
):
    group_len = row_ids.shape[0]
    head_cols = query_weight.shape[1]
    head_count = head_cols // HD
    inputs = layer_input.astype(jnp.float32)
    normed, norm_pull = jax.vjp(
        layer_norm, inputs, input_gain.astype(jnp.float32), input_shift.astype(jnp.float32)
    )
    normed_low = normed.astype(jnp.bfloat16)
    normed_all = lax.all_gather(normed_low, "tensor", axis=0, tiled=True)
    joined = jnp.concatenate([query_weight, key_weight, value_weight], axis=1)
    projected = jnp.dot(normed_all, joined, preferred_element_type=jnp.float32)
    queries = (
        (projected[:, :head_cols] + query_bias.astype(jnp.float32)) * (LOG2E * HD**-0.5)
    ).astype(jnp.bfloat16)
    key_rows = projected[:, head_cols : 2 * head_cols].astype(jnp.bfloat16)
    values = (projected[:, 2 * head_cols :] + value_bias.astype(jnp.float32)).astype(jnp.bfloat16)
    head_index = lax.axis_index("tensor") * head_count + jnp.arange(head_count)
    slopes = jnp.exp2(-8.0 * (head_index + 1).astype(jnp.float32) / HEADS) * LOG2E
    apart = (row_ids[:1] != row_ids[SHORT : SHORT + 1]).astype(jnp.int32)
    mixed_heads, log_total = attn_fwd(queries, key_rows, values, slopes, apart, bq=1024, bk=1024)
    attended = lax.psum_scatter(
        jnp.dot(mixed_heads, dense_weight, preferred_element_type=jnp.float32).astype(jnp.bfloat16),
        "tensor",
        scatter_dimension=0,
        tiled=True,
    ).astype(jnp.float32)
    residual = inputs + attended + dense_bias.astype(jnp.float32)
    post_rows, post_pull = jax.vjp(
        layer_norm, residual, post_gain.astype(jnp.float32), post_shift.astype(jnp.float32)
    )
    post_low = post_rows.astype(jnp.bfloat16)
    post_all = lax.all_gather(post_low, "tensor", axis=0, tiled=True)
    hidden = jnp.dot(post_all, up_weight, preferred_element_type=jnp.float32) + up_bias.astype(
        jnp.float32
    )
    active, gelu_pull = jax.vjp(gelu_tanh, hidden)
    active_low = active.astype(jnp.bfloat16)
    ffn_out = lax.psum_scatter(
        jnp.dot(active_low, down_weight, preferred_element_type=jnp.float32).astype(jnp.bfloat16),
        "tensor",
        scatter_dimension=0,
        tiled=True,
    ).astype(jnp.float32)
    layer_output = (residual + ffn_out + down_bias.astype(jnp.float32)).astype(jnp.bfloat16)
    grad_rows = cotangent.astype(jnp.float32)
    down_bias_part = jnp.sum(grad_rows, axis=0)
    grad_all = lax.all_gather(cotangent, "tensor", axis=0, tiled=True)
    act_grad = jnp.einsum("td,fd->tf", grad_all, down_weight, preferred_element_type=jnp.float32)
    hidden_grad = gelu_pull(act_grad)[0].astype(jnp.bfloat16)
    up_part = jnp.einsum("td,tf->df", post_all, hidden_grad, preferred_element_type=jnp.float32)
    down_part = jnp.einsum("tf,td->fd", active_low, grad_all, preferred_element_type=jnp.float32)
    up_bias_part = jnp.sum(hidden_grad.astype(jnp.float32), axis=0)
    post_grad = lax.psum_scatter(
        jnp.einsum("tf,df->td", hidden_grad, up_weight, preferred_element_type=jnp.float32).astype(jnp.bfloat16),
        "tensor",
        scatter_dimension=0,
        tiled=True,
    ).astype(jnp.float32)
    norm_grad_resid, post_gain_part, post_shift_part = post_pull(post_grad)
    resid_grad = grad_rows + norm_grad_resid
    dense_bias_part = jnp.sum(resid_grad, axis=0)
    attended_all = lax.all_gather(resid_grad.astype(jnp.bfloat16), "tensor", axis=0, tiled=True)
    dense_part = jnp.einsum(
        "tc,td->cd", mixed_heads, attended_all, preferred_element_type=jnp.float32
    )
    mixed_grad = jnp.einsum(
        "td,cd->tc", attended_all, dense_weight, preferred_element_type=jnp.float32
    ).astype(jnp.bfloat16)
    query_grad, key_grad, value_grad = attn_bwd(
        queries, key_rows, values, mixed_grad, mixed_heads, log_total, slopes, apart, bq=1024, bk=512
    )
    proj_grad = jnp.concatenate([query_grad, key_grad, value_grad], axis=1)
    joined_part = jnp.einsum("td,tc->dc", normed_all, proj_grad, preferred_element_type=jnp.float32)
    query_bias_part = jnp.sum(query_grad.astype(jnp.float32), axis=0)
    value_bias_part = jnp.sum(value_grad.astype(jnp.float32), axis=0)
    normed_grad = lax.psum_scatter(
        jnp.einsum("tc,dc->td", proj_grad, joined, preferred_element_type=jnp.float32).astype(jnp.bfloat16),
        "tensor",
        scatter_dimension=0,
        tiled=True,
    ).astype(jnp.float32)
    input_norm_grad, input_gain_part, input_shift_part = norm_pull(normed_grad)
    input_grad = resid_grad + input_norm_grad
    weight_parts = (
        joined_part[:, :head_cols],
        joined_part[:, head_cols : 2 * head_cols],
        joined_part[:, 2 * head_cols :],
        dense_part,
        up_part,
        down_part,
    )
    query_w, key_w, value_w, dense_w, up_w, down_w = (
        total.astype(jnp.float32)
        for total in lax.psum(tuple(part.astype(jnp.bfloat16) for part in weight_parts), "dp")
    )
    query_b, value_b, up_b = lax.psum((query_bias_part, value_bias_part, up_bias_part), "dp")
    summed = (query_w, query_b, key_w, value_w, value_b, dense_w, up_w, up_b, down_w)
    shared = lax.psum(
        (
            input_gain_part,
            input_shift_part,
            dense_bias_part,
            post_gain_part,
            post_shift_part,
            down_bias_part,
        ),
        ("dp", "tensor"),
    )
    return (
        layer_output,
        input_grad,
        shared[0],
        shared[1],
        summed[0],
        summed[1],
        summed[2],
        summed[3],
        summed[4],
        summed[5],
        shared[2],
        shared[3],
        shared[4],
        summed[6],
        summed[7],
        summed[8],
        shared[5],
    )


def solution(mesh):
    in_specs = (
        P(("dp", "tensor"), None),
        P("dp"),
        P(),
        P(),
        P(None, "tensor"),
        P("tensor"),
        P(None, "tensor"),
        P(None, "tensor"),
        P("tensor"),
        P("tensor", None),
        P(),
        P(),
        P(),
        P(None, "tensor"),
        P("tensor"),
        P("tensor", None),
        P(),
        P(("dp", "tensor"), None),
    )
    out_specs = (
        P(("dp", "tensor"), None),
        P(("dp", "tensor"), None),
        P(),
        P(),
        P(None, "tensor"),
        P("tensor"),
        P(None, "tensor"),
        P(None, "tensor"),
        P("tensor"),
        P("tensor", None),
        P(),
        P(),
        P(),
        P(None, "tensor"),
        P("tensor"),
        P("tensor", None),
        P(),
    )
    return jax.shard_map(shards, mesh=mesh, in_specs=in_specs, out_specs=out_specs, check_vma=False)
```

```python
import functools
import math

import jax
import jax.numpy as jnp
from jax import lax
from jax.experimental import pallas as pl
from jax.experimental.pallas import tpu as pltpu
from jax.sharding import PartitionSpec as P

HEADS = 16
HD = 64
SHORT = 2048
EPSILON = 1e-05
LOG2E = math.log2(math.e)
F32 = jnp.float32
BF16 = jnp.bfloat16
NT = (((1,), (1,)), ((), ()))
NN = (((1,), (0,)), ((), ()))
TN = (((0,), (0,)), ((), ()))


def dot(lhs, rhs, dims=NN):
    return lax.dot_general(lhs, rhs, dims, preferred_element_type=F32)


def low(array):
    return array.astype(BF16)


def norm_stats(rows):
    center = jnp.mean(rows, axis=-1, keepdims=True)
    centered = rows - center
    inverse = lax.rsqrt(jnp.mean(centered * centered, axis=-1, keepdims=True) + EPSILON)
    return centered * inverse, inverse


def norm_pull(grad, normal, inverse):
    grad_mean = jnp.mean(grad, axis=-1, keepdims=True)
    dot_mean = jnp.mean(grad * normal, axis=-1, keepdims=True)
    return inverse * (grad - grad_mean - normal * dot_mean)


def lanes(count):
    return lax.broadcasted_iota(jnp.int32, (count, 128), 1)


def places(count, first):
    return lax.broadcasted_iota(jnp.int32, (count, 128), 0) + first


def widen(head):
    return jnp.concatenate([head.astype(F32), jnp.zeros((head.shape[0], HD), F32)], axis=1)


def split3(value):
    high = low(value).astype(F32)
    middle = low(value - high).astype(F32)
    return high, middle, value - high - middle


def pick3(index, parts):
    return jnp.where(index == 0, parts[0], jnp.where(index == 1, parts[1], parts[2]))


def key_columns(head, first):
    count = head.shape[0]
    lane, place = lanes(count), places(count, first)
    coarse = ((place >> 6) << 6).astype(F32)
    fine = (place & 63).astype(F32)
    wall = jnp.where(place < SHORT, -1e30, 0.0)
    extra = jnp.where(lane < 73, -1.0, jnp.where(lane == 73, wall, 0.0))
    extra = jnp.where(lane < 67, coarse, jnp.where(lane < 70, fine, extra))
    return low(jnp.where(lane < HD, widen(head), extra))


def query_columns(head, first, slope, apart, log_total=None):
    count = head.shape[0]
    lane, place = lanes(count), places(count, first)
    extra = pick3(jnp.where(lane < 67, lane - 64, lane - 67), split3(slope))
    extra = jnp.where(lane < 70, extra, 0.0)
    if log_total is not None:
        extra = jnp.where((lane >= 70) & (lane < 73), pick3(lane - 70, split3(log_total)), extra)
    extra = jnp.where(lane == 73, jnp.where(place >= SHORT, apart, 0.0), extra)
    return low(jnp.where(lane < HD, widen(head), extra))


def ones_columns(head, count):
    lane = lanes(head.shape[0])
    return low(jnp.where(lane < HD, widen(head), jnp.where(lane < HD + count, 1.0, 0.0)))


def grad_columns(head, shift):
    lane = lanes(head.shape[0])
    extra = jnp.where(lane < 67, pick3(lane - 64, split3(shift)), 0.0)
    return low(jnp.where(lane < HD, widen(head), extra))


def each_chunk(me, slots, rows, body):
    chunk = min(rows, 512)
    for slot in range(slots):
        home = (me ^ slot) * rows

        @pl.loop(0, rows // chunk)
        def _(step):
            offset = pl.multiple_of(step * chunk, chunk)
            body(slot, pl.ds(offset, chunk), pl.ds(slot * rows + offset, chunk), home + offset)


def attend_kernel(
    me_ref, apart_ref, slope_ref, q_ref, k_ref, v_ref, o_ref, lse_ref, qa, ka, va, *, slots, pair, tile
):
    me = me_ref[0]
    total = q_ref.shape[0]
    rows = total // slots
    chunk = min(rows, 512)
    apart = apart_ref[0].astype(F32)

    def prepare(slot, inner, spot, place):
        place = pl.multiple_of(place, chunk)
        home = pl.ds(place, chunk)
        for s in range(pair):
            cols = slice(s * HD, (s + 1) * HD)
            qa[s, home, :] = query_columns(q_ref[spot, cols], place, slope_ref[s], apart)
            ka[s, home, :] = key_columns(k_ref[spot, cols], place)
            va[s, home, :] = ones_columns(v_ref[spot, cols], 1)

    each_chunk(me, slots, rows, prepare)
    causal = lax.broadcasted_iota(jnp.int32, (tile, tile), 1) <= lax.broadcasted_iota(
        jnp.int32, (tile, tile), 0
    )
    piece = min(rows, tile)

    def query_tile(index, _):
        first = pl.multiple_of(index * tile, tile)
        queries = [qa[s, pl.ds(first, tile), :] for s in range(pair)]

        def step(at, carry, diagonal):
            after = []
            for s in range(pair):
                top, mix = carry[s]
                scores = dot(queries[s], ka[s, pl.ds(at, tile), :], NT)
                if diagonal:
                    scores = jnp.where(causal, scores, -1e30)
                higher = jnp.maximum(top, jnp.max(scores, axis=1, keepdims=True))
                weights = low(jnp.exp2(scores - higher))
                mix = mix * jnp.exp2(top - higher) + dot(weights, va[s, pl.ds(at, tile), :])
                after.append((higher, mix))
            return tuple(after)

        carry = tuple(
            (jnp.full((tile, 1), -1e38, F32), jnp.zeros((tile, 128), F32)) for _ in range(pair)
        )
        carry = step(first, carry, True)
        carry = lax.fori_loop(
            0, index, lambda at, held: step(pl.multiple_of(at * tile, tile), held, False), carry
        )
        outs = []
        for s in range(pair):
            top, mix = carry[s]
            weight = mix[:, HD : HD + 1]
            outs.append(mix[:, :HD] * (1.0 / weight))
            lse_ref[s, 0, pl.ds(first, tile)] = (top + jnp.log2(weight))[:, 0]
        out = low(jnp.concatenate(outs, axis=1))
        for part in range(tile // piece):
            block = (index * (tile // piece) + part) // (rows // piece)
            offset = first + part * piece - block * rows
            spot = pl.multiple_of((block ^ me) * rows + offset, piece)
            o_ref[pl.ds(spot, piece), :] = out[part * piece : (part + 1) * piece]
        return 0

    lax.fori_loop(0, total // tile, query_tile, 0)


def attend(me, apart, slopes, queries, key_rows, values, slots, group, tile=1024):
    total, width = queries.shape
    pair = min(2, width // HD)
    cols = pair * HD
    spec = pl.BlockSpec((total, cols), lambda g: (0, group))
    scalars = pl.BlockSpec(memory_space=pltpu.SMEM)
    return pl.pallas_call(
        functools.partial(attend_kernel, slots=slots, pair=pair, tile=tile),
        grid=(1,),
        in_specs=[scalars] * 3 + [spec] * 3,
        out_specs=[
            pl.BlockSpec((total, cols), lambda g: (0, 0)),
            pl.BlockSpec((pair, 1, total), lambda g: (0, 0, 0)),
        ],
        out_shape=[
            jax.ShapeDtypeStruct((total, cols), BF16),
            jax.ShapeDtypeStruct((pair, 1, total), F32),
        ],
        scratch_shapes=[pltpu.VMEM((pair, total, 128), BF16)] * 3,
        compiler_params=pltpu.CompilerParams(vmem_limit_bytes=56 << 20),
        cost_estimate=pl.CostEstimate(
            flops=pair * 1100 * total * total, transcendentals=0, bytes_accessed=8 * total * cols
        ),
        name="attend",
    )(me, apart, slopes[group * pair : (group + 1) * pair], queries, key_rows, values)


def attend_back_kernel(*refs, slots, pair, tile, key_tile):
    me_ref, apart_ref, slope_ref, q_ref, k_ref, v_ref, o_ref, lse_ref = refs[:8]
    g_refs = refs[8 : 8 + slots]
    dq_ref, dk_ref, dv_ref, qa, ka, va, ga, kt, dq_sum = refs[8 + slots :]
    me = me_ref[0]
    total = q_ref.shape[0]
    rows = total // slots
    chunk = min(rows, 512)
    apart = apart_ref[0].astype(F32)

    def prepare(slot, inner, spot, place):
        place = pl.multiple_of(place, chunk)
        home = pl.ds(place, chunk)
        for s in range(pair):
            cols = slice(s * HD, (s + 1) * HD)
            log_total = lse_ref[s, :, home].T
            qa[s, home, :] = query_columns(q_ref[spot, cols], place, slope_ref[s], apart, log_total)
            keys = key_columns(k_ref[spot, cols], place)
            ka[s, home, :] = keys
            kt[s, :, home] = low(keys.astype(F32).T)
            va[s, home, :] = ones_columns(v_ref[spot, cols], 3)
            grad = g_refs[slot][inner, cols]
            row_dot = jnp.sum(
                grad.astype(F32) * o_ref[spot, cols].astype(F32), axis=1, keepdims=True
            )
            ga[s, home, :] = grad_columns(grad, -row_dot)
            dq_sum[s, :, home] = jnp.zeros((128, chunk), F32)

    each_chunk(me, slots, rows, prepare)
    causal = lax.broadcasted_iota(jnp.int32, (key_tile, key_tile), 0) <= lax.broadcasted_iota(
        jnp.int32, (key_tile, key_tile), 1
    )
    piece = min(rows, key_tile)

    def place_of(place, size):
        block = place // rows
        return pl.multiple_of((block ^ me) * rows + (place - block * rows), size)

    def keys_tile(index, _):
        first = pl.multiple_of(index * key_tile, key_tile)
        here = pl.ds(first, key_tile)

        def step(at, carry, diagonal, width):
            after = []
            for s in range(pair):
                dk, dv = carry[s]
                there = pl.ds(at, width)
                queries, grads = qa[s, there, :], ga[s, there, :]
                probs = jnp.exp2(dot(ka[s, here, :], queries, NT))
                if diagonal:
                    probs = jnp.where(causal, probs, 0.0)
                dv = dv + dot(low(probs), grads)
                score_grad = low(probs * dot(va[s, here, :], grads, NT))
                dk = dk + dot(score_grad, queries)
                dq_sum[s, :, there] += dot(kt[s, :, here], score_grad)
                after.append((dk, dv))
            return tuple(after)

        zeros = jnp.zeros((key_tile, 128), F32)
        carry = step(first, tuple((zeros, zeros) for _ in range(pair)), True, key_tile)
        start = first + key_tile
        short = jnp.minimum((-start) % tile, total - start) // key_tile
        if tile > key_tile:
            carry = lax.fori_loop(
                0,
                short,
                lambda at, held: step(
                    pl.multiple_of(start + at * key_tile, key_tile), held, False, key_tile
                ),
                carry,
            )
            start = start + short * key_tile
        carry = lax.fori_loop(
            0,
            (total - start) // tile,
            lambda at, held: step(
                pl.multiple_of(start + at * tile, min(tile, key_tile)), held, False, tile
            ),
            carry,
        )
        dk = low(jnp.concatenate([held[0][:, :HD] * (1.0 / LOG2E) for held in carry], axis=1))
        dv = low(jnp.concatenate([held[1][:, :HD] for held in carry], axis=1))
        for part in range(key_tile // piece):
            spot = pl.ds(place_of(first + part * piece, piece), piece)
            dk_ref[spot, :] = dk[part * piece : (part + 1) * piece]
            dv_ref[spot, :] = dv[part * piece : (part + 1) * piece]
        return 0

    lax.fori_loop(0, total // key_tile, keys_tile, 0)

    def finish(slot, inner, spot, place):
        home = pl.ds(pl.multiple_of(place, chunk), chunk)
        joined = jnp.concatenate([dq_sum[s, :HD, home] for s in range(pair)], axis=0)
        dq_ref[spot, :] = low(joined.T * HD**-0.5)

    each_chunk(me, slots, rows, finish)


def attend_back(
    me, apart, slopes, queries, key_rows, values, mixed, log_total, grads, group, tile=1024, key_tile=512
):
    slots = len(grads)
    total, width = queries.shape
    pair = min(2, width // HD)
    cols = pair * HD
    spec = pl.BlockSpec((total, cols), lambda g: (0, group))
    out_spec = pl.BlockSpec((total, cols), lambda g: (0, 0))
    scalars = pl.BlockSpec(memory_space=pltpu.SMEM)
    return pl.pallas_call(
        functools.partial(
            attend_back_kernel, slots=slots, pair=pair, tile=tile, key_tile=key_tile
        ),
        grid=(1,),
        in_specs=[scalars] * 3
        + [spec] * 3
        + [out_spec, pl.BlockSpec((pair, 1, total), lambda g: (0, 0, 0))]
        + [pl.BlockSpec((total // slots, cols), lambda g: (0, group))] * slots,
        out_specs=[out_spec] * 3,
        out_shape=[jax.ShapeDtypeStruct((total, cols), BF16)] * 3,
        scratch_shapes=[pltpu.VMEM((pair, total, 128), BF16)] * 4
        + [pltpu.VMEM((pair, 128, total), BF16), pltpu.VMEM((pair, 128, total), F32)],
        compiler_params=pltpu.CompilerParams(vmem_limit_bytes=60 << 20),
        cost_estimate=pl.CostEstimate(
            flops=pair * 2200 * total * total, transcendentals=0, bytes_accessed=16 * total * cols
        ),
        name="attend_back",
    )(
        me,
        apart,
        slopes[group * pair : (group + 1) * pair],
        queries,
        key_rows,
        values,
        mixed,
        log_total,
        *grads,
    )


def post_kernel(*refs, slots, groups):
    mixed_refs = refs[: slots * groups]
    x_ref, weight_ref, bias_ref, gain_ref, shift_ref, post_ref, residual_ref = refs[slots * groups :]
    mixed = jnp.concatenate([ref[...] for ref in mixed_refs], axis=1)
    residual = x_ref[...].astype(F32) + dot(mixed, weight_ref[...]) + bias_ref[...].astype(F32)
    normal, _ = norm_stats(residual)
    post_ref[...] = low(normal * gain_ref[...].astype(F32) + shift_ref[...].astype(F32))
    own = residual_ref.shape[0]
    step = pl.program_id(0)

    @pl.when(step < pl.num_programs(0) // slots)
    def _():
        residual_ref[...] = residual


def post_norm(mixed, x_all, weight, bias, gain, shift):
    slots, groups = len(mixed), len(mixed[0])
    total, width = x_all.shape
    rows = total // slots
    block = min(rows, 512)
    per = rows // block
    specs = []
    for slot in range(slots):
        for part in mixed[slot]:
            specs.append(
                pl.BlockSpec(
                    (block, part.shape[1]),
                    lambda i, slot=slot: (((i // per) ^ slot) * per + i % per, 0),
                )
            )
    whole = lambda shape: pl.BlockSpec(shape, lambda i: (0, 0))
    return pl.pallas_call(
        functools.partial(post_kernel, slots=slots, groups=groups),
        grid=(total // block,),
        in_specs=specs
        + [
            pl.BlockSpec((block, width), lambda i: (i, 0)),
            whole(weight.shape),
            whole((1, width)),
            whole((1, width)),
            whole((1, width)),
        ],
        out_specs=[
            pl.BlockSpec((block, width), lambda i: (i, 0)),
            pl.BlockSpec((block, width), lambda i: (jnp.minimum(i, per - 1), 0)),
        ],
        out_shape=[
            jax.ShapeDtypeStruct((total, width), BF16),
            jax.ShapeDtypeStruct((rows, width), F32),
        ],
        compiler_params=pltpu.CompilerParams(vmem_limit_bytes=48 << 20),
        cost_estimate=pl.CostEstimate(
            flops=2 * total * width * width, transcendentals=0, bytes_accessed=6 * total * width
        ),
        name="post_norm",
    )(
        *[part for parts in mixed for part in parts],
        x_all,
        weight,
        bias[None],
        gain[None],
        shift[None],
    )


def shards(
    slots,
    layer_input,
    row_ids,
    input_gain,
    input_shift,
    query_weight,
    query_bias,
    key_weight,
    value_weight,
    value_bias,
    dense_weight,
    dense_bias,
    post_gain,
    post_shift,
    up_weight,
    up_bias,
    down_weight,
    down_bias,
    cotangent,
):
    me = lax.axis_index("tensor")
    me_word = me.astype(jnp.int32)[None]
    rows = layer_input.shape[0]
    head_cols = query_weight.shape[1]
    head_count = head_cols // HD
    groups = max(1, head_count // 2)
    bits = [1 << level for level in range(slots.bit_length() - 1)]
    after = lambda array, *others: lax.optimization_barrier((array, *others))[0]

    def swap(array, mask):
        return lax.ppermute(array, "tensor", [(i, i ^ mask) for i in range(slots)])

    def gather(array):
        held = {0: array}
        for bit in reversed(bits):
            held.update({slot ^ bit: swap(part, bit) for slot, part in held.items()})
        return [held[slot] for slot in range(slots)]

    def scatter_sum(parts):
        held = dict(enumerate(parts))
        for bit in bits:
            held = {
                slot: part.astype(F32) + swap(low(held[slot | bit]), bit).astype(F32)
                for slot, part in held.items()
                if not slot & bit
            }
        return held[0]

    def blocks(array):
        return [array[slot * rows : (slot + 1) * rows] for slot in range(slots)]

    x_parts = gather(layer_input)
    cot_own = after(cotangent, x_parts[-1])
    dense_parts = gather(after(dense_weight, x_parts[-1]))
    cot_parts = gather(cot_own)

    x_all = jnp.concatenate(x_parts, axis=0)
    gain, shift = input_gain.astype(F32), input_shift.astype(F32)
    normed = low(norm_stats(x_all.astype(F32))[0] * gain + shift)
    joined = jnp.concatenate([query_weight, key_weight, value_weight], axis=1)
    projected = dot(normed, joined)
    queries = low((projected[:, :head_cols] + query_bias.astype(F32)) * (LOG2E * HD**-0.5))
    key_rows = low(projected[:, head_cols : 2 * head_cols])
    values = low(projected[:, 2 * head_cols :] + value_bias.astype(F32))
    heads = me * head_count + jnp.arange(head_count)
    slopes = jnp.exp2(-8.0 * (heads + 1).astype(F32) / HEADS) * LOG2E
    apart = (row_ids[:1] != row_ids[SHORT : SHORT + 1]).astype(jnp.int32)

    mixed_own, log_totals, mixed_parts = [], [], []
    for group in range(groups):
        mixed, log_total = attend(
            me_word, apart, slopes, queries, key_rows, values, slots, group
        )
        mixed_own.append(mixed)
        log_totals.append(log_total)
        mixed_parts.append(gather(mixed))
    mixed_all = [[mixed_parts[group][slot] for group in range(groups)] for slot in range(slots)]
    dense_all = jnp.concatenate(dense_parts, axis=0)
    post_all, residual = post_norm(mixed_all, x_all, dense_all, dense_bias, post_gain, post_shift)

    cot_all = jnp.concatenate(cot_parts, axis=0)
    hidden = dot(post_all, up_weight) + up_bias.astype(F32)
    active, gelu_pull = jax.vjp(lambda v: jax.nn.gelu(v, approximate=True), hidden)
    active = low(active)
    hidden_grad = low(gelu_pull(dot(cot_all, down_weight, NT))[0])
    half = slots // 2 * rows
    far = low(dot(hidden_grad[half:], up_weight, NT))
    near = low(dot(after(hidden_grad[:half], far), up_weight, NT))
    post_grad = scatter_sum(blocks(jnp.concatenate([near, far], axis=0)))
    hidden_late, active_late = lax.optimization_barrier((hidden_grad, active, near))[:2]
    up_part = dot(post_all, hidden_late, TN)
    down_part = dot(active_late, cot_all, TN)
    up_bias_part = jnp.sum(hidden_grad.astype(F32), axis=0)
    up_sum, down_sum = lax.psum((low(up_part), low(down_part)), "dp")

    cot_rows = cotangent.astype(F32)
    post_normal, post_inverse = norm_stats(residual)
    resid_grad = cot_rows + norm_pull(
        post_grad * post_gain.astype(F32), post_normal, post_inverse
    )
    attended_grad = low(resid_grad)
    mixed_grad = low(dot(attended_grad, dense_all, NT))
    mixed_grads = [
        swap(part, slot) if slot else part
        for slot, part in enumerate(jnp.split(mixed_grad, slots, axis=1))
    ]

    ffn_part = low(dot(after(active, *mixed_grads), down_weight))
    ffn_out = scatter_sum(blocks(ffn_part))
    layer_output = low(residual + ffn_out + down_bias.astype(F32))
    mixed_rows = jnp.concatenate(
        [
            part[slot * rows : (slot + 1) * rows]
            for slot, parts in enumerate(mixed_all)
            for part in parts
        ],
        axis=1,
    )
    dense_part = dot(mixed_rows, attended_grad, TN)
    dense_part = scatter_sum(
        [dense_part[slot * head_cols : (slot + 1) * head_cols] for slot in range(slots)]
    )

    def total_of(vectors, own):
        flat = jnp.concatenate(vectors + own)
        pad = -flat.shape[0] % 1024
        flat = jnp.pad(flat, (0, pad)).reshape(-1, 1024)
        every = lax.all_gather(flat, ("dp", "tensor"), axis=0)
        every = every.reshape(-1, slots, flat.size)
        shared = jnp.sum(every, axis=(0, 1))
        mine = jnp.sum(lax.dynamic_index_in_dim(every, me, 1, keepdims=False), axis=0)
        outs, at = [], 0
        for vector, source in [(v, shared) for v in vectors] + [(v, mine) for v in own]:
            outs.append(source[at : at + vector.shape[0]])
            at += vector.shape[0]
        return outs

    down_bias_grad, dense_bias_grad, post_gain_grad, post_shift_grad, up_bias_grad = total_of(
        [
            jnp.sum(cot_rows, axis=0),
            jnp.sum(resid_grad, axis=0),
            jnp.sum(post_grad * post_normal, axis=0),
            jnp.sum(post_grad, axis=0),
        ],
        [up_bias_part],
    )

    head_grads = [
        attend_back(
            me_word,
            apart,
            slopes,
            queries,
            key_rows,
            values,
            mixed_own[group],
            log_totals[group],
            mixed_grads,
            group,
        )
        for group in range(groups)
    ]
    proj_grad = jnp.concatenate(
        [head_grads[group][kind] for kind in range(3) for group in range(groups)], axis=1
    )
    far = low(dot(proj_grad[half:], joined, NT))
    near = low(dot(after(proj_grad[:half], far), joined, NT))
    normed_grad = scatter_sum(blocks(jnp.concatenate([near, far], axis=0)))
    proj_late = after(proj_grad, near)
    joined_part = dot(normed, proj_late, TN)
    proj_sum = jnp.sum(proj_grad.astype(F32), axis=0)
    joined_high = joined.astype(F32)
    shift_part = jnp.sum(joined_high * proj_sum, axis=1)
    gain_part = (jnp.sum(joined_high * joined_part, axis=1) - shift * shift_part) / gain
    late = lax.optimization_barrier((low(joined_part), low(dense_part), up_sum, down_sum))
    joined_sum, dense_sum = lax.psum(late[:2], "dp")
    input_gain_grad, input_shift_grad, query_bias_grad, value_bias_grad = total_of(
        [gain_part, shift_part], [proj_sum[:head_cols], proj_sum[2 * head_cols :]]
    )

    input_normal, input_inverse = norm_stats(layer_input.astype(F32))
    input_grad = resid_grad + norm_pull(normed_grad * gain, input_normal, input_inverse)
    joined_sum = joined_sum.astype(F32)
    return (
        layer_output,
        input_grad,
        input_gain_grad,
        input_shift_grad,
        joined_sum[:, :head_cols],
        query_bias_grad,
        joined_sum[:, head_cols : 2 * head_cols],
        joined_sum[:, 2 * head_cols :],
        value_bias_grad,
        dense_sum.astype(F32),
        dense_bias_grad,
        post_gain_grad,
        post_shift_grad,
        late[2].astype(F32),
        up_bias_grad,
        late[3].astype(F32),
        down_bias_grad,
    )


def solution(mesh):
    in_specs = (
        P(("dp", "tensor"), None),
        P("dp"),
        P(),
        P(),
        P(None, "tensor"),
        P("tensor"),
        P(None, "tensor"),
        P(None, "tensor"),
        P("tensor"),
        P("tensor", None),
        P(),
        P(),
        P(),
        P(None, "tensor"),
        P("tensor"),
        P("tensor", None),
        P(),
        P(("dp", "tensor"), None),
    )
    out_specs = (
        P(("dp", "tensor"), None),
        P(("dp", "tensor"), None),
        P(),
        P(),
        P(None, "tensor"),
        P("tensor"),
        P(None, "tensor"),
        P(None, "tensor"),
        P("tensor"),
        P("tensor", None),
        P(),
        P(),
        P(),
        P(None, "tensor"),
        P("tensor"),
        P("tensor", None),
        P(),
    )
    return jax.shard_map(
        functools.partial(shards, mesh.shape["tensor"]), mesh=mesh, in_specs=in_specs, out_specs=out_specs, check_vma=False)
```

```python
import functools
import math

import jax
import jax.numpy as jnp
from jax import lax
from jax.experimental import pallas as pl
from jax.experimental.pallas import tpu as pltpu
from jax.sharding import PartitionSpec as P

HEADS = 16
HD = 64
SHORT = 2048
EPSILON = 1e-05
LOG2E = math.log2(math.e)
F32 = jnp.float32
BF16 = jnp.bfloat16
NT = (((1,), (1,)), ((), ()))
NN = (((1,), (0,)), ((), ()))
TN = (((0,), (0,)), ((), ()))


def dot(lhs, rhs, dims=NN):
    return lax.dot_general(lhs, rhs, dims, preferred_element_type=F32)


def low(array):
    return array.astype(BF16)


def norm_stats(rows):
    center = jnp.mean(rows, axis=-1, keepdims=True)
    centered = rows - center
    inverse = lax.rsqrt(jnp.mean(centered * centered, axis=-1, keepdims=True) + EPSILON)
    return centered * inverse, inverse


def norm_pull(grad, normal, inverse):
    grad_mean = jnp.mean(grad, axis=-1, keepdims=True)
    dot_mean = jnp.mean(grad * normal, axis=-1, keepdims=True)
    return inverse * (grad - grad_mean - normal * dot_mean)


def lanes(count):
    return lax.broadcasted_iota(jnp.int32, (count, 128), 1)


def places(count, first):
    return lax.broadcasted_iota(jnp.int32, (count, 128), 0) + first


def widen(head):
    return jnp.concatenate([head.astype(F32), jnp.zeros((head.shape[0], HD), F32)], axis=1)


def split3(value):
    high = low(value).astype(F32)
    middle = low(value - high).astype(F32)
    return high, middle, value - high - middle


def pick3(index, parts):
    return jnp.where(index == 0, parts[0], jnp.where(index == 1, parts[1], parts[2]))


def key_columns(head, first):
    count = head.shape[0]
    lane, place = lanes(count), places(count, first)
    coarse = ((place >> 6) << 6).astype(F32)
    fine = (place & 63).astype(F32)
    wall = jnp.where(place < SHORT, -1e30, 0.0)
    extra = jnp.where(lane < 73, -1.0, jnp.where(lane == 73, wall, 0.0))
    extra = jnp.where(lane < 67, coarse, jnp.where(lane < 70, fine, extra))
    return low(jnp.where(lane < HD, widen(head), extra))


def query_columns(head, first, slope, apart, log_total=None):
    count = head.shape[0]
    lane, place = lanes(count), places(count, first)
    extra = pick3(jnp.where(lane < 67, lane - 64, lane - 67), split3(slope))
    extra = jnp.where(lane < 70, extra, 0.0)
    if log_total is not None:
        extra = jnp.where((lane >= 70) & (lane < 73), pick3(lane - 70, split3(log_total)), extra)
    extra = jnp.where(lane == 73, jnp.where(place >= SHORT, apart, 0.0), extra)
    return low(jnp.where(lane < HD, widen(head), extra))


def ones_columns(head, count):
    lane = lanes(head.shape[0])
    return low(jnp.where(lane < HD, widen(head), jnp.where(lane < HD + count, 1.0, 0.0)))


def grad_columns(head, shift):
    lane = lanes(head.shape[0])
    extra = jnp.where(lane < 67, pick3(lane - 64, split3(shift)), 0.0)
    return low(jnp.where(lane < HD, widen(head), extra))


def each_chunk(me, slots, rows, body):
    chunk = min(rows, 512)
    for slot in range(slots):
        home = (me ^ slot) * rows

        @pl.loop(0, rows // chunk)
        def _(step):
            offset = pl.multiple_of(step * chunk, chunk)
            body(slot, pl.ds(offset, chunk), pl.ds(slot * rows + offset, chunk), home + offset)


def attend_kernel(
    me_ref, apart_ref, slope_ref, q_ref, k_ref, v_ref, o_ref, lse_ref, qa, ka, va, *, slots, pair, tile
):
    me = me_ref[0]
    total = q_ref.shape[0]
    rows = total // slots
    chunk = min(rows, 512)
    apart = apart_ref[0].astype(F32)

    def prepare(slot, inner, spot, place):
        place = pl.multiple_of(place, chunk)
        home = pl.ds(place, chunk)
        for s in range(pair):
            cols = slice(s * HD, (s + 1) * HD)
            qa[s, home, :] = query_columns(q_ref[spot, cols], place, slope_ref[s], apart)
            ka[s, home, :] = key_columns(k_ref[spot, cols], place)
            va[s, home, :] = ones_columns(v_ref[spot, cols], 1)

    each_chunk(me, slots, rows, prepare)
    causal = lax.broadcasted_iota(jnp.int32, (tile, tile), 1) <= lax.broadcasted_iota(
        jnp.int32, (tile, tile), 0
    )
    piece = min(rows, tile)

    def query_tile(index, _):
        first = pl.multiple_of(index * tile, tile)
        queries = [qa[s, pl.ds(first, tile), :] for s in range(pair)]

        def step(at, carry, diagonal):
            after = []
            for s in range(pair):
                top, mix = carry[s]
                scores = dot(queries[s], ka[s, pl.ds(at, tile), :], NT)
                if diagonal:
                    scores = jnp.where(causal, scores, -1e30)
                higher = jnp.maximum(top, jnp.max(scores, axis=1, keepdims=True))
                weights = low(jnp.exp2(scores - higher))
                mix = mix * jnp.exp2(top - higher) + dot(weights, va[s, pl.ds(at, tile), :])
                after.append((higher, mix))
            return tuple(after)

        carry = tuple(
            (jnp.full((tile, 1), -1e38, F32), jnp.zeros((tile, 128), F32)) for _ in range(pair)
        )
        carry = step(first, carry, True)
        carry = lax.fori_loop(
            0, index, lambda at, held: step(pl.multiple_of(at * tile, tile), held, False), carry
        )
        outs = []
        for s in range(pair):
            top, mix = carry[s]
            weight = mix[:, HD : HD + 1]
            outs.append(mix[:, :HD] * (1.0 / weight))
            lse_ref[s, 0, pl.ds(first, tile)] = (top + jnp.log2(weight))[:, 0]
        out = low(jnp.concatenate(outs, axis=1))
        for part in range(tile // piece):
            block = (index * (tile // piece) + part) // (rows // piece)
            offset = first + part * piece - block * rows
            spot = pl.multiple_of((block ^ me) * rows + offset, piece)
            o_ref[pl.ds(spot, piece), :] = out[part * piece : (part + 1) * piece]
        return 0

    lax.fori_loop(0, total // tile, query_tile, 0)


def attend(me, apart, slopes, queries, key_rows, values, slots, group, tile=1024):
    total, width = queries.shape
    pair = min(2, width // HD)
    cols = pair * HD
    spec = pl.BlockSpec((total, cols), lambda g: (0, group))
    scalars = pl.BlockSpec(memory_space=pltpu.SMEM)
    return pl.pallas_call(
        functools.partial(attend_kernel, slots=slots, pair=pair, tile=tile),
        grid=(1,),
        in_specs=[scalars] * 3 + [spec] * 3,
        out_specs=[
            pl.BlockSpec((total, cols), lambda g: (0, 0)),
            pl.BlockSpec((pair, 1, total), lambda g: (0, 0, 0)),
        ],
        out_shape=[
            jax.ShapeDtypeStruct((total, cols), BF16),
            jax.ShapeDtypeStruct((pair, 1, total), F32),
        ],
        scratch_shapes=[pltpu.VMEM((pair, total, 128), BF16)] * 3,
        compiler_params=pltpu.CompilerParams(vmem_limit_bytes=56 << 20),
        cost_estimate=pl.CostEstimate(
            flops=pair * 1100 * total * total, transcendentals=0, bytes_accessed=8 * total * cols
        ),
        name="attend",
    )(me, apart, slopes[group * pair : (group + 1) * pair], queries, key_rows, values)


def attend_back_kernel(*refs, slots, pair, tile, key_tile):
    me_ref, apart_ref, slope_ref, q_ref, k_ref, v_ref, o_ref, lse_ref = refs[:8]
    g_refs = refs[8 : 8 + slots]
    out_ref, qa, ka, va, ga, kt, dq_sum = refs[8 + slots :]
    cols = pair * HD
    me = me_ref[0]
    total = q_ref.shape[0]
    rows = total // slots
    chunk = min(rows, 512)
    apart = apart_ref[0].astype(F32)

    def prepare(slot, inner, spot, place):
        place = pl.multiple_of(place, chunk)
        home = pl.ds(place, chunk)
        for s in range(pair):
            mine = slice(s * HD, (s + 1) * HD)
            log_total = lse_ref[s, :, home].T
            qa[s, home, :] = query_columns(q_ref[spot, mine], place, slope_ref[s], apart, log_total)
            keys = key_columns(k_ref[spot, mine], place)
            ka[s, home, :] = keys
            kt[s, :, home] = low(keys.astype(F32).T)
            va[s, home, :] = ones_columns(v_ref[spot, mine], 3)
            grad = g_refs[slot][inner, mine]
            row_dot = jnp.sum(
                grad.astype(F32) * o_ref[spot, mine].astype(F32), axis=1, keepdims=True
            )
            ga[s, home, :] = grad_columns(grad, -row_dot)
            dq_sum[s, :, home] = jnp.zeros((128, chunk), F32)

    each_chunk(me, slots, rows, prepare)
    causal = lax.broadcasted_iota(jnp.int32, (key_tile, key_tile), 0) <= lax.broadcasted_iota(
        jnp.int32, (key_tile, key_tile), 1
    )
    piece = min(rows, key_tile)

    def place_of(place, size):
        block = place // rows
        return pl.multiple_of((block ^ me) * rows + (place - block * rows), size)

    def keys_tile(index, _):
        first = pl.multiple_of(index * key_tile, key_tile)
        here = pl.ds(first, key_tile)

        def step(at, carry, diagonal, width):
            after = []
            for s in range(pair):
                dk, dv = carry[s]
                there = pl.ds(at, width)
                queries, grads = qa[s, there, :], ga[s, there, :]
                probs = jnp.exp2(dot(ka[s, here, :], queries, NT))
                if diagonal:
                    probs = jnp.where(causal, probs, 0.0)
                dv = dv + dot(low(probs), grads)
                score_grad = low(probs * dot(va[s, here, :], grads, NT))
                dk = dk + dot(score_grad, queries)
                dq_sum[s, :, there] += dot(kt[s, :, here], score_grad)
                after.append((dk, dv))
            return tuple(after)

        zeros = jnp.zeros((key_tile, 128), F32)
        carry = step(first, tuple((zeros, zeros) for _ in range(pair)), True, key_tile)
        start = first + key_tile
        short = jnp.minimum((-start) % tile, total - start) // key_tile
        if tile > key_tile:
            carry = lax.fori_loop(
                0,
                short,
                lambda at, held: step(
                    pl.multiple_of(start + at * key_tile, key_tile), held, False, key_tile
                ),
                carry,
            )
            start = start + short * key_tile
        carry = lax.fori_loop(
            0,
            (total - start) // tile,
            lambda at, held: step(
                pl.multiple_of(start + at * tile, min(tile, key_tile)), held, False, tile
            ),
            carry,
        )
        dk = low(jnp.concatenate([held[0][:, :HD] * (1.0 / LOG2E) for held in carry], axis=1))
        dv = low(jnp.concatenate([held[1][:, :HD] for held in carry], axis=1))
        for part in range(key_tile // piece):
            spot = pl.ds(place_of(first + part * piece, piece), piece)
            out_ref[spot, cols : 2 * cols] = dk[part * piece : (part + 1) * piece]
            out_ref[spot, 2 * cols :] = dv[part * piece : (part + 1) * piece]
        return 0

    lax.fori_loop(0, total // key_tile, keys_tile, 0)

    def finish(slot, inner, spot, place):
        home = pl.ds(pl.multiple_of(place, chunk), chunk)
        joined = jnp.concatenate([dq_sum[s, :HD, home] for s in range(pair)], axis=0)
        out_ref[spot, :cols] = low(joined.T * HD**-0.5)

    each_chunk(me, slots, rows, finish)


def attend_back(
    me, apart, slopes, queries, key_rows, values, mixed, log_total, grads, group, tile=1024, key_tile=512
):
    slots = len(grads)
    total, width = queries.shape
    pair = min(2, width // HD)
    cols = pair * HD
    spec = pl.BlockSpec((total, cols), lambda g: (0, group))
    out_spec = pl.BlockSpec((total, cols), lambda g: (0, 0))
    scalars = pl.BlockSpec(memory_space=pltpu.SMEM)
    return pl.pallas_call(
        functools.partial(
            attend_back_kernel, slots=slots, pair=pair, tile=tile, key_tile=key_tile
        ),
        grid=(1,),
        in_specs=[scalars] * 3
        + [spec] * 3
        + [out_spec, pl.BlockSpec((pair, 1, total), lambda g: (0, 0, 0))]
        + [pl.BlockSpec((total // slots, cols), lambda g: (0, group))] * slots,
        out_specs=pl.BlockSpec((total, 3 * cols), lambda g: (0, 0)),
        out_shape=jax.ShapeDtypeStruct((total, 3 * cols), BF16),
        scratch_shapes=[pltpu.VMEM((pair, total, 128), BF16)] * 4
        + [pltpu.VMEM((pair, 128, total), BF16), pltpu.VMEM((pair, 128, total), F32)],
        compiler_params=pltpu.CompilerParams(vmem_limit_bytes=60 << 20),
        cost_estimate=pl.CostEstimate(
            flops=pair * 2200 * total * total, transcendentals=0, bytes_accessed=16 * total * cols
        ),
        name="attend_back",
    )(
        me,
        apart,
        slopes[group * pair : (group + 1) * pair],
        queries,
        key_rows,
        values,
        mixed,
        log_total,
        *grads,
    )


def whole(shape):
    return pl.BlockSpec(shape, lambda i: (0,) * len(shape))


def choose(slot, refs, first=0):
    rows = refs[0][...]
    for at, ref in enumerate(refs[1:], 1):
        rows = jnp.where(slot == first + at, ref[...], rows)
    return rows


def slot_specs(count, per, block, width, order=lambda i: i):
    return [
        pl.BlockSpec(
            (block, width), lambda i, at=at: (jnp.clip(order(i) - at * per, 0, per - 1), 0)
        )
        for at in range(count)
    ]


def kernel_params(mib=56):
    return pltpu.CompilerParams(vmem_limit_bytes=mib << 20)


def project_kernel(*refs, count, per):
    x_refs = refs[:count]
    gain_ref, shift_ref = refs[count : count + 2]
    wq_ref, wk_ref, wv_ref, qb_ref, vb_ref = refs[count + 2 : count + 7]
    normed_ref, q_ref, k_ref, v_ref = refs[-4:]
    x = choose(pl.program_id(0) // per, x_refs).astype(F32)
    normed = low(norm_stats(x)[0] * gain_ref[...].astype(F32) + shift_ref[...].astype(F32))
    normed_ref[...] = normed
    q_ref[...] = low((dot(normed, wq_ref[...]) + qb_ref[...].astype(F32)) * (LOG2E * HD**-0.5))
    k_ref[...] = low(dot(normed, wk_ref[...]))
    v_ref[...] = low(dot(normed, wv_ref[...]) + vb_ref[...].astype(F32))


def project(x_parts, vectors, weights, biases, held, total):
    count = len(x_parts)
    rows, width = x_parts[0].shape
    block = min(rows, 512)
    per = rows // block
    first = 0 if held is None else count * per
    out_shape = [jax.ShapeDtypeStruct((total, width), BF16)] + [
        jax.ShapeDtypeStruct((total, weight.shape[1]), BF16) for weight in weights
    ]
    held = [] if held is None else list(held)
    inputs = [*x_parts, *[v[None] for v in vectors], *weights, *[v[None] for v in biases]]
    return pl.pallas_call(
        functools.partial(project_kernel, count=count, per=per),
        grid=(count * per,),
        in_specs=slot_specs(count, per, block, width)
        + [whole((1, width))] * 2
        + [whole(weight.shape) for weight in weights]
        + [whole((1, v.shape[0])) for v in biases]
        + [pl.BlockSpec(memory_space=pl.ANY)] * len(held),
        out_specs=[
            pl.BlockSpec((block, shape.shape[1]), lambda i: (i + first, 0)) for shape in out_shape
        ],
        out_shape=out_shape,
        input_output_aliases={len(inputs) + at: at for at in range(len(held))},
        compiler_params=kernel_params(),
        cost_estimate=pl.CostEstimate(
            flops=6 * count * rows * width * weights[0].shape[1],
            transcendentals=0,
            bytes_accessed=count * rows * width * 6,
        ),
        name="project",
    )(*inputs, *held)


def post_kernel(*refs, slots, groups, per):
    mixed_refs = refs[: slots * groups]
    x_refs = refs[slots * groups : slots * groups + slots]
    weight_ref, bias_ref, gain_ref, shift_ref, post_ref, residual_ref = refs[-6:]
    blocks = pl.num_programs(0)
    at = (pl.program_id(0) + blocks // 2) % blocks
    mixed = jnp.concatenate([ref[...] for ref in mixed_refs], axis=1)
    x = choose(at // per, x_refs).astype(F32)
    residual = x + dot(mixed, weight_ref[...]) + bias_ref[...].astype(F32)
    normal, _ = norm_stats(residual)
    post_ref[...] = low(normal * gain_ref[...].astype(F32) + shift_ref[...].astype(F32))

    @pl.when(at < per)
    def _():
        residual_ref[...] = residual


def post_norm(mixed, x_parts, weight, bias, gain, shift):
    slots, groups = len(mixed), len(mixed[0])
    rows, width = x_parts[0].shape
    total = slots * rows
    block = min(rows, 512)
    per = rows // block
    blocks = total // block
    order = lambda i: (i + blocks // 2) % blocks
    specs = []
    for slot in range(slots):
        for part in mixed[slot]:
            specs.append(
                pl.BlockSpec(
                    (block, part.shape[1]),
                    lambda i, slot=slot: (
                        ((order(i) // per) ^ slot) * per + order(i) % per,
                        0,
                    ),
                )
            )
    return pl.pallas_call(
        functools.partial(post_kernel, slots=slots, groups=groups, per=per),
        grid=(blocks,),
        in_specs=specs
        + slot_specs(slots, per, block, width, order)
        + [whole(weight.shape)]
        + [whole((1, width))] * 3,
        out_specs=[
            pl.BlockSpec((block, width), lambda i: (order(i), 0)),
            pl.BlockSpec(
                (block, width), lambda i: (jnp.clip(i - blocks // 2, 0, per - 1), 0)
            ),
        ],
        out_shape=[
            jax.ShapeDtypeStruct((total, width), BF16),
            jax.ShapeDtypeStruct((rows, width), F32),
        ],
        compiler_params=kernel_params(),
        cost_estimate=pl.CostEstimate(
            flops=2 * total * width * width, transcendentals=0, bytes_accessed=6 * total * width
        ),
        name="post_norm",
    )(
        *[part for parts in mixed for part in parts],
        *x_parts,
        weight,
        bias[None],
        gain[None],
        shift[None],
    )


def feed_kernel(*refs, count, per, held):
    post_ref = refs[0]
    cot_refs = refs[1 : 1 + count]
    up_ref, down_ref, bias_ref = refs[1 + count : 4 + count]
    active_ref, grad_ref, cot_ref, sum_ref = refs[4 + count + held : 8 + count + held]
    back_refs = refs[8 + count + held :]
    slot = pl.program_id(0) // per

    @pl.when(pl.program_id(0) == 0)
    def _():
        sum_ref[...] = jnp.zeros_like(sum_ref)

    post = post_ref[...]
    cot = choose(slot, cot_refs)
    cot_ref[...] = cot
    units = active_ref.shape[1]
    chunk = min(512, units)
    scale, cubic = math.sqrt(2 / math.pi), 0.044715
    for first in range(0, units, chunk):
        cols = slice(first, first + chunk)
        hidden = dot(post, up_ref[:, cols]) + bias_ref[:, cols].astype(F32)
        act_grad = dot(cot, down_ref[cols, :], NT)
        square = hidden * hidden
        curve = jnp.tanh(hidden * (scale + scale * cubic * square))
        half = 0.5 + 0.5 * curve
        active_ref[:, cols] = low(hidden * half)
        slope = half + (0.5 * hidden) * (1.0 - curve * curve) * (
            scale + 3 * scale * cubic * square
        )
        grad = low(act_grad * slope)
        grad_ref[:, cols] = grad
        sum_ref[:, cols] += jnp.sum(grad.astype(F32), axis=0, keepdims=True)
    back = low(dot(grad_ref[...], up_ref[...], NT))
    for at, back_ref in enumerate(back_refs):

        @pl.when(slot == at)
        def _():
            back_ref[...] = back


def feed(post_all, cot_parts, up, up_bias, down, half, held):
    count = len(cot_parts)
    rows, width = cot_parts[0].shape
    total, units = post_all.shape[0], up.shape[1]
    block = min(rows, 512)
    per = rows // block
    first = half * count * per
    tall = lambda cols: pl.BlockSpec((block, cols), lambda i: (i + first, 0))
    held = [] if held is None else list(held)
    inputs = [post_all, *cot_parts, up, down, up_bias[None]]
    return pl.pallas_call(
        functools.partial(feed_kernel, count=count, per=per, held=len(held)),
        grid=(count * per,),
        in_specs=[tall(width)]
        + slot_specs(count, per, block, width)
        + [whole(up.shape), whole(down.shape), whole((1, units))]
        + [pl.BlockSpec(memory_space=pl.ANY)] * len(held),
        out_specs=[tall(units), tall(units), tall(width), whole((1, units))]
        + slot_specs(count, per, block, width),
        out_shape=[
            jax.ShapeDtypeStruct((total, units), BF16),
            jax.ShapeDtypeStruct((total, units), BF16),
            jax.ShapeDtypeStruct((total, width), BF16),
            jax.ShapeDtypeStruct((1, units), F32),
        ]
        + [jax.ShapeDtypeStruct((rows, width), BF16)] * count,
        input_output_aliases={len(inputs) + at: at for at in range(len(held))},
        compiler_params=kernel_params(),
        cost_estimate=pl.CostEstimate(
            flops=6 * count * rows * width * units,
            transcendentals=0,
            bytes_accessed=count * rows * width * 12,
        ),
        name="feed",
    )(*inputs, *held)


def resid_kernel(*refs, terms, slots):
    term_refs = refs[:terms]
    residual_ref, cot_ref, gain_ref, weight_ref = refs[terms : terms + 4]
    grad_ref, low_ref, sums_ref = refs[terms + 4 : terms + 7]
    part_refs = refs[terms + 7 :]

    @pl.when(pl.program_id(0) == 0)
    def _():
        sums_ref[...] = jnp.zeros_like(sums_ref)

    post_grad = term_refs[0][...].astype(F32)
    for ref in term_refs[1:]:
        post_grad = post_grad + ref[...].astype(F32)
    cot = cot_ref[...].astype(F32)
    normal, inverse = norm_stats(residual_ref[...])
    grad = cot + norm_pull(post_grad * gain_ref[...].astype(F32), normal, inverse)
    grad_ref[...] = grad
    grad_low = low(grad)
    low_ref[...] = grad_low
    for at, value in enumerate((cot, grad, post_grad * normal, post_grad)):
        sums_ref[at : at + 1, :] += jnp.sum(value, axis=0, keepdims=True)
    mixed_grad = low(dot(grad_low, weight_ref[...], NT))
    cols = part_refs[0].shape[1]
    for slot, ref in enumerate(part_refs):
        ref[...] = mixed_grad[:, slot * cols : (slot + 1) * cols]


def resid_step(terms, residual, cotangent, gain, weight, slots):
    rows, width = residual.shape
    block = min(rows, 256)
    tall = lambda cols: pl.BlockSpec((block, cols), lambda i: (i, 0))
    cols = weight.shape[0] // slots
    return pl.pallas_call(
        functools.partial(resid_kernel, terms=len(terms), slots=slots),
        grid=(rows // block,),
        in_specs=[tall(width)] * (len(terms) + 2) + [whole((1, width)), whole(weight.shape)],
        out_specs=[tall(width), tall(width), whole((8, width))] + [tall(cols)] * slots,
        out_shape=[
            jax.ShapeDtypeStruct((rows, width), F32),
            jax.ShapeDtypeStruct((rows, width), BF16),
            jax.ShapeDtypeStruct((8, width), F32),
        ]
        + [jax.ShapeDtypeStruct((rows, cols), BF16)] * slots,
        compiler_params=kernel_params(),
        cost_estimate=pl.CostEstimate(
            flops=2 * rows * width * width, transcendentals=0, bytes_accessed=20 * rows * width
        ),
        name="resid_step",
    )(*terms, residual, cotangent, gain[None], weight)


def unproject_kernel(*refs, groups, per):
    grad_refs, weight_refs, out_refs = refs[:groups], refs[groups : 2 * groups], refs[2 * groups :]
    slot = pl.program_id(0) // per
    total = dot(grad_refs[0][...], weight_refs[0][...], NT)
    for grad_ref, weight_ref in zip(grad_refs[1:], weight_refs[1:]):
        total = total + dot(grad_ref[...], weight_ref[...], NT)
    total = low(total)
    for at, ref in enumerate(out_refs):

        @pl.when(slot == at)
        def _():
            ref[...] = total


def unproject(grads, weights, rows, count, half):
    width = weights[0].shape[0]
    block = min(rows, 512)
    per = rows // block
    first = half * count * per
    return pl.pallas_call(
        functools.partial(unproject_kernel, groups=len(grads), per=per),
        grid=(count * per,),
        in_specs=[
            pl.BlockSpec((block, grad.shape[1]), lambda i: (i + first, 0)) for grad in grads
        ]
        + [whole(weight.shape) for weight in weights],
        out_specs=slot_specs(count, per, block, width),
        out_shape=[jax.ShapeDtypeStruct((rows, width), BF16)] * count,
        compiler_params=kernel_params(),
        cost_estimate=pl.CostEstimate(
            flops=2 * count * rows * width * len(grads) * weights[0].shape[1],
            transcendentals=0,
            bytes_accessed=count * rows * width * 4,
        ),
        name="unproject",
    )(*grads, *weights)


def input_kernel(*refs, terms):
    x_ref, resid_ref, gain_ref, out_ref = refs[terms:]
    grad = refs[0][...].astype(F32)
    for ref in refs[1:terms]:
        grad = grad + ref[...].astype(F32)
    normal, inverse = norm_stats(x_ref[...].astype(F32))
    out_ref[...] = resid_ref[...] + norm_pull(grad * gain_ref[...].astype(F32), normal, inverse)


def input_step(terms, layer_input, resid_grad, gain):
    rows, width = resid_grad.shape
    block = min(rows, 256)
    tall = pl.BlockSpec((block, width), lambda i: (i, 0))
    return pl.pallas_call(
        functools.partial(input_kernel, terms=len(terms)),
        grid=(rows // block,),
        in_specs=[tall] * (len(terms) + 2) + [whole((1, width))],
        out_specs=tall,
        out_shape=jax.ShapeDtypeStruct((rows, width), F32),
        compiler_params=kernel_params(),
        cost_estimate=pl.CostEstimate(
            flops=20 * rows * width, transcendentals=0, bytes_accessed=16 * rows * width
        ),
        name="input_step",
    )(*terms, layer_input, resid_grad, gain[None])


def shards(
    slots,
    streams,
    layer_input,
    row_ids,
    input_gain,
    input_shift,
    query_weight,
    query_bias,
    key_weight,
    value_weight,
    value_bias,
    dense_weight,
    dense_bias,
    post_gain,
    post_shift,
    up_weight,
    up_bias,
    down_weight,
    down_bias,
    cotangent,
):
    me = lax.axis_index("tensor")
    me_word = me.astype(jnp.int32)[None]
    rows = layer_input.shape[0]
    head_cols = query_weight.shape[1]
    head_count = head_cols // HD
    groups = max(1, head_count // 2)
    bits = [1 << level for level in range(slots.bit_length() - 1)]
    after = lambda array, *others: lax.optimization_barrier((array, *others))[0]

    def swap(array, mask):
        return lax.ppermute(array, "tensor", [(i, i ^ mask) for i in range(slots)])

    def gather(array):
        held = {0: array}
        for bit in reversed(bits):
            held.update({slot ^ bit: swap(part, bit) for slot, part in held.items()})
        return [held[slot] for slot in range(slots)]

    def blocks(array):
        return [array[slot * rows : (slot + 1) * rows] for slot in range(slots)]

    def swap_data(array, mask):
        return lax.ppermute(array, "dp", [(i, i ^ mask) for i in range(streams)])

    def scatter_terms(parts):
        held, terms = dict(enumerate(parts)), [parts[0]]
        for bit in bits:
            come = {slot ^ bit: swap(part, bit) for slot, part in held.items() if slot & bit}
            terms.append(come.pop(0))
            held = {
                slot: low(held[slot].astype(F32) + part.astype(F32)) for slot, part in come.items()
            }
        return terms

    def add_up(terms):
        return functools.reduce(lambda sum_now, term: sum_now + term.astype(F32), terms[1:], terms[0].astype(F32))

    def total_of(shared, own):
        for bit in bits:
            shared = shared + swap(shared, bit)
        flat = jnp.concatenate([shared.reshape(-1), own])
        pad = -flat.shape[0] % 1024
        flat = jnp.pad(flat, (0, pad)).reshape(-1, 1024)
        for level in range(streams.bit_length() - 1):
            flat = flat + swap_data(flat, 1 << level)
        flat = flat.reshape(-1)
        return flat[: shared.size].reshape(shared.shape), flat[shared.size :][: own.shape[0]]

    x_parts = gather(layer_input)
    cot_own = after(cotangent, x_parts[-1])
    dense_parts = gather(after(dense_weight, x_parts[-1]))
    cot_parts = gather(cot_own)

    total = slots * rows
    half = slots // 2
    gain, shift = input_gain.astype(F32), input_shift.astype(F32)
    norm_vectors = (input_gain, input_shift)
    weights = (query_weight, key_weight, value_weight)
    biases = (query_bias, value_bias)
    held = project(x_parts[:half], norm_vectors, weights, biases, None, total)
    normed, queries, key_rows, values = project(
        x_parts[half:], norm_vectors, weights, biases, held, total
    )
    heads = me * head_count + jnp.arange(head_count)
    slopes = jnp.exp2(-8.0 * (heads + 1).astype(F32) / HEADS) * LOG2E
    apart = (row_ids[:1] != row_ids[SHORT : SHORT + 1]).astype(jnp.int32)

    mixed_own, log_totals, mixed_parts = [], [], []
    for group in range(groups):
        mixed, log_total = attend(
            me_word, apart, slopes, queries, key_rows, values, slots, group
        )
        mixed_own.append(mixed)
        log_totals.append(log_total)
        mixed_parts.append(gather(mixed))
    mixed_all = [[mixed_parts[group][slot] for group in range(groups)] for slot in range(slots)]
    dense_all = jnp.concatenate(dense_parts, axis=0)
    post_all, residual = post_norm(
        mixed_all, x_parts, dense_all, dense_bias, post_gain, post_shift
    )

    far = feed(post_all, cot_parts[half:], up_weight, up_bias, down_weight, 1, None)
    near = feed(post_all, cot_parts[:half], up_weight, up_bias, down_weight, 0, far[:3])
    active, hidden_grad, cot_all = near[:3]
    up_bias_part = far[3][0] + near[3][0]
    post_terms = scatter_terms([*near[4:], *far[4:]])
    up_part = low(dot(post_all, hidden_grad, TN))
    down_part = low(dot(active, cot_all, TN))
    up_sum, down_sum = lax.psum((up_part, down_part), "dp")

    resid_grad, attended_grad, row_sums, *mixed_grads = resid_step(
        post_terms, residual, cotangent, post_gain, dense_all, slots
    )
    mixed_grads = [swap(part, slot) if slot else part for slot, part in enumerate(mixed_grads)]

    ffn_part = low(dot(active, down_weight))
    ffn_terms = scatter_terms(blocks(ffn_part))
    layer_output = low(residual + add_up(ffn_terms) + down_bias.astype(F32))
    mixed_rows = jnp.concatenate(
        [
            part[slot * rows : (slot + 1) * rows]
            for slot, parts in enumerate(mixed_all)
            for part in parts
        ],
        axis=1,
    )
    dense_part = low(dot(mixed_rows, attended_grad, TN))
    dense_part = low(
        add_up(
            scatter_terms(
                [dense_part[slot * head_cols : (slot + 1) * head_cols] for slot in range(slots)]
            )
        )
    )
    row_sums, up_bias_grad = total_of(row_sums[:4], up_bias_part)

    cols = head_cols // groups
    pick = lambda array, group: array[:, group * cols : (group + 1) * cols]
    group_weights = [
        jnp.concatenate([pick(weight, group) for weight in weights], axis=1)
        for group in range(groups)
    ]
    head_grads, group_parts, group_sums = [], [], []
    chain = (up_sum, down_sum)
    for group in range(groups):
        grads = mixed_grads if not group else lax.optimization_barrier((*mixed_grads, head_grads[-1]))[:-1]
        head_grads.append(
            attend_back(
                me_word,
                apart,
                slopes,
                queries,
                key_rows,
                values,
                mixed_own[group],
                log_totals[group],
                grads,
                group,
            )
        )
        group_parts.append(dot(normed, head_grads[-1], TN))
        sending = (low(group_parts[-1]),) + ((dense_part,) if not group else ())
        sending = lax.optimization_barrier((*sending, *chain))
        chain = sending[-len(chain) :]
        sums = lax.psum(sending[: -len(chain)], "dp")
        if not group:
            up_sum, down_sum, dense_sum = *chain, sums[1]
        group_sums.append(sums[0])
        chain = (sums[0],)
    far = unproject(head_grads, group_weights, rows, half, 1)
    near = unproject(head_grads, group_weights, rows, half, 0)
    normed_terms = scatter_terms([*near, *far])

    shift_part, gain_part, proj_sums = 0.0, 0.0, []
    for weight, grad, part in zip(group_weights, head_grads, group_parts):
        proj_sums.append(jnp.sum(grad.astype(F32), axis=0))
        weight = weight.astype(F32)
        shift_part = shift_part + jnp.sum(weight * proj_sums[-1], axis=1)
        gain_part = gain_part + jnp.sum(weight * part, axis=1)
    gain_part = (gain_part - shift * shift_part) / gain
    norm_sums, bias_sums = total_of(
        jnp.stack([gain_part, shift_part]),
        jnp.concatenate([part[:cols] for part in proj_sums] + [part[2 * cols :] for part in proj_sums]),
    )
    weight_grads = [
        jnp.concatenate([array[:, kind * cols : (kind + 1) * cols] for array in group_sums], axis=1).astype(F32)
        for kind in range(3)
    ]
    input_grad = input_step(normed_terms, layer_input, resid_grad, input_gain)
    return (
        layer_output,
        input_grad,
        norm_sums[0],
        norm_sums[1],
        weight_grads[0],
        bias_sums[:head_cols],
        weight_grads[1],
        weight_grads[2],
        bias_sums[head_cols:],
        dense_sum.astype(F32),
        row_sums[1],
        row_sums[2],
        row_sums[3],
        up_sum.astype(F32),
        up_bias_grad,
        down_sum.astype(F32),
        row_sums[0],
    )


def solution(mesh):
    in_specs = (
        P(("dp", "tensor"), None),
        P("dp"),
        P(),
        P(),
        P(None, "tensor"),
        P("tensor"),
        P(None, "tensor"),
        P(None, "tensor"),
        P("tensor"),
        P("tensor", None),
        P(),
        P(),
        P(),
        P(None, "tensor"),
        P("tensor"),
        P("tensor", None),
        P(),
        P(("dp", "tensor"), None),
    )
    out_specs = (
        P(("dp", "tensor"), None),
        P(("dp", "tensor"), None),
        P(),
        P(),
        P(None, "tensor"),
        P("tensor"),
        P(None, "tensor"),
        P(None, "tensor"),
        P("tensor"),
        P("tensor", None),
        P(),
        P(),
        P(),
        P(None, "tensor"),
        P("tensor"),
        P("tensor", None),
        P(),
    )
    return jax.shard_map(
        functools.partial(shards, mesh.shape["tensor"], mesh.shape["dp"]), mesh=mesh, in_specs=in_specs, out_specs=out_specs, check_vma=False)
```

```python
import functools
import math

import jax
import jax.numpy as jnp
from jax import lax
from jax.experimental import pallas as pl
from jax.experimental.pallas import tpu as pltpu
from jax.sharding import PartitionSpec as P

HEADS = 16
HD = 64
SHORT = 2048
EPSILON = 1e-05
LOG2E = math.log2(math.e)
F32 = jnp.float32
BF16 = jnp.bfloat16
SMALL_COST = pl.CostEstimate(flops=1, transcendentals=0, bytes_accessed=1)
NT = (((1,), (1,)), ((), ()))
NN = (((1,), (0,)), ((), ()))
TN = (((0,), (0,)), ((), ()))


def dot(lhs, rhs, dims=NN):
    return lax.dot_general(lhs, rhs, dims, preferred_element_type=F32)


def low(array):
    return array.astype(BF16)


def norm_stats(rows):
    center = jnp.mean(rows, axis=-1, keepdims=True)
    centered = rows - center
    inverse = lax.rsqrt(jnp.mean(centered * centered, axis=-1, keepdims=True) + EPSILON)
    return centered * inverse, inverse


def norm_pull(grad, normal, inverse):
    grad_mean = jnp.mean(grad, axis=-1, keepdims=True)
    dot_mean = jnp.mean(grad * normal, axis=-1, keepdims=True)
    return inverse * (grad - grad_mean - normal * dot_mean)


def lanes(count):
    return lax.broadcasted_iota(jnp.int32, (count, 128), 1)


def places(count, first):
    return lax.broadcasted_iota(jnp.int32, (count, 128), 0) + first


def widen(head):
    return jnp.concatenate([head.astype(F32), jnp.zeros((head.shape[0], HD), F32)], axis=1)


def split3(value):
    high = low(value).astype(F32)
    middle = low(value - high).astype(F32)
    return high, middle, value - high - middle


def pick3(index, parts):
    return jnp.where(index == 0, parts[0], jnp.where(index == 1, parts[1], parts[2]))


def key_columns(head, first):
    count = head.shape[0]
    lane, place = lanes(count), places(count, first)
    coarse = ((place >> 6) << 6).astype(F32)
    fine = (place & 63).astype(F32)
    wall = jnp.where(place < SHORT, -1e30, 0.0)
    extra = jnp.where(lane < 73, -1.0, jnp.where(lane == 73, wall, 0.0))
    extra = jnp.where(lane < 67, coarse, jnp.where(lane < 70, fine, extra))
    return low(jnp.where(lane < HD, widen(head), extra))


def query_columns(head, first, slope, apart, log_total=None):
    count = head.shape[0]
    lane, place = lanes(count), places(count, first)
    extra = pick3(jnp.where(lane < 67, lane - 64, lane - 67), split3(slope))
    extra = jnp.where(lane < 70, extra, 0.0)
    if log_total is not None:
        extra = jnp.where((lane >= 70) & (lane < 73), pick3(lane - 70, split3(log_total)), extra)
    extra = jnp.where(lane == 73, jnp.where(place >= SHORT, apart, 0.0), extra)
    return low(jnp.where(lane < HD, widen(head), extra))


def ones_columns(head, count):
    lane = lanes(head.shape[0])
    return low(jnp.where(lane < HD, widen(head), jnp.where(lane < HD + count, 1.0, 0.0)))


def grad_columns(head, shift):
    lane = lanes(head.shape[0])
    extra = jnp.where(lane < 67, pick3(lane - 64, split3(shift)), 0.0)
    return low(jnp.where(lane < HD, widen(head), extra))


def each_chunk(me, slots, rows, body):
    chunk = min(rows, 512)
    for slot in range(slots):
        home = (me ^ slot) * rows

        @pl.loop(0, rows // chunk)
        def _(step):
            offset = pl.multiple_of(step * chunk, chunk)
            body(slot, pl.ds(offset, chunk), pl.ds(slot * rows + offset, chunk), home + offset)


def attend_kernel(
    me_ref, apart_ref, slope_ref, q_ref, k_ref, v_ref, o_ref, lse_ref, qa, ka, va, *, slots, pair, tile
):
    me = me_ref[0]
    total = q_ref.shape[0]
    rows = total // slots
    chunk = min(rows, 512)
    apart = apart_ref[0].astype(F32)

    def prepare(slot, inner, spot, place):
        place = pl.multiple_of(place, chunk)
        home = pl.ds(place, chunk)
        for s in range(pair):
            cols = slice(s * HD, (s + 1) * HD)
            qa[s, home, :] = query_columns(q_ref[spot, cols], place, slope_ref[s], apart)
            ka[s, home, :] = key_columns(k_ref[spot, cols], place)
            va[s, home, :] = ones_columns(v_ref[spot, cols], 1)

    each_chunk(me, slots, rows, prepare)
    causal = lax.broadcasted_iota(jnp.int32, (tile, tile), 1) <= lax.broadcasted_iota(
        jnp.int32, (tile, tile), 0
    )
    piece = min(rows, tile)

    def query_tile(index, _):
        first = pl.multiple_of(index * tile, tile)
        queries = [qa[s, pl.ds(first, tile), :] for s in range(pair)]

        def step(at, carry, diagonal):
            after = []
            for s in range(pair):
                top, mix = carry[s]
                scores = dot(queries[s], ka[s, pl.ds(at, tile), :], NT)
                if diagonal:
                    scores = jnp.where(causal, scores, -1e30)
                higher = jnp.maximum(top, jnp.max(scores, axis=1, keepdims=True))
                weights = low(jnp.exp2(scores - higher))
                mix = mix * jnp.exp2(top - higher) + dot(weights, va[s, pl.ds(at, tile), :])
                after.append((higher, mix))
            return tuple(after)

        carry = tuple(
            (jnp.full((tile, 1), -1e38, F32), jnp.zeros((tile, 128), F32)) for _ in range(pair)
        )
        carry = step(first, carry, True)
        carry = lax.fori_loop(
            0, index, lambda at, held: step(pl.multiple_of(at * tile, tile), held, False), carry
        )
        outs = []
        for s in range(pair):
            top, mix = carry[s]
            weight = mix[:, HD : HD + 1]
            outs.append(mix[:, :HD] * (1.0 / weight))
            lse_ref[s, 0, pl.ds(first, tile)] = (top + jnp.log2(weight))[:, 0]
        out = low(jnp.concatenate(outs, axis=1))
        for part in range(tile // piece):
            block = (index * (tile // piece) + part) // (rows // piece)
            offset = first + part * piece - block * rows
            spot = pl.multiple_of((block ^ me) * rows + offset, piece)
            o_ref[pl.ds(spot, piece), :] = out[part * piece : (part + 1) * piece]
        return 0

    lax.fori_loop(0, total // tile, query_tile, 0)


def attend(me, apart, slopes, queries, key_rows, values, slots, group, tile=1024):
    total, width = queries.shape
    pair = min(2, width // HD)
    cols = pair * HD
    spec = pl.BlockSpec((total, cols), lambda g: (0, group))
    scalars = pl.BlockSpec(memory_space=pltpu.SMEM)
    return pl.pallas_call(
        functools.partial(attend_kernel, slots=slots, pair=pair, tile=tile),
        grid=(1,),
        in_specs=[scalars] * 3 + [spec] * 3,
        out_specs=[
            pl.BlockSpec((total, cols), lambda g: (0, 0)),
            pl.BlockSpec((pair, 1, total), lambda g: (0, 0, 0)),
        ],
        out_shape=[
            jax.ShapeDtypeStruct((total, cols), BF16),
            jax.ShapeDtypeStruct((pair, 1, total), F32),
        ],
        scratch_shapes=[pltpu.VMEM((pair, total, 128), BF16)] * 3,
        compiler_params=pltpu.CompilerParams(vmem_limit_bytes=56 << 20),
        cost_estimate=SMALL_COST,
        name="attend",
    )(me, apart, slopes[group * pair : (group + 1) * pair], queries, key_rows, values)


def attend_back_kernel(*refs, slots, pair, tile, key_tile):
    me_ref, apart_ref, slope_ref, q_ref, k_ref, v_ref, o_ref, lse_ref = refs[:8]
    g_refs = refs[8 : 8 + slots]
    out_ref, qa, ka, va, ga, kt, dq_sum = refs[8 + slots :]
    cols = pair * HD
    me = me_ref[0]
    total = q_ref.shape[0]
    rows = total // slots
    chunk = min(rows, 512)
    apart = apart_ref[0].astype(F32)

    def prepare(slot, inner, spot, place):
        place = pl.multiple_of(place, chunk)
        home = pl.ds(place, chunk)
        for s in range(pair):
            mine = slice(s * HD, (s + 1) * HD)
            log_total = lse_ref[s, :, home].T
            qa[s, home, :] = query_columns(q_ref[spot, mine], place, slope_ref[s], apart, log_total)
            keys = key_columns(k_ref[spot, mine], place)
            ka[s, home, :] = keys
            kt[s, :, home] = low(keys.astype(F32).T)
            va[s, home, :] = ones_columns(v_ref[spot, mine], 3)
            grad = g_refs[slot][inner, mine]
            row_dot = jnp.sum(
                grad.astype(F32) * o_ref[spot, mine].astype(F32), axis=1, keepdims=True
            )
            ga[s, home, :] = grad_columns(grad, -row_dot)
            dq_sum[s, :, home] = jnp.zeros((128, chunk), F32)

    each_chunk(me, slots, rows, prepare)
    causal = lax.broadcasted_iota(jnp.int32, (key_tile, key_tile), 0) <= lax.broadcasted_iota(
        jnp.int32, (key_tile, key_tile), 1
    )
    piece = min(rows, key_tile)

    def place_of(place, size):
        block = place // rows
        return pl.multiple_of((block ^ me) * rows + (place - block * rows), size)

    def keys_tile(index, _):
        first = pl.multiple_of(index * key_tile, key_tile)
        here = pl.ds(first, key_tile)

        def step(at, carry, diagonal, width):
            after = []
            for s in range(pair):
                dk, dv = carry[s]
                there = pl.ds(at, width)
                queries, grads = qa[s, there, :], ga[s, there, :]
                probs = jnp.exp2(dot(ka[s, here, :], queries, NT))
                if diagonal:
                    probs = jnp.where(causal, probs, 0.0)
                dv = dv + dot(low(probs), grads)
                score_grad = low(probs * dot(va[s, here, :], grads, NT))
                dk = dk + dot(score_grad, queries)
                dq_sum[s, :, there] += dot(kt[s, :, here], score_grad)
                after.append((dk, dv))
            return tuple(after)

        zeros = jnp.zeros((key_tile, 128), F32)
        carry = step(first, tuple((zeros, zeros) for _ in range(pair)), True, key_tile)
        start = first + key_tile
        short = jnp.minimum((-start) % tile, total - start) // key_tile
        if tile > key_tile:
            carry = lax.fori_loop(
                0,
                short,
                lambda at, held: step(
                    pl.multiple_of(start + at * key_tile, key_tile), held, False, key_tile
                ),
                carry,
            )
            start = start + short * key_tile
        carry = lax.fori_loop(
            0,
            (total - start) // tile,
            lambda at, held: step(
                pl.multiple_of(start + at * tile, min(tile, key_tile)), held, False, tile
            ),
            carry,
        )
        dk = low(jnp.concatenate([held[0][:, :HD] * (1.0 / LOG2E) for held in carry], axis=1))
        dv = low(jnp.concatenate([held[1][:, :HD] for held in carry], axis=1))
        for part in range(key_tile // piece):
            spot = pl.ds(place_of(first + part * piece, piece), piece)
            out_ref[spot, cols : 2 * cols] = dk[part * piece : (part + 1) * piece]
            out_ref[spot, 2 * cols :] = dv[part * piece : (part + 1) * piece]
        return 0

    lax.fori_loop(0, total // key_tile, keys_tile, 0)

    def finish(slot, inner, spot, place):
        home = pl.ds(pl.multiple_of(place, chunk), chunk)
        joined = jnp.concatenate([dq_sum[s, :HD, home] for s in range(pair)], axis=0)
        out_ref[spot, :cols] = low(joined.T * HD**-0.5)

    each_chunk(me, slots, rows, finish)


def attend_back(
    me, apart, slopes, queries, key_rows, values, mixed, log_total, grads, group, tile=1024, key_tile=512
):
    slots = len(grads)
    total, width = queries.shape
    pair = min(2, width // HD)
    cols = pair * HD
    spec = pl.BlockSpec((total, cols), lambda g: (0, group))
    out_spec = pl.BlockSpec((total, cols), lambda g: (0, 0))
    scalars = pl.BlockSpec(memory_space=pltpu.SMEM)
    return pl.pallas_call(
        functools.partial(
            attend_back_kernel, slots=slots, pair=pair, tile=tile, key_tile=key_tile
        ),
        grid=(1,),
        in_specs=[scalars] * 3
        + [spec] * 3
        + [out_spec, pl.BlockSpec((pair, 1, total), lambda g: (0, 0, 0))]
        + [pl.BlockSpec((total // slots, cols), lambda g: (0, group))] * slots,
        out_specs=pl.BlockSpec((total, 3 * cols), lambda g: (0, 0)),
        out_shape=jax.ShapeDtypeStruct((total, 3 * cols), BF16),
        scratch_shapes=[pltpu.VMEM((pair, total, 128), BF16)] * 4
        + [pltpu.VMEM((pair, 128, total), BF16), pltpu.VMEM((pair, 128, total), F32)],
        compiler_params=pltpu.CompilerParams(vmem_limit_bytes=60 << 20),
        cost_estimate=SMALL_COST,
        name="attend_back",
    )(
        me,
        apart,
        slopes[group * pair : (group + 1) * pair],
        queries,
        key_rows,
        values,
        mixed,
        log_total,
        *grads,
    )


def whole(shape):
    return pl.BlockSpec(shape, lambda i: (0,) * len(shape))


def row(ref):
    return ref[...].astype(F32)[None, :]


def choose(slot, refs):
    rows = refs[0][...]
    for at, ref in enumerate(refs[1:], 1):
        rows = jnp.where(slot == at, ref[...], rows)
    return rows


def slot_specs(count, per, block, width, order=lambda i: i):
    return [
        pl.BlockSpec(
            (block, width), lambda i, at=at: (jnp.clip(order(i) - at * per, 0, per - 1), 0)
        )
        for at in range(count)
    ]


def tall_spec(chosen, per, block, width):
    return pl.BlockSpec(
        (block, width),
        lambda i: ((chosen.start + chosen.step * (i // per)) * per + i % per, 0),
    )


def kernel_call(kernel, grid, in_specs, out_specs, out_shape, inputs, held=(), **more):
    return pl.pallas_call(
        kernel,
        grid=grid,
        in_specs=in_specs + [pl.BlockSpec(memory_space=pl.ANY)] * len(held),
        out_specs=out_specs,
        out_shape=out_shape,
        input_output_aliases={len(inputs) + at: at for at in range(len(held))},
        compiler_params=pltpu.CompilerParams(vmem_limit_bytes=56 << 20),
        cost_estimate=SMALL_COST,
        **more,
    )(*inputs, *held)


def shape_of(rows, cols, kind=BF16):
    return jax.ShapeDtypeStruct((rows, cols), kind)


def project_kernel(*refs, count, per):
    x_refs = refs[:count]
    gain_ref, shift_ref, wq_ref, wk_ref, wv_ref, qb_ref, vb_ref = refs[count : count + 7]
    normed_ref, q_ref, k_ref, v_ref = refs[-4:]
    x = choose(pl.program_id(0) // per, x_refs).astype(F32)
    normed = low(norm_stats(x)[0] * row(gain_ref) + row(shift_ref))
    normed_ref[...] = normed
    q_ref[...] = low((dot(normed, wq_ref[...]) + row(qb_ref)) * (LOG2E * HD**-0.5))
    k_ref[...] = low(dot(normed, wk_ref[...]))
    v_ref[...] = low(dot(normed, wv_ref[...]) + row(vb_ref))


def project(x_parts, chosen, slots, vectors, weights, biases, held):
    rows, width = x_parts[0].shape
    block = min(rows, 512)
    per = rows // block
    widths = [width] + [weight.shape[1] for weight in weights]
    return kernel_call(
        functools.partial(project_kernel, count=len(chosen), per=per),
        (len(chosen) * per,),
        slot_specs(len(chosen), per, block, width)
        + [whole(a.shape) for a in (*vectors, *weights, *biases)],
        [tall_spec(chosen, per, block, cols) for cols in widths],
        [shape_of(slots * rows, cols) for cols in widths],
        [*x_parts, *vectors, *weights, *biases],
        held,
        name="project",
    )


def act_grad_kernel(*refs, count, per):
    down_ref, grad_ref, cot_ref = refs[count:]
    cot = choose(pl.program_id(0) // per, refs[:count])
    cot_ref[...] = cot
    grad_ref[...] = low(dot(cot, down_ref[...], NT))


def act_grad_step(cot_parts, down):
    slots = len(cot_parts)
    rows, width = cot_parts[0].shape
    block = min(rows, 1024)
    per = rows // block
    units = down.shape[0]
    return kernel_call(
        functools.partial(act_grad_kernel, count=slots, per=per),
        (slots * per,),
        slot_specs(slots, per, block, width) + [whole(down.shape)],
        [pl.BlockSpec((block, cols), lambda i: (i, 0)) for cols in (units, width)],
        [shape_of(slots * rows, cols) for cols in (units, width)],
        [*cot_parts, down],
        (),
        name="act_grad",
    )


def post_kernel(*refs, slots, groups, per):
    mixed_refs = refs[: slots * groups]
    x_refs = refs[slots * groups : slots * groups + slots]
    weight_refs = refs[slots * groups + slots : slots * groups + 2 * slots]
    bias_ref, gain_ref, shift_ref, post_ref, residual_ref = refs[-5:]
    blocks = pl.num_programs(0)
    at = (pl.program_id(0) + blocks // 2) % blocks
    residual = choose(at // per, x_refs).astype(F32) + row(bias_ref)
    for slot in range(slots):
        mixed = [ref[...] for ref in mixed_refs[slot * groups : (slot + 1) * groups]]
        residual = residual + dot(jnp.concatenate(mixed, axis=1), weight_refs[slot][...])
    normal, _ = norm_stats(residual)
    post_ref[...] = low(normal * row(gain_ref) + row(shift_ref))

    @pl.when(at < per)
    def _():
        residual_ref[...] = residual


def post_norm(mixed, x_parts, weights, bias, gain, shift):
    slots, groups = len(mixed), len(mixed[0])
    rows, width = x_parts[0].shape
    block = min(rows, 512)
    per = rows // block
    blocks = slots * per
    order = lambda i: (i + blocks // 2) % blocks
    specs = [
        pl.BlockSpec(
            (block, part.shape[1]),
            lambda i, slot=slot: (((order(i) // per) ^ slot) * per + order(i) % per, 0),
        )
        for slot in range(slots)
        for part in mixed[slot]
    ]
    return kernel_call(
        functools.partial(post_kernel, slots=slots, groups=groups, per=per),
        (blocks,),
        specs
        + slot_specs(slots, per, block, width, order)
        + [whole(a.shape) for a in (*weights, bias, gain, shift)],
        [
            pl.BlockSpec((block, width), lambda i: (order(i), 0)),
            pl.BlockSpec((block, width), lambda i: (jnp.clip(i - blocks // 2, 0, per - 1), 0)),
        ],
        [shape_of(slots * rows, width), shape_of(rows, width, F32)],
        [*[part for parts in mixed for part in parts], *x_parts, *weights, bias, gain, shift],
        (),
        name="post_norm",
    )


def feed_kernel(*refs, count, per, extras, held):
    post_ref, act_grad_ref, up_ref, bias_ref = refs[:4]
    extra_refs = refs[4 : 4 + extras]
    active_ref, grad_ref, sum_ref = refs[4 + extras + held : 7 + extras + held]
    back_refs = refs[7 + extras + held :]
    slot = pl.program_id(0) // per

    @pl.when(pl.program_id(0) == 0)
    def _():
        sum_ref[...] = jnp.zeros_like(sum_ref)

    post = post_ref[...]
    units = active_ref.shape[1]
    chunk = min(512, units)
    scale, cubic = math.sqrt(2 / math.pi), 0.044715
    for first in range(0, units, chunk):
        cols = slice(first, first + chunk)
        hidden = dot(post, up_ref[:, cols]) + row(bias_ref)[:, cols]
        square = hidden * hidden
        curve = jnp.tanh(hidden * (scale + scale * cubic * square))
        half = 0.5 + 0.5 * curve
        active_ref[:, cols] = low(hidden * half)
        slope = half + (0.5 * hidden) * (1.0 - curve * curve) * (
            scale + 3 * scale * cubic * square
        )
        grad = low(act_grad_ref[:, cols].astype(F32) * slope)
        grad_ref[:, cols] = grad
        sum_ref[:, cols] += jnp.sum(grad.astype(F32), axis=0, keepdims=True)
    back = dot(grad_ref[...], up_ref[...], NT)
    if extras:
        back = back + choose(slot, extra_refs).astype(F32)
    back = low(back)
    for at, back_ref in enumerate(back_refs):

        @pl.when(slot == at)
        def _():
            back_ref[...] = back


def feed(post_all, act_grad, up, up_bias, slots, chosen, extras, held):
    count = len(chosen)
    total, width = post_all.shape
    rows, units = total // slots, up.shape[1]
    block = min(rows, 512)
    per = rows // block
    tall = lambda cols: tall_spec(chosen, per, block, cols)
    active, grad, sums, *backs = kernel_call(
        functools.partial(
            feed_kernel, count=count, per=per, extras=len(extras), held=len(held)
        ),
        (count * per,),
        [tall(width), tall(units), whole(up.shape), whole(up_bias.shape)]
        + slot_specs(len(extras), per, block, width),
        [tall(units), tall(units), whole((1, units))] + slot_specs(count, per, block, width),
        [shape_of(total, units), shape_of(total, units), shape_of(1, units, F32)]
        + [shape_of(rows, width)] * count,
        [post_all, act_grad, up, up_bias, *extras],
        held,
        name="feed",
    )
    return (active, grad), sums, backs


def outer_kernel(left_ref, right_ref, out_ref, total):
    step = pl.program_id(0)

    @pl.when(step == 0)
    def _():
        total[...] = dot(left_ref[...], right_ref[...], TN)

    @pl.when(step > 0)
    def _():
        total[...] += dot(left_ref[...], right_ref[...], TN)

    @pl.when(step == pl.num_programs(0) - 1)
    def _():
        out_ref[...] = low(total[...])


def outer_step(left, right):
    total = left.shape[0]
    block = min(total, 1024)
    shape = (left.shape[1], right.shape[1])
    return kernel_call(
        outer_kernel,
        (total // block,),
        [pl.BlockSpec((block, cols), lambda i: (i, 0)) for cols in shape],
        [whole(shape)],
        [shape_of(*shape)],
        [left, right],
        scratch_shapes=[pltpu.VMEM(shape, F32)],
        name="outer_step",
    )[0]


def pack_kernel(*refs, groups):
    sums_ref, gain_ref, shift_ref = refs[:3]
    row_refs, count_refs = refs[3 : 3 + groups], refs[3 + groups : 3 + 2 * groups]
    unit_refs, (shared_ref, own_ref) = refs[3 + 2 * groups : -2], refs[-2:]
    shared_ref[...] = sums_ref[...]
    rows = row_refs[0][...]
    for ref in row_refs[1:]:
        rows = rows + ref[...]
    shared_ref[4:5, :] = (rows[0:1] - row(shift_ref) * rows[1:2]) / row(gain_ref)
    shared_ref[5:6, :] = rows[1:2]
    own_ref[...] = jnp.zeros_like(own_ref)
    units = unit_refs[0][...]
    for ref in unit_refs[1:]:
        units = units + ref[...]
    own_ref[0:1, : units.shape[1]] = units
    for at, ref in enumerate(count_refs):
        own_ref[1 + at : 2 + at, : ref.shape[1]] = ref[...]


def pack(row_sums, gain, shift, group_rows, group_counts, unit_sums):
    width = row_sums.shape[1]
    inputs = [row_sums, gain, shift, *group_rows, *group_counts, *unit_sums]
    wide = max(a.shape[1] for a in (*group_counts, *unit_sums))
    return kernel_call(
        functools.partial(pack_kernel, groups=len(group_rows)),
        (1,),
        [whole(a.shape) for a in inputs],
        [whole((8, width)), whole((8, wide))],
        [shape_of(8, width, F32), shape_of(8, wide, F32)],
        inputs,
        name="pack",
    )


def resid_kernel(*refs, terms, slots):
    term_refs = refs[:terms]
    residual_ref, cot_ref, gain_ref = refs[terms : terms + 3]
    weight_refs = refs[terms + 3 : terms + 3 + slots]
    grad_ref, low_ref, sums_ref = refs[terms + 3 + slots : terms + 6 + slots]
    part_refs = refs[terms + 6 + slots :]

    @pl.when(pl.program_id(0) == 0)
    def _():
        sums_ref[...] = jnp.zeros_like(sums_ref)

    post_grad = term_refs[0][...].astype(F32)
    for ref in term_refs[1:]:
        post_grad = post_grad + ref[...].astype(F32)
    cot = cot_ref[...].astype(F32)
    normal, inverse = norm_stats(residual_ref[...])
    grad = cot + norm_pull(post_grad * row(gain_ref), normal, inverse)
    grad_ref[...] = grad
    grad_low = low(grad)
    low_ref[...] = grad_low
    for weight_ref, part_ref in zip(weight_refs, part_refs):
        part_ref[...] = low(dot(grad_low, weight_ref[...], NT))
    for at, value in enumerate((cot, grad, post_grad * normal, post_grad)):
        sums_ref[at : at + 1, :] += jnp.sum(value, axis=0, keepdims=True)


def resid_step(terms, residual, cotangent, gain, weights):
    rows, width = residual.shape
    block = min(rows, 256)
    tall = lambda cols: pl.BlockSpec((block, cols), lambda i: (i, 0))
    cols = weights[0].shape[0]
    return kernel_call(
        functools.partial(resid_kernel, terms=len(terms), slots=len(weights)),
        (rows // block,),
        [tall(width)] * (len(terms) + 2) + [whole(a.shape) for a in (gain, *weights)],
        [tall(width), tall(width), whole((8, width))] + [tall(cols)] * len(weights),
        [shape_of(rows, width, F32), shape_of(rows, width), shape_of(8, width, F32)]
        + [shape_of(rows, cols)] * len(weights),
        [*terms, residual, cotangent, gain, *weights],
        (),
        name="resid_step",
    )


def dense_grad_kernel(*refs, slots, groups):
    mixed_refs, grad_ref = refs[: slots * groups], refs[slots * groups]
    out_refs, sum_refs = refs[slots * groups + 1 :][:slots], refs[slots * groups + 1 :][slots:]
    step = pl.program_id(0)
    grad = grad_ref[...]
    for slot in range(slots):
        mixed = [ref[...] for ref in mixed_refs[slot * groups : (slot + 1) * groups]]
        part = dot(jnp.concatenate(mixed, axis=1), grad, TN)
        sum_refs[slot][...] = jnp.where(step == 0, 0.0, sum_refs[slot][...]) + part

    @pl.when(step == pl.num_programs(0) - 1)
    def _():
        for out_ref, sum_ref in zip(out_refs, sum_refs):
            out_ref[...] = low(sum_ref[...])


def dense_grad(mixed, grad):
    slots, groups = len(mixed), len(mixed[0])
    rows, width = grad.shape
    block = min(rows, 512)
    per = rows // block
    cols = sum(part.shape[1] for part in mixed[0])
    return kernel_call(
        functools.partial(dense_grad_kernel, slots=slots, groups=groups),
        (per,),
        [
            pl.BlockSpec((block, part.shape[1]), lambda i, slot=slot: (slot * per + i, 0))
            for slot in range(slots)
            for part in mixed[slot]
        ]
        + [pl.BlockSpec((block, width), lambda i: (i, 0))],
        [whole((cols, width))] * slots,
        [shape_of(cols, width)] * slots,
        [*[part for parts in mixed for part in parts], grad],
        (),
        scratch_shapes=[pltpu.VMEM((cols, width), F32)] * slots,
        name="dense_grad",
    )


def weight_kernel(normed_ref, grad_ref, wq_ref, wk_ref, wv_ref, out_ref, sums_ref, count_ref, total, count):
    step = pl.program_id(0)

    @pl.when(step == 0)
    def _():
        total[...] = jnp.zeros_like(total)
        count[...] = jnp.zeros_like(count)

    grad = grad_ref[...]
    total[...] += dot(normed_ref[...], grad, TN)
    count[...] += jnp.sum(grad.astype(F32), axis=0, keepdims=True)

    @pl.when(step == pl.num_programs(0) - 1)
    def _():
        weight = jnp.concatenate([wq_ref[...], wk_ref[...], wv_ref[...]], axis=1).astype(F32)
        out_ref[...] = low(total[...])
        count_ref[...] = count[...]
        lane = lanes(weight.shape[0])
        cross = jnp.sum(weight * total[...], axis=1, keepdims=True)
        plain = jnp.sum(weight * count[...], axis=1, keepdims=True)
        both = jnp.where(lane == 0, cross, jnp.where(lane == 1, plain, 0.0))
        sums_ref[...] = both.T[:8]


def weight_step(normed, grad, weights, group):
    total, width = normed.shape
    cols = grad.shape[1]
    block = min(total, 1024)
    return kernel_call(
        weight_kernel,
        (total // block,),
        [pl.BlockSpec((block, count), lambda i: (i, 0)) for count in (width, cols)]
        + [pl.BlockSpec((width, cols // 3), lambda i: (0, group))] * 3,
        [whole((width, cols)), whole((8, width)), whole((1, cols))],
        [shape_of(width, cols), shape_of(8, width, F32), shape_of(1, cols, F32)],
        [normed, grad, *weights],
        (),
        scratch_shapes=[pltpu.VMEM((width, cols), F32), pltpu.VMEM((1, cols), F32)],
        name="weight_step",
    )


def unproject_kernel(*refs, groups, per, extras):
    grad_refs, weight_refs = refs[:groups], refs[groups : 4 * groups]
    extra_refs = refs[4 * groups : 4 * groups + extras]
    out_refs = refs[4 * groups + extras : -1]
    joined = refs[-1]
    slot = pl.program_id(0) // per

    @pl.when(pl.program_id(0) == 0)
    def _():
        joined[...] = jnp.concatenate([ref[...] for ref in weight_refs], axis=1)

    total = dot(jnp.concatenate([ref[...] for ref in grad_refs], axis=1), joined[...], NT)
    if extras:
        total = total + choose(slot, extra_refs).astype(F32)
    total = low(total)
    for at, ref in enumerate(out_refs):

        @pl.when(slot == at)
        def _():
            ref[...] = total


def unproject(grads, weights, slots, chosen, extras):
    width = weights[0].shape[0]
    count, groups = len(chosen), len(grads)
    total, cols = grads[0].shape
    rows = total // slots
    block = min(rows, 512)
    per = rows // block
    return kernel_call(
        functools.partial(unproject_kernel, groups=groups, per=per, extras=len(extras)),
        (count * per,),
        [tall_spec(chosen, per, block, cols)] * groups
        + [
            pl.BlockSpec((width, cols // 3), lambda i, group=group: (0, group))
            for group in range(groups)
            for _ in weights
        ]
        + slot_specs(len(extras), per, block, width),
        slot_specs(count, per, block, width),
        [shape_of(rows, width)] * count,
        [*grads, *[weight for _ in grads for weight in weights], *extras],
        (),
        scratch_shapes=[pltpu.VMEM((width, cols * groups), BF16)],
        name="unproject",
    )


def ffn_kernel(*refs, per, extras):
    active_ref, weight_ref = refs[:2]
    slot = pl.program_id(0) // per
    total = dot(active_ref[...], weight_ref[...])
    if extras:
        total = total + choose(slot, refs[2 : 2 + extras]).astype(F32)
    total = low(total)
    for at, ref in enumerate(refs[2 + extras :]):

        @pl.when(slot == at)
        def _():
            ref[...] = total


def ffn_step(active, weight, slots, chosen, extras):
    total, units = active.shape
    width = weight.shape[1]
    rows = total // slots
    block = min(rows, 1024)
    per = rows // block
    count = len(chosen)
    return kernel_call(
        functools.partial(ffn_kernel, per=per, extras=len(extras)),
        (count * per,),
        [tall_spec(chosen, per, block, units), whole(weight.shape)]
        + slot_specs(len(extras), per, block, width),
        slot_specs(count, per, block, width),
        [shape_of(rows, width)] * count,
        [active, weight, *extras],
        name="ffn_step",
    )


def spread_kernel(*refs, groups):
    cols = refs[0].shape[1] // 3
    for kind in range(3):
        for group in range(groups):
            refs[groups + kind][:, group * cols : (group + 1) * cols] = refs[group][
                :, kind * cols : (kind + 1) * cols
            ].astype(F32)


def spread(group_sums):
    width, cols = group_sums[0].shape
    groups = len(group_sums)
    block = min(width, 256)
    return kernel_call(
        functools.partial(spread_kernel, groups=groups),
        (width // block,),
        [pl.BlockSpec((block, cols), lambda i: (i, 0))] * groups,
        [pl.BlockSpec((block, cols // 3 * groups), lambda i: (i, 0))] * 3,
        [shape_of(width, cols // 3 * groups, F32)] * 3,
        list(group_sums),
        name="spread",
    )


def input_kernel(*refs, terms):
    x_ref, resid_ref, gain_ref, out_ref = refs[terms:]
    grad = refs[0][...].astype(F32)
    for ref in refs[1:terms]:
        grad = grad + ref[...].astype(F32)
    normal, inverse = norm_stats(x_ref[...].astype(F32))
    out_ref[...] = resid_ref[...] + norm_pull(grad * row(gain_ref), normal, inverse)


def input_step(terms, layer_input, resid_grad, gain):
    rows, width = resid_grad.shape
    block = min(rows, 256)
    tall = pl.BlockSpec((block, width), lambda i: (i, 0))
    return kernel_call(
        functools.partial(input_kernel, terms=len(terms)),
        (rows // block,),
        [tall] * (len(terms) + 2) + [whole(gain.shape)],
        [tall],
        [shape_of(rows, width, F32)],
        [*terms, layer_input, resid_grad, gain],
        name="input_step",
    )[0]


def shards(
    slots,
    streams,
    layer_input,
    row_ids,
    input_gain,
    input_shift,
    query_weight,
    query_bias,
    key_weight,
    value_weight,
    value_bias,
    dense_weight,
    dense_bias,
    post_gain,
    post_shift,
    up_weight,
    up_bias,
    down_weight,
    down_bias,
    cotangent,
):
    me = lax.axis_index("tensor")
    me_word = me.astype(jnp.int32)[None]
    rows = layer_input.shape[0]
    head_cols = query_weight.shape[1]
    head_count = head_cols // HD
    groups = max(1, head_count // 2)
    bits = [1 << level for level in range(slots.bit_length() - 1)]
    half = slots // 2
    after = lambda array, *others: lax.optimization_barrier((array, *others))[0]

    def swap(array, mask):
        return lax.ppermute(array, "tensor", [(i, i ^ mask) for i in range(slots)])

    def gather(array):
        held = {0: array}
        for bit in reversed(bits):
            held.update({slot ^ bit: swap(part, bit) for slot, part in held.items()})
        return [held[slot] for slot in range(slots)]

    def blocks(array):
        return [array[slot * rows : (slot + 1) * rows] for slot in range(slots)]

    def swap_data(array, mask):
        return lax.ppermute(array, "dp", [(i, i ^ mask) for i in range(streams)])

    def finish_terms(held, terms, levels):
        for bit in levels:
            come = {slot ^ bit: swap(part, bit) for slot, part in held.items() if slot & bit}
            if 0 in come:
                terms.append(come.pop(0))
            held = {
                slot: low(held[slot].astype(F32) + part.astype(F32)) for slot, part in come.items()
            }
        return terms

    def scatter_terms(parts):
        return finish_terms(dict(enumerate(parts)), [parts[0]], bits)

    far_odd = range(half + 1, slots, 2)
    far_even = range(half, slots, 2)
    near_odd = range(1, half, 2)
    near_even = range(0, half, 2)

    def ordered_terms(make):
        far = make(far_odd, (), None)
        far_come = [swap(part, 1) for part in far]
        near = make(near_odd, (), far[-1])
        near_come = [swap(part, 1) for part in near]
        far = make(far_even, far_come, near[-1])
        near = make(near_even, near_come, far[-1])
        held = dict(zip((*far_even, *near_even), (*far, *near)))
        return finish_terms(held, [held.pop(0)], bits[1:])

    def add_up(terms):
        return functools.reduce(
            lambda sum_now, term: sum_now + term.astype(F32), terms[1:], terms[0].astype(F32)
        )

    def total_of(shared, own):
        for bit in bits:
            shared = shared + swap(shared, bit)
        for level in range(streams.bit_length() - 1):
            shared = shared + swap_data(shared, 1 << level)
            own = own + swap_data(own, 1 << level)
        return shared, own

    norm_vectors = (input_gain, input_shift)
    weights = (query_weight, key_weight, value_weight)
    biases = (query_bias, value_bias)
    x_held = {0: layer_input}
    for bit in reversed(bits[1:]):
        x_held.update({slot ^ bit: swap(part, bit) for slot, part in x_held.items()})
    x_held[1] = swap(x_held[0], 1)
    near_parts = [x_held[0], x_held[1]]
    first = range(2)
    held = project(near_parts, first, slots, norm_vectors, weights, biases, ())
    rest = sorted(slot for slot in x_held if slot > 1)
    *arrived, normed = lax.optimization_barrier((*[x_held[slot] for slot in rest], held[0]))
    held = (normed, *held[1:])
    for slot, part in zip(rest, arrived):
        x_held[slot], x_held[slot ^ 1] = part, swap(part, 1)
    x_parts = [x_held[slot] for slot in range(slots)]
    dense_parts = gather(after(dense_weight, arrived[-1]))
    cot_own = after(cotangent, arrived[-1])
    cot_parts = gather(cot_own)
    normed, queries, key_rows, values = project(
        x_parts[2:], range(2, slots), slots, norm_vectors, weights, biases, held
    )

    heads = me * head_count + jnp.arange(head_count)
    slopes = jnp.exp2(-8.0 * (heads + 1).astype(F32) / HEADS) * LOG2E
    apart = (row_ids[:1] != row_ids[SHORT : SHORT + 1]).astype(jnp.int32)

    mixed_own, log_totals, mixed_parts = [], [], []
    for group in range(groups):
        mixed, log_total = attend(
            me_word,
            apart,
            slopes,
            queries if not group else after(queries, cot_parts[half], dense_parts[half], mixed_own[-1]),
            key_rows,
            values,
            slots,
            group,
        )
        mixed_own.append(mixed)
        log_totals.append(log_total)
        if group < groups - 1:
            mixed_parts.append(gather(mixed))
    act_grad, cot_all = act_grad_step(
        lax.optimization_barrier((*cot_parts, mixed_own[-1]))[:-1], down_weight
    )
    came = {0: mixed_own[-1]}
    for bit in reversed(bits[1:]):
        came.update({slot ^ bit: swap(part, bit) for slot, part in came.items()})
    far_slots = sorted(came)[1:]
    *arrived, act_grad = lax.optimization_barrier((*[came[slot] for slot in far_slots], act_grad))
    came.update(zip(far_slots, arrived))
    came.update({slot ^ 1: swap(part, 1) for slot, part in came.items()})
    mixed_parts.append([came[slot] for slot in range(slots)])
    mixed_all = [[mixed_parts[group][slot] for group in range(groups)] for slot in range(slots)]
    post_all, residual = post_norm(
        mixed_all, x_parts, dense_parts, dense_bias, post_gain, post_shift
    )

    fed, up_bias_parts = [()], []

    def make_feed(chosen, extras, gate):
        held, sums, backs = feed(
            post_all, act_grad, up_weight, up_bias, slots, chosen, extras, fed[-1]
        )
        fed.append(held)
        up_bias_parts.append(sums)
        return backs

    post_terms = ordered_terms(make_feed)
    active, hidden_grad = fed[-1]
    up_part = outer_step(post_all, hidden_grad)
    down_part = outer_step(active, after(cot_all, up_part))
    resid_grad, attended_grad, row_sums, *mixed_grads = resid_step(
        [after(post_terms[0], down_part), *post_terms[1:]],
        residual,
        cotangent,
        post_gain,
        dense_parts,
    )
    up_sum, down_sum = lax.psum((up_part, down_part), "dp")
    mixed_grads = [swap(part, slot) if slot else part for slot, part in enumerate(mixed_grads)]
    dense_grads = dense_grad(mixed_all, attended_grad)
    ffn_parts = ffn_step(after(active, dense_grads[-1]), down_weight, slots, range(slots), ())
    *mixed_grads, dense_last, ffn_last = lax.optimization_barrier(
        (*mixed_grads, dense_grads[-1], ffn_parts[-1])
    )
    dense_grads = [*dense_grads[:-1], dense_last]
    dense_terms = [swap(part, slot) if slot else part for slot, part in enumerate(dense_grads)]
    ffn_parts = [*ffn_parts[:-1], ffn_last]
    ffn_come = [swap(part, 1) for part in ffn_parts[1::2]]
    ffn_held = dict(zip(range(0, slots, 2), [
        low(part.astype(F32) + come.astype(F32))
        for part, come in zip(ffn_parts[::2], ffn_come)
    ]))
    ffn_first = ffn_held.pop(0)

    cols = head_cols // groups
    head_grads, group_sums, group_rows, group_counts = [], [], [], []
    for group in range(groups):
        head_grads.append(
            attend_back(
                me_word,
                apart,
                slopes,
                queries,
                key_rows,
                values,
                mixed_own[group],
                log_totals[group],
                mixed_grads,
                group,
            )
        )
        grad = head_grads[-1]
        if not group:
            keys = sorted(ffn_held)
            grad, *parts = lax.optimization_barrier((grad, *[ffn_held[key] for key in keys]))
            ffn_terms = finish_terms(dict(zip(keys, parts)), [ffn_first], bits[1:])
        if group == groups - 1:
            waited = (*ffn_terms, *([group_sums[0], dense_sum] if group else []))
            grad, *waited = lax.optimization_barrier((grad, *waited))
            ffn_terms = waited[: len(ffn_terms)]
            if group:
                group_sums[0], dense_sum = waited[len(ffn_terms) :]
        part, row_part, count_part = weight_step(normed, grad, weights, group)
        group_rows.append(row_part)
        group_counts.append(count_part)
        if not group:
            dense_part = low(add_up(dense_terms))
            part, dense_part, up_sum, down_sum = lax.optimization_barrier(
                (part, dense_part, up_sum, down_sum)
            )
            sums = lax.psum((part, dense_part), "dp")
            dense_sum = sums[1]
            *mixed_grads, _ = lax.optimization_barrier((*mixed_grads, part))
        else:
            sums = lax.psum((part,), "dp")
        group_sums.append(sums[0])
    last = after(head_grads[-1], part)
    normed_terms = ordered_terms(
        lambda chosen, extras, gate: unproject(
            [*head_grads[:-1], last if gate is None else after(last, gate)],
            weights,
            slots,
            chosen,
            extras,
        )
    )
    shared, own = total_of(
        *pack(row_sums, input_gain, input_shift, group_rows, group_counts, up_bias_parts)
    )
    up_bias_grad = own[0, : up_bias.shape[0]]
    counts = own[1 : 1 + groups]
    query_bias_grad = counts[:, :cols].reshape(-1)
    value_bias_grad = counts[:, 2 * cols : 3 * cols].reshape(-1)
    layer_output = low(residual + add_up(ffn_terms) + down_bias.astype(F32))
    weight_grads = spread(group_sums)
    input_grad = input_step(normed_terms, layer_input, resid_grad, input_gain)
    return (
        layer_output,
        input_grad,
        shared[4],
        shared[5],
        weight_grads[0],
        query_bias_grad,
        weight_grads[1],
        weight_grads[2],
        value_bias_grad,
        dense_sum.astype(F32),
        shared[1],
        shared[2],
        shared[3],
        up_sum.astype(F32),
        up_bias_grad,
        down_sum.astype(F32),
        shared[0],
    )


def solution(mesh):
    in_specs = (
        P(("dp", "tensor"), None),
        P("dp"),
        P(),
        P(),
        P(None, "tensor"),
        P("tensor"),
        P(None, "tensor"),
        P(None, "tensor"),
        P("tensor"),
        P("tensor", None),
        P(),
        P(),
        P(),
        P(None, "tensor"),
        P("tensor"),
        P("tensor", None),
        P(),
        P(("dp", "tensor"), None),
    )
    out_specs = (
        P(("dp", "tensor"), None),
        P(("dp", "tensor"), None),
        P(),
        P(),
        P(None, "tensor"),
        P("tensor"),
        P(None, "tensor"),
        P(None, "tensor"),
        P("tensor"),
        P("tensor", None),
        P(),
        P(),
        P(),
        P(None, "tensor"),
        P("tensor"),
        P("tensor", None),
        P(),
    )
    return jax.shard_map(
        functools.partial(shards, mesh.shape["tensor"], mesh.shape["dp"]), mesh=mesh, in_specs=in_specs, out_specs=out_specs, check_vma=False)
```

```python
import functools
import math

import jax
import jax.numpy as jnp
from jax import lax
from jax.experimental import pallas as pl
from jax.experimental.pallas import tpu as pltpu
from jax.sharding import PartitionSpec as P

HEADS = 16
HD = 64
SHORT = 2048
EPSILON = 1e-05
LOG2E = math.log2(math.e)
F32 = jnp.float32
BF16 = jnp.bfloat16
SMALL_COST = pl.CostEstimate(flops=1, transcendentals=0, bytes_accessed=1)
NT = (((1,), (1,)), ((), ()))
NN = (((1,), (0,)), ((), ()))
TN = (((0,), (0,)), ((), ()))


def dot(lhs, rhs, dims=NN):
    return lax.dot_general(lhs, rhs, dims, preferred_element_type=F32)


def low(array):
    return array.astype(BF16)


def norm_stats(rows):
    center = jnp.mean(rows, axis=-1, keepdims=True)
    centered = rows - center
    inverse = lax.rsqrt(jnp.mean(centered * centered, axis=-1, keepdims=True) + EPSILON)
    return centered * inverse, inverse


def norm_pull(grad, normal, inverse):
    grad_mean = jnp.mean(grad, axis=-1, keepdims=True)
    dot_mean = jnp.mean(grad * normal, axis=-1, keepdims=True)
    return inverse * (grad - grad_mean - normal * dot_mean)


def lanes(count):
    return lax.broadcasted_iota(jnp.int32, (count, 128), 1)


def places(count, first):
    return lax.broadcasted_iota(jnp.int32, (count, 128), 0) + first


def widen(head):
    return jnp.concatenate([head.astype(F32), jnp.zeros((head.shape[0], HD), F32)], axis=1)


def split3(value):
    high = low(value).astype(F32)
    middle = low(value - high).astype(F32)
    return high, middle, value - high - middle


def pick3(index, parts):
    return jnp.where(index == 0, parts[0], jnp.where(index == 1, parts[1], parts[2]))


def key_columns(head, first):
    count = head.shape[0]
    lane, place = lanes(count), places(count, first)
    coarse = ((place >> 6) << 6).astype(F32)
    fine = (place & 63).astype(F32)
    wall = jnp.where(place < SHORT, -1e30, 0.0)
    extra = jnp.where(lane < 73, -1.0, jnp.where(lane == 73, wall, 0.0))
    extra = jnp.where(lane < 67, coarse, jnp.where(lane < 70, fine, extra))
    return low(jnp.where(lane < HD, widen(head), extra))


def query_columns(head, first, slope, apart, log_total=None):
    count = head.shape[0]
    lane, place = lanes(count), places(count, first)
    extra = pick3(jnp.where(lane < 67, lane - 64, lane - 67), split3(slope))
    extra = jnp.where(lane < 70, extra, 0.0)
    if log_total is not None:
        extra = jnp.where((lane >= 70) & (lane < 73), pick3(lane - 70, split3(log_total)), extra)
    extra = jnp.where(lane == 73, jnp.where(place >= SHORT, apart, 0.0), extra)
    return low(jnp.where(lane < HD, widen(head), extra))


def ones_columns(head, count):
    lane = lanes(head.shape[0])
    return low(jnp.where(lane < HD, widen(head), jnp.where(lane < HD + count, 1.0, 0.0)))


def grad_columns(head, shift):
    lane = lanes(head.shape[0])
    extra = jnp.where(lane < 67, pick3(lane - 64, split3(shift)), 0.0)
    return low(jnp.where(lane < HD, widen(head), extra))


def each_chunk(me, slots, rows, body):
    chunk = min(rows, 512)
    for slot in range(slots):
        home = (me ^ slot) * rows

        @pl.loop(0, rows // chunk)
        def _(step):
            offset = pl.multiple_of(step * chunk, chunk)
            body(slot, pl.ds(offset, chunk), pl.ds(slot * rows + offset, chunk), home + offset)


def attend_kernel(
    me_ref, apart_ref, slope_ref, q_ref, k_ref, v_ref, o_ref, lse_ref, qa, ka, va, *, slots, pair, tile
):
    me = me_ref[0]
    total = q_ref.shape[0]
    rows = total // slots
    chunk = min(rows, 512)
    apart = apart_ref[0].astype(F32)

    def prepare(slot, inner, spot, place):
        place = pl.multiple_of(place, chunk)
        home = pl.ds(place, chunk)
        for s in range(pair):
            cols = slice(s * HD, (s + 1) * HD)
            qa[s, home, :] = query_columns(q_ref[spot, cols], place, slope_ref[s], apart)
            ka[s, home, :] = key_columns(k_ref[spot, cols], place)
            va[s, home, :] = ones_columns(v_ref[spot, cols], 1)

    each_chunk(me, slots, rows, prepare)
    causal = lax.broadcasted_iota(jnp.int32, (tile, tile), 1) <= lax.broadcasted_iota(
        jnp.int32, (tile, tile), 0
    )
    piece = min(rows, tile)

    def query_tile(index, _):
        first = pl.multiple_of(index * tile, tile)
        queries = [qa[s, pl.ds(first, tile), :] for s in range(pair)]

        def step(at, carry, diagonal):
            after = []
            for s in range(pair):
                top, mix = carry[s]
                scores = dot(queries[s], ka[s, pl.ds(at, tile), :], NT)
                if diagonal:
                    scores = jnp.where(causal, scores, -1e30)
                higher = jnp.maximum(top, jnp.max(scores, axis=1, keepdims=True))
                weights = low(jnp.exp2(scores - higher))
                mix = mix * jnp.exp2(top - higher) + dot(weights, va[s, pl.ds(at, tile), :])
                after.append((higher, mix))
            return tuple(after)

        carry = tuple(
            (jnp.full((tile, 1), -1e38, F32), jnp.zeros((tile, 128), F32)) for _ in range(pair)
        )
        carry = step(first, carry, True)
        carry = lax.fori_loop(
            0, index, lambda at, held: step(pl.multiple_of(at * tile, tile), held, False), carry
        )
        outs = []
        for s in range(pair):
            top, mix = carry[s]
            weight = mix[:, HD : HD + 1]
            outs.append(mix[:, :HD] * (1.0 / weight))
            lse_ref[s, 0, pl.ds(first, tile)] = (top + jnp.log2(weight))[:, 0]
        out = low(jnp.concatenate(outs, axis=1))
        for part in range(tile // piece):
            block = (index * (tile // piece) + part) // (rows // piece)
            offset = first + part * piece - block * rows
            spot = pl.multiple_of((block ^ me) * rows + offset, piece)
            o_ref[pl.ds(spot, piece), :] = out[part * piece : (part + 1) * piece]
        return 0

    lax.fori_loop(0, total // tile, query_tile, 0)


def attend(me, apart, slopes, queries, key_rows, values, slots, group, tile=1024):
    total, width = queries.shape
    pair = min(2, width // HD)
    cols = pair * HD
    spec = pl.BlockSpec((total, cols), lambda g: (0, group))
    scalars = pl.BlockSpec(memory_space=pltpu.SMEM)
    return pl.pallas_call(
        functools.partial(attend_kernel, slots=slots, pair=pair, tile=tile),
        grid=(1,),
        in_specs=[scalars] * 3 + [spec] * 3,
        out_specs=[
            pl.BlockSpec((total, cols), lambda g: (0, 0)),
            pl.BlockSpec((pair, 1, total), lambda g: (0, 0, 0)),
        ],
        out_shape=[
            jax.ShapeDtypeStruct((total, cols), BF16),
            jax.ShapeDtypeStruct((pair, 1, total), F32),
        ],
        scratch_shapes=[pltpu.VMEM((pair, total, 128), BF16)] * 3,
        compiler_params=pltpu.CompilerParams(vmem_limit_bytes=56 << 20),
        cost_estimate=pl.CostEstimate(
            flops=pair * 1200 * total * total, transcendentals=0, bytes_accessed=8 * total * cols
        ),
        name="attend",
    )(me, apart, slopes[group * pair : (group + 1) * pair], queries, key_rows, values)


def attend_back_kernel(*refs, slots, pair, tile, key_tile):
    me_ref, apart_ref, slope_ref, q_ref, k_ref, v_ref, o_ref, lse_ref = refs[:8]
    g_refs = refs[8 : 8 + slots]
    out_ref, qa, ka, va, ga, kt, dq_sum = refs[8 + slots :]
    cols = pair * HD
    me = me_ref[0]
    total = q_ref.shape[0]
    rows = total // slots
    chunk = min(rows, 512)
    apart = apart_ref[0].astype(F32)

    def prepare(slot, inner, spot, place):
        place = pl.multiple_of(place, chunk)
        home = pl.ds(place, chunk)
        for s in range(pair):
            mine = slice(s * HD, (s + 1) * HD)
            log_total = lse_ref[s, :, home].T
            qa[s, home, :] = query_columns(q_ref[spot, mine], place, slope_ref[s], apart, log_total)
            keys = key_columns(k_ref[spot, mine], place)
            ka[s, home, :] = keys
            kt[s, :, home] = low(keys.astype(F32).T)
            va[s, home, :] = ones_columns(v_ref[spot, mine], 3)
            grad = g_refs[slot][inner, mine]
            row_dot = jnp.sum(
                grad.astype(F32) * o_ref[spot, mine].astype(F32), axis=1, keepdims=True
            )
            ga[s, home, :] = grad_columns(grad, -row_dot)
            dq_sum[s, :, home] = jnp.zeros((128, chunk), F32)

    each_chunk(me, slots, rows, prepare)
    causal = lax.broadcasted_iota(jnp.int32, (key_tile, key_tile), 0) <= lax.broadcasted_iota(
        jnp.int32, (key_tile, key_tile), 1
    )
    piece = min(rows, key_tile)

    def place_of(place, size):
        block = place // rows
        return pl.multiple_of((block ^ me) * rows + (place - block * rows), size)

    def keys_tile(index, _):
        first = pl.multiple_of(index * key_tile, key_tile)
        here = pl.ds(first, key_tile)

        def step(at, carry, diagonal, width):
            after = []
            for s in range(pair):
                dk, dv = carry[s]
                there = pl.ds(at, width)
                queries, grads = qa[s, there, :], ga[s, there, :]
                probs = jnp.exp2(dot(ka[s, here, :], queries, NT))
                if diagonal:
                    probs = jnp.where(causal, probs, 0.0)
                dv = dv + dot(low(probs), grads)
                score_grad = low(probs * dot(va[s, here, :], grads, NT))
                dk = dk + dot(score_grad, queries)
                dq_sum[s, :, there] += dot(kt[s, :, here], score_grad)
                after.append((dk, dv))
            return tuple(after)

        zeros = jnp.zeros((key_tile, 128), F32)
        carry = step(first, tuple((zeros, zeros) for _ in range(pair)), True, key_tile)
        start = first + key_tile
        short = jnp.minimum((-start) % tile, total - start) // key_tile
        if tile > key_tile:
            carry = lax.fori_loop(
                0,
                short,
                lambda at, held: step(
                    pl.multiple_of(start + at * key_tile, key_tile), held, False, key_tile
                ),
                carry,
            )
            start = start + short * key_tile
        carry = lax.fori_loop(
            0,
            (total - start) // tile,
            lambda at, held: step(
                pl.multiple_of(start + at * tile, min(tile, key_tile)), held, False, tile
            ),
            carry,
        )
        dk = low(jnp.concatenate([held[0][:, :HD] * (1.0 / LOG2E) for held in carry], axis=1))
        dv = low(jnp.concatenate([held[1][:, :HD] for held in carry], axis=1))
        for part in range(key_tile // piece):
            spot = pl.ds(place_of(first + part * piece, piece), piece)
            out_ref[spot, cols : 2 * cols] = dk[part * piece : (part + 1) * piece]
            out_ref[spot, 2 * cols :] = dv[part * piece : (part + 1) * piece]
        return 0

    lax.fori_loop(0, total // key_tile, keys_tile, 0)

    def finish(slot, inner, spot, place):
        home = pl.ds(pl.multiple_of(place, chunk), chunk)
        joined = jnp.concatenate([dq_sum[s, :HD, home] for s in range(pair)], axis=0)
        out_ref[spot, :cols] = low(joined.T * HD**-0.5)

    each_chunk(me, slots, rows, finish)


def attend_back(
    me, apart, slopes, queries, key_rows, values, mixed, log_total, grads, group, tile=1024, key_tile=512
):
    slots = len(grads)
    total, width = queries.shape
    pair = min(2, width // HD)
    cols = pair * HD
    spec = pl.BlockSpec((total, cols), lambda g: (0, group))
    out_spec = pl.BlockSpec((total, cols), lambda g: (0, 0))
    scalars = pl.BlockSpec(memory_space=pltpu.SMEM)
    return pl.pallas_call(
        functools.partial(
            attend_back_kernel, slots=slots, pair=pair, tile=tile, key_tile=key_tile
        ),
        grid=(1,),
        in_specs=[scalars] * 3
        + [spec] * 3
        + [out_spec, pl.BlockSpec((pair, 1, total), lambda g: (0, 0, 0))]
        + [pl.BlockSpec((total // slots, cols), lambda g: (0, group))] * slots,
        out_specs=pl.BlockSpec((total, 3 * cols), lambda g: (0, 0)),
        out_shape=jax.ShapeDtypeStruct((total, 3 * cols), BF16),
        scratch_shapes=[pltpu.VMEM((pair, total, 128), BF16)] * 4
        + [pltpu.VMEM((pair, 128, total), BF16), pltpu.VMEM((pair, 128, total), F32)],
        compiler_params=pltpu.CompilerParams(vmem_limit_bytes=60 << 20),
        cost_estimate=pl.CostEstimate(
            flops=pair * 2400 * total * total, transcendentals=0, bytes_accessed=16 * total * cols
        ),
        name="attend_back",
    )(
        me,
        apart,
        slopes[group * pair : (group + 1) * pair],
        queries,
        key_rows,
        values,
        mixed,
        log_total,
        *grads,
    )


def whole(shape):
    return pl.BlockSpec(shape, lambda i: (0,) * len(shape))


def row(ref):
    return ref[...].astype(F32)[None, :]


def choose(slot, refs):
    rows = refs[0][...]
    for at, ref in enumerate(refs[1:], 1):
        rows = jnp.where(slot == at, ref[...], rows)
    return rows


def slot_specs(count, per, block, width, order=lambda i: i):
    return [
        pl.BlockSpec(
            (block, width), lambda i, at=at: (jnp.clip(order(i) - at * per, 0, per - 1), 0)
        )
        for at in range(count)
    ]


def tall_spec(chosen, per, block, width):
    return pl.BlockSpec(
        (block, width),
        lambda i: ((chosen.start + chosen.step * (i // per)) * per + i % per, 0),
    )


def kernel_call(kernel, grid, in_specs, out_specs, out_shape, inputs, held=(), **more):
    return pl.pallas_call(
        kernel,
        grid=grid,
        in_specs=in_specs + [pl.BlockSpec(memory_space=pl.ANY)] * len(held),
        out_specs=out_specs,
        out_shape=out_shape,
        input_output_aliases={len(inputs) + at: at for at in range(len(held))},
        compiler_params=pltpu.CompilerParams(vmem_limit_bytes=56 << 20),
        cost_estimate=SMALL_COST,
        **more,
    )(*inputs, *held)


def shape_of(rows, cols, kind=BF16):
    return jax.ShapeDtypeStruct((rows, cols), kind)


def project_kernel(*refs, count, per):
    x_refs = refs[:count]
    gain_ref, shift_ref, wq_ref, wk_ref, wv_ref, qb_ref, vb_ref = refs[count : count + 7]
    normed_ref, q_ref, k_ref, v_ref = refs[-4:]
    x = choose(pl.program_id(0) // per, x_refs).astype(F32)
    normed = low(norm_stats(x)[0] * row(gain_ref) + row(shift_ref))
    normed_ref[...] = normed
    q_ref[...] = low((dot(normed, wq_ref[...]) + row(qb_ref)) * (LOG2E * HD**-0.5))
    k_ref[...] = low(dot(normed, wk_ref[...]))
    v_ref[...] = low(dot(normed, wv_ref[...]) + row(vb_ref))


def project(x_parts, chosen, slots, vectors, weights, biases, held):
    rows, width = x_parts[0].shape
    block = min(rows, 512)
    per = rows // block
    widths = [width] + [weight.shape[1] for weight in weights]
    return kernel_call(
        functools.partial(project_kernel, count=len(chosen), per=per),
        (len(chosen) * per,),
        slot_specs(len(chosen), per, block, width)
        + [whole(a.shape) for a in (*vectors, *weights, *biases)],
        [tall_spec(chosen, per, block, cols) for cols in widths],
        [shape_of(slots * rows, cols) for cols in widths],
        [*x_parts, *vectors, *weights, *biases],
        held,
        name="project",
    )


def act_grad_kernel(*refs, count, per):
    down_ref, grad_ref, cot_ref = refs[count:]
    cot = choose(pl.program_id(0) // per, refs[:count])
    cot_ref[...] = cot
    grad_ref[...] = low(dot(cot, down_ref[...], NT))


def act_grad_step(cot_parts, down):
    slots = len(cot_parts)
    rows, width = cot_parts[0].shape
    block = min(rows, 1024)
    per = rows // block
    units = down.shape[0]
    return kernel_call(
        functools.partial(act_grad_kernel, count=slots, per=per),
        (slots * per,),
        slot_specs(slots, per, block, width) + [whole(down.shape)],
        [pl.BlockSpec((block, cols), lambda i: (i, 0)) for cols in (units, width)],
        [shape_of(slots * rows, cols) for cols in (units, width)],
        [*cot_parts, down],
        (),
        name="act_grad",
    )


def post_kernel(*refs, slots, groups, per):
    mixed_refs = refs[: slots * groups]
    x_refs = refs[slots * groups : slots * groups + slots]
    weight_refs = refs[slots * groups + slots : slots * groups + 2 * slots]
    bias_ref, gain_ref, shift_ref, post_ref, residual_ref = refs[-5:]
    blocks = pl.num_programs(0)
    at = (pl.program_id(0) + blocks // 2) % blocks
    residual = choose(at // per, x_refs).astype(F32) + row(bias_ref)
    for slot in range(slots):
        mixed = [ref[...] for ref in mixed_refs[slot * groups : (slot + 1) * groups]]
        residual = residual + dot(jnp.concatenate(mixed, axis=1), weight_refs[slot][...])
    normal, _ = norm_stats(residual)
    post_ref[...] = low(normal * row(gain_ref) + row(shift_ref))

    @pl.when(at < per)
    def _():
        residual_ref[...] = residual


def post_norm(mixed, x_parts, weights, bias, gain, shift):
    slots, groups = len(mixed), len(mixed[0])
    rows, width = x_parts[0].shape
    block = min(rows, 512)
    per = rows // block
    blocks = slots * per
    order = lambda i: (i + blocks // 2) % blocks
    specs = [
        pl.BlockSpec(
            (block, part.shape[1]),
            lambda i, slot=slot: (((order(i) // per) ^ slot) * per + order(i) % per, 0),
        )
        for slot in range(slots)
        for part in mixed[slot]
    ]
    return kernel_call(
        functools.partial(post_kernel, slots=slots, groups=groups, per=per),
        (blocks,),
        specs
        + slot_specs(slots, per, block, width, order)
        + [whole(a.shape) for a in (*weights, bias, gain, shift)],
        [
            pl.BlockSpec((block, width), lambda i: (order(i), 0)),
            pl.BlockSpec((block, width), lambda i: (jnp.clip(i - blocks // 2, 0, per - 1), 0)),
        ],
        [shape_of(slots * rows, width), shape_of(rows, width, F32)],
        [*[part for parts in mixed for part in parts], *x_parts, *weights, bias, gain, shift],
        (),
        name="post_norm",
    )


def feed_kernel(*refs, count, per, extras, held):
    post_ref, act_grad_ref, up_ref, bias_ref = refs[:4]
    extra_refs = refs[4 : 4 + extras]
    active_ref, grad_ref, sum_ref = refs[4 + extras + held : 7 + extras + held]
    back_refs = refs[7 + extras + held :]
    slot = pl.program_id(0) // per

    @pl.when(pl.program_id(0) == 0)
    def _():
        sum_ref[...] = jnp.zeros_like(sum_ref)

    post = post_ref[...]
    units = active_ref.shape[1]
    chunk = min(512, units)
    scale, cubic = math.sqrt(2 / math.pi), 0.044715
    for first in range(0, units, chunk):
        cols = slice(first, first + chunk)
        hidden = dot(post, up_ref[:, cols]) + row(bias_ref)[:, cols]
        square = hidden * hidden
        curve = jnp.tanh(hidden * (scale + scale * cubic * square))
        half = 0.5 + 0.5 * curve
        active_ref[:, cols] = low(hidden * half)
        slope = half + (0.5 * hidden) * (1.0 - curve * curve) * (
            scale + 3 * scale * cubic * square
        )
        grad = low(act_grad_ref[:, cols].astype(F32) * slope)
        grad_ref[:, cols] = grad
        sum_ref[:, cols] += jnp.sum(grad.astype(F32), axis=0, keepdims=True)
    back = dot(grad_ref[...], up_ref[...], NT)
    if extras:
        back = back + choose(slot, extra_refs).astype(F32)
    back = low(back)
    for at, back_ref in enumerate(back_refs):

        @pl.when(slot == at)
        def _():
            back_ref[...] = back


def feed(post_all, act_grad, up, up_bias, slots, chosen, extras, held):
    count = len(chosen)
    total, width = post_all.shape
    rows, units = total // slots, up.shape[1]
    block = min(rows, 512)
    per = rows // block
    tall = lambda cols: tall_spec(chosen, per, block, cols)
    active, grad, sums, *backs = kernel_call(
        functools.partial(
            feed_kernel, count=count, per=per, extras=len(extras), held=len(held)
        ),
        (count * per,),
        [tall(width), tall(units), whole(up.shape), whole(up_bias.shape)]
        + slot_specs(len(extras), per, block, width),
        [tall(units), tall(units), whole((1, units))] + slot_specs(count, per, block, width),
        [shape_of(total, units), shape_of(total, units), shape_of(1, units, F32)]
        + [shape_of(rows, width)] * count,
        [post_all, act_grad, up, up_bias, *extras],
        held,
        name="feed",
    )
    return (active, grad), sums, backs


def split_rows(total, me, keep_ref, send_ref, streams):
    rows = total.shape[0] // streams
    for slot in range(streams):
        part = low(total[pl.ds(pl.multiple_of((me ^ slot) * rows, rows), rows), :])
        ref = send_ref if slot % 2 else keep_ref
        ref[slot // 2 * rows : (slot // 2 + 1) * rows, :] = part


def outer_kernel(me_ref, left_ref, right_ref, keep_ref, send_ref, total, *, streams):
    step = pl.program_id(0)

    @pl.when(step == 0)
    def _():
        total[...] = dot(left_ref[...], right_ref[...], TN)

    @pl.when(step > 0)
    def _():
        total[...] += dot(left_ref[...], right_ref[...], TN)

    @pl.when(step == pl.num_programs(0) - 1)
    def _():
        split_rows(total, me_ref[0], keep_ref, send_ref, streams)


def outer_step(left, right, me, streams):
    total = left.shape[0]
    block = min(total, 1024)
    shape = (left.shape[1], right.shape[1])
    half = (shape[0] // 2, shape[1])
    return kernel_call(
        functools.partial(outer_kernel, streams=streams),
        (total // block,),
        [pl.BlockSpec(memory_space=pltpu.SMEM)]
        + [pl.BlockSpec((block, cols), lambda i: (i, 0)) for cols in shape],
        [whole(half)] * 2,
        [shape_of(*half)] * 2,
        [me, left, right],
        scratch_shapes=[pltpu.VMEM(shape, F32)],
        name="outer_step",
    )


def join_kernel(me_ref, *refs, early, streams):
    parts, (keep_ref, send_ref) = refs[:-2], refs[-2:]
    rows = parts[0].shape[0] // streams
    for slot in range(streams):
        home = pl.ds(pl.multiple_of((me_ref[0] ^ slot) * rows, rows), rows)
        out = send_ref if slot % 2 else keep_ref
        here = slice(slot // 2 * rows, (slot // 2 + 1) * rows)
        at = 0
        for part in parts[:early]:
            out[here, at : at + part.shape[1]] = part[home, :]
            at += part.shape[1]
        total = parts[early][home, :].astype(F32)
        for part in parts[early + 1 :]:
            total = total + part[home, :].astype(F32)
        out[here, at:] = low(total)


def join_step(early, terms, me, streams):
    inputs = [*early, *terms]
    cols = sum(part.shape[1] for part in early) + terms[0].shape[1]
    half = (terms[0].shape[0] // 2, cols)
    return kernel_call(
        functools.partial(join_kernel, early=len(early), streams=streams),
        (1,),
        [pl.BlockSpec(memory_space=pltpu.SMEM)] + [whole(a.shape) for a in inputs],
        [whole(half)] * 2,
        [shape_of(*half)] * 2,
        [me, *inputs],
        name="join_step",
    )


def late_kernel(*refs):
    (keep, come, keep_late, come_late), outs = refs[:4], refs[4:]
    rows, cols = outs[0].shape[0], keep.shape[1]
    for slot, out in enumerate(outs):
        here = slice(slot * rows, (slot + 1) * rows)
        out[:, :cols] = low(keep[here, :].astype(F32) + come[here, :].astype(F32))
        out[:, cols:] = low(keep_late[here, :].astype(F32) + come_late[here, :].astype(F32))


def late_step(pairs, slots):
    inputs = [array for pair in pairs for array in pair]
    shape = (inputs[0].shape[0] // slots, inputs[0].shape[1] + inputs[2].shape[1])
    return kernel_call(
        late_kernel,
        (1,),
        [whole(a.shape) for a in inputs],
        [whole(shape)] * slots,
        [shape_of(*shape)] * slots,
        inputs,
        name="late_step",
    )


def pair_kernel(*refs, count):
    parts, outs = refs[: 2 * count], refs[2 * count :]
    rows = outs[0].shape[0] // count
    for at in range(count):
        keep, come = parts[2 * at : 2 * at + 2]
        for slot, out in enumerate(outs):
            here = slice(slot * rows, (slot + 1) * rows)
            out[at * rows : (at + 1) * rows, :] = low(
                keep[here, :].astype(F32) + come[here, :].astype(F32)
            )


def pair_step(pairs, slots):
    inputs = [array for pair in pairs for array in pair]
    rows, cols = inputs[0].shape
    shape = (rows // slots * len(pairs), cols)
    return kernel_call(
        functools.partial(pair_kernel, count=len(pairs)),
        (1,),
        [whole(a.shape) for a in inputs],
        [whole(shape)] * slots,
        [shape_of(*shape)] * slots,
        inputs,
        name="pair_step",
    )


def stack_kernel(*refs):
    rows = refs[0].shape[0]
    for at, ref in enumerate(refs[:-1]):
        refs[-1][at * rows : (at + 1) * rows, :] = ref[...]


def stack_step(parts):
    rows, cols = parts[0].shape
    return kernel_call(
        stack_kernel,
        (1,),
        [whole((rows, cols))] * len(parts),
        [whole((rows * len(parts), cols))],
        [shape_of(rows * len(parts), cols)],
        list(parts),
        name="stack_step",
    )[0]


def shard_views(even_ref, odd_ref, streams):
    rows = even_ref.shape[0] // (streams // 2)
    return [
        (slot, ref.at[slot // 2 * rows : (slot // 2 + 1) * rows])
        for slot, ref in enumerate([even_ref, odd_ref] * (streams // 2))
    ]


def feed_grads_kernel(me_ref, even_ref, odd_ref, up_ref, down_ref, up_rows, *, streams):
    rows = even_ref.shape[0] // streams
    for slot, part in shard_views(even_ref, odd_ref, streams):
        home = pl.ds(pl.multiple_of((me_ref[0] ^ slot) * rows, rows), rows)
        up_rows[home, :] = part[:rows, :].astype(F32)
        down_ref[home, :] = part[rows:, :].astype(F32)
    up_ref[...] = up_rows[...].T


def feed_grads(even, odd, me, streams):
    units, width = even.shape
    return kernel_call(
        functools.partial(feed_grads_kernel, streams=streams),
        (1,),
        [pl.BlockSpec(memory_space=pltpu.SMEM)] + [whole(even.shape)] * 2,
        [whole((width, units)), whole((units, width))],
        [shape_of(width, units, F32), shape_of(units, width, F32)],
        [me, even, odd],
        scratch_shapes=[pltpu.VMEM((units, width), F32)],
        name="feed_grads",
    )


def pack_kernel(*refs, groups):
    sums_ref, gain_ref, shift_ref = refs[:3]
    row_refs, count_refs = refs[3 : 3 + groups], refs[3 + groups : 3 + 2 * groups]
    unit_refs, out_ref = refs[3 + 2 * groups : -1], refs[-1]
    out_ref[...] = jnp.zeros_like(out_ref)
    out_ref[:4, : sums_ref.shape[1]] = sums_ref[:4, :]
    rows = row_refs[0][...]
    for ref in row_refs[1:]:
        rows = rows + ref[...]
    out_ref[4:5, : rows.shape[1]] = (rows[0:1] - row(shift_ref) * rows[1:2]) / row(gain_ref)
    out_ref[5:6, : rows.shape[1]] = rows[1:2]
    units = unit_refs[0][...]
    for ref in unit_refs[1:]:
        units = units + ref[...]
    out_ref[8:9, : units.shape[1]] = units
    for at, ref in enumerate(count_refs):
        out_ref[9 + at : 10 + at, : ref.shape[1]] = ref[...]


def pack(row_sums, gain, shift, group_rows, group_counts, unit_sums):
    inputs = [row_sums, gain, shift, *group_rows, *group_counts, *unit_sums]
    wide = max(a.shape[1] for a in (row_sums, *group_counts, *unit_sums))
    return kernel_call(
        functools.partial(pack_kernel, groups=len(group_rows)),
        (1,),
        [whole(a.shape) for a in inputs],
        [whole((16, wide))],
        [shape_of(16, wide, F32)],
        inputs,
        name="pack",
    )[0]


def resid_kernel(*refs, terms, slots):
    term_refs = refs[:terms]
    residual_ref, cot_ref, gain_ref = refs[terms : terms + 3]
    weight_refs = refs[terms + 3 : terms + 3 + slots]
    grad_ref, low_ref, sums_ref = refs[terms + 3 + slots : terms + 6 + slots]
    part_refs = refs[terms + 6 + slots :]

    @pl.when(pl.program_id(0) == 0)
    def _():
        sums_ref[...] = jnp.zeros_like(sums_ref)

    post_grad = term_refs[0][...].astype(F32)
    for ref in term_refs[1:]:
        post_grad = post_grad + ref[...].astype(F32)
    cot = cot_ref[...].astype(F32)
    normal, inverse = norm_stats(residual_ref[...])
    grad = cot + norm_pull(post_grad * row(gain_ref), normal, inverse)
    grad_ref[...] = grad
    grad_low = low(grad)
    low_ref[...] = grad_low
    for weight_ref, part_ref in zip(weight_refs, part_refs):
        part_ref[...] = low(dot(grad_low, weight_ref[...], NT))
    for at, value in enumerate((cot, grad, post_grad * normal, post_grad)):
        sums_ref[at : at + 1, :] += jnp.sum(value, axis=0, keepdims=True)


def resid_step(terms, residual, cotangent, gain, weights):
    rows, width = residual.shape
    block = min(rows, 256)
    tall = lambda cols: pl.BlockSpec((block, cols), lambda i: (i, 0))
    cols = weights[0].shape[0]
    return kernel_call(
        functools.partial(resid_kernel, terms=len(terms), slots=len(weights)),
        (rows // block,),
        [tall(width)] * (len(terms) + 2) + [whole(a.shape) for a in (gain, *weights)],
        [tall(width), tall(width), whole((8, width))] + [tall(cols)] * len(weights),
        [shape_of(rows, width, F32), shape_of(rows, width), shape_of(8, width, F32)]
        + [shape_of(rows, cols)] * len(weights),
        [*terms, residual, cotangent, gain, *weights],
        (),
        name="resid_step",
    )


def dense_grad_kernel(*refs, slots, groups):
    mixed_refs, grad_ref = refs[: slots * groups], refs[slots * groups]
    even_ref, odd_ref, *sum_refs = refs[slots * groups + 1 :]
    step = pl.program_id(0)
    grad = grad_ref[...]
    for slot in range(slots):
        mixed = [ref[...] for ref in mixed_refs[slot * groups : (slot + 1) * groups]]
        part = dot(grad, jnp.concatenate(mixed, axis=1), TN)
        sum_refs[slot][...] = jnp.where(step == 0, 0.0, sum_refs[slot][...]) + part

    @pl.when(step == pl.num_programs(0) - 1)
    def _():
        rows = sum_refs[0].shape[0]
        for slot, sum_ref in enumerate(sum_refs):
            out_ref = odd_ref if slot % 2 else even_ref
            out_ref[slot // 2 * rows : (slot // 2 + 1) * rows, :] = low(sum_ref[...])


def dense_grad(mixed, grad):
    slots, groups = len(mixed), len(mixed[0])
    rows, width = grad.shape
    block = min(rows, 512)
    per = rows // block
    cols = sum(part.shape[1] for part in mixed[0])
    return kernel_call(
        functools.partial(dense_grad_kernel, slots=slots, groups=groups),
        (per,),
        [
            pl.BlockSpec((block, part.shape[1]), lambda i, slot=slot: (slot * per + i, 0))
            for slot in range(slots)
            for part in mixed[slot]
        ]
        + [pl.BlockSpec((block, width), lambda i: (i, 0))],
        [whole((width * slots // 2, cols))] * 2,
        [shape_of(width * slots // 2, cols)] * 2,
        [*[part for parts in mixed for part in parts], grad],
        (),
        scratch_shapes=[pltpu.VMEM((width, cols), F32)] * slots,
        name="dense_grad",
    )


def weight_kernel(me_ref, normed_ref, grad_ref, wq_ref, wk_ref, wv_ref, *refs, streams):
    *out_refs, sums_ref, count_ref, total, count = refs
    step = pl.program_id(0)

    @pl.when(step == 0)
    def _():
        total[...] = jnp.zeros_like(total)
        count[...] = jnp.zeros_like(count)

    grad = grad_ref[...]
    total[...] += dot(normed_ref[...], grad, TN)
    count[...] += jnp.sum(grad.astype(F32), axis=0, keepdims=True)

    @pl.when(step == pl.num_programs(0) - 1)
    def _():
        weight = jnp.concatenate([wq_ref[...], wk_ref[...], wv_ref[...]], axis=1).astype(F32)
        if streams:
            split_rows(total, me_ref[0], *out_refs, streams)
        else:
            out_refs[0][...] = low(total[...])
        count_ref[...] = count[...]
        lane = lanes(weight.shape[0])
        cross = jnp.sum(weight * total[...], axis=1, keepdims=True)
        plain = jnp.sum(weight * count[...], axis=1, keepdims=True)
        both = jnp.where(lane == 0, cross, jnp.where(lane == 1, plain, 0.0))
        sums_ref[...] = both.T[:8]


def weight_step(normed, grad, weights, group, me, streams):
    total, width = normed.shape
    cols = grad.shape[1]
    block = min(total, 1024)
    outs = [(width // 2, cols)] * 2 if streams else [(width, cols)]
    *parts, sums, count = kernel_call(
        functools.partial(weight_kernel, streams=streams),
        (total // block,),
        [pl.BlockSpec(memory_space=pltpu.SMEM)]
        + [pl.BlockSpec((block, count), lambda i: (i, 0)) for count in (width, cols)]
        + [pl.BlockSpec((width, cols // 3), lambda i: (0, group))] * 3,
        [whole(shape) for shape in outs] + [whole((8, width)), whole((1, cols))],
        [shape_of(*shape) for shape in outs] + [shape_of(8, width, F32), shape_of(1, cols, F32)],
        [me, normed, grad, *weights],
        scratch_shapes=[pltpu.VMEM((width, cols), F32), pltpu.VMEM((1, cols), F32)],
        name="weight_step",
    )
    return parts, sums, count


def unproject_kernel(*refs, groups, per, extras):
    grad_refs, weight_refs = refs[:groups], refs[groups : 4 * groups]
    extra_refs = refs[4 * groups : 4 * groups + extras]
    out_refs = refs[4 * groups + extras : -1]
    joined = refs[-1]
    slot = pl.program_id(0) // per

    @pl.when(pl.program_id(0) == 0)
    def _():
        joined[...] = jnp.concatenate([ref[...] for ref in weight_refs], axis=1)

    total = dot(jnp.concatenate([ref[...] for ref in grad_refs], axis=1), joined[...], NT)
    if extras:
        total = total + choose(slot, extra_refs).astype(F32)
    total = low(total)
    for at, ref in enumerate(out_refs):

        @pl.when(slot == at)
        def _():
            ref[...] = total


def unproject(grads, weights, slots, chosen, extras):
    width = weights[0].shape[0]
    count, groups = len(chosen), len(grads)
    total, cols = grads[0].shape
    rows = total // slots
    block = min(rows, 512)
    per = rows // block
    return kernel_call(
        functools.partial(unproject_kernel, groups=groups, per=per, extras=len(extras)),
        (count * per,),
        [tall_spec(chosen, per, block, cols)] * groups
        + [
            pl.BlockSpec((width, cols // 3), lambda i, group=group: (0, group))
            for group in range(groups)
            for _ in weights
        ]
        + slot_specs(len(extras), per, block, width),
        slot_specs(count, per, block, width),
        [shape_of(rows, width)] * count,
        [*grads, *[weight for _ in grads for weight in weights], *extras],
        (),
        scratch_shapes=[pltpu.VMEM((width, cols * groups), BF16)],
        name="unproject",
    )


def ffn_kernel(active_ref, weight_ref, even_ref, odd_ref, *, per):
    total = low(dot(active_ref[...], weight_ref[...]))
    odd = pl.program_id(0) // per % 2

    @pl.when(odd == 0)
    def _():
        even_ref[...] = total

    @pl.when(odd == 1)
    def _():
        odd_ref[...] = total


def ffn_step(active, weight, slots):
    total, units = active.shape
    width = weight.shape[1]
    rows = total // slots
    block = min(rows, 1024)
    per = rows // block
    half = (total // 2, width)

    def half_spec(odd):
        def place(i):
            slot, step = i // per, i % per
            now = slot // 2 * per
            if odd:
                return (jnp.where(slot % 2 == 1, now + step, jnp.maximum(now - 1, 0)), 0)
            return (jnp.where(slot % 2 == 0, now + step, now + per - 1), 0)

        return pl.BlockSpec((block, width), place)

    return kernel_call(
        functools.partial(ffn_kernel, per=per),
        (slots * per,),
        [pl.BlockSpec((block, units), lambda i: (i, 0)), whole(weight.shape)],
        [half_spec(0), half_spec(1)],
        [shape_of(*half)] * 2,
        [active, weight],
        name="ffn_step",
    )


def spread_kernel(me_ref, even_ref, odd_ref, *refs, groups, streams):
    *out_refs, dense_ref, dense_rows = refs
    cols = out_refs[0].shape[1] // groups
    heads = dense_ref.shape[0]
    rows = even_ref.shape[0] * 2 // streams
    for slot, part in shard_views(even_ref, odd_ref, streams):
        home = pl.ds(pl.multiple_of((me_ref[0] ^ slot) * rows, rows), rows)
        for group in range(groups):
            first = group * 3 * cols + (heads if group == groups - 1 else 0)
            for kind in range(3):
                at = first + kind * cols
                out_refs[kind][home, group * cols : (group + 1) * cols] = part[
                    :, at : at + cols
                ].astype(F32)
        first = (groups - 1) * 3 * cols
        dense_rows[home, :] = part[:, first : first + heads].astype(F32)
    dense_ref[...] = dense_rows[...].T


def spread(even, odd, me, streams, groups, heads):
    width = even.shape[0] * 2
    shapes = [(width, heads)] * 3 + [(heads, width)]
    return kernel_call(
        functools.partial(spread_kernel, groups=groups, streams=streams),
        (1,),
        [pl.BlockSpec(memory_space=pltpu.SMEM)] + [whole(even.shape)] * 2,
        [whole(shape) for shape in shapes],
        [shape_of(*shape, F32) for shape in shapes],
        [me, even, odd],
        scratch_shapes=[pltpu.VMEM((width, heads), F32)],
        name="spread",
    )


def input_kernel(*refs, terms):
    x_ref, resid_ref, gain_ref, out_ref = refs[terms:]
    grad = refs[0][...].astype(F32)
    for ref in refs[1:terms]:
        grad = grad + ref[...].astype(F32)
    normal, inverse = norm_stats(x_ref[...].astype(F32))
    out_ref[...] = resid_ref[...] + norm_pull(grad * row(gain_ref), normal, inverse)


def input_step(terms, layer_input, resid_grad, gain):
    rows, width = resid_grad.shape
    block = min(rows, 256)
    tall = pl.BlockSpec((block, width), lambda i: (i, 0))
    return kernel_call(
        functools.partial(input_kernel, terms=len(terms)),
        (rows // block,),
        [tall] * (len(terms) + 2) + [whole(gain.shape)],
        [tall],
        [shape_of(rows, width, F32)],
        [*terms, layer_input, resid_grad, gain],
        name="input_step",
    )[0]


def shards(
    slots,
    streams,
    layer_input,
    row_ids,
    input_gain,
    input_shift,
    query_weight,
    query_bias,
    key_weight,
    value_weight,
    value_bias,
    dense_weight,
    dense_bias,
    post_gain,
    post_shift,
    up_weight,
    up_bias,
    down_weight,
    down_bias,
    cotangent,
):
    me = lax.axis_index("tensor")
    me_word = me.astype(jnp.int32)[None]
    stream = lax.axis_index("dp").astype(jnp.int32)[None]
    rows = layer_input.shape[0]
    head_cols = query_weight.shape[1]
    head_count = head_cols // HD
    groups = max(1, head_count // 2)
    bits = [1 << level for level in range(slots.bit_length() - 1)]
    half = slots // 2
    after = lambda array, *others: lax.optimization_barrier((array, *others))[0]

    def swap(array, mask):
        return lax.ppermute(array, "tensor", [(i, i ^ mask) for i in range(slots)])

    def gather(array):
        held = {0: array}
        for bit in reversed(bits):
            held.update({slot ^ bit: swap(part, bit) for slot, part in held.items()})
        return [held[slot] for slot in range(slots)]

    def blocks(array):
        return [array[slot * rows : (slot + 1) * rows] for slot in range(slots)]

    def swap_data(array, mask):
        return lax.ppermute(array, "dp", [(i, i ^ mask) for i in range(streams)])

    def finish_terms(held, terms, levels):
        for bit in levels:
            come = {slot ^ bit: swap(part, bit) for slot, part in held.items() if slot & bit}
            if 0 in come:
                terms.append(come.pop(0))
            held = {
                slot: low(held[slot].astype(F32) + part.astype(F32)) for slot, part in come.items()
            }
        return terms

    def scatter_terms(parts):
        return finish_terms(dict(enumerate(parts)), [parts[0]], bits)

    far_odd = range(half + 1, slots, 2)
    far_even = range(half, slots, 2)
    near_odd = range(1, half, 2)
    near_even = range(0, half, 2)

    def ordered_terms(make):
        far = make(far_odd, (), None)
        far_come = [swap(part, 1) for part in far]
        near = make(near_odd, (), far[-1])
        near_come = [swap(part, 1) for part in near]
        far = make(far_even, far_come, near[-1])
        near = make(near_even, near_come, far[-1])
        held = dict(zip((*far_even, *near_even), (*far, *near)))
        return finish_terms(held, [held.pop(0)], bits[1:])

    def add_up(terms):
        return functools.reduce(
            lambda sum_now, term: sum_now + term.astype(F32), terms[1:], terms[0].astype(F32)
        )

    far_streams = range(2, streams, 2)

    def exchange(parts):
        return low(add_up([parts[0], *[swap_data(parts[k // 2], k) for k in far_streams]]))

    def collect_far(shard):
        return [shard, *[swap_data(shard, k) for k in far_streams]]

    norm_vectors = (input_gain, input_shift)
    weights = (query_weight, key_weight, value_weight)
    biases = (query_bias, value_bias)
    x_held = {0: layer_input}
    for bit in reversed(bits[1:]):
        x_held.update({slot ^ bit: swap(part, bit) for slot, part in x_held.items()})
    x_held[1] = swap(x_held[0], 1)
    near_parts = [x_held[0], x_held[1]]
    first = range(2)
    held = project(near_parts, first, slots, norm_vectors, weights, biases, ())
    rest = sorted(slot for slot in x_held if slot > 1)
    *arrived, normed = lax.optimization_barrier((*[x_held[slot] for slot in rest], held[0]))
    held = (normed, *held[1:])
    for slot, part in zip(rest, arrived):
        x_held[slot], x_held[slot ^ 1] = part, swap(part, 1)
    x_parts = [x_held[slot] for slot in range(slots)]
    dense_parts = gather(after(dense_weight, arrived[-1]))
    cot_own = after(cotangent, arrived[-1])
    cot_held = {0: cot_own}
    for bit in reversed(bits[1:]):
        cot_held.update({slot ^ bit: swap(part, bit) for slot, part in cot_held.items()})
    normed, queries, key_rows, values = project(
        x_parts[2:], range(2, slots), slots, norm_vectors, weights, biases, held
    )

    heads = me * head_count + jnp.arange(head_count)
    slopes = jnp.exp2(-8.0 * (heads + 1).astype(F32) / HEADS) * LOG2E
    apart = (row_ids[:1] != row_ids[SHORT : SHORT + 1]).astype(jnp.int32)

    mixed_own, log_totals, mixed_parts = [], [], []
    for group in range(groups):
        mixed, log_total = attend(
            me_word,
            apart,
            slopes,
            queries if not group else after(queries, cot_held[half], mixed_own[-1]),
            key_rows,
            values,
            slots,
            group,
        )
        mixed_own.append(mixed)
        log_totals.append(log_total)
        if not group:
            keys = sorted(cot_held)
            held = lax.optimization_barrier((*[cot_held[key] for key in keys], mixed))[:-1]
            cot_held.update(zip(keys, held))
            cot_held.update({slot ^ 1: swap(part, 1) for slot, part in cot_held.items()})
            cot_parts = [cot_held[slot] for slot in range(slots)]
        if group < groups - 1:
            mixed_parts.append(gather(mixed))
    act_grad, cot_all = act_grad_step(
        lax.optimization_barrier((*cot_parts, mixed_own[-1], *dense_parts[2:]))[:slots], down_weight
    )
    came = {0: mixed_own[-1]}
    for bit in reversed(bits[1:]):
        came.update({slot ^ bit: swap(part, bit) for slot, part in came.items()})
    far_slots = sorted(came)[1:]
    *arrived, act_grad = lax.optimization_barrier((*[came[slot] for slot in far_slots], act_grad))
    came.update(zip(far_slots, arrived))
    came.update({slot ^ 1: swap(part, 1) for slot, part in came.items()})
    mixed_parts.append([came[slot] for slot in range(slots)])
    mixed_all = [[mixed_parts[group][slot] for group in range(groups)] for slot in range(slots)]
    post_all, residual = post_norm(
        mixed_all, x_parts, dense_parts, dense_bias, post_gain, post_shift
    )

    fed, up_bias_parts = [()], []

    def make_feed(chosen, extras, gate):
        held, sums, backs = feed(
            post_all, act_grad, up_weight, up_bias, slots, chosen, extras, fed[-1]
        )
        fed.append(held)
        up_bias_parts.append(sums)
        return backs

    post_terms = ordered_terms(make_feed)
    active, hidden_grad = fed[-1]
    up_keep, up_send = outer_step(hidden_grad, post_all, stream, streams)
    down_keep, down_send = outer_step(active, after(cot_all, up_keep), stream, streams)
    up_come, down_come = swap_data(up_send, 1), swap_data(down_send, 1)
    resid_grad, attended_grad, row_sums, *mixed_grads = resid_step(
        [after(post_terms[0], down_keep), *post_terms[1:]],
        residual,
        cotangent,
        post_gain,
        dense_parts,
    )
    mixed_grads = [swap(part, slot) if slot else part for slot, part in enumerate(mixed_grads)]
    dense_even, dense_odd = dense_grad(mixed_all, attended_grad)
    ffn_even, ffn_odd = ffn_step(after(active, dense_odd), down_weight, slots)
    feed_parts = pair_step(
        [(after(up_keep, ffn_odd), up_come), (down_keep, down_come)], streams // 2
    )
    moved = lax.optimization_barrier((*mixed_grads, dense_odd, ffn_odd, *feed_parts))
    mixed_grads, (dense_odd, ffn_odd), feed_parts = (
        moved[:slots],
        moved[slots : slots + 2],
        moved[slots + 2 :],
    )
    dense_come, ffn_come = swap(dense_odd, 1), swap(ffn_odd, 1)

    def partner_sums(even, come):
        size = even.shape[0] * 2 // slots
        cuts = [slice(at * size, (at + 1) * size) for at in range(slots // 2)]
        return [low(even[cut].astype(F32) + come[cut].astype(F32)) for cut in cuts]

    cols = head_cols // groups
    head_grads, early_parts, group_rows, group_counts = [], [], [], []

    def backward(group):
        return attend_back(
            me_word,
            apart,
            slopes,
            queries,
            key_rows,
            values,
            mixed_own[group],
            log_totals[group],
            mixed_grads,
            group,
        )

    dense_sums = partner_sums(dense_even, dense_come)
    for group in range(groups - 1):
        head_grads.append(backward(group))
        grad = head_grads[-1]
        if group == groups - 2:
            grad, *dense_sums = lax.optimization_barrier((grad, *dense_sums))
        parts, row_part, count_part = weight_step(normed, grad, weights, group, stream, 0)
        early_parts += parts
        group_rows.append(row_part)
        group_counts.append(count_part)
        mixed_grads = lax.optimization_barrier((*mixed_grads, parts[-1]))[:-1]
    even_slots = range(2, slots, 2)
    dense_terms = finish_terms(dict(zip(even_slots, dense_sums[1:])), [dense_sums[0]], bits[1:])
    early_keep, early_send = join_step(early_parts, dense_terms, stream, streams)
    moved = lax.optimization_barrier(
        (*mixed_grads, early_send, exchange(feed_parts), *partner_sums(ffn_even, ffn_come))
    )
    mixed_grads, (early_send, feed_shard), ffn_sums = (
        moved[:slots],
        moved[slots : slots + 2],
        moved[slots + 2 :],
    )
    early_come = swap_data(early_send, 1)
    feed_shards = collect_far(feed_shard)
    ffn_terms = finish_terms(dict(zip(even_slots, ffn_sums[1:])), [ffn_sums[0]], bits[1:])
    head_grads.append(backward(groups - 1))
    grad, early_come, *arrived = lax.optimization_barrier(
        (head_grads[-1], early_come, *feed_shards, *ffn_terms)
    )
    feed_shards, ffn_terms = arrived[: len(feed_shards)], arrived[len(feed_shards) :]
    (late_keep, late_send), row_part, count_part = weight_step(
        normed, grad, weights, groups - 1, stream, streams
    )
    group_rows.append(row_part)
    group_counts.append(count_part)
    late_come = swap_data(late_send, 1)
    vectors = pack(row_sums, input_gain, input_shift, group_rows, group_counts, up_bias_parts)
    feed_even = stack_step([*feed_shards[:-1], after(feed_shards[-1], vectors)])
    summed = vectors + swap_data(vectors, 1)
    feed_odd = swap_data(after(feed_even, late_come, summed), 1)
    seen = []

    def make_unproject(chosen, extras, gate):
        gates = [feed_even if gate is None else gate]
        if not seen:
            gates += [late_come, summed]
        seen.append(0)
        return unproject(
            [*head_grads[:-1], after(head_grads[-1], *gates)], weights, slots, chosen, extras
        )

    normed_terms = ordered_terms(make_unproject)
    late_parts = late_step(
        [(early_keep, early_come), (after(late_keep, normed_terms[0]), late_come)], streams // 2
    )
    layer_output = low(residual + add_up(ffn_terms) + down_bias.astype(F32))
    *late_shards, feed_odd, layer_output = lax.optimization_barrier(
        (*collect_far(exchange(late_parts)), feed_odd, layer_output)
    )
    late_even = stack_step(late_shards)
    late_odd = swap_data(late_even, 1)
    for level in range(1, streams.bit_length() - 1):
        summed = summed + swap_data(summed, 1 << level)
    own = summed[8:]
    shared = after(summed, normed_terms[-1])[:8]
    for bit in reversed(bits):
        shared = shared + swap(shared, bit)
    shared = shared[:, : resid_grad.shape[1]]
    up_grad, down_grad = feed_grads(after(feed_even, late_even), feed_odd, stream, streams)
    up_bias_grad = own[0, : up_bias.shape[0]]
    counts = own[1 : 1 + groups]
    query_bias_grad = counts[:, :cols].reshape(-1)
    value_bias_grad = counts[:, 2 * cols : 3 * cols].reshape(-1)
    normed_terms[-1] = after(normed_terms[-1], feed_odd)
    input_grad = input_step(normed_terms, layer_input, resid_grad, input_gain)
    late_even = after(late_even, input_grad)
    *weight_grads, dense_weight_grad = spread(
        late_even, late_odd, stream, streams, groups, head_cols
    )
    return (
        layer_output,
        input_grad,
        shared[4],
        shared[5],
        weight_grads[0],
        query_bias_grad,
        weight_grads[1],
        weight_grads[2],
        value_bias_grad,
        dense_weight_grad,
        shared[1],
        shared[2],
        shared[3],
        up_grad,
        up_bias_grad,
        down_grad,
        shared[0],
    )


def solution(mesh):
    in_specs = (
        P(("dp", "tensor"), None),
        P("dp"),
        P(),
        P(),
        P(None, "tensor"),
        P("tensor"),
        P(None, "tensor"),
        P(None, "tensor"),
        P("tensor"),
        P("tensor", None),
        P(),
        P(),
        P(),
        P(None, "tensor"),
        P("tensor"),
        P("tensor", None),
        P(),
        P(("dp", "tensor"), None),
    )
    out_specs = (
        P(("dp", "tensor"), None),
        P(("dp", "tensor"), None),
        P(),
        P(),
        P(None, "tensor"),
        P("tensor"),
        P(None, "tensor"),
        P(None, "tensor"),
        P("tensor"),
        P("tensor", None),
        P(),
        P(),
        P(),
        P(None, "tensor"),
        P("tensor"),
        P("tensor", None),
        P(),
    )
    return jax.shard_map(
        functools.partial(shards, mesh.shape["tensor"], mesh.shape["dp"]), mesh=mesh, in_specs=in_specs, out_specs=out_specs, check_vma=False)
```

```python
import functools
import math

import jax
import jax.numpy as jnp
from jax import lax
from jax.experimental import pallas as pl
from jax.experimental.pallas import tpu as pltpu
from jax.sharding import PartitionSpec as P

HEADS = 16
HD = 64
SHORT = 2048
EPSILON = 1e-05
LOG2E = math.log2(math.e)
F32 = jnp.float32
BF16 = jnp.bfloat16
SMALL_COST = pl.CostEstimate(flops=1, transcendentals=0, bytes_accessed=1)
NT = (((1,), (1,)), ((), ()))
NN = (((1,), (0,)), ((), ()))
TN = (((0,), (0,)), ((), ()))


def dot(lhs, rhs, dims=NN):
    return lax.dot_general(lhs, rhs, dims, preferred_element_type=F32)


def low(array):
    return array.astype(BF16)


def norm_stats(rows):
    center = jnp.mean(rows, axis=-1, keepdims=True)
    centered = rows - center
    inverse = lax.rsqrt(jnp.mean(centered * centered, axis=-1, keepdims=True) + EPSILON)
    return centered * inverse, inverse


def norm_pull(grad, normal, inverse):
    grad_mean = jnp.mean(grad, axis=-1, keepdims=True)
    dot_mean = jnp.mean(grad * normal, axis=-1, keepdims=True)
    return inverse * (grad - grad_mean - normal * dot_mean)


def lanes(count):
    return lax.broadcasted_iota(jnp.int32, (count, 128), 1)


def places(count, first):
    return lax.broadcasted_iota(jnp.int32, (count, 128), 0) + first


def widen(head):
    return jnp.concatenate([head.astype(F32), jnp.zeros((head.shape[0], HD), F32)], axis=1)


def split3(value):
    high = low(value).astype(F32)
    middle = low(value - high).astype(F32)
    return high, middle, value - high - middle


def pick3(index, parts):
    return jnp.where(index == 0, parts[0], jnp.where(index == 1, parts[1], parts[2]))


def key_columns(head, first):
    count = head.shape[0]
    lane, place = lanes(count), places(count, first)
    coarse = ((place >> 6) << 6).astype(F32)
    fine = (place & 63).astype(F32)
    wall = jnp.where(place < SHORT, -1e30, 0.0)
    extra = jnp.where(lane < 73, -1.0, jnp.where(lane == 73, wall, 0.0))
    extra = jnp.where(lane < 67, coarse, jnp.where(lane < 70, fine, extra))
    return low(jnp.where(lane < HD, widen(head), extra))


def query_columns(head, first, slope, apart, log_total=None):
    count = head.shape[0]
    lane, place = lanes(count), places(count, first)
    extra = pick3(jnp.where(lane < 67, lane - 64, lane - 67), split3(slope))
    extra = jnp.where(lane < 70, extra, 0.0)
    if log_total is not None:
        extra = jnp.where((lane >= 70) & (lane < 73), pick3(lane - 70, split3(log_total)), extra)
    extra = jnp.where(lane == 73, jnp.where(place >= SHORT, apart, 0.0), extra)
    return low(jnp.where(lane < HD, widen(head), extra))


def ones_columns(head, count):
    lane = lanes(head.shape[0])
    return low(jnp.where(lane < HD, widen(head), jnp.where(lane < HD + count, 1.0, 0.0)))


def grad_columns(head, shift):
    lane = lanes(head.shape[0])
    extra = jnp.where(lane < 67, pick3(lane - 64, split3(shift)), 0.0)
    return low(jnp.where(lane < HD, widen(head), extra))


def each_chunk(me, slots, rows, body):
    chunk = min(rows, 512)
    for slot in range(slots):
        home = (me ^ slot) * rows

        @pl.loop(0, rows // chunk)
        def _(step):
            offset = pl.multiple_of(step * chunk, chunk)
            body(slot, pl.ds(offset, chunk), pl.ds(slot * rows + offset, chunk), home + offset)


def attend_kernel(
    me_ref, apart_ref, slope_ref, q_ref, k_ref, v_ref, o_ref, lse_ref, qa, ka, va, *, slots, pair, tile
):
    me = me_ref[0]
    total = q_ref.shape[0]
    rows = total // slots
    chunk = min(rows, 512)
    apart = apart_ref[0].astype(F32)

    def prepare(slot, inner, spot, place):
        place = pl.multiple_of(place, chunk)
        home = pl.ds(place, chunk)
        for s in range(pair):
            cols = slice(s * HD, (s + 1) * HD)
            qa[s, home, :] = query_columns(q_ref[spot, cols], place, slope_ref[s], apart)
            ka[s, home, :] = key_columns(k_ref[spot, cols], place)
            va[s, home, :] = ones_columns(v_ref[spot, cols], 1)

    each_chunk(me, slots, rows, prepare)
    causal = lax.broadcasted_iota(jnp.int32, (tile, tile), 1) <= lax.broadcasted_iota(
        jnp.int32, (tile, tile), 0
    )
    piece = min(rows, tile)

    def query_tile(index, _):
        first = pl.multiple_of(index * tile, tile)
        queries = [qa[s, pl.ds(first, tile), :] for s in range(pair)]

        def step(at, carry, diagonal):
            after = []
            for s in range(pair):
                top, mix = carry[s]
                scores = dot(queries[s], ka[s, pl.ds(at, tile), :], NT)
                if diagonal:
                    scores = jnp.where(causal, scores, -1e30)
                higher = jnp.maximum(top, jnp.max(scores, axis=1, keepdims=True))
                weights = low(jnp.exp2(scores - higher))
                mix = mix * jnp.exp2(top - higher) + dot(weights, va[s, pl.ds(at, tile), :])
                after.append((higher, mix))
            return tuple(after)

        carry = tuple(
            (jnp.full((tile, 1), -1e38, F32), jnp.zeros((tile, 128), F32)) for _ in range(pair)
        )
        carry = step(first, carry, True)
        carry = lax.fori_loop(
            0, index, lambda at, held: step(pl.multiple_of(at * tile, tile), held, False), carry
        )
        outs = []
        for s in range(pair):
            top, mix = carry[s]
            weight = mix[:, HD : HD + 1]
            outs.append(mix[:, :HD] * (1.0 / weight))
            lse_ref[s, 0, pl.ds(first, tile)] = (top + jnp.log2(weight))[:, 0]
        out = low(jnp.concatenate(outs, axis=1))
        for part in range(tile // piece):
            block = (index * (tile // piece) + part) // (rows // piece)
            offset = first + part * piece - block * rows
            spot = pl.multiple_of((block ^ me) * rows + offset, piece)
            o_ref[pl.ds(spot, piece), :] = out[part * piece : (part + 1) * piece]
        return 0

    lax.fori_loop(0, total // tile, query_tile, 0)


def attend(me, apart, slopes, queries, key_rows, values, slots, group, tile=1024):
    total, width = queries.shape
    pair = min(2, width // HD)
    cols = pair * HD
    spec = pl.BlockSpec((total, cols), lambda g: (0, group))
    scalars = pl.BlockSpec(memory_space=pltpu.SMEM)
    return pl.pallas_call(
        functools.partial(attend_kernel, slots=slots, pair=pair, tile=tile),
        grid=(1,),
        in_specs=[scalars] * 3 + [spec] * 3,
        out_specs=[
            pl.BlockSpec((total, cols), lambda g: (0, 0)),
            pl.BlockSpec((pair, 1, total), lambda g: (0, 0, 0)),
        ],
        out_shape=[
            jax.ShapeDtypeStruct((total, cols), BF16),
            jax.ShapeDtypeStruct((pair, 1, total), F32),
        ],
        scratch_shapes=[pltpu.VMEM((pair, total, 128), BF16)] * 3,
        compiler_params=pltpu.CompilerParams(vmem_limit_bytes=56 << 20),
        cost_estimate=pl.CostEstimate(
            flops=pair * 1200 * total * total, transcendentals=0, bytes_accessed=8 * total * cols
        ),
        name="attend",
    )(me, apart, slopes[group * pair : (group + 1) * pair], queries, key_rows, values)


def attend_back_kernel(*refs, slots, pair, tile, key_tile):
    me_ref, apart_ref, slope_ref, q_ref, k_ref, v_ref, o_ref, lse_ref = refs[:8]
    g_refs = refs[8 : 8 + slots]
    out_ref, qa, ka, va, ga, kt, dq_sum = refs[8 + slots :]
    cols = pair * HD
    me = me_ref[0]
    total = q_ref.shape[0]
    rows = total // slots
    chunk = min(rows, 512)
    apart = apart_ref[0].astype(F32)

    def prepare(slot, inner, spot, place):
        place = pl.multiple_of(place, chunk)
        home = pl.ds(place, chunk)
        for s in range(pair):
            mine = slice(s * HD, (s + 1) * HD)
            log_total = lse_ref[s, :, home].T
            qa[s, home, :] = query_columns(q_ref[spot, mine], place, slope_ref[s], apart, log_total)
            keys = key_columns(k_ref[spot, mine], place)
            ka[s, home, :] = keys
            kt[s, :, home] = low(keys.astype(F32).T)
            va[s, home, :] = ones_columns(v_ref[spot, mine], 3)
            grad = g_refs[slot][inner, mine]
            row_dot = jnp.sum(
                grad.astype(F32) * o_ref[spot, mine].astype(F32), axis=1, keepdims=True
            )
            ga[s, home, :] = grad_columns(grad, -row_dot)
            dq_sum[s, :, home] = jnp.zeros((128, chunk), F32)

    each_chunk(me, slots, rows, prepare)
    causal = lax.broadcasted_iota(jnp.int32, (key_tile, key_tile), 0) <= lax.broadcasted_iota(
        jnp.int32, (key_tile, key_tile), 1
    )
    piece = min(rows, key_tile)

    def place_of(place, size):
        block = place // rows
        return pl.multiple_of((block ^ me) * rows + (place - block * rows), size)

    def keys_tile(index, _):
        first = pl.multiple_of(index * key_tile, key_tile)
        here = pl.ds(first, key_tile)

        def step(at, carry, diagonal, width):
            after = []
            for s in range(pair):
                dk, dv = carry[s]
                there = pl.ds(at, width)
                queries, grads = qa[s, there, :], ga[s, there, :]
                probs = jnp.exp2(dot(ka[s, here, :], queries, NT))
                if diagonal:
                    probs = jnp.where(causal, probs, 0.0)
                dv = dv + dot(low(probs), grads)
                score_grad = low(probs * dot(va[s, here, :], grads, NT))
                dk = dk + dot(score_grad, queries)
                dq_sum[s, :, there] += dot(kt[s, :, here], score_grad)
                after.append((dk, dv))
            return tuple(after)

        zeros = jnp.zeros((key_tile, 128), F32)
        carry = step(first, tuple((zeros, zeros) for _ in range(pair)), True, key_tile)
        start = first + key_tile
        short = jnp.minimum((-start) % tile, total - start) // key_tile
        if tile > key_tile:
            carry = lax.fori_loop(
                0,
                short,
                lambda at, held: step(
                    pl.multiple_of(start + at * key_tile, key_tile), held, False, key_tile
                ),
                carry,
            )
            start = start + short * key_tile
        carry = lax.fori_loop(
            0,
            (total - start) // tile,
            lambda at, held: step(
                pl.multiple_of(start + at * tile, min(tile, key_tile)), held, False, tile
            ),
            carry,
        )
        dk = low(jnp.concatenate([held[0][:, :HD] * (1.0 / LOG2E) for held in carry], axis=1))
        dv = low(jnp.concatenate([held[1][:, :HD] for held in carry], axis=1))
        for part in range(key_tile // piece):
            spot = pl.ds(place_of(first + part * piece, piece), piece)
            out_ref[spot, cols : 2 * cols] = dk[part * piece : (part + 1) * piece]
            out_ref[spot, 2 * cols :] = dv[part * piece : (part + 1) * piece]
        return 0

    lax.fori_loop(0, total // key_tile, keys_tile, 0)

    def finish(slot, inner, spot, place):
        home = pl.ds(pl.multiple_of(place, chunk), chunk)
        joined = jnp.concatenate([dq_sum[s, :HD, home] for s in range(pair)], axis=0)
        out_ref[spot, :cols] = low(joined.T * HD**-0.5)

    each_chunk(me, slots, rows, finish)


def attend_back(
    me, apart, slopes, queries, key_rows, values, mixed, log_total, grads, group, tile=1024, key_tile=512
):
    slots = len(grads)
    total, width = queries.shape
    pair = min(2, width // HD)
    cols = pair * HD
    spec = pl.BlockSpec((total, cols), lambda g: (0, group))
    out_spec = pl.BlockSpec((total, cols), lambda g: (0, 0))
    scalars = pl.BlockSpec(memory_space=pltpu.SMEM)
    return pl.pallas_call(
        functools.partial(
            attend_back_kernel, slots=slots, pair=pair, tile=tile, key_tile=key_tile
        ),
        grid=(1,),
        in_specs=[scalars] * 3
        + [spec] * 3
        + [out_spec, pl.BlockSpec((pair, 1, total), lambda g: (0, 0, 0))]
        + [pl.BlockSpec((total // slots, cols), lambda g: (0, group))] * slots,
        out_specs=pl.BlockSpec((total, 3 * cols), lambda g: (0, 0)),
        out_shape=jax.ShapeDtypeStruct((total, 3 * cols), BF16),
        scratch_shapes=[pltpu.VMEM((pair, total, 128), BF16)] * 4
        + [pltpu.VMEM((pair, 128, total), BF16), pltpu.VMEM((pair, 128, total), F32)],
        compiler_params=pltpu.CompilerParams(vmem_limit_bytes=60 << 20),
        cost_estimate=pl.CostEstimate(
            flops=pair * 2400 * total * total, transcendentals=0, bytes_accessed=16 * total * cols
        ),
        name="attend_back",
    )(
        me,
        apart,
        slopes[group * pair : (group + 1) * pair],
        queries,
        key_rows,
        values,
        mixed,
        log_total,
        *grads,
    )


def whole(shape):
    return pl.BlockSpec(shape, lambda i: (0,) * len(shape))


def row(ref):
    return ref[...].astype(F32)[None, :]


def choose(slot, refs):
    rows = refs[0][...]
    for at, ref in enumerate(refs[1:], 1):
        rows = jnp.where(slot == at, ref[...], rows)
    return rows


def slot_specs(count, per, block, width, order=lambda i: i):
    return [
        pl.BlockSpec(
            (block, width), lambda i, at=at: (jnp.clip(order(i) - at * per, 0, per - 1), 0)
        )
        for at in range(count)
    ]


def tall_spec(chosen, per, block, width):
    return pl.BlockSpec(
        (block, width),
        lambda i: ((chosen.start + chosen.step * (i // per)) * per + i % per, 0),
    )


def kernel_call(kernel, grid, in_specs, out_specs, out_shape, inputs, held=(), **more):
    return pl.pallas_call(
        kernel,
        grid=grid,
        in_specs=in_specs + [pl.BlockSpec(memory_space=pl.ANY)] * len(held),
        out_specs=out_specs,
        out_shape=out_shape,
        input_output_aliases={len(inputs) + at: at for at in range(len(held))},
        compiler_params=pltpu.CompilerParams(vmem_limit_bytes=56 << 20),
        cost_estimate=SMALL_COST,
        **more,
    )(*inputs, *held)


def shape_of(rows, cols, kind=BF16):
    return jax.ShapeDtypeStruct((rows, cols), kind)


def project_kernel(*refs, count, per):
    x_refs = refs[:count]
    gain_ref, shift_ref, wq_ref, wk_ref, wv_ref, qb_ref, vb_ref = refs[count : count + 7]
    normed_ref, q_ref, k_ref, v_ref = refs[-4:]
    x = choose(pl.program_id(0) // per, x_refs).astype(F32)
    normed = low(norm_stats(x)[0] * row(gain_ref) + row(shift_ref))
    normed_ref[...] = normed
    q_ref[...] = low((dot(normed, wq_ref[...]) + row(qb_ref)) * (LOG2E * HD**-0.5))
    k_ref[...] = low(dot(normed, wk_ref[...]))
    v_ref[...] = low(dot(normed, wv_ref[...]) + row(vb_ref))


def project(x_parts, chosen, slots, vectors, weights, biases, held):
    rows, width = x_parts[0].shape
    block = min(rows, 512)
    per = rows // block
    widths = [width] + [weight.shape[1] for weight in weights]
    return kernel_call(
        functools.partial(project_kernel, count=len(chosen), per=per),
        (len(chosen) * per,),
        slot_specs(len(chosen), per, block, width)
        + [whole(a.shape) for a in (*vectors, *weights, *biases)],
        [tall_spec(chosen, per, block, cols) for cols in widths],
        [shape_of(slots * rows, cols) for cols in widths],
        [*x_parts, *vectors, *weights, *biases],
        held,
        name="project",
    )


def act_grad_kernel(*refs, count, per):
    down_ref, grad_ref, cot_ref = refs[count:]
    cot = choose(pl.program_id(0) // per, refs[:count])
    cot_ref[...] = cot
    grad_ref[...] = low(dot(cot, down_ref[...], NT))


def act_grad_step(cot_parts, down):
    slots = len(cot_parts)
    rows, width = cot_parts[0].shape
    block = min(rows, 1024)
    per = rows // block
    units = down.shape[0]
    return kernel_call(
        functools.partial(act_grad_kernel, count=slots, per=per),
        (slots * per,),
        slot_specs(slots, per, block, width) + [whole(down.shape)],
        [pl.BlockSpec((block, cols), lambda i: (i, 0)) for cols in (units, width)],
        [shape_of(slots * rows, cols) for cols in (units, width)],
        [*cot_parts, down],
        (),
        name="act_grad",
    )


def post_kernel(*refs, slots, groups, per):
    mixed_refs = refs[: slots * groups]
    x_refs = refs[slots * groups : slots * groups + slots]
    weight_refs = refs[slots * groups + slots : slots * groups + 2 * slots]
    bias_ref, gain_ref, shift_ref, post_ref, residual_ref = refs[-5:]
    blocks = pl.num_programs(0)
    at = (pl.program_id(0) + blocks // 2) % blocks
    residual = choose(at // per, x_refs).astype(F32) + row(bias_ref)
    for slot in range(slots):
        mixed = [ref[...] for ref in mixed_refs[slot * groups : (slot + 1) * groups]]
        residual = residual + dot(jnp.concatenate(mixed, axis=1), weight_refs[slot][...])
    normal, _ = norm_stats(residual)
    post_ref[...] = low(normal * row(gain_ref) + row(shift_ref))

    @pl.when(at < per)
    def _():
        residual_ref[...] = residual


def post_norm(mixed, x_parts, weights, bias, gain, shift):
    slots, groups = len(mixed), len(mixed[0])
    rows, width = x_parts[0].shape
    block = min(rows, 512)
    per = rows // block
    blocks = slots * per
    order = lambda i: (i + blocks // 2) % blocks
    specs = [
        pl.BlockSpec(
            (block, part.shape[1]),
            lambda i, slot=slot: (((order(i) // per) ^ slot) * per + order(i) % per, 0),
        )
        for slot in range(slots)
        for part in mixed[slot]
    ]
    return kernel_call(
        functools.partial(post_kernel, slots=slots, groups=groups, per=per),
        (blocks,),
        specs
        + slot_specs(slots, per, block, width, order)
        + [whole(a.shape) for a in (*weights, bias, gain, shift)],
        [
            pl.BlockSpec((block, width), lambda i: (order(i), 0)),
            pl.BlockSpec((block, width), lambda i: (jnp.clip(i - blocks // 2, 0, per - 1), 0)),
        ],
        [shape_of(slots * rows, width), shape_of(rows, width, F32)],
        [*[part for parts in mixed for part in parts], *x_parts, *weights, bias, gain, shift],
        (),
        name="post_norm",
    )


def feed_kernel(*refs, count, per, extras, held):
    post_ref, act_grad_ref, up_ref, bias_ref = refs[:4]
    extra_refs = refs[4 : 4 + extras]
    active_ref, grad_ref, sum_ref = refs[4 + extras + held : 7 + extras + held]
    back_refs = refs[7 + extras + held :]
    slot = pl.program_id(0) // per

    @pl.when(pl.program_id(0) == 0)
    def _():
        sum_ref[...] = jnp.zeros_like(sum_ref)

    post = post_ref[...]
    units = active_ref.shape[1]
    chunk = min(512, units)
    scale, cubic = math.sqrt(2 / math.pi), 0.044715
    for first in range(0, units, chunk):
        cols = slice(first, first + chunk)
        hidden = dot(post, up_ref[:, cols]) + row(bias_ref)[:, cols]
        square = hidden * hidden
        curve = jnp.tanh(hidden * (scale + scale * cubic * square))
        half = 0.5 + 0.5 * curve
        active_ref[:, cols] = low(hidden * half)
        slope = half + (0.5 * hidden) * (1.0 - curve * curve) * (
            scale + 3 * scale * cubic * square
        )
        grad = low(act_grad_ref[:, cols].astype(F32) * slope)
        grad_ref[:, cols] = grad
        sum_ref[:, cols] += jnp.sum(grad.astype(F32), axis=0, keepdims=True)
    back = dot(grad_ref[...], up_ref[...], NT)
    if extras:
        back = back + choose(slot, extra_refs).astype(F32)
    back = low(back)
    for at, back_ref in enumerate(back_refs):

        @pl.when(slot == at)
        def _():
            back_ref[...] = back


def feed(post_all, act_grad, up, up_bias, slots, chosen, extras, held):
    count = len(chosen)
    total, width = post_all.shape
    rows, units = total // slots, up.shape[1]
    block = min(rows, 512)
    per = rows // block
    tall = lambda cols: tall_spec(chosen, per, block, cols)
    active, grad, sums, *backs = kernel_call(
        functools.partial(
            feed_kernel, count=count, per=per, extras=len(extras), held=len(held)
        ),
        (count * per,),
        [tall(width), tall(units), whole(up.shape), whole(up_bias.shape)]
        + slot_specs(len(extras), per, block, width),
        [tall(units), tall(units), whole((1, units))] + slot_specs(count, per, block, width),
        [shape_of(total, units), shape_of(total, units), shape_of(1, units, F32)]
        + [shape_of(rows, width)] * count,
        [post_all, act_grad, up, up_bias, *extras],
        held,
        name="feed",
    )
    return (active, grad), sums, backs


def split_rows(total, me, keep_ref, send_ref, streams):
    rows = total.shape[0] // streams
    for slot in range(streams):
        part = low(total[pl.ds(pl.multiple_of((me ^ slot) * rows, rows), rows), :])
        ref = send_ref if slot % 2 else keep_ref
        ref[slot // 2 * rows : (slot // 2 + 1) * rows, :] = part


def outer_kernel(me_ref, left_ref, right_ref, keep_ref, send_ref, total, *, streams):
    step = pl.program_id(0)

    @pl.when(step == 0)
    def _():
        total[...] = dot(left_ref[...], right_ref[...], TN)

    @pl.when(step > 0)
    def _():
        total[...] += dot(left_ref[...], right_ref[...], TN)

    @pl.when(step == pl.num_programs(0) - 1)
    def _():
        split_rows(total, me_ref[0], keep_ref, send_ref, streams)


def outer_step(left, right, me, streams):
    total = left.shape[0]
    block = min(total, 1024)
    shape = (left.shape[1], right.shape[1])
    half = (shape[0] // 2, shape[1])
    return kernel_call(
        functools.partial(outer_kernel, streams=streams),
        (total // block,),
        [pl.BlockSpec(memory_space=pltpu.SMEM)]
        + [pl.BlockSpec((block, cols), lambda i: (i, 0)) for cols in shape],
        [whole(half)] * 2,
        [shape_of(*half)] * 2,
        [me, left, right],
        scratch_shapes=[pltpu.VMEM(shape, F32)],
        name="outer_step",
    )


def join_kernel(me_ref, *refs, early, streams):
    parts, (keep_ref, send_ref) = refs[:-2], refs[-2:]
    rows = parts[0].shape[0] // streams
    for slot in range(streams):
        home = pl.ds(pl.multiple_of((me_ref[0] ^ slot) * rows, rows), rows)
        out = send_ref if slot % 2 else keep_ref
        here = slice(slot // 2 * rows, (slot // 2 + 1) * rows)
        at = 0
        for part in parts[:early]:
            out[here, at : at + part.shape[1]] = part[home, :]
            at += part.shape[1]
        total = parts[early][home, :].astype(F32)
        for part in parts[early + 1 :]:
            total = total + part[home, :].astype(F32)
        out[here, at:] = low(total)


def join_step(early, terms, me, streams):
    inputs = [*early, *terms]
    cols = sum(part.shape[1] for part in early) + terms[0].shape[1]
    half = (terms[0].shape[0] // 2, cols)
    return kernel_call(
        functools.partial(join_kernel, early=len(early), streams=streams),
        (1,),
        [pl.BlockSpec(memory_space=pltpu.SMEM)] + [whole(a.shape) for a in inputs],
        [whole(half)] * 2,
        [shape_of(*half)] * 2,
        [me, *inputs],
        name="join_step",
    )


def late_kernel(*refs):
    (keep, come, keep_late, come_late), outs = refs[:4], refs[4:]
    rows, cols = outs[0].shape[0], keep.shape[1]
    for slot, out in enumerate(outs):
        here = slice(slot * rows, (slot + 1) * rows)
        out[:, :cols] = low(keep[here, :].astype(F32) + come[here, :].astype(F32))
        out[:, cols:] = low(keep_late[here, :].astype(F32) + come_late[here, :].astype(F32))


def late_step(pairs, slots):
    inputs = [array for pair in pairs for array in pair]
    shape = (inputs[0].shape[0] // slots, inputs[0].shape[1] + inputs[2].shape[1])
    return kernel_call(
        late_kernel,
        (1,),
        [whole(a.shape) for a in inputs],
        [whole(shape)] * slots,
        [shape_of(*shape)] * slots,
        inputs,
        name="late_step",
    )


def pair_kernel(*refs, count):
    parts, outs = refs[: 2 * count], refs[2 * count :]
    rows = outs[0].shape[0] // count
    for at in range(count):
        keep, come = parts[2 * at : 2 * at + 2]
        for slot, out in enumerate(outs):
            here = slice(slot * rows, (slot + 1) * rows)
            out[at * rows : (at + 1) * rows, :] = low(
                keep[here, :].astype(F32) + come[here, :].astype(F32)
            )


def pair_step(pairs, slots):
    inputs = [array for pair in pairs for array in pair]
    rows, cols = inputs[0].shape
    shape = (rows // slots * len(pairs), cols)
    return kernel_call(
        functools.partial(pair_kernel, count=len(pairs)),
        (1,),
        [whole(a.shape) for a in inputs],
        [whole(shape)] * slots,
        [shape_of(*shape)] * slots,
        inputs,
        name="pair_step",
    )


def stack_kernel(*refs):
    rows = refs[0].shape[0]
    for at, ref in enumerate(refs[:-1]):
        refs[-1][at * rows : (at + 1) * rows, :] = ref[...]


def stack_step(parts):
    rows, cols = parts[0].shape
    return kernel_call(
        stack_kernel,
        (1,),
        [whole((rows, cols))] * len(parts),
        [whole((rows * len(parts), cols))],
        [shape_of(rows * len(parts), cols)],
        list(parts),
        name="stack_step",
    )[0]


def shard_views(even_ref, odd_ref, streams):
    rows = even_ref.shape[0] // (streams // 2)
    return [
        (slot, ref.at[slot // 2 * rows : (slot // 2 + 1) * rows])
        for slot, ref in enumerate([even_ref, odd_ref] * (streams // 2))
    ]


def feed_grads_kernel(me_ref, even_ref, odd_ref, up_ref, down_ref, up_rows, *, streams):
    rows = even_ref.shape[0] // streams
    for slot, part in shard_views(even_ref, odd_ref, streams):
        home = pl.ds(pl.multiple_of((me_ref[0] ^ slot) * rows, rows), rows)
        up_rows[home, :] = part[:rows, :].astype(F32)
        down_ref[home, :] = part[rows:, :].astype(F32)
    up_ref[...] = up_rows[...].T


def feed_grads(even, odd, me, streams):
    units, width = even.shape
    return kernel_call(
        functools.partial(feed_grads_kernel, streams=streams),
        (1,),
        [pl.BlockSpec(memory_space=pltpu.SMEM)] + [whole(even.shape)] * 2,
        [whole((width, units)), whole((units, width))],
        [shape_of(width, units, F32), shape_of(units, width, F32)],
        [me, even, odd],
        scratch_shapes=[pltpu.VMEM((units, width), F32)],
        name="feed_grads",
    )


def pack_kernel(*refs, groups):
    sums_ref, gain_ref, shift_ref = refs[:3]
    row_refs, count_refs = refs[3 : 3 + groups], refs[3 + groups : 3 + 2 * groups]
    unit_refs, out_ref = refs[3 + 2 * groups : -1], refs[-1]
    out_ref[...] = jnp.zeros_like(out_ref)
    out_ref[:4, : sums_ref.shape[1]] = sums_ref[:4, :]
    rows = row_refs[0][...]
    for ref in row_refs[1:]:
        rows = rows + ref[...]
    out_ref[4:5, : rows.shape[1]] = (rows[0:1] - row(shift_ref) * rows[1:2]) / row(gain_ref)
    out_ref[5:6, : rows.shape[1]] = rows[1:2]
    units = unit_refs[0][...]
    for ref in unit_refs[1:]:
        units = units + ref[...]
    out_ref[8:9, : units.shape[1]] = units
    for at, ref in enumerate(count_refs):
        out_ref[9 + at : 10 + at, : ref.shape[1]] = ref[...]


def pack(row_sums, gain, shift, group_rows, group_counts, unit_sums):
    inputs = [row_sums, gain, shift, *group_rows, *group_counts, *unit_sums]
    wide = max(a.shape[1] for a in (row_sums, *group_counts, *unit_sums))
    return kernel_call(
        functools.partial(pack_kernel, groups=len(group_rows)),
        (1,),
        [whole(a.shape) for a in inputs],
        [whole((16, wide))],
        [shape_of(16, wide, F32)],
        inputs,
        name="pack",
    )[0]


def resid_kernel(*refs, terms, slots):
    term_refs = refs[:terms]
    residual_ref, cot_ref, gain_ref = refs[terms : terms + 3]
    weight_refs = refs[terms + 3 : terms + 3 + slots]
    grad_ref, low_ref, sums_ref = refs[terms + 3 + slots : terms + 6 + slots]
    part_refs = refs[terms + 6 + slots :]

    @pl.when(pl.program_id(0) == 0)
    def _():
        sums_ref[...] = jnp.zeros_like(sums_ref)

    post_grad = term_refs[0][...].astype(F32)
    for ref in term_refs[1:]:
        post_grad = post_grad + ref[...].astype(F32)
    cot = cot_ref[...].astype(F32)
    normal, inverse = norm_stats(residual_ref[...])
    grad = cot + norm_pull(post_grad * row(gain_ref), normal, inverse)
    grad_ref[...] = grad
    grad_low = low(grad)
    low_ref[...] = grad_low
    for weight_ref, part_ref in zip(weight_refs, part_refs):
        part_ref[...] = low(dot(grad_low, weight_ref[...], NT))
    for at, value in enumerate((cot, grad, post_grad * normal, post_grad)):
        sums_ref[at : at + 1, :] += jnp.sum(value, axis=0, keepdims=True)


def resid_step(terms, residual, cotangent, gain, weights):
    rows, width = residual.shape
    block = min(rows, 256)
    tall = lambda cols: pl.BlockSpec((block, cols), lambda i: (i, 0))
    cols = weights[0].shape[0]
    return kernel_call(
        functools.partial(resid_kernel, terms=len(terms), slots=len(weights)),
        (rows // block,),
        [tall(width)] * (len(terms) + 2) + [whole(a.shape) for a in (gain, *weights)],
        [tall(width), tall(width), whole((8, width))] + [tall(cols)] * len(weights),
        [shape_of(rows, width, F32), shape_of(rows, width), shape_of(8, width, F32)]
        + [shape_of(rows, cols)] * len(weights),
        [*terms, residual, cotangent, gain, *weights],
        (),
        name="resid_step",
    )


def dense_grad_kernel(*refs, slots, groups):
    mixed_refs, grad_ref = refs[: slots * groups], refs[slots * groups]
    even_ref, odd_ref, *sum_refs = refs[slots * groups + 1 :]
    step = pl.program_id(0)
    grad = grad_ref[...]
    for slot in range(slots):
        mixed = [ref[...] for ref in mixed_refs[slot * groups : (slot + 1) * groups]]
        part = dot(grad, jnp.concatenate(mixed, axis=1), TN)
        sum_refs[slot][...] = jnp.where(step == 0, 0.0, sum_refs[slot][...]) + part

    @pl.when(step == pl.num_programs(0) - 1)
    def _():
        rows = sum_refs[0].shape[0]
        for slot, sum_ref in enumerate(sum_refs):
            out_ref = odd_ref if slot % 2 else even_ref
            out_ref[slot // 2 * rows : (slot // 2 + 1) * rows, :] = low(sum_ref[...])


def dense_grad(mixed, grad):
    slots, groups = len(mixed), len(mixed[0])
    rows, width = grad.shape
    block = min(rows, 512)
    per = rows // block
    cols = sum(part.shape[1] for part in mixed[0])
    return kernel_call(
        functools.partial(dense_grad_kernel, slots=slots, groups=groups),
        (per,),
        [
            pl.BlockSpec((block, part.shape[1]), lambda i, slot=slot: (slot * per + i, 0))
            for slot in range(slots)
            for part in mixed[slot]
        ]
        + [pl.BlockSpec((block, width), lambda i: (i, 0))],
        [whole((width * slots // 2, cols))] * 2,
        [shape_of(width * slots // 2, cols)] * 2,
        [*[part for parts in mixed for part in parts], grad],
        (),
        scratch_shapes=[pltpu.VMEM((width, cols), F32)] * slots,
        name="dense_grad",
    )


def weight_kernel(me_ref, normed_ref, grad_ref, wq_ref, wk_ref, wv_ref, *refs, streams):
    *out_refs, sums_ref, count_ref, total, count = refs
    step = pl.program_id(0)

    @pl.when(step == 0)
    def _():
        total[...] = jnp.zeros_like(total)
        count[...] = jnp.zeros_like(count)

    grad = grad_ref[...]
    total[...] += dot(normed_ref[...], grad, TN)
    count[...] += jnp.sum(grad.astype(F32), axis=0, keepdims=True)

    @pl.when(step == pl.num_programs(0) - 1)
    def _():
        weight = jnp.concatenate([wq_ref[...], wk_ref[...], wv_ref[...]], axis=1).astype(F32)
        if streams:
            split_rows(total, me_ref[0], *out_refs, streams)
        else:
            out_refs[0][...] = low(total[...])
        count_ref[...] = count[...]
        lane = lanes(weight.shape[0])
        cross = jnp.sum(weight * total[...], axis=1, keepdims=True)
        plain = jnp.sum(weight * count[...], axis=1, keepdims=True)
        both = jnp.where(lane == 0, cross, jnp.where(lane == 1, plain, 0.0))
        sums_ref[...] = both.T[:8]


def weight_step(normed, grad, weights, group, me, streams):
    total, width = normed.shape
    cols = grad.shape[1]
    block = min(total, 1024)
    outs = [(width // 2, cols)] * 2 if streams else [(width, cols)]
    *parts, sums, count = kernel_call(
        functools.partial(weight_kernel, streams=streams),
        (total // block,),
        [pl.BlockSpec(memory_space=pltpu.SMEM)]
        + [pl.BlockSpec((block, count), lambda i: (i, 0)) for count in (width, cols)]
        + [pl.BlockSpec((width, cols // 3), lambda i: (0, group))] * 3,
        [whole(shape) for shape in outs] + [whole((8, width)), whole((1, cols))],
        [shape_of(*shape) for shape in outs] + [shape_of(8, width, F32), shape_of(1, cols, F32)],
        [me, normed, grad, *weights],
        scratch_shapes=[pltpu.VMEM((width, cols), F32), pltpu.VMEM((1, cols), F32)],
        name="weight_step",
    )
    return parts, sums, count


def unproject_kernel(*refs, groups, per, extras):
    grad_refs, weight_refs = refs[:groups], refs[groups : 4 * groups]
    extra_refs = refs[4 * groups : 4 * groups + extras]
    out_refs = refs[4 * groups + extras : -1]
    joined = refs[-1]
    slot = pl.program_id(0) // per

    @pl.when(pl.program_id(0) == 0)
    def _():
        joined[...] = jnp.concatenate([ref[...] for ref in weight_refs], axis=1)

    total = dot(jnp.concatenate([ref[...] for ref in grad_refs], axis=1), joined[...], NT)
    if extras:
        total = total + choose(slot, extra_refs).astype(F32)
    total = low(total)
    for at, ref in enumerate(out_refs):

        @pl.when(slot == at)
        def _():
            ref[...] = total


def unproject(grads, weights, slots, chosen, extras):
    width = weights[0].shape[0]
    count, groups = len(chosen), len(grads)
    total, cols = grads[0].shape
    rows = total // slots
    block = min(rows, 512)
    per = rows // block
    return kernel_call(
        functools.partial(unproject_kernel, groups=groups, per=per, extras=len(extras)),
        (count * per,),
        [tall_spec(chosen, per, block, cols)] * groups
        + [
            pl.BlockSpec((width, cols // 3), lambda i, group=group: (0, group))
            for group in range(groups)
            for _ in weights
        ]
        + slot_specs(len(extras), per, block, width),
        slot_specs(count, per, block, width),
        [shape_of(rows, width)] * count,
        [*grads, *[weight for _ in grads for weight in weights], *extras],
        (),
        scratch_shapes=[pltpu.VMEM((width, cols * groups), BF16)],
        name="unproject",
    )


def ffn_kernel(active_ref, weight_ref, even_ref, odd_ref, *, per):
    total = low(dot(active_ref[...], weight_ref[...]))
    odd = pl.program_id(0) // per % 2

    @pl.when(odd == 0)
    def _():
        even_ref[...] = total

    @pl.when(odd == 1)
    def _():
        odd_ref[...] = total


def ffn_step(active, weight, slots):
    total, units = active.shape
    width = weight.shape[1]
    rows = total // slots
    block = min(rows, 1024)
    per = rows // block
    half = (total // 2, width)

    def half_spec(odd):
        def place(i):
            slot, step = i // per, i % per
            now = slot // 2 * per
            if odd:
                return (jnp.where(slot % 2 == 1, now + step, jnp.maximum(now - 1, 0)), 0)
            return (jnp.where(slot % 2 == 0, now + step, now + per - 1), 0)

        return pl.BlockSpec((block, width), place)

    return kernel_call(
        functools.partial(ffn_kernel, per=per),
        (slots * per,),
        [pl.BlockSpec((block, units), lambda i: (i, 0)), whole(weight.shape)],
        [half_spec(0), half_spec(1)],
        [shape_of(*half)] * 2,
        [active, weight],
        name="ffn_step",
    )


def spread_kernel(me_ref, even_ref, odd_ref, *refs, groups, streams):
    *out_refs, dense_ref, dense_rows = refs
    cols = out_refs[0].shape[1] // groups
    heads = dense_ref.shape[0]
    rows = even_ref.shape[0] * 2 // streams
    for slot, part in shard_views(even_ref, odd_ref, streams):
        home = pl.ds(pl.multiple_of((me_ref[0] ^ slot) * rows, rows), rows)
        for group in range(groups):
            first = group * 3 * cols + (heads if group == groups - 1 else 0)
            for kind in range(3):
                at = first + kind * cols
                out_refs[kind][home, group * cols : (group + 1) * cols] = part[
                    :, at : at + cols
                ].astype(F32)
        first = (groups - 1) * 3 * cols
        dense_rows[home, :] = part[:, first : first + heads].astype(F32)
    dense_ref[...] = dense_rows[...].T


def spread(even, odd, me, streams, groups, heads):
    width = even.shape[0] * 2
    shapes = [(width, heads)] * 3 + [(heads, width)]
    return kernel_call(
        functools.partial(spread_kernel, groups=groups, streams=streams),
        (1,),
        [pl.BlockSpec(memory_space=pltpu.SMEM)] + [whole(even.shape)] * 2,
        [whole(shape) for shape in shapes],
        [shape_of(*shape, F32) for shape in shapes],
        [me, even, odd],
        scratch_shapes=[pltpu.VMEM((width, heads), F32)],
        name="spread",
    )


def input_kernel(*refs, terms):
    x_ref, resid_ref, gain_ref, out_ref = refs[terms:]
    grad = refs[0][...].astype(F32)
    for ref in refs[1:terms]:
        grad = grad + ref[...].astype(F32)
    normal, inverse = norm_stats(x_ref[...].astype(F32))
    out_ref[...] = resid_ref[...] + norm_pull(grad * row(gain_ref), normal, inverse)


def input_step(terms, layer_input, resid_grad, gain):
    rows, width = resid_grad.shape
    block = min(rows, 256)
    tall = pl.BlockSpec((block, width), lambda i: (i, 0))
    return kernel_call(
        functools.partial(input_kernel, terms=len(terms)),
        (rows // block,),
        [tall] * (len(terms) + 2) + [whole(gain.shape)],
        [tall],
        [shape_of(rows, width, F32)],
        [*terms, layer_input, resid_grad, gain],
        name="input_step",
    )[0]


def shards(
    slots,
    streams,
    layer_input,
    row_ids,
    input_gain,
    input_shift,
    query_weight,
    query_bias,
    key_weight,
    value_weight,
    value_bias,
    dense_weight,
    dense_bias,
    post_gain,
    post_shift,
    up_weight,
    up_bias,
    down_weight,
    down_bias,
    cotangent,
):
    me = lax.axis_index("tensor")
    me_word = me.astype(jnp.int32)[None]
    stream = lax.axis_index("dp").astype(jnp.int32)[None]
    rows = layer_input.shape[0]
    head_cols = query_weight.shape[1]
    head_count = head_cols // HD
    groups = max(1, head_count // 2)
    bits = [1 << level for level in range(slots.bit_length() - 1)]
    half = slots // 2
    after = lambda array, *others: lax.optimization_barrier((array, *others))[0]

    def swap(array, mask):
        return lax.ppermute(array, "tensor", [(i, i ^ mask) for i in range(slots)])

    def gather(array):
        held = {0: array}
        for bit in reversed(bits):
            held.update({slot ^ bit: swap(part, bit) for slot, part in held.items()})
        return [held[slot] for slot in range(slots)]

    def blocks(array):
        return [array[slot * rows : (slot + 1) * rows] for slot in range(slots)]

    def swap_data(array, mask):
        return lax.ppermute(array, "dp", [(i, i ^ mask) for i in range(streams)])

    def finish_terms(held, terms, levels):
        for bit in levels:
            come = {slot ^ bit: swap(part, bit) for slot, part in held.items() if slot & bit}
            if 0 in come:
                terms.append(come.pop(0))
            held = {
                slot: low(held[slot].astype(F32) + part.astype(F32)) for slot, part in come.items()
            }
        return terms

    def scatter_terms(parts):
        return finish_terms(dict(enumerate(parts)), [parts[0]], bits)

    far_odd = range(half + 1, slots, 2)
    far_even = range(half, slots, 2)
    near_odd = range(1, half, 2)
    near_even = range(0, half, 2)

    def ordered_terms(make):
        far = make(far_odd, (), None)
        far_come = [swap(part, 1) for part in far]
        near = make(near_odd, (), far[-1])
        near_come = [swap(part, 1) for part in near]
        far = make(far_even, far_come, near[-1])
        near = make(near_even, near_come, far[-1])
        held = dict(zip((*far_even, *near_even), (*far, *near)))
        return finish_terms(held, [held.pop(0)], bits[1:])

    def add_up(terms):
        return functools.reduce(
            lambda sum_now, term: sum_now + term.astype(F32), terms[1:], terms[0].astype(F32)
        )

    far_streams = range(2, streams, 2)

    def exchange(parts):
        return low(add_up([parts[0], *[swap_data(parts[k // 2], k) for k in far_streams]]))

    def collect_far(shard):
        return [shard, *[swap_data(shard, k) for k in far_streams]]

    norm_vectors = (input_gain, input_shift)
    weights = (query_weight, key_weight, value_weight)
    biases = (query_bias, value_bias)
    x_held = {0: layer_input}
    for bit in reversed(bits[1:]):
        x_held.update({slot ^ bit: swap(part, bit) for slot, part in x_held.items()})
    x_held[1] = swap(x_held[0], 1)
    near_parts = [x_held[0], x_held[1]]
    first = range(2)
    held = project(near_parts, first, slots, norm_vectors, weights, biases, ())
    rest = sorted(slot for slot in x_held if slot > 1)
    *arrived, normed = lax.optimization_barrier((*[x_held[slot] for slot in rest], held[0]))
    held = (normed, *held[1:])
    for slot, part in zip(rest, arrived):
        x_held[slot], x_held[slot ^ 1] = part, swap(part, 1)
    x_parts = [x_held[slot] for slot in range(slots)]
    dense_parts = gather(after(dense_weight, arrived[-1]))
    cot_own = after(cotangent, arrived[-1])
    cot_held = {0: cot_own}
    for bit in reversed(bits[1:]):
        cot_held.update({slot ^ bit: swap(part, bit) for slot, part in cot_held.items()})
    normed, queries, key_rows, values = project(
        x_parts[2:], range(2, slots), slots, norm_vectors, weights, biases, held
    )

    heads = me * head_count + jnp.arange(head_count)
    slopes = jnp.exp2(-8.0 * (heads + 1).astype(F32) / HEADS) * LOG2E
    apart = (row_ids[:1] != row_ids[SHORT : SHORT + 1]).astype(jnp.int32)

    mixed_own, log_totals, mixed_parts = [], [], []
    for group in range(groups):
        mixed, log_total = attend(
            me_word,
            apart,
            slopes,
            queries if not group else after(queries, cot_held[half], mixed_own[-1]),
            key_rows,
            values,
            slots,
            group,
        )
        mixed_own.append(mixed)
        log_totals.append(log_total)
        if not group:
            keys = sorted(cot_held)
            held = lax.optimization_barrier((*[cot_held[key] for key in keys], mixed))[:-1]
            cot_held.update(zip(keys, held))
            cot_held.update({slot ^ 1: swap(part, 1) for slot, part in cot_held.items()})
            cot_parts = [cot_held[slot] for slot in range(slots)]
        if group < groups - 1:
            mixed_parts.append(gather(mixed))
    act_grad, cot_all = act_grad_step(
        lax.optimization_barrier((*cot_parts, mixed_own[-1], *dense_parts[2:]))[:slots], down_weight
    )
    came = {0: mixed_own[-1]}
    for bit in reversed(bits[1:]):
        came.update({slot ^ bit: swap(part, bit) for slot, part in came.items()})
    far_slots = sorted(came)[1:]
    *arrived, act_grad = lax.optimization_barrier((*[came[slot] for slot in far_slots], act_grad))
    came.update(zip(far_slots, arrived))
    came.update({slot ^ 1: swap(part, 1) for slot, part in came.items()})
    mixed_parts.append([came[slot] for slot in range(slots)])
    mixed_all = [[mixed_parts[group][slot] for group in range(groups)] for slot in range(slots)]
    post_all, residual = post_norm(
        mixed_all, x_parts, dense_parts, dense_bias, post_gain, post_shift
    )

    fed, up_bias_parts = [()], []

    def make_feed(chosen, extras, gate):
        held, sums, backs = feed(
            post_all, act_grad, up_weight, up_bias, slots, chosen, extras, fed[-1]
        )
        fed.append(held)
        up_bias_parts.append(sums)
        return backs

    post_terms = ordered_terms(make_feed)
    active, hidden_grad = fed[-1]
    up_keep, up_send = outer_step(hidden_grad, post_all, stream, streams)
    down_keep, down_send = outer_step(active, after(cot_all, up_keep), stream, streams)
    up_come, down_come = swap_data(up_send, 1), swap_data(down_send, 1)
    resid_grad, attended_grad, row_sums, *mixed_grads = resid_step(
        [after(post_terms[0], down_keep), *post_terms[1:]],
        residual,
        cotangent,
        post_gain,
        dense_parts,
    )
    mixed_grads = [swap(part, slot) if slot else part for slot, part in enumerate(mixed_grads)]
    dense_even, dense_odd = dense_grad(mixed_all, attended_grad)
    ffn_even, ffn_odd = ffn_step(after(active, dense_odd), down_weight, slots)
    feed_parts = pair_step(
        [(after(up_keep, ffn_odd), up_come), (down_keep, down_come)], streams // 2
    )
    moved = lax.optimization_barrier((*mixed_grads, dense_odd, ffn_odd, *feed_parts))
    mixed_grads, (dense_odd, ffn_odd), feed_parts = (
        moved[:slots],
        moved[slots : slots + 2],
        moved[slots + 2 :],
    )
    dense_come, ffn_come = swap(dense_odd, 1), swap(ffn_odd, 1)

    def partner_sums(even, come):
        size = even.shape[0] * 2 // slots
        cuts = [slice(at * size, (at + 1) * size) for at in range(slots // 2)]
        return [low(even[cut].astype(F32) + come[cut].astype(F32)) for cut in cuts]

    cols = head_cols // groups
    head_grads, early_parts, group_rows, group_counts = [], [], [], []

    def backward(group):
        return attend_back(
            me_word,
            apart,
            slopes,
            queries,
            key_rows,
            values,
            mixed_own[group],
            log_totals[group],
            mixed_grads,
            group,
        )

    dense_sums = partner_sums(dense_even, dense_come)
    for group in range(groups - 1):
        head_grads.append(backward(group))
        grad = head_grads[-1]
        if group == groups - 2:
            grad, *dense_sums = lax.optimization_barrier((grad, *dense_sums))
        parts, row_part, count_part = weight_step(normed, grad, weights, group, stream, 0)
        early_parts += parts
        group_rows.append(row_part)
        group_counts.append(count_part)
        mixed_grads = lax.optimization_barrier((*mixed_grads, parts[-1]))[:-1]
    even_slots = range(2, slots, 2)
    dense_terms = finish_terms(dict(zip(even_slots, dense_sums[1:])), [dense_sums[0]], bits[1:])
    early_keep, early_send = join_step(early_parts, dense_terms, stream, streams)
    moved = lax.optimization_barrier(
        (*mixed_grads, early_send, exchange(feed_parts), *partner_sums(ffn_even, ffn_come))
    )
    mixed_grads, (early_send, feed_shard), ffn_sums = (
        moved[:slots],
        moved[slots : slots + 2],
        moved[slots + 2 :],
    )
    early_come = swap_data(early_send, 1)
    feed_shards = collect_far(feed_shard)
    ffn_terms = finish_terms(dict(zip(even_slots, ffn_sums[1:])), [ffn_sums[0]], bits[1:])
    head_grads.append(backward(groups - 1))
    grad, early_come, *arrived = lax.optimization_barrier(
        (head_grads[-1], early_come, *feed_shards, *ffn_terms)
    )
    feed_shards, ffn_terms = arrived[: len(feed_shards)], arrived[len(feed_shards) :]
    (late_keep, late_send), row_part, count_part = weight_step(
        normed, grad, weights, groups - 1, stream, streams
    )
    group_rows.append(row_part)
    group_counts.append(count_part)
    late_come = swap_data(late_send, 1)
    vectors = pack(row_sums, input_gain, input_shift, group_rows, group_counts, up_bias_parts)
    feed_even = stack_step([*feed_shards[:-1], after(feed_shards[-1], vectors)])
    summed = vectors + swap_data(vectors, 1)
    feed_odd = swap_data(after(feed_even, late_come, summed), 1)
    seen = []

    def make_unproject(chosen, extras, gate):
        gates = [feed_even if gate is None else gate]
        if not seen:
            gates += [late_come, summed]
        seen.append(0)
        return unproject(
            [*head_grads[:-1], after(head_grads[-1], *gates)], weights, slots, chosen, extras
        )

    normed_terms = ordered_terms(make_unproject)
    late_parts = late_step(
        [(early_keep, early_come), (after(late_keep, normed_terms[0]), late_come)], streams // 2
    )
    layer_output = low(residual + add_up(ffn_terms) + down_bias.astype(F32))
    up_grad, down_grad = feed_grads(feed_even, feed_odd, stream, streams)
    input_grad = input_step(
        [*normed_terms[:-1], after(normed_terms[-1], up_grad)],
        layer_input,
        resid_grad,
        input_gain,
    )
    *late_shards, layer_output, input_grad = lax.optimization_barrier(
        (*collect_far(exchange(late_parts)), layer_output, input_grad)
    )
    late_even = stack_step(late_shards)
    late_odd = swap_data(late_even, 1)
    for level in range(1, streams.bit_length() - 1):
        summed = summed + swap_data(summed, 1 << level)
    own = summed[8:]
    shared = after(summed, normed_terms[-1])[:8]
    for bit in reversed(bits):
        shared = shared + swap(shared, bit)
    shared = shared[:, : resid_grad.shape[1]]
    up_bias_grad = own[0, : up_bias.shape[0]]
    counts = own[1 : 1 + groups]
    query_bias_grad = counts[:, :cols].reshape(-1)
    value_bias_grad = counts[:, 2 * cols : 3 * cols].reshape(-1)
    *weight_grads, dense_weight_grad = spread(
        late_even, late_odd, stream, streams, groups, head_cols
    )
    return (
        layer_output,
        input_grad,
        shared[4],
        shared[5],
        weight_grads[0],
        query_bias_grad,
        weight_grads[1],
        weight_grads[2],
        value_bias_grad,
        dense_weight_grad,
        shared[1],
        shared[2],
        shared[3],
        up_grad,
        up_bias_grad,
        down_grad,
        shared[0],
    )


def solution(mesh):
    in_specs = (
        P(("dp", "tensor"), None),
        P("dp"),
        P(),
        P(),
        P(None, "tensor"),
        P("tensor"),
        P(None, "tensor"),
        P(None, "tensor"),
        P("tensor"),
        P("tensor", None),
        P(),
        P(),
        P(),
        P(None, "tensor"),
        P("tensor"),
        P("tensor", None),
        P(),
        P(("dp", "tensor"), None),
    )
    out_specs = (
        P(("dp", "tensor"), None),
        P(("dp", "tensor"), None),
        P(),
        P(),
        P(None, "tensor"),
        P("tensor"),
        P(None, "tensor"),
        P(None, "tensor"),
        P("tensor"),
        P("tensor", None),
        P(),
        P(),
        P(),
        P(None, "tensor"),
        P("tensor"),
        P("tensor", None),
        P(),
    )
    return jax.shard_map(
        functools.partial(shards, mesh.shape["tensor"], mesh.shape["dp"]), mesh=mesh, in_specs=in_specs, out_specs=out_specs, check_vma=False)
```

```python
import functools
import math

import jax
import jax.numpy as jnp
from jax import lax
from jax.experimental import pallas as pl
from jax.experimental.pallas import tpu as pltpu
from jax.sharding import PartitionSpec as P

HEADS = 16
HD = 64
SHORT = 2048
EPSILON = 1e-05
LOG2E = math.log2(math.e)
F32 = jnp.float32
BF16 = jnp.bfloat16
SMALL_COST = pl.CostEstimate(flops=1, transcendentals=0, bytes_accessed=1)
NT = (((1,), (1,)), ((), ()))
NN = (((1,), (0,)), ((), ()))
TN = (((0,), (0,)), ((), ()))


def dot(lhs, rhs, dims=NN):
    return lax.dot_general(lhs, rhs, dims, preferred_element_type=F32)


def low(array):
    return array.astype(BF16)


def norm_stats(rows):
    center = jnp.mean(rows, axis=-1, keepdims=True)
    centered = rows - center
    inverse = lax.rsqrt(jnp.mean(centered * centered, axis=-1, keepdims=True) + EPSILON)
    return centered * inverse, inverse


def norm_pull(grad, normal, inverse):
    grad_mean = jnp.mean(grad, axis=-1, keepdims=True)
    dot_mean = jnp.mean(grad * normal, axis=-1, keepdims=True)
    return inverse * (grad - grad_mean - normal * dot_mean)


def lanes(count):
    return lax.broadcasted_iota(jnp.int32, (count, 128), 1)


def places(count, first):
    return lax.broadcasted_iota(jnp.int32, (count, 128), 0) + first


def widen(head):
    return jnp.concatenate([head.astype(F32), jnp.zeros((head.shape[0], HD), F32)], axis=1)


def split3(value):
    high = low(value).astype(F32)
    middle = low(value - high).astype(F32)
    return high, middle, value - high - middle


def pick3(index, parts):
    return jnp.where(index == 0, parts[0], jnp.where(index == 1, parts[1], parts[2]))


def key_columns(head, first):
    count = head.shape[0]
    lane, place = lanes(count), places(count, first)
    coarse = ((place >> 6) << 6).astype(F32)
    fine = (place & 63).astype(F32)
    wall = jnp.where(place < SHORT, -1e30, 0.0)
    extra = jnp.where(lane < 73, -1.0, jnp.where(lane == 73, wall, 0.0))
    extra = jnp.where(lane < 67, coarse, jnp.where(lane < 70, fine, extra))
    return low(jnp.where(lane < HD, widen(head), extra))


def query_columns(head, first, slope, apart, log_total=None):
    count = head.shape[0]
    lane, place = lanes(count), places(count, first)
    extra = pick3(jnp.where(lane < 67, lane - 64, lane - 67), split3(slope))
    extra = jnp.where(lane < 70, extra, 0.0)
    if log_total is not None:
        extra = jnp.where((lane >= 70) & (lane < 73), pick3(lane - 70, split3(log_total)), extra)
    extra = jnp.where(lane == 73, jnp.where(place >= SHORT, apart, 0.0), extra)
    return low(jnp.where(lane < HD, widen(head), extra))


def ones_columns(head, count):
    lane = lanes(head.shape[0])
    return low(jnp.where(lane < HD, widen(head), jnp.where(lane < HD + count, 1.0, 0.0)))


def grad_columns(head, shift):
    lane = lanes(head.shape[0])
    extra = jnp.where(lane < 67, pick3(lane - 64, split3(shift)), 0.0)
    return low(jnp.where(lane < HD, widen(head), extra))


def each_chunk(me, slots, rows, body):
    chunk = min(rows, 512)
    for slot in range(slots):
        home = (me ^ slot) * rows

        @pl.loop(0, rows // chunk)
        def _(step):
            offset = pl.multiple_of(step * chunk, chunk)
            body(slot, pl.ds(offset, chunk), pl.ds(slot * rows + offset, chunk), home + offset)


def attend_kernel(
    me_ref, apart_ref, slope_ref, q_ref, k_ref, v_ref, o_ref, lse_ref, qa, ka, va, *, slots, pair, tile
):
    me = me_ref[0]
    total = q_ref.shape[0]
    rows = total // slots
    chunk = min(rows, 512)
    apart = apart_ref[0].astype(F32)

    def prepare(slot, inner, spot, place):
        place = pl.multiple_of(place, chunk)
        home = pl.ds(place, chunk)
        for s in range(pair):
            cols = slice(s * HD, (s + 1) * HD)
            qa[s, home, :] = query_columns(q_ref[spot, cols], place, slope_ref[s], apart)
            ka[s, home, :] = key_columns(k_ref[spot, cols], place)
            va[s, home, :] = ones_columns(v_ref[spot, cols], 1)

    each_chunk(me, slots, rows, prepare)
    causal = lax.broadcasted_iota(jnp.int32, (tile, tile), 1) <= lax.broadcasted_iota(
        jnp.int32, (tile, tile), 0
    )
    piece = min(rows, tile)

    def query_tile(index, _):
        first = pl.multiple_of(index * tile, tile)
        queries = [qa[s, pl.ds(first, tile), :] for s in range(pair)]

        def step(at, carry, diagonal):
            after = []
            for s in range(pair):
                top, mix = carry[s]
                scores = dot(queries[s], ka[s, pl.ds(at, tile), :], NT)
                if diagonal:
                    scores = jnp.where(causal, scores, -1e30)
                higher = jnp.maximum(top, jnp.max(scores, axis=1, keepdims=True))
                weights = low(jnp.exp2(scores - higher))
                mix = mix * jnp.exp2(top - higher) + dot(weights, va[s, pl.ds(at, tile), :])
                after.append((higher, mix))
            return tuple(after)

        carry = tuple(
            (jnp.full((tile, 1), -1e38, F32), jnp.zeros((tile, 128), F32)) for _ in range(pair)
        )
        carry = step(first, carry, True)
        carry = lax.fori_loop(
            0, index, lambda at, held: step(pl.multiple_of(at * tile, tile), held, False), carry
        )
        outs = []
        for s in range(pair):
            top, mix = carry[s]
            weight = mix[:, HD : HD + 1]
            outs.append(mix[:, :HD] * (1.0 / weight))
            lse_ref[s, 0, pl.ds(first, tile)] = (top + jnp.log2(weight))[:, 0]
        out = low(jnp.concatenate(outs, axis=1))
        for part in range(tile // piece):
            block = (index * (tile // piece) + part) // (rows // piece)
            offset = first + part * piece - block * rows
            spot = pl.multiple_of((block ^ me) * rows + offset, piece)
            o_ref[pl.ds(spot, piece), :] = out[part * piece : (part + 1) * piece]
        return 0

    lax.fori_loop(0, total // tile, query_tile, 0)


def attend(me, apart, slopes, queries, key_rows, values, slots, group, tile=1024):
    total, width = queries.shape
    pair = min(2, width // HD)
    cols = pair * HD
    spec = pl.BlockSpec((total, cols), lambda g: (0, group))
    scalars = pl.BlockSpec(memory_space=pltpu.SMEM)
    return pl.pallas_call(
        functools.partial(attend_kernel, slots=slots, pair=pair, tile=tile),
        grid=(1,),
        in_specs=[scalars] * 3 + [spec] * 3,
        out_specs=[
            pl.BlockSpec((total, cols), lambda g: (0, 0)),
            pl.BlockSpec((pair, 1, total), lambda g: (0, 0, 0)),
        ],
        out_shape=[
            jax.ShapeDtypeStruct((total, cols), BF16),
            jax.ShapeDtypeStruct((pair, 1, total), F32),
        ],
        scratch_shapes=[pltpu.VMEM((pair, total, 128), BF16)] * 3,
        compiler_params=pltpu.CompilerParams(vmem_limit_bytes=56 << 20),
        cost_estimate=pl.CostEstimate(
            flops=pair * 1200 * total * total, transcendentals=0, bytes_accessed=8 * total * cols
        ),
        name="attend",
    )(me, apart, slopes[group * pair : (group + 1) * pair], queries, key_rows, values)


def attend_back_kernel(*refs, slots, pair, tile, key_tile):
    me_ref, apart_ref, slope_ref, q_ref, k_ref, v_ref, o_ref, lse_ref = refs[:8]
    g_refs = refs[8 : 8 + slots]
    out_ref, qa, ka, va, ga, kt, dq_sum = refs[8 + slots :]
    cols = pair * HD
    me = me_ref[0]
    total = q_ref.shape[0]
    rows = total // slots
    chunk = min(rows, 512)
    apart = apart_ref[0].astype(F32)

    def prepare(slot, inner, spot, place):
        place = pl.multiple_of(place, chunk)
        home = pl.ds(place, chunk)
        for s in range(pair):
            mine = slice(s * HD, (s + 1) * HD)
            log_total = lse_ref[s, :, home].T
            qa[s, home, :] = query_columns(q_ref[spot, mine], place, slope_ref[s], apart, log_total)
            keys = key_columns(k_ref[spot, mine], place)
            ka[s, home, :] = keys
            kt[s, :, home] = low(keys.astype(F32).T)
            va[s, home, :] = ones_columns(v_ref[spot, mine], 3)
            grad = g_refs[slot][inner, mine]
            row_dot = jnp.sum(
                grad.astype(F32) * o_ref[spot, mine].astype(F32), axis=1, keepdims=True
            )
            ga[s, home, :] = grad_columns(grad, -row_dot)
            dq_sum[s, :, home] = jnp.zeros((128, chunk), F32)

    each_chunk(me, slots, rows, prepare)
    causal = lax.broadcasted_iota(jnp.int32, (key_tile, key_tile), 0) <= lax.broadcasted_iota(
        jnp.int32, (key_tile, key_tile), 1
    )
    piece = min(rows, key_tile)

    def place_of(place, size):
        block = place // rows
        return pl.multiple_of((block ^ me) * rows + (place - block * rows), size)

    def keys_tile(index, _):
        first = pl.multiple_of(index * key_tile, key_tile)
        here = pl.ds(first, key_tile)

        def step(at, carry, diagonal, width):
            after = []
            for s in range(pair):
                dk, dv = carry[s]
                there = pl.ds(at, width)
                queries, grads = qa[s, there, :], ga[s, there, :]
                probs = jnp.exp2(dot(ka[s, here, :], queries, NT))
                if diagonal:
                    probs = jnp.where(causal, probs, 0.0)
                dv = dv + dot(low(probs), grads)
                score_grad = low(probs * dot(va[s, here, :], grads, NT))
                dk = dk + dot(score_grad, queries)
                dq_sum[s, :, there] += dot(kt[s, :, here], score_grad)
                after.append((dk, dv))
            return tuple(after)

        zeros = jnp.zeros((key_tile, 128), F32)
        carry = step(first, tuple((zeros, zeros) for _ in range(pair)), True, key_tile)
        start = first + key_tile
        short = jnp.minimum((-start) % tile, total - start) // key_tile
        if tile > key_tile:
            carry = lax.fori_loop(
                0,
                short,
                lambda at, held: step(
                    pl.multiple_of(start + at * key_tile, key_tile), held, False, key_tile
                ),
                carry,
            )
            start = start + short * key_tile
        carry = lax.fori_loop(
            0,
            (total - start) // tile,
            lambda at, held: step(
                pl.multiple_of(start + at * tile, min(tile, key_tile)), held, False, tile
            ),
            carry,
        )
        dk = low(jnp.concatenate([held[0][:, :HD] * (1.0 / LOG2E) for held in carry], axis=1))
        dv = low(jnp.concatenate([held[1][:, :HD] for held in carry], axis=1))
        for part in range(key_tile // piece):
            spot = pl.ds(place_of(first + part * piece, piece), piece)
            out_ref[spot, cols : 2 * cols] = dk[part * piece : (part + 1) * piece]
            out_ref[spot, 2 * cols :] = dv[part * piece : (part + 1) * piece]
        return 0

    lax.fori_loop(0, total // key_tile, keys_tile, 0)

    def finish(slot, inner, spot, place):
        home = pl.ds(pl.multiple_of(place, chunk), chunk)
        joined = jnp.concatenate([dq_sum[s, :HD, home] for s in range(pair)], axis=0)
        out_ref[spot, :cols] = low(joined.T * HD**-0.5)

    each_chunk(me, slots, rows, finish)


def attend_back(
    me, apart, slopes, queries, key_rows, values, mixed, log_total, grads, group, tile=1024, key_tile=512
):
    slots = len(grads)
    total, width = queries.shape
    pair = min(2, width // HD)
    cols = pair * HD
    spec = pl.BlockSpec((total, cols), lambda g: (0, group))
    out_spec = pl.BlockSpec((total, cols), lambda g: (0, 0))
    scalars = pl.BlockSpec(memory_space=pltpu.SMEM)
    return pl.pallas_call(
        functools.partial(
            attend_back_kernel, slots=slots, pair=pair, tile=tile, key_tile=key_tile
        ),
        grid=(1,),
        in_specs=[scalars] * 3
        + [spec] * 3
        + [out_spec, pl.BlockSpec((pair, 1, total), lambda g: (0, 0, 0))]
        + [pl.BlockSpec((total // slots, cols), lambda g: (0, group))] * slots,
        out_specs=pl.BlockSpec((total, 3 * cols), lambda g: (0, 0)),
        out_shape=jax.ShapeDtypeStruct((total, 3 * cols), BF16),
        scratch_shapes=[pltpu.VMEM((pair, total, 128), BF16)] * 4
        + [pltpu.VMEM((pair, 128, total), BF16), pltpu.VMEM((pair, 128, total), F32)],
        compiler_params=pltpu.CompilerParams(vmem_limit_bytes=60 << 20),
        cost_estimate=pl.CostEstimate(
            flops=pair * 2400 * total * total, transcendentals=0, bytes_accessed=16 * total * cols
        ),
        name="attend_back",
    )(
        me,
        apart,
        slopes[group * pair : (group + 1) * pair],
        queries,
        key_rows,
        values,
        mixed,
        log_total,
        *grads,
    )


def whole(shape):
    return pl.BlockSpec(shape, lambda i: (0,) * len(shape))


def row(ref):
    return ref[...].astype(F32)[None, :]


def choose(slot, refs):
    rows = refs[0][...]
    for at, ref in enumerate(refs[1:], 1):
        rows = jnp.where(slot == at, ref[...], rows)
    return rows


def slot_specs(count, per, block, width, order=lambda i: i):
    return [
        pl.BlockSpec(
            (block, width), lambda i, at=at: (jnp.clip(order(i) - at * per, 0, per - 1), 0)
        )
        for at in range(count)
    ]


def tall_spec(chosen, per, block, width):
    return pl.BlockSpec(
        (block, width),
        lambda i: ((chosen.start + chosen.step * (i // per)) * per + i % per, 0),
    )


def kernel_call(kernel, grid, in_specs, out_specs, out_shape, inputs, held=(), **more):
    return pl.pallas_call(
        kernel,
        grid=grid,
        in_specs=in_specs + [pl.BlockSpec(memory_space=pl.ANY)] * len(held),
        out_specs=out_specs,
        out_shape=out_shape,
        input_output_aliases={len(inputs) + at: at for at in range(len(held))},
        compiler_params=pltpu.CompilerParams(vmem_limit_bytes=56 << 20),
        cost_estimate=SMALL_COST,
        **more,
    )(*inputs, *held)


def shape_of(rows, cols, kind=BF16):
    return jax.ShapeDtypeStruct((rows, cols), kind)


def project_kernel(*refs, count, per):
    x_refs = refs[:count]
    gain_ref, shift_ref, wq_ref, wk_ref, wv_ref, qb_ref, vb_ref = refs[count : count + 7]
    normed_ref, q_ref, k_ref, v_ref = refs[-4:]
    x = choose(pl.program_id(0) // per, x_refs).astype(F32)
    normed = low(norm_stats(x)[0] * row(gain_ref) + row(shift_ref))
    normed_ref[...] = normed
    q_ref[...] = low((dot(normed, wq_ref[...]) + row(qb_ref)) * (LOG2E * HD**-0.5))
    k_ref[...] = low(dot(normed, wk_ref[...]))
    v_ref[...] = low(dot(normed, wv_ref[...]) + row(vb_ref))


def project(x_parts, chosen, slots, vectors, weights, biases, held):
    rows, width = x_parts[0].shape
    block = min(rows, 512)
    per = rows // block
    widths = [width] + [weight.shape[1] for weight in weights]
    return kernel_call(
        functools.partial(project_kernel, count=len(chosen), per=per),
        (len(chosen) * per,),
        slot_specs(len(chosen), per, block, width)
        + [whole(a.shape) for a in (*vectors, *weights, *biases)],
        [tall_spec(chosen, per, block, cols) for cols in widths],
        [shape_of(slots * rows, cols) for cols in widths],
        [*x_parts, *vectors, *weights, *biases],
        held,
        name="project",
    )


def act_grad_kernel(*refs, count, per):
    down_ref, grad_ref, cot_ref = refs[count:]
    cot = choose(pl.program_id(0) // per, refs[:count])
    cot_ref[...] = cot
    grad_ref[...] = low(dot(cot, down_ref[...], NT))


def act_grad_step(cot_parts, down):
    slots = len(cot_parts)
    rows, width = cot_parts[0].shape
    block = min(rows, 1024)
    per = rows // block
    units = down.shape[0]
    return kernel_call(
        functools.partial(act_grad_kernel, count=slots, per=per),
        (slots * per,),
        slot_specs(slots, per, block, width) + [whole(down.shape)],
        [pl.BlockSpec((block, cols), lambda i: (i, 0)) for cols in (units, width)],
        [shape_of(slots * rows, cols) for cols in (units, width)],
        [*cot_parts, down],
        (),
        name="act_grad",
    )


def post_kernel(*refs, slots, groups, per):
    mixed_refs = refs[: slots * groups]
    x_refs = refs[slots * groups : slots * groups + slots]
    weight_refs = refs[slots * groups + slots : slots * groups + 2 * slots]
    bias_ref, gain_ref, shift_ref, post_ref, residual_ref = refs[-5:]
    blocks = pl.num_programs(0)
    at = (pl.program_id(0) + blocks // 2) % blocks
    residual = choose(at // per, x_refs).astype(F32) + row(bias_ref)
    for slot in range(slots):
        mixed = [ref[...] for ref in mixed_refs[slot * groups : (slot + 1) * groups]]
        residual = residual + dot(jnp.concatenate(mixed, axis=1), weight_refs[slot][...])
    normal, _ = norm_stats(residual)
    post_ref[...] = low(normal * row(gain_ref) + row(shift_ref))

    @pl.when(at < per)
    def _():
        residual_ref[...] = residual


def post_norm(mixed, x_parts, weights, bias, gain, shift):
    slots, groups = len(mixed), len(mixed[0])
    rows, width = x_parts[0].shape
    block = min(rows, 512)
    per = rows // block
    blocks = slots * per
    order = lambda i: (i + blocks // 2) % blocks
    specs = [
        pl.BlockSpec(
            (block, part.shape[1]),
            lambda i, slot=slot: (((order(i) // per) ^ slot) * per + order(i) % per, 0),
        )
        for slot in range(slots)
        for part in mixed[slot]
    ]
    return kernel_call(
        functools.partial(post_kernel, slots=slots, groups=groups, per=per),
        (blocks,),
        specs
        + slot_specs(slots, per, block, width, order)
        + [whole(a.shape) for a in (*weights, bias, gain, shift)],
        [
            pl.BlockSpec((block, width), lambda i: (order(i), 0)),
            pl.BlockSpec((block, width), lambda i: (jnp.clip(i - blocks // 2, 0, per - 1), 0)),
        ],
        [shape_of(slots * rows, width), shape_of(rows, width, F32)],
        [*[part for parts in mixed for part in parts], *x_parts, *weights, bias, gain, shift],
        (),
        name="post_norm",
    )


def feed_kernel(*refs, count, per, extras, held):
    post_ref, act_grad_ref, up_ref, bias_ref = refs[:4]
    extra_refs = refs[4 : 4 + extras]
    active_ref, grad_ref, sum_ref = refs[4 + extras + held : 7 + extras + held]
    back_refs = refs[7 + extras + held :]
    slot = pl.program_id(0) // per

    @pl.when(pl.program_id(0) == 0)
    def _():
        sum_ref[...] = jnp.zeros_like(sum_ref)

    post = post_ref[...]
    units = active_ref.shape[1]
    chunk = min(512, units)
    scale, cubic = math.sqrt(2 / math.pi), 0.044715
    for first in range(0, units, chunk):
        cols = slice(first, first + chunk)
        hidden = dot(post, up_ref[:, cols]) + row(bias_ref)[:, cols]
        square = hidden * hidden
        curve = jnp.tanh(hidden * (scale + scale * cubic * square))
        half = 0.5 + 0.5 * curve
        active_ref[:, cols] = low(hidden * half)
        slope = half + (0.5 * hidden) * (1.0 - curve * curve) * (
            scale + 3 * scale * cubic * square
        )
        grad = low(act_grad_ref[:, cols].astype(F32) * slope)
        grad_ref[:, cols] = grad
        sum_ref[:, cols] += jnp.sum(grad.astype(F32), axis=0, keepdims=True)
    back = dot(grad_ref[...], up_ref[...], NT)
    if extras:
        back = back + choose(slot, extra_refs).astype(F32)
    back = low(back)
    for at, back_ref in enumerate(back_refs):

        @pl.when(slot == at)
        def _():
            back_ref[...] = back


def feed(post_all, act_grad, up, up_bias, slots, chosen, extras, held):
    count = len(chosen)
    total, width = post_all.shape
    rows, units = total // slots, up.shape[1]
    block = min(rows, 512)
    per = rows // block
    tall = lambda cols: tall_spec(chosen, per, block, cols)
    active, grad, sums, *backs = kernel_call(
        functools.partial(
            feed_kernel, count=count, per=per, extras=len(extras), held=len(held)
        ),
        (count * per,),
        [tall(width), tall(units), whole(up.shape), whole(up_bias.shape)]
        + slot_specs(len(extras), per, block, width),
        [tall(units), tall(units), whole((1, units))] + slot_specs(count, per, block, width),
        [shape_of(total, units), shape_of(total, units), shape_of(1, units, F32)]
        + [shape_of(rows, width)] * count,
        [post_all, act_grad, up, up_bias, *extras],
        held,
        name="feed",
    )
    return (active, grad), sums, backs


def split_rows(total, me, keep_ref, send_ref, streams):
    rows = total.shape[0] // streams
    for slot in range(streams):
        part = low(total[pl.ds(pl.multiple_of((me ^ slot) * rows, rows), rows), :])
        ref = send_ref if slot % 2 else keep_ref
        ref[slot // 2 * rows : (slot // 2 + 1) * rows, :] = part


def outer_kernel(me_ref, left_ref, right_ref, keep_ref, send_ref, total, *, streams):
    step = pl.program_id(0)

    @pl.when(step == 0)
    def _():
        total[...] = dot(left_ref[...], right_ref[...], TN)

    @pl.when(step > 0)
    def _():
        total[...] += dot(left_ref[...], right_ref[...], TN)

    @pl.when(step == pl.num_programs(0) - 1)
    def _():
        split_rows(total, me_ref[0], keep_ref, send_ref, streams)


def outer_step(left, right, me, streams):
    total = left.shape[0]
    block = min(total, 1024)
    shape = (left.shape[1], right.shape[1])
    half = (shape[0] // 2, shape[1])
    return kernel_call(
        functools.partial(outer_kernel, streams=streams),
        (total // block,),
        [pl.BlockSpec(memory_space=pltpu.SMEM)]
        + [pl.BlockSpec((block, cols), lambda i: (i, 0)) for cols in shape],
        [whole(half)] * 2,
        [shape_of(*half)] * 2,
        [me, left, right],
        scratch_shapes=[pltpu.VMEM(shape, F32)],
        name="outer_step",
    )


def join_kernel(me_ref, *refs, early, streams):
    parts, (keep_ref, send_ref) = refs[:-2], refs[-2:]
    rows = parts[0].shape[0] // streams
    for slot in range(streams):
        home = pl.ds(pl.multiple_of((me_ref[0] ^ slot) * rows, rows), rows)
        out = send_ref if slot % 2 else keep_ref
        here = slice(slot // 2 * rows, (slot // 2 + 1) * rows)
        at = 0
        for part in parts[:early]:
            out[here, at : at + part.shape[1]] = part[home, :]
            at += part.shape[1]
        total = parts[early][home, :].astype(F32)
        for part in parts[early + 1 :]:
            total = total + part[home, :].astype(F32)
        out[here, at:] = low(total)


def join_step(early, terms, me, streams):
    inputs = [*early, *terms]
    cols = sum(part.shape[1] for part in early) + terms[0].shape[1]
    half = (terms[0].shape[0] // 2, cols)
    return kernel_call(
        functools.partial(join_kernel, early=len(early), streams=streams),
        (1,),
        [pl.BlockSpec(memory_space=pltpu.SMEM)] + [whole(a.shape) for a in inputs],
        [whole(half)] * 2,
        [shape_of(*half)] * 2,
        [me, *inputs],
        name="join_step",
    )


def late_kernel(*refs):
    (keep, come, keep_late, come_late), outs = refs[:4], refs[4:]
    rows, cols = outs[0].shape[0], keep.shape[1]
    for slot, out in enumerate(outs):
        here = slice(slot * rows, (slot + 1) * rows)
        out[:, :cols] = low(keep[here, :].astype(F32) + come[here, :].astype(F32))
        out[:, cols:] = low(keep_late[here, :].astype(F32) + come_late[here, :].astype(F32))


def late_step(pairs, slots):
    inputs = [array for pair in pairs for array in pair]
    shape = (inputs[0].shape[0] // slots, inputs[0].shape[1] + inputs[2].shape[1])
    return kernel_call(
        late_kernel,
        (1,),
        [whole(a.shape) for a in inputs],
        [whole(shape)] * slots,
        [shape_of(*shape)] * slots,
        inputs,
        name="late_step",
    )


def pair_kernel(*refs, count):
    parts, outs = refs[: 2 * count], refs[2 * count :]
    rows = outs[0].shape[0] // count
    for at in range(count):
        keep, come = parts[2 * at : 2 * at + 2]
        for slot, out in enumerate(outs):
            here = slice(slot * rows, (slot + 1) * rows)
            out[at * rows : (at + 1) * rows, :] = low(
                keep[here, :].astype(F32) + come[here, :].astype(F32)
            )


def pair_step(pairs, slots):
    inputs = [array for pair in pairs for array in pair]
    rows, cols = inputs[0].shape
    shape = (rows // slots * len(pairs), cols)
    return kernel_call(
        functools.partial(pair_kernel, count=len(pairs)),
        (1,),
        [whole(a.shape) for a in inputs],
        [whole(shape)] * slots,
        [shape_of(*shape)] * slots,
        inputs,
        name="pair_step",
    )


def stack_kernel(*refs):
    rows = refs[0].shape[0]
    for at, ref in enumerate(refs[:-1]):
        refs[-1][at * rows : (at + 1) * rows, :] = ref[...]


def stack_step(parts):
    rows, cols = parts[0].shape
    return kernel_call(
        stack_kernel,
        (1,),
        [whole((rows, cols))] * len(parts),
        [whole((rows * len(parts), cols))],
        [shape_of(rows * len(parts), cols)],
        list(parts),
        name="stack_step",
    )[0]


def shard_views(even_ref, odd_ref, streams):
    rows = even_ref.shape[0] // (streams // 2)
    return [
        (slot, ref.at[slot // 2 * rows : (slot // 2 + 1) * rows])
        for slot, ref in enumerate([even_ref, odd_ref] * (streams // 2))
    ]


def feed_grads_kernel(me_ref, even_ref, odd_ref, up_ref, down_ref, up_rows, *, streams):
    rows = even_ref.shape[0] // streams
    for slot, part in shard_views(even_ref, odd_ref, streams):
        home = pl.ds(pl.multiple_of((me_ref[0] ^ slot) * rows, rows), rows)
        up_rows[home, :] = part[:rows, :].astype(F32)
        down_ref[home, :] = part[rows:, :].astype(F32)
    up_ref[...] = up_rows[...].T


def feed_grads(even, odd, me, streams):
    units, width = even.shape
    return kernel_call(
        functools.partial(feed_grads_kernel, streams=streams),
        (1,),
        [pl.BlockSpec(memory_space=pltpu.SMEM)] + [whole(even.shape)] * 2,
        [whole((width, units)), whole((units, width))],
        [shape_of(width, units, F32), shape_of(units, width, F32)],
        [me, even, odd],
        scratch_shapes=[pltpu.VMEM((units, width), F32)],
        name="feed_grads",
    )


def pack_kernel(*refs, groups):
    sums_ref, gain_ref, shift_ref = refs[:3]
    row_refs, count_refs = refs[3 : 3 + groups], refs[3 + groups : 3 + 2 * groups]
    unit_refs, out_ref = refs[3 + 2 * groups : -1], refs[-1]
    out_ref[...] = jnp.zeros_like(out_ref)
    out_ref[:4, : sums_ref.shape[1]] = sums_ref[:4, :]
    rows = row_refs[0][...]
    for ref in row_refs[1:]:
        rows = rows + ref[...]
    out_ref[4:5, : rows.shape[1]] = (rows[0:1] - row(shift_ref) * rows[1:2]) / row(gain_ref)
    out_ref[5:6, : rows.shape[1]] = rows[1:2]
    units = unit_refs[0][...]
    for ref in unit_refs[1:]:
        units = units + ref[...]
    out_ref[8:9, : units.shape[1]] = units
    for at, ref in enumerate(count_refs):
        out_ref[9 + at : 10 + at, : ref.shape[1]] = ref[...]


def pack(row_sums, gain, shift, group_rows, group_counts, unit_sums):
    inputs = [row_sums, gain, shift, *group_rows, *group_counts, *unit_sums]
    wide = max(a.shape[1] for a in (row_sums, *group_counts, *unit_sums))
    return kernel_call(
        functools.partial(pack_kernel, groups=len(group_rows)),
        (1,),
        [whole(a.shape) for a in inputs],
        [whole((16, wide))],
        [shape_of(16, wide, F32)],
        inputs,
        name="pack",
    )[0]


def resid_kernel(*refs, terms, slots):
    term_refs = refs[:terms]
    residual_ref, cot_ref, gain_ref = refs[terms : terms + 3]
    weight_refs = refs[terms + 3 : terms + 3 + slots]
    grad_ref, low_ref, sums_ref = refs[terms + 3 + slots : terms + 6 + slots]
    part_refs = refs[terms + 6 + slots :]

    @pl.when(pl.program_id(0) == 0)
    def _():
        sums_ref[...] = jnp.zeros_like(sums_ref)

    post_grad = term_refs[0][...].astype(F32)
    for ref in term_refs[1:]:
        post_grad = post_grad + ref[...].astype(F32)
    cot = cot_ref[...].astype(F32)
    normal, inverse = norm_stats(residual_ref[...])
    grad = cot + norm_pull(post_grad * row(gain_ref), normal, inverse)
    grad_ref[...] = grad
    grad_low = low(grad)
    low_ref[...] = grad_low
    for weight_ref, part_ref in zip(weight_refs, part_refs):
        part_ref[...] = low(dot(grad_low, weight_ref[...], NT))
    for at, value in enumerate((cot, grad, post_grad * normal, post_grad)):
        sums_ref[at : at + 1, :] += jnp.sum(value, axis=0, keepdims=True)


def resid_step(terms, residual, cotangent, gain, weights):
    rows, width = residual.shape
    block = min(rows, 256)
    tall = lambda cols: pl.BlockSpec((block, cols), lambda i: (i, 0))
    cols = weights[0].shape[0]
    return kernel_call(
        functools.partial(resid_kernel, terms=len(terms), slots=len(weights)),
        (rows // block,),
        [tall(width)] * (len(terms) + 2) + [whole(a.shape) for a in (gain, *weights)],
        [tall(width), tall(width), whole((8, width))] + [tall(cols)] * len(weights),
        [shape_of(rows, width, F32), shape_of(rows, width), shape_of(8, width, F32)]
        + [shape_of(rows, cols)] * len(weights),
        [*terms, residual, cotangent, gain, *weights],
        (),
        name="resid_step",
    )


def dense_grad_kernel(*refs, slots, groups):
    mixed_refs, grad_ref = refs[: slots * groups], refs[slots * groups]
    even_ref, odd_ref, *sum_refs = refs[slots * groups + 1 :]
    step = pl.program_id(0)
    grad = grad_ref[...]
    for slot in range(slots):
        mixed = [ref[...] for ref in mixed_refs[slot * groups : (slot + 1) * groups]]
        part = dot(grad, jnp.concatenate(mixed, axis=1), TN)
        sum_refs[slot][...] = jnp.where(step == 0, 0.0, sum_refs[slot][...]) + part

    @pl.when(step == pl.num_programs(0) - 1)
    def _():
        rows = sum_refs[0].shape[0]
        for slot, sum_ref in enumerate(sum_refs):
            out_ref = odd_ref if slot % 2 else even_ref
            out_ref[slot // 2 * rows : (slot // 2 + 1) * rows, :] = low(sum_ref[...])


def dense_grad(mixed, grad):
    slots, groups = len(mixed), len(mixed[0])
    rows, width = grad.shape
    block = min(rows, 512)
    per = rows // block
    cols = sum(part.shape[1] for part in mixed[0])
    return kernel_call(
        functools.partial(dense_grad_kernel, slots=slots, groups=groups),
        (per,),
        [
            pl.BlockSpec((block, part.shape[1]), lambda i, slot=slot: (slot * per + i, 0))
            for slot in range(slots)
            for part in mixed[slot]
        ]
        + [pl.BlockSpec((block, width), lambda i: (i, 0))],
        [whole((width * slots // 2, cols))] * 2,
        [shape_of(width * slots // 2, cols)] * 2,
        [*[part for parts in mixed for part in parts], grad],
        (),
        scratch_shapes=[pltpu.VMEM((width, cols), F32)] * slots,
        name="dense_grad",
    )


def weight_kernel(me_ref, normed_ref, grad_ref, wq_ref, wk_ref, wv_ref, *refs, streams):
    *out_refs, sums_ref, count_ref, total, count = refs
    step = pl.program_id(0)

    @pl.when(step == 0)
    def _():
        total[...] = jnp.zeros_like(total)
        count[...] = jnp.zeros_like(count)

    grad = grad_ref[...]
    total[...] += dot(normed_ref[...], grad, TN)
    count[...] += jnp.sum(grad.astype(F32), axis=0, keepdims=True)

    @pl.when(step == pl.num_programs(0) - 1)
    def _():
        weight = jnp.concatenate([wq_ref[...], wk_ref[...], wv_ref[...]], axis=1).astype(F32)
        if streams:
            split_rows(total, me_ref[0], *out_refs, streams)
        else:
            out_refs[0][...] = low(total[...])
        count_ref[...] = count[...]
        lane = lanes(weight.shape[0])
        cross = jnp.sum(weight * total[...], axis=1, keepdims=True)
        plain = jnp.sum(weight * count[...], axis=1, keepdims=True)
        both = jnp.where(lane == 0, cross, jnp.where(lane == 1, plain, 0.0))
        sums_ref[...] = both.T[:8]


def weight_step(normed, grad, weights, group, me, streams):
    total, width = normed.shape
    cols = grad.shape[1]
    block = min(total, 1024)
    outs = [(width // 2, cols)] * 2 if streams else [(width, cols)]
    *parts, sums, count = kernel_call(
        functools.partial(weight_kernel, streams=streams),
        (total // block,),
        [pl.BlockSpec(memory_space=pltpu.SMEM)]
        + [pl.BlockSpec((block, count), lambda i: (i, 0)) for count in (width, cols)]
        + [pl.BlockSpec((width, cols // 3), lambda i: (0, group))] * 3,
        [whole(shape) for shape in outs] + [whole((8, width)), whole((1, cols))],
        [shape_of(*shape) for shape in outs] + [shape_of(8, width, F32), shape_of(1, cols, F32)],
        [me, normed, grad, *weights],
        scratch_shapes=[pltpu.VMEM((width, cols), F32), pltpu.VMEM((1, cols), F32)],
        name="weight_step",
    )
    return parts, sums, count


def unproject_kernel(*refs, groups, per, extras):
    grad_refs, weight_refs = refs[:groups], refs[groups : 4 * groups]
    extra_refs = refs[4 * groups : 4 * groups + extras]
    out_refs = refs[4 * groups + extras : -1]
    joined = refs[-1]
    slot = pl.program_id(0) // per

    @pl.when(pl.program_id(0) == 0)
    def _():
        joined[...] = jnp.concatenate([ref[...] for ref in weight_refs], axis=1)

    total = dot(jnp.concatenate([ref[...] for ref in grad_refs], axis=1), joined[...], NT)
    if extras:
        total = total + choose(slot, extra_refs).astype(F32)
    total = low(total)
    for at, ref in enumerate(out_refs):

        @pl.when(slot == at)
        def _():
            ref[...] = total


def unproject(grads, weights, slots, chosen, extras):
    width = weights[0].shape[0]
    count, groups = len(chosen), len(grads)
    total, cols = grads[0].shape
    rows = total // slots
    block = min(rows, 512)
    per = rows // block
    return kernel_call(
        functools.partial(unproject_kernel, groups=groups, per=per, extras=len(extras)),
        (count * per,),
        [tall_spec(chosen, per, block, cols)] * groups
        + [
            pl.BlockSpec((width, cols // 3), lambda i, group=group: (0, group))
            for group in range(groups)
            for _ in weights
        ]
        + slot_specs(len(extras), per, block, width),
        slot_specs(count, per, block, width),
        [shape_of(rows, width)] * count,
        [*grads, *[weight for _ in grads for weight in weights], *extras],
        (),
        scratch_shapes=[pltpu.VMEM((width, cols * groups), BF16)],
        name="unproject",
    )


def ffn_kernel(active_ref, weight_ref, even_ref, odd_ref, *, per):
    total = low(dot(active_ref[...], weight_ref[...]))
    odd = pl.program_id(0) // per % 2

    @pl.when(odd == 0)
    def _():
        even_ref[...] = total

    @pl.when(odd == 1)
    def _():
        odd_ref[...] = total


def ffn_step(active, weight, slots):
    total, units = active.shape
    width = weight.shape[1]
    rows = total // slots
    block = min(rows, 1024)
    per = rows // block
    half = (total // 2, width)

    def half_spec(odd):
        def place(i):
            slot, step = i // per, i % per
            now = slot // 2 * per
            if odd:
                return (jnp.where(slot % 2 == 1, now + step, jnp.maximum(now - 1, 0)), 0)
            return (jnp.where(slot % 2 == 0, now + step, now + per - 1), 0)

        return pl.BlockSpec((block, width), place)

    return kernel_call(
        functools.partial(ffn_kernel, per=per),
        (slots * per,),
        [pl.BlockSpec((block, units), lambda i: (i, 0)), whole(weight.shape)],
        [half_spec(0), half_spec(1)],
        [shape_of(*half)] * 2,
        [active, weight],
        name="ffn_step",
    )


def spread_kernel(me_ref, even_ref, odd_ref, *refs, groups, streams):
    *out_refs, dense_ref, dense_rows = refs
    cols = out_refs[0].shape[1] // groups
    heads = dense_ref.shape[0]
    rows = even_ref.shape[0] * 2 // streams
    for slot, part in shard_views(even_ref, odd_ref, streams):
        home = pl.ds(pl.multiple_of((me_ref[0] ^ slot) * rows, rows), rows)
        for group in range(groups):
            first = group * 3 * cols + (heads if group == groups - 1 else 0)
            for kind in range(3):
                at = first + kind * cols
                out_refs[kind][home, group * cols : (group + 1) * cols] = part[
                    :, at : at + cols
                ].astype(F32)
        first = (groups - 1) * 3 * cols
        dense_rows[home, :] = part[:, first : first + heads].astype(F32)
    dense_ref[...] = dense_rows[...].T


def spread(even, odd, me, streams, groups, heads):
    width = even.shape[0] * 2
    shapes = [(width, heads)] * 3 + [(heads, width)]
    return kernel_call(
        functools.partial(spread_kernel, groups=groups, streams=streams),
        (1,),
        [pl.BlockSpec(memory_space=pltpu.SMEM)] + [whole(even.shape)] * 2,
        [whole(shape) for shape in shapes],
        [shape_of(*shape, F32) for shape in shapes],
        [me, even, odd],
        scratch_shapes=[pltpu.VMEM((width, heads), F32)],
        name="spread",
    )


def input_kernel(*refs, terms):
    x_ref, resid_ref, gain_ref, out_ref = refs[terms:]
    grad = refs[0][...].astype(F32)
    for ref in refs[1:terms]:
        grad = grad + ref[...].astype(F32)
    normal, inverse = norm_stats(x_ref[...].astype(F32))
    out_ref[...] = resid_ref[...] + norm_pull(grad * row(gain_ref), normal, inverse)


def input_step(terms, layer_input, resid_grad, gain):
    rows, width = resid_grad.shape
    block = min(rows, 256)
    tall = pl.BlockSpec((block, width), lambda i: (i, 0))
    return kernel_call(
        functools.partial(input_kernel, terms=len(terms)),
        (rows // block,),
        [tall] * (len(terms) + 2) + [whole(gain.shape)],
        [tall],
        [shape_of(rows, width, F32)],
        [*terms, layer_input, resid_grad, gain],
        name="input_step",
    )[0]


def shards(
    slots,
    streams,
    layer_input,
    row_ids,
    input_gain,
    input_shift,
    query_weight,
    query_bias,
    key_weight,
    value_weight,
    value_bias,
    dense_weight,
    dense_bias,
    post_gain,
    post_shift,
    up_weight,
    up_bias,
    down_weight,
    down_bias,
    cotangent,
):
    me = lax.axis_index("tensor")
    me_word = me.astype(jnp.int32)[None]
    stream = lax.axis_index("dp").astype(jnp.int32)[None]
    rows = layer_input.shape[0]
    head_cols = query_weight.shape[1]
    head_count = head_cols // HD
    groups = max(1, head_count // 2)
    bits = [1 << level for level in range(slots.bit_length() - 1)]
    half = slots // 2
    after = lambda array, *others: lax.optimization_barrier((array, *others))[0]

    def swap(array, mask):
        return lax.ppermute(array, "tensor", [(i, i ^ mask) for i in range(slots)])

    def gather(array):
        held = {0: array}
        for bit in reversed(bits):
            held.update({slot ^ bit: swap(part, bit) for slot, part in held.items()})
        return [held[slot] for slot in range(slots)]

    def blocks(array):
        return [array[slot * rows : (slot + 1) * rows] for slot in range(slots)]

    def swap_data(array, mask):
        return lax.ppermute(array, "dp", [(i, i ^ mask) for i in range(streams)])

    def finish_terms(held, terms, levels):
        for bit in levels:
            come = {slot ^ bit: swap(part, bit) for slot, part in held.items() if slot & bit}
            if 0 in come:
                terms.append(come.pop(0))
            held = {
                slot: low(held[slot].astype(F32) + part.astype(F32)) for slot, part in come.items()
            }
        return terms

    def scatter_terms(parts):
        return finish_terms(dict(enumerate(parts)), [parts[0]], bits)

    far_odd = range(half + 1, slots, 2)
    far_even = range(half, slots, 2)
    near_odd = range(1, half, 2)
    near_even = range(0, half, 2)

    def ordered_terms(make):
        far = make(far_odd, (), None)
        far_come = [swap(part, 1) for part in far]
        near = make(near_odd, (), far[-1])
        near_come = [swap(part, 1) for part in near]
        far = make(far_even, far_come, near[-1])
        near = make(near_even, near_come, far[-1])
        held = dict(zip((*far_even, *near_even), (*far, *near)))
        return finish_terms(held, [held.pop(0)], bits[1:])

    def add_up(terms):
        return functools.reduce(
            lambda sum_now, term: sum_now + term.astype(F32), terms[1:], terms[0].astype(F32)
        )

    far_streams = range(2, streams, 2)

    def exchange(parts):
        return low(add_up([parts[0], *[swap_data(parts[k // 2], k) for k in far_streams]]))

    def collect_far(shard):
        return [shard, *[swap_data(shard, k) for k in far_streams]]

    norm_vectors = (input_gain, input_shift)
    weights = (query_weight, key_weight, value_weight)
    biases = (query_bias, value_bias)
    x_held = {0: layer_input}
    for bit in reversed(bits[1:]):
        x_held.update({slot ^ bit: swap(part, bit) for slot, part in x_held.items()})
    x_held[1] = swap(x_held[0], 1)
    near_parts = [x_held[0], x_held[1]]
    first = range(2)
    held = project(near_parts, first, slots, norm_vectors, weights, biases, ())
    rest = sorted(slot for slot in x_held if slot > 1)
    *arrived, normed = lax.optimization_barrier((*[x_held[slot] for slot in rest], held[0]))
    held = (normed, *held[1:])
    for slot, part in zip(rest, arrived):
        x_held[slot], x_held[slot ^ 1] = part, swap(part, 1)
    x_parts = [x_held[slot] for slot in range(slots)]
    dense_parts = gather(after(dense_weight, arrived[-1]))
    cot_own = after(cotangent, arrived[-1])
    cot_held = {0: cot_own}
    for bit in reversed(bits[1:]):
        cot_held.update({slot ^ bit: swap(part, bit) for slot, part in cot_held.items()})
    normed, queries, key_rows, values = project(
        x_parts[2:], range(2, slots), slots, norm_vectors, weights, biases, held
    )

    heads = me * head_count + jnp.arange(head_count)
    slopes = jnp.exp2(-8.0 * (heads + 1).astype(F32) / HEADS) * LOG2E
    apart = (row_ids[:1] != row_ids[SHORT : SHORT + 1]).astype(jnp.int32)

    mixed_own, log_totals, mixed_parts = [], [], []
    for group in range(groups):
        mixed, log_total = attend(
            me_word,
            apart,
            slopes,
            queries if not group else after(queries, cot_held[half], mixed_own[-1]),
            key_rows,
            values,
            slots,
            group,
        )
        mixed_own.append(mixed)
        log_totals.append(log_total)
        if not group:
            keys = sorted(cot_held)
            held = lax.optimization_barrier((*[cot_held[key] for key in keys], mixed))[:-1]
            cot_held.update(zip(keys, held))
            cot_held.update({slot ^ 1: swap(part, 1) for slot, part in cot_held.items()})
            cot_parts = [cot_held[slot] for slot in range(slots)]
        if group < groups - 1:
            mixed_parts.append(gather(mixed))
    act_grad, cot_all = act_grad_step(
        lax.optimization_barrier((*cot_parts, mixed_own[-1], *dense_parts[2:]))[:slots], down_weight
    )
    came = {0: mixed_own[-1]}
    for bit in reversed(bits[1:]):
        came.update({slot ^ bit: swap(part, bit) for slot, part in came.items()})
    far_slots = sorted(came)[1:]
    *arrived, act_grad = lax.optimization_barrier((*[came[slot] for slot in far_slots], act_grad))
    came.update(zip(far_slots, arrived))
    came.update({slot ^ 1: swap(part, 1) for slot, part in came.items()})
    mixed_parts.append([came[slot] for slot in range(slots)])
    mixed_all = [[mixed_parts[group][slot] for group in range(groups)] for slot in range(slots)]
    post_all, residual = post_norm(
        mixed_all, x_parts, dense_parts, dense_bias, post_gain, post_shift
    )

    fed, up_bias_parts = [()], []

    def make_feed(chosen, extras, gate):
        held, sums, backs = feed(
            post_all, act_grad, up_weight, up_bias, slots, chosen, extras, fed[-1]
        )
        fed.append(held)
        up_bias_parts.append(sums)
        return backs

    post_terms = ordered_terms(make_feed)
    active, hidden_grad = fed[-1]
    up_keep, up_send = outer_step(hidden_grad, post_all, stream, streams)
    down_keep, down_send = outer_step(active, after(cot_all, up_keep), stream, streams)
    up_come, down_come = swap_data(up_send, 1), swap_data(down_send, 1)
    resid_grad, attended_grad, row_sums, *mixed_grads = resid_step(
        [after(post_terms[0], down_keep), *post_terms[1:]],
        residual,
        cotangent,
        post_gain,
        dense_parts,
    )
    mixed_grads = [swap(part, slot) if slot else part for slot, part in enumerate(mixed_grads)]
    dense_even, dense_odd = dense_grad(mixed_all, attended_grad)
    ffn_even, ffn_odd = ffn_step(after(active, dense_odd), down_weight, slots)
    feed_parts = pair_step(
        [(after(up_keep, ffn_odd), up_come), (down_keep, down_come)], streams // 2
    )
    moved = lax.optimization_barrier((*mixed_grads, dense_odd, ffn_odd, *feed_parts))
    mixed_grads, (dense_odd, ffn_odd), feed_parts = (
        moved[:slots],
        moved[slots : slots + 2],
        moved[slots + 2 :],
    )
    dense_come, ffn_come = swap(dense_odd, 1), swap(ffn_odd, 1)

    def partner_sums(even, come):
        size = even.shape[0] * 2 // slots
        cuts = [slice(at * size, (at + 1) * size) for at in range(slots // 2)]
        return [low(even[cut].astype(F32) + come[cut].astype(F32)) for cut in cuts]

    cols = head_cols // groups
    head_grads, early_parts, group_rows, group_counts = [], [], [], []

    def backward(group):
        return attend_back(
            me_word,
            apart,
            slopes,
            queries,
            key_rows,
            values,
            mixed_own[group],
            log_totals[group],
            mixed_grads,
            group,
        )

    dense_sums = partner_sums(dense_even, dense_come)
    for group in range(groups - 1):
        head_grads.append(backward(group))
        grad = head_grads[-1]
        if group == groups - 2:
            grad, *dense_sums = lax.optimization_barrier((grad, *dense_sums))
        parts, row_part, count_part = weight_step(normed, grad, weights, group, stream, 0)
        early_parts += parts
        group_rows.append(row_part)
        group_counts.append(count_part)
        mixed_grads = lax.optimization_barrier((*mixed_grads, parts[-1]))[:-1]
    even_slots = range(2, slots, 2)
    dense_terms = finish_terms(dict(zip(even_slots, dense_sums[1:])), [dense_sums[0]], bits[1:])
    early_keep, early_send = join_step(early_parts, dense_terms, stream, streams)
    moved = lax.optimization_barrier(
        (*mixed_grads, early_send, exchange(feed_parts), *partner_sums(ffn_even, ffn_come))
    )
    mixed_grads, (early_send, feed_shard), ffn_sums = (
        moved[:slots],
        moved[slots : slots + 2],
        moved[slots + 2 :],
    )
    early_come = swap_data(early_send, 1)
    feed_shards = collect_far(feed_shard)
    ffn_terms = finish_terms(dict(zip(even_slots, ffn_sums[1:])), [ffn_sums[0]], bits[1:])
    head_grads.append(backward(groups - 1))
    grad, early_come, *arrived = lax.optimization_barrier(
        (head_grads[-1], early_come, *feed_shards, *ffn_terms)
    )
    feed_shards, ffn_terms = arrived[: len(feed_shards)], arrived[len(feed_shards) :]
    (late_keep, late_send), row_part, count_part = weight_step(
        normed, grad, weights, groups - 1, stream, streams
    )
    group_rows.append(row_part)
    group_counts.append(count_part)
    late_come = swap_data(late_send, 1)
    vectors = pack(row_sums, input_gain, input_shift, group_rows, group_counts, up_bias_parts)
    feed_even = stack_step([*feed_shards[:-1], after(feed_shards[-1], vectors)])
    summed = vectors + swap_data(vectors, 1)
    feed_odd = swap_data(after(feed_even, late_come, summed), 1)
    late_parts = late_step(
        [(early_keep, early_come), (after(late_keep, feed_even), late_come)], streams // 2
    )
    late_shard = exchange(late_parts)
    seen = []

    def make_unproject(chosen, extras, gate):
        gates = [feed_even if gate is None else gate]
        if not seen:
            gates += [late_parts[-1], summed]
        if len(seen) == 2:
            gates.append(late_shard)
        seen.append(0)
        return unproject(
            [*head_grads[:-1], after(head_grads[-1], *gates)], weights, slots, chosen, extras
        )

    normed_terms = ordered_terms(make_unproject)
    layer_output = low(residual + add_up(ffn_terms) + down_bias.astype(F32))
    up_grad, down_grad = feed_grads(after(feed_even, normed_terms[0]), feed_odd, stream, streams)
    *late_shards, layer_output, up_grad = lax.optimization_barrier(
        (*collect_far(late_shard), layer_output, up_grad)
    )
    late_even = stack_step(late_shards)
    late_odd = swap_data(late_even, 1)
    input_grad = input_step(
        [*normed_terms[:-1], after(normed_terms[-1], late_even)],
        layer_input,
        resid_grad,
        input_gain,
    )
    for level in range(1, streams.bit_length() - 1):
        summed = summed + swap_data(summed, 1 << level)
    own = summed[8:]
    shared = after(summed, normed_terms[-1])[:8]
    for bit in reversed(bits):
        shared = shared + swap(shared, bit)
    shared = shared[:, : resid_grad.shape[1]]
    up_bias_grad = own[0, : up_bias.shape[0]]
    counts = own[1 : 1 + groups]
    query_bias_grad = counts[:, :cols].reshape(-1)
    value_bias_grad = counts[:, 2 * cols : 3 * cols].reshape(-1)
    *weight_grads, dense_weight_grad = spread(
        after(late_even, input_grad), late_odd, stream, streams, groups, head_cols
    )
    return (
        layer_output,
        input_grad,
        shared[4],
        shared[5],
        weight_grads[0],
        query_bias_grad,
        weight_grads[1],
        weight_grads[2],
        value_bias_grad,
        dense_weight_grad,
        shared[1],
        shared[2],
        shared[3],
        up_grad,
        up_bias_grad,
        down_grad,
        shared[0],
    )


def solution(mesh):
    in_specs = (
        P(("dp", "tensor"), None),
        P("dp"),
        P(),
        P(),
        P(None, "tensor"),
        P("tensor"),
        P(None, "tensor"),
        P(None, "tensor"),
        P("tensor"),
        P("tensor", None),
        P(),
        P(),
        P(),
        P(None, "tensor"),
        P("tensor"),
        P("tensor", None),
        P(),
        P(("dp", "tensor"), None),
    )
    out_specs = (
        P(("dp", "tensor"), None),
        P(("dp", "tensor"), None),
        P(),
        P(),
        P(None, "tensor"),
        P("tensor"),
        P(None, "tensor"),
        P(None, "tensor"),
        P("tensor"),
        P("tensor", None),
        P(),
        P(),
        P(),
        P(None, "tensor"),
        P("tensor"),
        P("tensor", None),
        P(),
    )
    return jax.shard_map(
        functools.partial(shards, mesh.shape["tensor"], mesh.shape["dp"]), mesh=mesh, in_specs=in_specs, out_specs=out_specs, check_vma=False)
```

```python
import functools
import math

import jax
import jax.numpy as jnp
from jax import lax
from jax.experimental import pallas as pl
from jax.experimental.pallas import tpu as pltpu
from jax.sharding import PartitionSpec as P

HEADS = 16
HD = 64
SHORT = 2048
EPSILON = 1e-05
LOG2E = math.log2(math.e)
F32 = jnp.float32
BF16 = jnp.bfloat16
SMALL_COST = pl.CostEstimate(flops=1, transcendentals=0, bytes_accessed=1)
NT = (((1,), (1,)), ((), ()))
NN = (((1,), (0,)), ((), ()))
TN = (((0,), (0,)), ((), ()))


def dot(lhs, rhs, dims=NN):
    return lax.dot_general(lhs, rhs, dims, preferred_element_type=F32)


def low(array):
    return array.astype(BF16)


def norm_stats(rows):
    center = jnp.mean(rows, axis=-1, keepdims=True)
    centered = rows - center
    inverse = lax.rsqrt(jnp.mean(centered * centered, axis=-1, keepdims=True) + EPSILON)
    return centered * inverse, inverse


def norm_pull(grad, normal, inverse):
    grad_mean = jnp.mean(grad, axis=-1, keepdims=True)
    dot_mean = jnp.mean(grad * normal, axis=-1, keepdims=True)
    return inverse * (grad - grad_mean - normal * dot_mean)


def lanes(count):
    return lax.broadcasted_iota(jnp.int32, (count, 128), 1)


def places(count, first):
    return lax.broadcasted_iota(jnp.int32, (count, 128), 0) + first


def widen(head):
    return jnp.concatenate([head.astype(F32), jnp.zeros((head.shape[0], HD), F32)], axis=1)


def split3(value):
    high = low(value).astype(F32)
    middle = low(value - high).astype(F32)
    return high, middle, value - high - middle


def pick3(index, parts):
    return jnp.where(index == 0, parts[0], jnp.where(index == 1, parts[1], parts[2]))


def key_columns(head, first):
    count = head.shape[0]
    lane, place = lanes(count), places(count, first)
    coarse = ((place >> 6) << 6).astype(F32)
    fine = (place & 63).astype(F32)
    wall = jnp.where(place < SHORT, -1e30, 0.0)
    extra = jnp.where(lane < 73, -1.0, jnp.where(lane == 73, wall, 0.0))
    extra = jnp.where(lane < 67, coarse, jnp.where(lane < 70, fine, extra))
    return low(jnp.where(lane < HD, widen(head), extra))


def query_columns(head, first, slope, apart, log_total=None):
    count = head.shape[0]
    lane, place = lanes(count), places(count, first)
    extra = pick3(jnp.where(lane < 67, lane - 64, lane - 67), split3(slope))
    extra = jnp.where(lane < 70, extra, 0.0)
    if log_total is not None:
        extra = jnp.where((lane >= 70) & (lane < 73), pick3(lane - 70, split3(log_total)), extra)
    extra = jnp.where(lane == 73, jnp.where(place >= SHORT, apart, 0.0), extra)
    return low(jnp.where(lane < HD, widen(head), extra))


def ones_columns(head, count):
    lane = lanes(head.shape[0])
    return low(jnp.where(lane < HD, widen(head), jnp.where(lane < HD + count, 1.0, 0.0)))


def grad_columns(head, shift):
    lane = lanes(head.shape[0])
    extra = jnp.where(lane < 67, pick3(lane - 64, split3(shift)), 0.0)
    return low(jnp.where(lane < HD, widen(head), extra))


def each_chunk(me, slots, rows, body):
    chunk = min(rows, 512)
    for slot in range(slots):
        home = (me ^ slot) * rows

        @pl.loop(0, rows // chunk)
        def _(step):
            offset = pl.multiple_of(step * chunk, chunk)
            body(slot, pl.ds(offset, chunk), pl.ds(slot * rows + offset, chunk), home + offset)


def attend_columns(slot_map, refs, scratch, pair, slope_ref, apart, first=0):
    (q_ref, k_ref, v_ref), (qa, ka, va) = refs, scratch
    me, slots, rows = slot_map
    chunk = min(rows, 512)

    def prepare(slot, inner, spot, place):
        place = pl.multiple_of(place, chunk)
        home = pl.ds(pl.multiple_of(place - first, chunk), chunk)
        for s in range(pair):
            cols = slice(s * HD, (s + 1) * HD)
            qa[s, home, :] = query_columns(q_ref[spot, cols], place, slope_ref[s], apart)
            ka[s, home, :] = key_columns(k_ref[spot, cols], place)
            va[s, home, :] = ones_columns(v_ref[spot, cols], 1)

    each_chunk(me, slots, rows, prepare)


def attend_step(queries, carry, keys, values, mask):
    after = []
    for query, (top, mix), key, value in zip(queries, carry, keys, values):
        scores = dot(query, key, NT)
        if mask is not None:
            scores = jnp.where(mask, scores, -1e30)
        higher = jnp.maximum(top, jnp.max(scores, axis=1, keepdims=True))
        weights = low(jnp.exp2(scores - higher))
        mix = mix * jnp.exp2(top - higher) + dot(weights, value)
        after.append((higher, mix))
    return tuple(after)


def attend_start(tile, pair):
    return tuple(
        (jnp.full((tile, 1), -1e38, F32), jnp.zeros((tile, 128), F32)) for _ in range(pair)
    )


def causal_mask(tile):
    return lax.broadcasted_iota(jnp.int32, (tile, tile), 1) <= lax.broadcasted_iota(
        jnp.int32, (tile, tile), 0
    )


def tiles_of(ref, pair, at, tile):
    return [ref[s, pl.ds(pl.multiple_of(at, tile), tile), :] for s in range(pair)]


def attend_own_kernel(
    me_ref, apart_ref, slope_ref, q_ref, k_ref, v_ref, state_ref, qa, ka, va, *, pair, tile
):
    me = me_ref[0]
    total = q_ref.shape[0]
    rows = total // 2
    apart = apart_ref[0].astype(F32)
    attend_columns(
        (me, 2, rows), (q_ref, k_ref, v_ref), (qa, ka, va), pair, slope_ref, apart,
        me // 2 * total,
    )
    mask = causal_mask(tile)
    lane = lanes(tile)

    def query_tile(index, _):
        first = index * tile
        queries = tiles_of(qa, pair, first, tile)

        def step(at, carry, mask):
            keys, values = tiles_of(ka, pair, at, tile), tiles_of(va, pair, at, tile)
            return attend_step(queries, carry, keys, values, mask)

        carry = step(first, attend_start(tile, pair), mask)
        carry = lax.fori_loop(0, index, lambda at, held: step(at * tile, held, None), carry)
        for s, (top, mix) in enumerate(carry):
            state_ref[s, pl.ds(pl.multiple_of(first, tile), tile), :] = jnp.where(
                lane == HD + 1, top, mix
            )
        return 0

    lax.fori_loop(0, total // tile, query_tile, 0)


def attend_own(me, apart, slopes, queries, key_rows, values, rows, group, tile=1024):
    width = queries.shape[1]
    pair = min(2, width // HD)
    spec = pl.BlockSpec((2 * rows, pair * HD), lambda g: (0, group))
    scalars = pl.BlockSpec(memory_space=pltpu.SMEM)
    shape = (pair, 2 * rows, 128)
    return pl.pallas_call(
        functools.partial(attend_own_kernel, pair=pair, tile=tile),
        grid=(1,),
        in_specs=[scalars] * 3 + [spec] * 3,
        out_specs=pl.BlockSpec(shape, lambda g: (0, 0, 0)),
        out_shape=jax.ShapeDtypeStruct(shape, F32),
        scratch_shapes=[pltpu.VMEM(shape, BF16)] * 3,
        compiler_params=pltpu.CompilerParams(vmem_limit_bytes=56 << 20),
        cost_estimate=SMALL_COST,
        name="attend_own",
    )(me, apart, slopes[group * pair : (group + 1) * pair], queries, key_rows, values)


def attend_kernel(*refs, slots, pair, tile, own):
    me_ref, apart_ref, slope_ref, q_ref, k_ref, v_ref = refs[:6]
    own_ref = refs[6] if own else None
    o_ref, lse_ref, qa, ka, va, state = refs[-6:]
    me = me_ref[0]
    total = q_ref.shape[0]
    rows = total // slots
    apart = apart_ref[0].astype(F32)
    attend_columns(
        (me, slots, rows), (q_ref, k_ref, v_ref), (qa, ka, va), pair, slope_ref, apart
    )
    mask = causal_mask(tile)
    piece = min(rows, tile)
    part_tiles = 2 * rows // tile if own else 0
    own_first = me // 2 * part_tiles

    def query_tile(index, _):
        first = pl.multiple_of(index * tile, tile)
        queries = tiles_of(qa, pair, first, tile)

        def step(at, carry, mask):
            keys, values = tiles_of(ka, pair, at, tile), tiles_of(va, pair, at, tile)
            return attend_step(queries, carry, keys, values, mask)

        def begin():
            return step(first, attend_start(tile, pair), mask)

        count = index
        if own:
            inside = (index >= own_first) & (index < own_first + part_tiles)
            lane = lanes(tile)

            @pl.when(inside)
            def _():
                spot = pl.multiple_of((index - own_first) * tile, tile)
                for s in range(pair):
                    state[s] = own_ref[s, pl.ds(spot, tile), :]

            @pl.when(jnp.logical_not(inside))
            def _():
                for s, (top, mix) in enumerate(begin()):
                    state[s] = jnp.where(lane == HD + 1, top, mix)

            carry = tuple((state[s, :, HD + 1 : HD + 2], state[s]) for s in range(pair))
            count = jnp.where(inside, own_first, index)
        else:
            carry = begin()
        carry = lax.fori_loop(0, count, lambda at, held: step(at * tile, held, None), carry)
        outs = []
        for s in range(pair):
            top, mix = carry[s]
            weight = mix[:, HD : HD + 1]
            outs.append(mix[:, :HD] * (1.0 / weight))
            lse_ref[s, 0, pl.ds(first, tile)] = (top + jnp.log2(weight))[:, 0]
        out = low(jnp.concatenate(outs, axis=1))
        for part in range(tile // piece):
            block = (index * (tile // piece) + part) // (rows // piece)
            offset = first + part * piece - block * rows
            spot = pl.multiple_of((block ^ me) * rows + offset, piece)
            o_ref[pl.ds(spot, piece), :] = out[part * piece : (part + 1) * piece]
        return 0

    lax.fori_loop(0, total // tile, query_tile, 0)


def attend(me, apart, slopes, queries, key_rows, values, slots, group, own, tile=1024):
    total, width = queries.shape
    pair = min(2, width // HD)
    cols = pair * HD
    spec = pl.BlockSpec((total, cols), lambda g: (0, group))
    scalars = pl.BlockSpec(memory_space=pltpu.SMEM)
    return pl.pallas_call(
        functools.partial(attend_kernel, slots=slots, pair=pair, tile=tile, own=bool(own)),
        grid=(1,),
        in_specs=[scalars] * 3
        + [spec] * 3
        + [pl.BlockSpec(state.shape, lambda g: (0, 0, 0)) for state in own],
        out_specs=[
            pl.BlockSpec((total, cols), lambda g: (0, 0)),
            pl.BlockSpec((pair, 1, total), lambda g: (0, 0, 0)),
        ],
        out_shape=[
            jax.ShapeDtypeStruct((total, cols), BF16),
            jax.ShapeDtypeStruct((pair, 1, total), F32),
        ],
        scratch_shapes=[pltpu.VMEM((pair, total, 128), BF16)] * 3
        + [pltpu.VMEM((pair, tile, 128), F32)],
        compiler_params=pltpu.CompilerParams(vmem_limit_bytes=56 << 20),
        cost_estimate=pl.CostEstimate(
            flops=pair * 1200 * total * total, transcendentals=0, bytes_accessed=8 * total * cols
        ),
        name="attend",
    )(me, apart, slopes[group * pair : (group + 1) * pair], queries, key_rows, values, *own)


def attend_back_kernel(*refs, slots, pair, tile, key_tile):
    me_ref, apart_ref, slope_ref, q_ref, k_ref, v_ref, o_ref, lse_ref = refs[:8]
    g_refs = refs[8 : 8 + slots]
    out_ref, qa, ka, va, ga, kt, dq_sum = refs[8 + slots :]
    cols = pair * HD
    me = me_ref[0]
    total = q_ref.shape[0]
    rows = total // slots
    chunk = min(rows, 512)
    apart = apart_ref[0].astype(F32)

    def prepare(slot, inner, spot, place):
        place = pl.multiple_of(place, chunk)
        home = pl.ds(place, chunk)
        for s in range(pair):
            mine = slice(s * HD, (s + 1) * HD)
            log_total = lse_ref[s, :, home].T
            qa[s, home, :] = query_columns(q_ref[spot, mine], place, slope_ref[s], apart, log_total)
            keys = key_columns(k_ref[spot, mine], place)
            ka[s, home, :] = keys
            kt[s, :, home] = low(keys.astype(F32).T)
            va[s, home, :] = ones_columns(v_ref[spot, mine], 3)
            grad = g_refs[slot][inner, mine]
            row_dot = jnp.sum(
                grad.astype(F32) * o_ref[spot, mine].astype(F32), axis=1, keepdims=True
            )
            ga[s, home, :] = grad_columns(grad, -row_dot)
            dq_sum[s, :, home] = jnp.zeros((128, chunk), F32)

    each_chunk(me, slots, rows, prepare)
    causal = lax.broadcasted_iota(jnp.int32, (key_tile, key_tile), 0) <= lax.broadcasted_iota(
        jnp.int32, (key_tile, key_tile), 1
    )
    piece = min(rows, key_tile)

    def place_of(place, size):
        block = place // rows
        return pl.multiple_of((block ^ me) * rows + (place - block * rows), size)

    def keys_tile(index, _):
        first = pl.multiple_of(index * key_tile, key_tile)
        here = pl.ds(first, key_tile)

        def step(at, carry, diagonal, width):
            after = []
            for s in range(pair):
                dk, dv = carry[s]
                there = pl.ds(at, width)
                queries, grads = qa[s, there, :], ga[s, there, :]
                probs = jnp.exp2(dot(ka[s, here, :], queries, NT))
                if diagonal:
                    probs = jnp.where(causal, probs, 0.0)
                dv = dv + dot(low(probs), grads)
                score_grad = low(probs * dot(va[s, here, :], grads, NT))
                dk = dk + dot(score_grad, queries)
                dq_sum[s, :, there] += dot(kt[s, :, here], score_grad)
                after.append((dk, dv))
            return tuple(after)

        zeros = jnp.zeros((key_tile, 128), F32)
        carry = step(first, tuple((zeros, zeros) for _ in range(pair)), True, key_tile)
        start = first + key_tile
        short = jnp.minimum((-start) % tile, total - start) // key_tile
        if tile > key_tile:
            carry = lax.fori_loop(
                0,
                short,
                lambda at, held: step(
                    pl.multiple_of(start + at * key_tile, key_tile), held, False, key_tile
                ),
                carry,
            )
            start = start + short * key_tile
        carry = lax.fori_loop(
            0,
            (total - start) // tile,
            lambda at, held: step(
                pl.multiple_of(start + at * tile, min(tile, key_tile)), held, False, tile
            ),
            carry,
        )
        dk = low(jnp.concatenate([held[0][:, :HD] * (1.0 / LOG2E) for held in carry], axis=1))
        dv = low(jnp.concatenate([held[1][:, :HD] for held in carry], axis=1))
        for part in range(key_tile // piece):
            spot = pl.ds(place_of(first + part * piece, piece), piece)
            out_ref[spot, cols : 2 * cols] = dk[part * piece : (part + 1) * piece]
            out_ref[spot, 2 * cols :] = dv[part * piece : (part + 1) * piece]
        return 0

    lax.fori_loop(0, total // key_tile, keys_tile, 0)

    def finish(slot, inner, spot, place):
        home = pl.ds(pl.multiple_of(place, chunk), chunk)
        joined = jnp.concatenate([dq_sum[s, :HD, home] for s in range(pair)], axis=0)
        out_ref[spot, :cols] = low(joined.T * HD**-0.5)

    each_chunk(me, slots, rows, finish)


def attend_back(
    me, apart, slopes, queries, key_rows, values, mixed, log_total, grads, group, tile=1024, key_tile=512
):
    slots = len(grads)
    total, width = queries.shape
    pair = min(2, width // HD)
    cols = pair * HD
    spec = pl.BlockSpec((total, cols), lambda g: (0, group))
    out_spec = pl.BlockSpec((total, cols), lambda g: (0, 0))
    scalars = pl.BlockSpec(memory_space=pltpu.SMEM)
    return pl.pallas_call(
        functools.partial(
            attend_back_kernel, slots=slots, pair=pair, tile=tile, key_tile=key_tile
        ),
        grid=(1,),
        in_specs=[scalars] * 3
        + [spec] * 3
        + [out_spec, pl.BlockSpec((pair, 1, total), lambda g: (0, 0, 0))]
        + [pl.BlockSpec((total // slots, cols), lambda g: (0, group))] * slots,
        out_specs=pl.BlockSpec((total, 3 * cols), lambda g: (0, 0)),
        out_shape=jax.ShapeDtypeStruct((total, 3 * cols), BF16),
        scratch_shapes=[pltpu.VMEM((pair, total, 128), BF16)] * 4
        + [pltpu.VMEM((pair, 128, total), BF16), pltpu.VMEM((pair, 128, total), F32)],
        compiler_params=pltpu.CompilerParams(vmem_limit_bytes=60 << 20),
        cost_estimate=pl.CostEstimate(
            flops=pair * 2400 * total * total, transcendentals=0, bytes_accessed=16 * total * cols
        ),
        name="attend_back",
    )(
        me,
        apart,
        slopes[group * pair : (group + 1) * pair],
        queries,
        key_rows,
        values,
        mixed,
        log_total,
        *grads,
    )


def whole(shape):
    return pl.BlockSpec(shape, lambda i: (0,) * len(shape))


def row(ref):
    return ref[...].astype(F32)[None, :]


def choose(slot, refs):
    rows = refs[0][...]
    for at, ref in enumerate(refs[1:], 1):
        rows = jnp.where(slot == at, ref[...], rows)
    return rows


def slot_specs(count, per, block, width, order=lambda i: i):
    return [
        pl.BlockSpec(
            (block, width), lambda i, at=at: (jnp.clip(order(i) - at * per, 0, per - 1), 0)
        )
        for at in range(count)
    ]


def tall_spec(chosen, per, block, width):
    return pl.BlockSpec(
        (block, width),
        lambda i: ((chosen.start + chosen.step * (i // per)) * per + i % per, 0),
    )


def kernel_call(kernel, grid, in_specs, out_specs, out_shape, inputs, held=(), **more):
    return pl.pallas_call(
        kernel,
        grid=grid,
        in_specs=in_specs + [pl.BlockSpec(memory_space=pl.ANY)] * len(held),
        out_specs=out_specs,
        out_shape=out_shape,
        input_output_aliases={len(inputs) + at: at for at in range(len(held))},
        compiler_params=pltpu.CompilerParams(vmem_limit_bytes=56 << 20),
        cost_estimate=SMALL_COST,
        **more,
    )(*inputs, *held)


def shape_of(rows, cols, kind=BF16):
    return jax.ShapeDtypeStruct((rows, cols), kind)


def project_kernel(*refs, count, per):
    x_refs = refs[:count]
    gain_ref, shift_ref, wq_ref, wk_ref, wv_ref, qb_ref, vb_ref = refs[count : count + 7]
    normed_ref, q_ref, k_ref, v_ref = refs[-4:]
    x = choose(pl.program_id(0) // per, x_refs).astype(F32)
    normed = low(norm_stats(x)[0] * row(gain_ref) + row(shift_ref))
    normed_ref[...] = normed
    q_ref[...] = low((dot(normed, wq_ref[...]) + row(qb_ref)) * (LOG2E * HD**-0.5))
    k_ref[...] = low(dot(normed, wk_ref[...]))
    v_ref[...] = low(dot(normed, wv_ref[...]) + row(vb_ref))


def project(x_parts, chosen, slots, vectors, weights, biases, held):
    rows, width = x_parts[0].shape
    block = min(rows, 512)
    per = rows // block
    widths = [width] + [weight.shape[1] for weight in weights]
    return kernel_call(
        functools.partial(project_kernel, count=len(chosen), per=per),
        (len(chosen) * per,),
        slot_specs(len(chosen), per, block, width)
        + [whole(a.shape) for a in (*vectors, *weights, *biases)],
        [tall_spec(chosen, per, block, cols) for cols in widths],
        [shape_of(slots * rows, cols) for cols in widths],
        [*x_parts, *vectors, *weights, *biases],
        held,
        name="project",
    )


def act_grad_kernel(*refs, count, per):
    down_ref, grad_ref, cot_ref = refs[count:]
    cot = choose(pl.program_id(0) // per, refs[:count])
    cot_ref[...] = cot
    grad_ref[...] = low(dot(cot, down_ref[...], NT))


def act_grad_step(cot_parts, down):
    slots = len(cot_parts)
    rows, width = cot_parts[0].shape
    block = min(rows, 1024)
    per = rows // block
    units = down.shape[0]
    return kernel_call(
        functools.partial(act_grad_kernel, count=slots, per=per),
        (slots * per,),
        slot_specs(slots, per, block, width) + [whole(down.shape)],
        [pl.BlockSpec((block, cols), lambda i: (i, 0)) for cols in (units, width)],
        [shape_of(slots * rows, cols) for cols in (units, width)],
        [*cot_parts, down],
        (),
        name="act_grad",
    )


def post_kernel(*refs, slots, groups, per):
    mixed_refs = refs[: slots * groups]
    x_refs = refs[slots * groups : slots * groups + slots]
    weight_refs = refs[slots * groups + slots : slots * groups + 2 * slots]
    bias_ref, gain_ref, shift_ref, post_ref, residual_ref = refs[-5:]
    blocks = pl.num_programs(0)
    at = (pl.program_id(0) + blocks // 2) % blocks
    residual = choose(at // per, x_refs).astype(F32) + row(bias_ref)
    for slot in range(slots):
        mixed = [ref[...] for ref in mixed_refs[slot * groups : (slot + 1) * groups]]
        residual = residual + dot(jnp.concatenate(mixed, axis=1), weight_refs[slot][...])
    normal, _ = norm_stats(residual)
    post_ref[...] = low(normal * row(gain_ref) + row(shift_ref))

    @pl.when(at < per)
    def _():
        residual_ref[...] = residual


def post_norm(mixed, x_parts, weights, bias, gain, shift):
    slots, groups = len(mixed), len(mixed[0])
    rows, width = x_parts[0].shape
    block = min(rows, 512)
    per = rows // block
    blocks = slots * per
    order = lambda i: (i + blocks // 2) % blocks
    specs = [
        pl.BlockSpec(
            (block, part.shape[1]),
            lambda i, slot=slot: (((order(i) // per) ^ slot) * per + order(i) % per, 0),
        )
        for slot in range(slots)
        for part in mixed[slot]
    ]
    return kernel_call(
        functools.partial(post_kernel, slots=slots, groups=groups, per=per),
        (blocks,),
        specs
        + slot_specs(slots, per, block, width, order)
        + [whole(a.shape) for a in (*weights, bias, gain, shift)],
        [
            pl.BlockSpec((block, width), lambda i: (order(i), 0)),
            pl.BlockSpec((block, width), lambda i: (jnp.clip(i - blocks // 2, 0, per - 1), 0)),
        ],
        [shape_of(slots * rows, width), shape_of(rows, width, F32)],
        [*[part for parts in mixed for part in parts], *x_parts, *weights, bias, gain, shift],
        (),
        name="post_norm",
    )


def feed_kernel(*refs, count, per, extras, held):
    post_ref, act_grad_ref, up_ref, bias_ref = refs[:4]
    extra_refs = refs[4 : 4 + extras]
    active_ref, grad_ref, sum_ref = refs[4 + extras + held : 7 + extras + held]
    back_refs = refs[7 + extras + held :]
    slot = pl.program_id(0) // per

    @pl.when(pl.program_id(0) == 0)
    def _():
        sum_ref[...] = jnp.zeros_like(sum_ref)

    post = post_ref[...]
    units = active_ref.shape[1]
    chunk = min(512, units)
    scale, cubic = math.sqrt(2 / math.pi), 0.044715
    for first in range(0, units, chunk):
        cols = slice(first, first + chunk)
        hidden = dot(post, up_ref[:, cols]) + row(bias_ref)[:, cols]
        square = hidden * hidden
        curve = jnp.tanh(hidden * (scale + scale * cubic * square))
        half = 0.5 + 0.5 * curve
        active_ref[:, cols] = low(hidden * half)
        slope = half + (0.5 * hidden) * (1.0 - curve * curve) * (
            scale + 3 * scale * cubic * square
        )
        grad = low(act_grad_ref[:, cols].astype(F32) * slope)
        grad_ref[:, cols] = grad
        sum_ref[:, cols] += jnp.sum(grad.astype(F32), axis=0, keepdims=True)
    back = dot(grad_ref[...], up_ref[...], NT)
    if extras:
        back = back + choose(slot, extra_refs).astype(F32)
    back = low(back)
    for at, back_ref in enumerate(back_refs):

        @pl.when(slot == at)
        def _():
            back_ref[...] = back


def feed(post_all, act_grad, up, up_bias, slots, chosen, extras, held):
    count = len(chosen)
    total, width = post_all.shape
    rows, units = total // slots, up.shape[1]
    block = min(rows, 512)
    per = rows // block
    tall = lambda cols: tall_spec(chosen, per, block, cols)
    active, grad, sums, *backs = kernel_call(
        functools.partial(
            feed_kernel, count=count, per=per, extras=len(extras), held=len(held)
        ),
        (count * per,),
        [tall(width), tall(units), whole(up.shape), whole(up_bias.shape)]
        + slot_specs(len(extras), per, block, width),
        [tall(units), tall(units), whole((1, units))] + slot_specs(count, per, block, width),
        [shape_of(total, units), shape_of(total, units), shape_of(1, units, F32)]
        + [shape_of(rows, width)] * count,
        [post_all, act_grad, up, up_bias, *extras],
        held,
        name="feed",
    )
    return (active, grad), sums, backs


def split_rows(total, me, keep_ref, send_ref, streams):
    rows = total.shape[0] // streams
    for slot in range(streams):
        part = low(total[pl.ds(pl.multiple_of((me ^ slot) * rows, rows), rows), :])
        ref = send_ref if slot % 2 else keep_ref
        ref[slot // 2 * rows : (slot // 2 + 1) * rows, :] = part


def outer_kernel(me_ref, left_ref, right_ref, keep_ref, send_ref, total, *, streams):
    step = pl.program_id(0)

    @pl.when(step == 0)
    def _():
        total[...] = dot(left_ref[...], right_ref[...], TN)

    @pl.when(step > 0)
    def _():
        total[...] += dot(left_ref[...], right_ref[...], TN)

    @pl.when(step == pl.num_programs(0) - 1)
    def _():
        split_rows(total, me_ref[0], keep_ref, send_ref, streams)


def outer_step(left, right, me, streams):
    total = left.shape[0]
    block = min(total, 1024)
    shape = (left.shape[1], right.shape[1])
    half = (shape[0] // 2, shape[1])
    return kernel_call(
        functools.partial(outer_kernel, streams=streams),
        (total // block,),
        [pl.BlockSpec(memory_space=pltpu.SMEM)]
        + [pl.BlockSpec((block, cols), lambda i: (i, 0)) for cols in shape],
        [whole(half)] * 2,
        [shape_of(*half)] * 2,
        [me, left, right],
        scratch_shapes=[pltpu.VMEM(shape, F32)],
        name="outer_step",
    )


def join_kernel(me_ref, *refs, early, streams):
    parts, (keep_ref, send_ref) = refs[:-2], refs[-2:]
    rows = parts[0].shape[0] // streams
    for slot in range(streams):
        home = pl.ds(pl.multiple_of((me_ref[0] ^ slot) * rows, rows), rows)
        out = send_ref if slot % 2 else keep_ref
        here = slice(slot // 2 * rows, (slot // 2 + 1) * rows)
        at = 0
        for part in parts[:early]:
            out[here, at : at + part.shape[1]] = part[home, :]
            at += part.shape[1]
        total = parts[early][home, :].astype(F32)
        for part in parts[early + 1 :]:
            total = total + part[home, :].astype(F32)
        out[here, at:] = low(total)


def join_step(early, terms, me, streams):
    inputs = [*early, *terms]
    cols = sum(part.shape[1] for part in early) + terms[0].shape[1]
    half = (terms[0].shape[0] // 2, cols)
    return kernel_call(
        functools.partial(join_kernel, early=len(early), streams=streams),
        (1,),
        [pl.BlockSpec(memory_space=pltpu.SMEM)] + [whole(a.shape) for a in inputs],
        [whole(half)] * 2,
        [shape_of(*half)] * 2,
        [me, *inputs],
        name="join_step",
    )


def late_kernel(*refs):
    (keep, come, keep_late, come_late), outs = refs[:4], refs[4:]
    rows, cols = outs[0].shape[0], keep.shape[1]
    for slot, out in enumerate(outs):
        here = slice(slot * rows, (slot + 1) * rows)
        out[:, :cols] = low(keep[here, :].astype(F32) + come[here, :].astype(F32))
        out[:, cols:] = low(keep_late[here, :].astype(F32) + come_late[here, :].astype(F32))


def late_step(pairs, slots):
    inputs = [array for pair in pairs for array in pair]
    shape = (inputs[0].shape[0] // slots, inputs[0].shape[1] + inputs[2].shape[1])
    return kernel_call(
        late_kernel,
        (1,),
        [whole(a.shape) for a in inputs],
        [whole(shape)] * slots,
        [shape_of(*shape)] * slots,
        inputs,
        name="late_step",
    )


def pair_kernel(*refs, count):
    parts, outs = refs[: 2 * count], refs[2 * count :]
    rows = outs[0].shape[0] // count
    for at in range(count):
        keep, come = parts[2 * at : 2 * at + 2]
        for slot, out in enumerate(outs):
            here = slice(slot * rows, (slot + 1) * rows)
            out[at * rows : (at + 1) * rows, :] = low(
                keep[here, :].astype(F32) + come[here, :].astype(F32)
            )


def pair_step(pairs, slots):
    inputs = [array for pair in pairs for array in pair]
    rows, cols = inputs[0].shape
    shape = (rows // slots * len(pairs), cols)
    return kernel_call(
        functools.partial(pair_kernel, count=len(pairs)),
        (1,),
        [whole(a.shape) for a in inputs],
        [whole(shape)] * slots,
        [shape_of(*shape)] * slots,
        inputs,
        name="pair_step",
    )


def stack_kernel(*refs):
    rows = refs[0].shape[0]
    for at, ref in enumerate(refs[:-1]):
        refs[-1][at * rows : (at + 1) * rows, :] = ref[...]


def stack_step(parts):
    rows, cols = parts[0].shape
    return kernel_call(
        stack_kernel,
        (1,),
        [whole((rows, cols))] * len(parts),
        [whole((rows * len(parts), cols))],
        [shape_of(rows * len(parts), cols)],
        list(parts),
        name="stack_step",
    )[0]


def shard_views(even_ref, odd_ref, streams):
    rows = even_ref.shape[0] // (streams // 2)
    return [
        (slot, ref.at[slot // 2 * rows : (slot // 2 + 1) * rows])
        for slot, ref in enumerate([even_ref, odd_ref] * (streams // 2))
    ]


def feed_grads_kernel(me_ref, even_ref, odd_ref, up_ref, down_ref, up_rows, *, streams):
    rows = even_ref.shape[0] // streams
    for slot, part in shard_views(even_ref, odd_ref, streams):
        home = pl.ds(pl.multiple_of((me_ref[0] ^ slot) * rows, rows), rows)
        up_rows[home, :] = part[:rows, :].astype(F32)
        down_ref[home, :] = part[rows:, :].astype(F32)
    up_ref[...] = up_rows[...].T


def feed_grads(even, odd, me, streams):
    units, width = even.shape
    return kernel_call(
        functools.partial(feed_grads_kernel, streams=streams),
        (1,),
        [pl.BlockSpec(memory_space=pltpu.SMEM)] + [whole(even.shape)] * 2,
        [whole((width, units)), whole((units, width))],
        [shape_of(width, units, F32), shape_of(units, width, F32)],
        [me, even, odd],
        scratch_shapes=[pltpu.VMEM((units, width), F32)],
        name="feed_grads",
    )


def pack_kernel(*refs, groups):
    sums_ref, gain_ref, shift_ref = refs[:3]
    row_refs, count_refs = refs[3 : 3 + groups], refs[3 + groups : 3 + 2 * groups]
    unit_refs, out_ref = refs[3 + 2 * groups : -1], refs[-1]
    out_ref[...] = jnp.zeros_like(out_ref)
    out_ref[:4, : sums_ref.shape[1]] = sums_ref[:4, :]
    rows = row_refs[0][...]
    for ref in row_refs[1:]:
        rows = rows + ref[...]
    out_ref[4:5, : rows.shape[1]] = (rows[0:1] - row(shift_ref) * rows[1:2]) / row(gain_ref)
    out_ref[5:6, : rows.shape[1]] = rows[1:2]
    units = unit_refs[0][...]
    for ref in unit_refs[1:]:
        units = units + ref[...]
    out_ref[8:9, : units.shape[1]] = units
    for at, ref in enumerate(count_refs):
        out_ref[9 + at : 10 + at, : ref.shape[1]] = ref[...]


def pack(row_sums, gain, shift, group_rows, group_counts, unit_sums):
    inputs = [row_sums, gain, shift, *group_rows, *group_counts, *unit_sums]
    wide = max(a.shape[1] for a in (row_sums, *group_counts, *unit_sums))
    return kernel_call(
        functools.partial(pack_kernel, groups=len(group_rows)),
        (1,),
        [whole(a.shape) for a in inputs],
        [whole((16, wide))],
        [shape_of(16, wide, F32)],
        inputs,
        name="pack",
    )[0]


def resid_kernel(*refs, terms, slots):
    term_refs = refs[:terms]
    residual_ref, cot_ref, gain_ref = refs[terms : terms + 3]
    weight_refs = refs[terms + 3 : terms + 3 + slots]
    grad_ref, low_ref, sums_ref = refs[terms + 3 + slots : terms + 6 + slots]
    part_refs = refs[terms + 6 + slots :]

    @pl.when(pl.program_id(0) == 0)
    def _():
        sums_ref[...] = jnp.zeros_like(sums_ref)

    post_grad = term_refs[0][...].astype(F32)
    for ref in term_refs[1:]:
        post_grad = post_grad + ref[...].astype(F32)
    cot = cot_ref[...].astype(F32)
    normal, inverse = norm_stats(residual_ref[...])
    grad = cot + norm_pull(post_grad * row(gain_ref), normal, inverse)
    grad_ref[...] = grad
    grad_low = low(grad)
    low_ref[...] = grad_low
    for weight_ref, part_ref in zip(weight_refs, part_refs):
        part_ref[...] = low(dot(grad_low, weight_ref[...], NT))
    for at, value in enumerate((cot, grad, post_grad * normal, post_grad)):
        sums_ref[at : at + 1, :] += jnp.sum(value, axis=0, keepdims=True)


def resid_step(terms, residual, cotangent, gain, weights):
    rows, width = residual.shape
    block = min(rows, 256)
    tall = lambda cols: pl.BlockSpec((block, cols), lambda i: (i, 0))
    cols = weights[0].shape[0]
    return kernel_call(
        functools.partial(resid_kernel, terms=len(terms), slots=len(weights)),
        (rows // block,),
        [tall(width)] * (len(terms) + 2) + [whole(a.shape) for a in (gain, *weights)],
        [tall(width), tall(width), whole((8, width))] + [tall(cols)] * len(weights),
        [shape_of(rows, width, F32), shape_of(rows, width), shape_of(8, width, F32)]
        + [shape_of(rows, cols)] * len(weights),
        [*terms, residual, cotangent, gain, *weights],
        (),
        name="resid_step",
    )


def dense_grad_kernel(*refs, slots, groups):
    mixed_refs, grad_ref = refs[: slots * groups], refs[slots * groups]
    even_ref, odd_ref, *sum_refs = refs[slots * groups + 1 :]
    step = pl.program_id(0)
    grad = grad_ref[...]
    for slot in range(slots):
        mixed = [ref[...] for ref in mixed_refs[slot * groups : (slot + 1) * groups]]
        part = dot(grad, jnp.concatenate(mixed, axis=1), TN)
        sum_refs[slot][...] = jnp.where(step == 0, 0.0, sum_refs[slot][...]) + part

    @pl.when(step == pl.num_programs(0) - 1)
    def _():
        rows = sum_refs[0].shape[0]
        for slot, sum_ref in enumerate(sum_refs):
            out_ref = odd_ref if slot % 2 else even_ref
            out_ref[slot // 2 * rows : (slot // 2 + 1) * rows, :] = low(sum_ref[...])


def dense_grad(mixed, grad):
    slots, groups = len(mixed), len(mixed[0])
    rows, width = grad.shape
    block = min(rows, 512)
    per = rows // block
    cols = sum(part.shape[1] for part in mixed[0])
    return kernel_call(
        functools.partial(dense_grad_kernel, slots=slots, groups=groups),
        (per,),
        [
            pl.BlockSpec((block, part.shape[1]), lambda i, slot=slot: (slot * per + i, 0))
            for slot in range(slots)
            for part in mixed[slot]
        ]
        + [pl.BlockSpec((block, width), lambda i: (i, 0))],
        [whole((width * slots // 2, cols))] * 2,
        [shape_of(width * slots // 2, cols)] * 2,
        [*[part for parts in mixed for part in parts], grad],
        (),
        scratch_shapes=[pltpu.VMEM((width, cols), F32)] * slots,
        name="dense_grad",
    )


def weight_kernel(me_ref, normed_ref, grad_ref, wq_ref, wk_ref, wv_ref, *refs, streams):
    *out_refs, sums_ref, count_ref, total, count = refs
    step = pl.program_id(0)

    @pl.when(step == 0)
    def _():
        total[...] = jnp.zeros_like(total)
        count[...] = jnp.zeros_like(count)

    grad = grad_ref[...]
    total[...] += dot(normed_ref[...], grad, TN)
    count[...] += jnp.sum(grad.astype(F32), axis=0, keepdims=True)

    @pl.when(step == pl.num_programs(0) - 1)
    def _():
        weight = jnp.concatenate([wq_ref[...], wk_ref[...], wv_ref[...]], axis=1).astype(F32)
        if streams:
            split_rows(total, me_ref[0], *out_refs, streams)
        else:
            out_refs[0][...] = low(total[...])
        count_ref[...] = count[...]
        lane = lanes(weight.shape[0])
        cross = jnp.sum(weight * total[...], axis=1, keepdims=True)
        plain = jnp.sum(weight * count[...], axis=1, keepdims=True)
        both = jnp.where(lane == 0, cross, jnp.where(lane == 1, plain, 0.0))
        sums_ref[...] = both.T[:8]


def weight_step(normed, grad, weights, group, me, streams):
    total, width = normed.shape
    cols = grad.shape[1]
    block = min(total, 1024)
    outs = [(width // 2, cols)] * 2 if streams else [(width, cols)]
    *parts, sums, count = kernel_call(
        functools.partial(weight_kernel, streams=streams),
        (total // block,),
        [pl.BlockSpec(memory_space=pltpu.SMEM)]
        + [pl.BlockSpec((block, count), lambda i: (i, 0)) for count in (width, cols)]
        + [pl.BlockSpec((width, cols // 3), lambda i: (0, group))] * 3,
        [whole(shape) for shape in outs] + [whole((8, width)), whole((1, cols))],
        [shape_of(*shape) for shape in outs] + [shape_of(8, width, F32), shape_of(1, cols, F32)],
        [me, normed, grad, *weights],
        scratch_shapes=[pltpu.VMEM((width, cols), F32), pltpu.VMEM((1, cols), F32)],
        name="weight_step",
    )
    return parts, sums, count


def unproject_kernel(*refs, groups, per, extras):
    grad_refs, weight_refs = refs[:groups], refs[groups : 4 * groups]
    extra_refs = refs[4 * groups : 4 * groups + extras]
    out_refs = refs[4 * groups + extras : -1]
    joined = refs[-1]
    slot = pl.program_id(0) // per

    @pl.when(pl.program_id(0) == 0)
    def _():
        joined[...] = jnp.concatenate([ref[...] for ref in weight_refs], axis=1)

    total = dot(jnp.concatenate([ref[...] for ref in grad_refs], axis=1), joined[...], NT)
    if extras:
        total = total + choose(slot, extra_refs).astype(F32)
    total = low(total)
    for at, ref in enumerate(out_refs):

        @pl.when(slot == at)
        def _():
            ref[...] = total


def unproject(grads, weights, slots, chosen, extras):
    width = weights[0].shape[0]
    count, groups = len(chosen), len(grads)
    total, cols = grads[0].shape
    rows = total // slots
    block = min(rows, 512)
    per = rows // block
    return kernel_call(
        functools.partial(unproject_kernel, groups=groups, per=per, extras=len(extras)),
        (count * per,),
        [tall_spec(chosen, per, block, cols)] * groups
        + [
            pl.BlockSpec((width, cols // 3), lambda i, group=group: (0, group))
            for group in range(groups)
            for _ in weights
        ]
        + slot_specs(len(extras), per, block, width),
        slot_specs(count, per, block, width),
        [shape_of(rows, width)] * count,
        [*grads, *[weight for _ in grads for weight in weights], *extras],
        (),
        scratch_shapes=[pltpu.VMEM((width, cols * groups), BF16)],
        name="unproject",
    )


def ffn_kernel(active_ref, weight_ref, even_ref, odd_ref, *, per):
    total = low(dot(active_ref[...], weight_ref[...]))
    odd = pl.program_id(0) // per % 2

    @pl.when(odd == 0)
    def _():
        even_ref[...] = total

    @pl.when(odd == 1)
    def _():
        odd_ref[...] = total


def ffn_step(active, weight, slots):
    total, units = active.shape
    width = weight.shape[1]
    rows = total // slots
    block = min(rows, 1024)
    per = rows // block
    half = (total // 2, width)

    def half_spec(odd):
        def place(i):
            slot, step = i // per, i % per
            now = slot // 2 * per
            if odd:
                return (jnp.where(slot % 2 == 1, now + step, jnp.maximum(now - 1, 0)), 0)
            return (jnp.where(slot % 2 == 0, now + step, now + per - 1), 0)

        return pl.BlockSpec((block, width), place)

    return kernel_call(
        functools.partial(ffn_kernel, per=per),
        (slots * per,),
        [pl.BlockSpec((block, units), lambda i: (i, 0)), whole(weight.shape)],
        [half_spec(0), half_spec(1)],
        [shape_of(*half)] * 2,
        [active, weight],
        name="ffn_step",
    )


def spread_kernel(me_ref, even_ref, odd_ref, *refs, groups, streams):
    *out_refs, dense_ref, dense_rows = refs
    cols = out_refs[0].shape[1] // groups
    heads = dense_ref.shape[0]
    rows = even_ref.shape[0] * 2 // streams
    for slot, part in shard_views(even_ref, odd_ref, streams):
        home = pl.ds(pl.multiple_of((me_ref[0] ^ slot) * rows, rows), rows)
        for group in range(groups):
            first = group * 3 * cols + (heads if group == groups - 1 else 0)
            for kind in range(3):
                at = first + kind * cols
                out_refs[kind][home, group * cols : (group + 1) * cols] = part[
                    :, at : at + cols
                ].astype(F32)
        first = (groups - 1) * 3 * cols
        dense_rows[home, :] = part[:, first : first + heads].astype(F32)
    dense_ref[...] = dense_rows[...].T


def spread(even, odd, me, streams, groups, heads):
    width = even.shape[0] * 2
    shapes = [(width, heads)] * 3 + [(heads, width)]
    return kernel_call(
        functools.partial(spread_kernel, groups=groups, streams=streams),
        (1,),
        [pl.BlockSpec(memory_space=pltpu.SMEM)] + [whole(even.shape)] * 2,
        [whole(shape) for shape in shapes],
        [shape_of(*shape, F32) for shape in shapes],
        [me, even, odd],
        scratch_shapes=[pltpu.VMEM((width, heads), F32)],
        name="spread",
    )


def input_kernel(*refs, terms):
    x_ref, resid_ref, gain_ref, out_ref = refs[terms:]
    grad = refs[0][...].astype(F32)
    for ref in refs[1:terms]:
        grad = grad + ref[...].astype(F32)
    normal, inverse = norm_stats(x_ref[...].astype(F32))
    out_ref[...] = resid_ref[...] + norm_pull(grad * row(gain_ref), normal, inverse)


def input_step(terms, layer_input, resid_grad, gain):
    rows, width = resid_grad.shape
    block = min(rows, 256)
    tall = pl.BlockSpec((block, width), lambda i: (i, 0))
    return kernel_call(
        functools.partial(input_kernel, terms=len(terms)),
        (rows // block,),
        [tall] * (len(terms) + 2) + [whole(gain.shape)],
        [tall],
        [shape_of(rows, width, F32)],
        [*terms, layer_input, resid_grad, gain],
        name="input_step",
    )[0]


def shards(
    slots,
    streams,
    layer_input,
    row_ids,
    input_gain,
    input_shift,
    query_weight,
    query_bias,
    key_weight,
    value_weight,
    value_bias,
    dense_weight,
    dense_bias,
    post_gain,
    post_shift,
    up_weight,
    up_bias,
    down_weight,
    down_bias,
    cotangent,
):
    me = lax.axis_index("tensor")
    me_word = me.astype(jnp.int32)[None]
    stream = lax.axis_index("dp").astype(jnp.int32)[None]
    rows = layer_input.shape[0]
    head_cols = query_weight.shape[1]
    head_count = head_cols // HD
    groups = max(1, head_count // 2)
    bits = [1 << level for level in range(slots.bit_length() - 1)]
    half = slots // 2
    after = lambda array, *others: lax.optimization_barrier((array, *others))[0]

    def swap(array, mask):
        return lax.ppermute(array, "tensor", [(i, i ^ mask) for i in range(slots)])

    def gather(array):
        held = {0: array}
        for bit in reversed(bits):
            held.update({slot ^ bit: swap(part, bit) for slot, part in held.items()})
        return [held[slot] for slot in range(slots)]

    def blocks(array):
        return [array[slot * rows : (slot + 1) * rows] for slot in range(slots)]

    def swap_data(array, mask):
        return lax.ppermute(array, "dp", [(i, i ^ mask) for i in range(streams)])

    def finish_terms(held, terms, levels):
        for bit in levels:
            come = {slot ^ bit: swap(part, bit) for slot, part in held.items() if slot & bit}
            if 0 in come:
                terms.append(come.pop(0))
            held = {
                slot: low(held[slot].astype(F32) + part.astype(F32)) for slot, part in come.items()
            }
        return terms

    def scatter_terms(parts):
        return finish_terms(dict(enumerate(parts)), [parts[0]], bits)

    far_odd = range(half + 1, slots, 2)
    far_even = range(half, slots, 2)
    near_odd = range(1, half, 2)
    near_even = range(0, half, 2)

    def ordered_terms(make):
        far = make(far_odd, (), None)
        far_come = [swap(part, 1) for part in far]
        near = make(near_odd, (), far[-1])
        near_come = [swap(part, 1) for part in near]
        far = make(far_even, far_come, near[-1])
        near = make(near_even, near_come, far[-1])
        held = dict(zip((*far_even, *near_even), (*far, *near)))
        return finish_terms(held, [held.pop(0)], bits[1:])

    def add_up(terms):
        return functools.reduce(
            lambda sum_now, term: sum_now + term.astype(F32), terms[1:], terms[0].astype(F32)
        )

    far_streams = range(2, streams, 2)

    def exchange(parts):
        return low(add_up([parts[0], *[swap_data(parts[k // 2], k) for k in far_streams]]))

    def collect_far(shard):
        return [shard, *[swap_data(shard, k) for k in far_streams]]

    norm_vectors = (input_gain, input_shift)
    weights = (query_weight, key_weight, value_weight)
    biases = (query_bias, value_bias)
    x_held = {0: layer_input}
    for bit in reversed(bits[1:]):
        x_held.update({slot ^ bit: swap(part, bit) for slot, part in x_held.items()})
    x_held[1] = swap(x_held[0], 1)
    near_parts = [x_held[0], x_held[1]]
    first = range(2)
    held = project(near_parts, first, slots, norm_vectors, weights, biases, ())
    heads = me * head_count + jnp.arange(head_count)
    slopes = jnp.exp2(-8.0 * (heads + 1).astype(F32) / HEADS) * LOG2E
    apart = (row_ids[:1] != row_ids[SHORT : SHORT + 1]).astype(jnp.int32)
    own_states = [()] * groups
    if slots > 2 and 2 * rows % 1024 == 0:
        own_states = [
            (attend_own(me_word, apart, slopes, *held[1:], rows, group),) for group in range(groups)
        ]
    rest = sorted(slot for slot in x_held if slot > 1)
    moved = lax.optimization_barrier(
        (*[x_held[slot] for slot in rest], *held, *[state for own in own_states for state in own])
    )
    arrived, held = moved[: len(rest)], moved[len(rest) : len(rest) + 4]
    if own_states[0]:
        own_states = [(state,) for state in moved[len(rest) + 4 :]]
    for slot, part in zip(rest, arrived):
        x_held[slot], x_held[slot ^ 1] = part, swap(part, 1)
    x_parts = [x_held[slot] for slot in range(slots)]
    dense_parts = gather(after(dense_weight, arrived[-1]))
    cot_own = after(cotangent, arrived[-1])
    cot_held = {0: cot_own}
    for bit in reversed(bits[1:]):
        cot_held.update({slot ^ bit: swap(part, bit) for slot, part in cot_held.items()})
    normed, queries, key_rows, values = project(
        x_parts[2:], range(2, slots), slots, norm_vectors, weights, biases, held
    )

    mixed_own, log_totals, mixed_parts = [], [], []
    for group in range(groups):
        mixed, log_total = attend(
            me_word,
            apart,
            slopes,
            queries if not group else after(queries, cot_held[half], mixed_own[-1]),
            key_rows,
            values,
            slots,
            group,
            own_states[group],
        )
        mixed_own.append(mixed)
        log_totals.append(log_total)
        if not group:
            keys = sorted(cot_held)
            held = lax.optimization_barrier((*[cot_held[key] for key in keys], mixed))[:-1]
            cot_held.update(zip(keys, held))
            cot_held.update({slot ^ 1: swap(part, 1) for slot, part in cot_held.items()})
            cot_parts = [cot_held[slot] for slot in range(slots)]
        if group < groups - 1:
            mixed_parts.append(gather(mixed))
    act_grad, cot_all = act_grad_step(
        lax.optimization_barrier((*cot_parts, mixed_own[-1], *dense_parts[2:]))[:slots], down_weight
    )
    came = {0: mixed_own[-1]}
    for bit in reversed(bits[1:]):
        came.update({slot ^ bit: swap(part, bit) for slot, part in came.items()})
    far_slots = sorted(came)[1:]
    *arrived, act_grad = lax.optimization_barrier((*[came[slot] for slot in far_slots], act_grad))
    came.update(zip(far_slots, arrived))
    came.update({slot ^ 1: swap(part, 1) for slot, part in came.items()})
    mixed_parts.append([came[slot] for slot in range(slots)])
    mixed_all = [[mixed_parts[group][slot] for group in range(groups)] for slot in range(slots)]
    post_all, residual = post_norm(
        mixed_all, x_parts, dense_parts, dense_bias, post_gain, post_shift
    )

    fed, up_bias_parts = [()], []

    def make_feed(chosen, extras, gate):
        held, sums, backs = feed(
            post_all, act_grad, up_weight, up_bias, slots, chosen, extras, fed[-1]
        )
        fed.append(held)
        up_bias_parts.append(sums)
        return backs

    post_terms = ordered_terms(make_feed)
    active, hidden_grad = fed[-1]
    up_keep, up_send = outer_step(hidden_grad, post_all, stream, streams)
    down_keep, down_send = outer_step(active, after(cot_all, up_keep), stream, streams)
    up_come, down_come = swap_data(up_send, 1), swap_data(down_send, 1)
    resid_grad, attended_grad, row_sums, *mixed_grads = resid_step(
        [after(post_terms[0], down_keep), *post_terms[1:]],
        residual,
        cotangent,
        post_gain,
        dense_parts,
    )
    mixed_grads = [swap(part, slot) if slot else part for slot, part in enumerate(mixed_grads)]
    dense_even, dense_odd = dense_grad(mixed_all, attended_grad)
    ffn_even, ffn_odd = ffn_step(after(active, dense_odd), down_weight, slots)
    feed_parts = pair_step(
        [(after(up_keep, ffn_odd), up_come), (down_keep, down_come)], streams // 2
    )
    moved = lax.optimization_barrier((*mixed_grads, dense_odd, ffn_odd, *feed_parts))
    mixed_grads, (dense_odd, ffn_odd), feed_parts = (
        moved[:slots],
        moved[slots : slots + 2],
        moved[slots + 2 :],
    )
    dense_come, ffn_come = swap(dense_odd, 1), swap(ffn_odd, 1)

    def partner_sums(even, come):
        size = even.shape[0] * 2 // slots
        cuts = [slice(at * size, (at + 1) * size) for at in range(slots // 2)]
        return [low(even[cut].astype(F32) + come[cut].astype(F32)) for cut in cuts]

    cols = head_cols // groups
    head_grads, early_parts, group_rows, group_counts = [], [], [], []

    def backward(group):
        return attend_back(
            me_word,
            apart,
            slopes,
            queries,
            key_rows,
            values,
            mixed_own[group],
            log_totals[group],
            mixed_grads,
            group,
        )

    dense_sums = partner_sums(dense_even, dense_come)
    for group in range(groups - 1):
        head_grads.append(backward(group))
        grad = head_grads[-1]
        if group == groups - 2:
            grad, *dense_sums = lax.optimization_barrier((grad, *dense_sums))
        parts, row_part, count_part = weight_step(normed, grad, weights, group, stream, 0)
        early_parts += parts
        group_rows.append(row_part)
        group_counts.append(count_part)
        mixed_grads = lax.optimization_barrier((*mixed_grads, parts[-1]))[:-1]
    even_slots = range(2, slots, 2)
    dense_terms = finish_terms(dict(zip(even_slots, dense_sums[1:])), [dense_sums[0]], bits[1:])
    early_keep, early_send = join_step(early_parts, dense_terms, stream, streams)
    moved = lax.optimization_barrier(
        (*mixed_grads, early_send, exchange(feed_parts), *partner_sums(ffn_even, ffn_come))
    )
    mixed_grads, (early_send, feed_shard), ffn_sums = (
        moved[:slots],
        moved[slots : slots + 2],
        moved[slots + 2 :],
    )
    early_come = swap_data(early_send, 1)
    feed_shards = collect_far(feed_shard)
    ffn_terms = finish_terms(dict(zip(even_slots, ffn_sums[1:])), [ffn_sums[0]], bits[1:])
    head_grads.append(backward(groups - 1))
    grad, early_come, *arrived = lax.optimization_barrier(
        (head_grads[-1], early_come, *feed_shards, *ffn_terms)
    )
    feed_shards, ffn_terms = arrived[: len(feed_shards)], arrived[len(feed_shards) :]
    (late_keep, late_send), row_part, count_part = weight_step(
        normed, grad, weights, groups - 1, stream, streams
    )
    group_rows.append(row_part)
    group_counts.append(count_part)
    late_come = swap_data(late_send, 1)
    vectors = pack(row_sums, input_gain, input_shift, group_rows, group_counts, up_bias_parts)
    feed_even = stack_step([*feed_shards[:-1], after(feed_shards[-1], vectors)])
    summed = vectors + swap_data(vectors, 1)
    feed_odd = swap_data(after(feed_even, late_come, summed), 1)
    seen = []

    def make_unproject(chosen, extras, gate):
        gates = [feed_even if gate is None else gate]
        if not seen:
            gates += [late_come, summed]
        seen.append(0)
        return unproject(
            [*head_grads[:-1], after(head_grads[-1], *gates)], weights, slots, chosen, extras
        )

    normed_terms = ordered_terms(make_unproject)
    late_parts = late_step(
        [(early_keep, early_come), (after(late_keep, normed_terms[0]), late_come)], streams // 2
    )
    layer_output = low(residual + add_up(ffn_terms) + down_bias.astype(F32))
    up_grad, down_grad = feed_grads(feed_even, feed_odd, stream, streams)
    input_grad = input_step(
        [*normed_terms[:-1], after(normed_terms[-1], up_grad)],
        layer_input,
        resid_grad,
        input_gain,
    )
    *late_shards, layer_output, input_grad = lax.optimization_barrier(
        (*collect_far(exchange(late_parts)), layer_output, input_grad)
    )
    late_even = stack_step(late_shards)
    late_odd = swap_data(late_even, 1)
    for level in range(1, streams.bit_length() - 1):
        summed = summed + swap_data(summed, 1 << level)
    own = summed[8:]
    shared = after(summed, normed_terms[-1])[:8]
    for bit in reversed(bits):
        shared = shared + swap(shared, bit)
    shared = shared[:, : resid_grad.shape[1]]
    up_bias_grad = own[0, : up_bias.shape[0]]
    counts = own[1 : 1 + groups]
    query_bias_grad = counts[:, :cols].reshape(-1)
    value_bias_grad = counts[:, 2 * cols : 3 * cols].reshape(-1)
    *weight_grads, dense_weight_grad = spread(
        late_even, late_odd, stream, streams, groups, head_cols
    )
    return (
        layer_output,
        input_grad,
        shared[4],
        shared[5],
        weight_grads[0],
        query_bias_grad,
        weight_grads[1],
        weight_grads[2],
        value_bias_grad,
        dense_weight_grad,
        shared[1],
        shared[2],
        shared[3],
        up_grad,
        up_bias_grad,
        down_grad,
        shared[0],
    )


def solution(mesh):
    in_specs = (
        P(("dp", "tensor"), None),
        P("dp"),
        P(),
        P(),
        P(None, "tensor"),
        P("tensor"),
        P(None, "tensor"),
        P(None, "tensor"),
        P("tensor"),
        P("tensor", None),
        P(),
        P(),
        P(),
        P(None, "tensor"),
        P("tensor"),
        P("tensor", None),
        P(),
        P(("dp", "tensor"), None),
    )
    out_specs = (
        P(("dp", "tensor"), None),
        P(("dp", "tensor"), None),
        P(),
        P(),
        P(None, "tensor"),
        P("tensor"),
        P(None, "tensor"),
        P(None, "tensor"),
        P("tensor"),
        P("tensor", None),
        P(),
        P(),
        P(),
        P(None, "tensor"),
        P("tensor"),
        P("tensor", None),
        P(),
    )
    return jax.shard_map(
        functools.partial(shards, mesh.shape["tensor"], mesh.shape["dp"]), mesh=mesh, in_specs=in_specs, out_specs=out_specs, check_vma=False)
```

```python
import functools
import math

import jax
import jax.numpy as jnp
from jax import lax
from jax.experimental import pallas as pl
from jax.experimental.pallas import tpu as pltpu
from jax.sharding import PartitionSpec as P

HEADS = 16
HD = 64
SHORT = 2048
EPSILON = 1e-05
LOG2E = math.log2(math.e)
F32 = jnp.float32
BF16 = jnp.bfloat16
SMALL_COST = pl.CostEstimate(flops=1, transcendentals=0, bytes_accessed=1)
NT = (((1,), (1,)), ((), ()))
NN = (((1,), (0,)), ((), ()))
TN = (((0,), (0,)), ((), ()))


def dot(lhs, rhs, dims=NN):
    return lax.dot_general(lhs, rhs, dims, preferred_element_type=F32)


def low(array):
    return array.astype(BF16)


def norm_stats(rows):
    center = jnp.mean(rows, axis=-1, keepdims=True)
    centered = rows - center
    inverse = lax.rsqrt(jnp.mean(centered * centered, axis=-1, keepdims=True) + EPSILON)
    return centered * inverse, inverse


def norm_pull(grad, normal, inverse):
    grad_mean = jnp.mean(grad, axis=-1, keepdims=True)
    dot_mean = jnp.mean(grad * normal, axis=-1, keepdims=True)
    return inverse * (grad - grad_mean - normal * dot_mean)


def lanes(count):
    return lax.broadcasted_iota(jnp.int32, (count, 128), 1)


def places(count, first):
    return lax.broadcasted_iota(jnp.int32, (count, 128), 0) + first


def widen(head):
    return jnp.concatenate([head.astype(F32), jnp.zeros((head.shape[0], HD), F32)], axis=1)


def split3(value):
    high = low(value).astype(F32)
    middle = low(value - high).astype(F32)
    return high, middle, value - high - middle


def pick3(index, parts):
    return jnp.where(index == 0, parts[0], jnp.where(index == 1, parts[1], parts[2]))


def key_columns(head, first):
    count = head.shape[0]
    lane, place = lanes(count), places(count, first)
    coarse = ((place >> 6) << 6).astype(F32)
    fine = (place & 63).astype(F32)
    wall = jnp.where(place < SHORT, -1e30, 0.0)
    extra = jnp.where(lane < 73, -1.0, jnp.where(lane == 73, wall, 0.0))
    extra = jnp.where(lane < 67, coarse, jnp.where(lane < 70, fine, extra))
    return low(jnp.where(lane < HD, widen(head), extra))


def query_columns(head, first, slope, apart):
    count = head.shape[0]
    lane, place = lanes(count), places(count, first)
    extra = pick3(jnp.where(lane < 67, lane - 64, lane - 67), split3(slope))
    extra = jnp.where(lane < 70, extra, 0.0)
    extra = jnp.where(lane == 73, jnp.where(place >= SHORT, apart, 0.0), extra)
    return low(jnp.where(lane < HD, widen(head), extra))


def ones_columns(head, count):
    lane = lanes(head.shape[0])
    return low(jnp.where(lane < HD, widen(head), jnp.where(lane < HD + count, 1.0, 0.0)))


def grad_columns(head, shift):
    lane = lanes(head.shape[0])
    extra = jnp.where(lane < 67, pick3(lane - 64, split3(shift)), 0.0)
    return low(jnp.where(lane < HD, widen(head), extra))


def each_chunk(me, slots, rows, body):
    chunk = min(rows, 512)
    for slot in range(slots):
        home = (me ^ slot) * rows

        @pl.loop(0, rows // chunk)
        def _(step):
            offset = pl.multiple_of(step * chunk, chunk)
            body(slot, pl.ds(offset, chunk), pl.ds(slot * rows + offset, chunk), home + offset)


def attend_kernel(
    me_ref, apart_ref, slope_ref, q_ref, k_ref, v_ref, o_ref, qa, ka, va, *, slots, pair, tile
):
    me = me_ref[0]
    total = q_ref.shape[0]
    rows = total // slots
    chunk = min(rows, 512)
    apart = apart_ref[0].astype(F32)

    def prepare(slot, inner, spot, place):
        place = pl.multiple_of(place, chunk)
        home = pl.ds(place, chunk)
        for s in range(pair):
            cols = slice(s * HD, (s + 1) * HD)
            qa[s, home, :] = query_columns(q_ref[spot, cols], place, slope_ref[s], apart)
            ka[s, home, :] = key_columns(k_ref[spot, cols], place)
            va[s, home, :] = ones_columns(v_ref[spot, cols], 1)

    each_chunk(me, slots, rows, prepare)
    causal = lax.broadcasted_iota(jnp.int32, (tile, tile), 1) <= lax.broadcasted_iota(
        jnp.int32, (tile, tile), 0
    )
    piece = min(rows, tile)
    lane = lanes(tile)

    def query_tile(index, _):
        first = pl.multiple_of(index * tile, tile)
        queries = [qa[s, pl.ds(first, tile), :] for s in range(pair)]

        def step(at, carry, diagonal):
            after = []
            for s in range(pair):
                top, mix = carry[s]
                scores = dot(queries[s], ka[s, pl.ds(at, tile), :], NT)
                if diagonal:
                    scores = jnp.where(causal, scores, -1e30)
                higher = jnp.maximum(top, jnp.max(scores, axis=1, keepdims=True))
                weights = low(jnp.exp2(scores - higher))
                mix = mix * jnp.exp2(top - higher) + dot(weights, va[s, pl.ds(at, tile), :])
                after.append((higher, mix))
            return tuple(after)

        carry = tuple(
            (jnp.full((tile, 1), -1e38, F32), jnp.zeros((tile, 128), F32)) for _ in range(pair)
        )
        carry = step(first, carry, True)
        carry = lax.fori_loop(
            0, index, lambda at, held: step(pl.multiple_of(at * tile, tile), held, False), carry
        )
        outs = []
        for s in range(pair):
            top, mix = carry[s]
            weight = mix[:, HD : HD + 1]
            outs.append(mix[:, :HD] * (1.0 / weight))
            log_total = pick3(lane - 70, split3(top + jnp.log2(weight)))
            qa[s, pl.ds(first, tile), :] = low(
                jnp.where((lane >= 70) & (lane < 73), log_total, queries[s].astype(F32))
            )
        out = low(jnp.concatenate(outs, axis=1))
        for part in range(tile // piece):
            block = (index * (tile // piece) + part) // (rows // piece)
            offset = first + part * piece - block * rows
            spot = pl.multiple_of((block ^ me) * rows + offset, piece)
            o_ref[pl.ds(spot, piece), :] = out[part * piece : (part + 1) * piece]
        return 0

    lax.fori_loop(0, total // tile, query_tile, 0)


def attend(me, apart, slopes, queries, key_rows, values, slots, group, tile=1024):
    total, width = queries.shape
    pair = min(2, width // HD)
    cols = pair * HD
    spec = pl.BlockSpec((total, cols), lambda g: (0, group))
    scalars = pl.BlockSpec(memory_space=pltpu.SMEM)
    return pl.pallas_call(
        functools.partial(attend_kernel, slots=slots, pair=pair, tile=tile),
        grid=(1,),
        in_specs=[scalars] * 3 + [spec] * 3,
        out_specs=[
            pl.BlockSpec((total, cols), lambda g: (0, 0)),
            pl.BlockSpec((pair, total, 128), lambda g: (0, 0, 0)),
            pl.BlockSpec((pair, total, 128), lambda g: (0, 0, 0)),
        ],
        out_shape=[
            jax.ShapeDtypeStruct((total, cols), BF16),
            jax.ShapeDtypeStruct((pair, total, 128), BF16),
            jax.ShapeDtypeStruct((pair, total, 128), BF16),
        ],
        scratch_shapes=[pltpu.VMEM((pair, total, 128), BF16)],
        compiler_params=pltpu.CompilerParams(vmem_limit_bytes=56 << 20),
        cost_estimate=pl.CostEstimate(
            flops=pair * 1200 * total * total, transcendentals=0, bytes_accessed=8 * total * cols
        ),
        name="attend",
    )(me, apart, slopes[group * pair : (group + 1) * pair], queries, key_rows, values)


def attend_back_kernel(*refs, slots, pair, tile, key_tile):
    me_ref, qa, ka, v_ref, o_ref = refs[:5]
    g_refs = refs[5 : 5 + slots]
    out_ref, va, ga, kt, dq_sum = refs[5 + slots :]
    cols = pair * HD
    me = me_ref[0]
    total = v_ref.shape[0]
    rows = total // slots
    chunk = min(rows, 512)

    def prepare(slot, inner, spot, place):
        place = pl.multiple_of(place, chunk)
        home = pl.ds(place, chunk)
        for s in range(pair):
            mine = slice(s * HD, (s + 1) * HD)
            kt[s, :, home] = low(ka[s, home, :].astype(F32).T)
            va[s, home, :] = ones_columns(v_ref[spot, mine], 3)
            grad = g_refs[slot][inner, mine]
            row_dot = jnp.sum(
                grad.astype(F32) * o_ref[spot, mine].astype(F32), axis=1, keepdims=True
            )
            ga[s, home, :] = grad_columns(grad, -row_dot)
            dq_sum[s, :, home] = jnp.zeros((128, chunk), F32)

    each_chunk(me, slots, rows, prepare)
    causal = lax.broadcasted_iota(jnp.int32, (key_tile, key_tile), 0) <= lax.broadcasted_iota(
        jnp.int32, (key_tile, key_tile), 1
    )
    piece = min(rows, key_tile)

    def place_of(place, size):
        block = place // rows
        return pl.multiple_of((block ^ me) * rows + (place - block * rows), size)

    def keys_tile(index, _):
        first = pl.multiple_of(index * key_tile, key_tile)
        here = pl.ds(first, key_tile)

        def step(at, carry, diagonal, width):
            after = []
            for s in range(pair):
                dk, dv = carry[s]
                there = pl.ds(at, width)
                queries, grads = qa[s, there, :], ga[s, there, :]
                probs = jnp.exp2(dot(ka[s, here, :], queries, NT))
                if diagonal:
                    probs = jnp.where(causal, probs, 0.0)
                dv = dv + dot(low(probs), grads)
                score_grad = low(probs * dot(va[s, here, :], grads, NT))
                dk = dk + dot(score_grad, queries)
                dq_sum[s, :, there] += dot(kt[s, :, here], score_grad)
                after.append((dk, dv))
            return tuple(after)

        zeros = jnp.zeros((key_tile, 128), F32)
        carry = step(first, tuple((zeros, zeros) for _ in range(pair)), True, key_tile)
        start = first + key_tile
        short = jnp.minimum((-start) % tile, total - start) // key_tile
        if tile > key_tile:
            carry = lax.fori_loop(
                0,
                short,
                lambda at, held: step(
                    pl.multiple_of(start + at * key_tile, key_tile), held, False, key_tile
                ),
                carry,
            )
            start = start + short * key_tile
        carry = lax.fori_loop(
            0,
            (total - start) // tile,
            lambda at, held: step(
                pl.multiple_of(start + at * tile, min(tile, key_tile)), held, False, tile
            ),
            carry,
        )
        dk = low(jnp.concatenate([held[0][:, :HD] * (1.0 / LOG2E) for held in carry], axis=1))
        dv = low(jnp.concatenate([held[1][:, :HD] for held in carry], axis=1))
        for part in range(key_tile // piece):
            spot = pl.ds(place_of(first + part * piece, piece), piece)
            out_ref[spot, cols : 2 * cols] = dk[part * piece : (part + 1) * piece]
            out_ref[spot, 2 * cols :] = dv[part * piece : (part + 1) * piece]
        return 0

    lax.fori_loop(0, total // key_tile, keys_tile, 0)

    def finish(slot, inner, spot, place):
        home = pl.ds(pl.multiple_of(place, chunk), chunk)
        joined = jnp.concatenate([dq_sum[s, :HD, home] for s in range(pair)], axis=0)
        out_ref[spot, :cols] = low(joined.T * HD**-0.5)

    each_chunk(me, slots, rows, finish)


def attend_back(me, columns, values, mixed, grads, group, tile=1024, key_tile=512):
    slots = len(grads)
    total, width = values.shape
    pair = columns[0].shape[0]
    cols = pair * HD
    out_spec = pl.BlockSpec((total, cols), lambda g: (0, 0))
    column_spec = pl.BlockSpec((pair, total, 128), lambda g: (0, 0, 0))
    return pl.pallas_call(
        functools.partial(
            attend_back_kernel, slots=slots, pair=pair, tile=tile, key_tile=key_tile
        ),
        grid=(1,),
        in_specs=[pl.BlockSpec(memory_space=pltpu.SMEM), column_spec, column_spec]
        + [pl.BlockSpec((total, cols), lambda g: (0, group)), out_spec]
        + [pl.BlockSpec((total // slots, cols), lambda g: (0, group))] * slots,
        out_specs=pl.BlockSpec((total, 3 * cols), lambda g: (0, 0)),
        out_shape=jax.ShapeDtypeStruct((total, 3 * cols), BF16),
        scratch_shapes=[pltpu.VMEM((pair, total, 128), BF16)] * 2
        + [pltpu.VMEM((pair, 128, total), BF16), pltpu.VMEM((pair, 128, total), F32)],
        compiler_params=pltpu.CompilerParams(vmem_limit_bytes=60 << 20),
        cost_estimate=pl.CostEstimate(
            flops=pair * 2400 * total * total, transcendentals=0, bytes_accessed=16 * total * cols
        ),
        name="attend_back",
    )(me, *columns, values, mixed, *grads)


def whole(shape):
    return pl.BlockSpec(shape, lambda i: (0,) * len(shape))


def row(ref):
    return ref[...].astype(F32)[None, :]


def choose(slot, refs):
    rows = refs[0][...]
    for at, ref in enumerate(refs[1:], 1):
        rows = jnp.where(slot == at, ref[...], rows)
    return rows


def slot_specs(count, per, block, width, order=lambda i: i):
    return [
        pl.BlockSpec(
            (block, width), lambda i, at=at: (jnp.clip(order(i) - at * per, 0, per - 1), 0)
        )
        for at in range(count)
    ]


def tall_spec(chosen, per, block, width):
    return pl.BlockSpec(
        (block, width),
        lambda i: ((chosen.start + chosen.step * (i // per)) * per + i % per, 0),
    )


def kernel_call(kernel, grid, in_specs, out_specs, out_shape, inputs, held=(), **more):
    return pl.pallas_call(
        kernel,
        grid=grid,
        in_specs=in_specs + [pl.BlockSpec(memory_space=pl.ANY)] * len(held),
        out_specs=out_specs,
        out_shape=out_shape,
        input_output_aliases={len(inputs) + at: at for at in range(len(held))},
        compiler_params=pltpu.CompilerParams(vmem_limit_bytes=56 << 20),
        cost_estimate=SMALL_COST,
        **more,
    )(*inputs, *held)


def shape_of(rows, cols, kind=BF16):
    return jax.ShapeDtypeStruct((rows, cols), kind)


def project_kernel(*refs, count, per):
    x_refs = refs[:count]
    gain_ref, shift_ref, wq_ref, wk_ref, wv_ref, qb_ref, vb_ref = refs[count : count + 7]
    normed_ref, q_ref, k_ref, v_ref = refs[-4:]
    x = choose(pl.program_id(0) // per, x_refs).astype(F32)
    normed = low(norm_stats(x)[0] * row(gain_ref) + row(shift_ref))
    normed_ref[...] = normed
    q_ref[...] = low((dot(normed, wq_ref[...]) + row(qb_ref)) * (LOG2E * HD**-0.5))
    k_ref[...] = low(dot(normed, wk_ref[...]))
    v_ref[...] = low(dot(normed, wv_ref[...]) + row(vb_ref))


def project(x_parts, chosen, slots, vectors, weights, biases, held):
    rows, width = x_parts[0].shape
    block = min(rows, 512)
    per = rows // block
    widths = [width] + [weight.shape[1] for weight in weights]
    return kernel_call(
        functools.partial(project_kernel, count=len(chosen), per=per),
        (len(chosen) * per,),
        slot_specs(len(chosen), per, block, width)
        + [whole(a.shape) for a in (*vectors, *weights, *biases)],
        [tall_spec(chosen, per, block, cols) for cols in widths],
        [shape_of(slots * rows, cols) for cols in widths],
        [*x_parts, *vectors, *weights, *biases],
        held,
        name="project",
    )


def act_grad_kernel(*refs, count, per):
    down_ref, grad_ref, cot_ref = refs[count:]
    cot = choose(pl.program_id(0) // per, refs[:count])
    cot_ref[...] = cot
    grad_ref[...] = low(dot(cot, down_ref[...], NT))


def act_grad_step(cot_parts, down):
    slots = len(cot_parts)
    rows, width = cot_parts[0].shape
    block = min(rows, 1024)
    per = rows // block
    units = down.shape[0]
    return kernel_call(
        functools.partial(act_grad_kernel, count=slots, per=per),
        (slots * per,),
        slot_specs(slots, per, block, width) + [whole(down.shape)],
        [pl.BlockSpec((block, cols), lambda i: (i, 0)) for cols in (units, width)],
        [shape_of(slots * rows, cols) for cols in (units, width)],
        [*cot_parts, down],
        (),
        name="act_grad",
    )


def post_kernel(*refs, slots, groups, per):
    mixed_refs = refs[: slots * groups]
    x_refs = refs[slots * groups : slots * groups + slots]
    weight_refs = refs[slots * groups + slots : slots * groups + 2 * slots]
    bias_ref, gain_ref, shift_ref, post_ref, residual_ref = refs[-5:]
    blocks = pl.num_programs(0)
    at = (pl.program_id(0) + blocks // 2) % blocks
    residual = choose(at // per, x_refs).astype(F32) + row(bias_ref)
    for slot in range(slots):
        mixed = [ref[...] for ref in mixed_refs[slot * groups : (slot + 1) * groups]]
        residual = residual + dot(jnp.concatenate(mixed, axis=1), weight_refs[slot][...])
    normal, _ = norm_stats(residual)
    post_ref[...] = low(normal * row(gain_ref) + row(shift_ref))

    @pl.when(at < per)
    def _():
        residual_ref[...] = residual


def post_norm(mixed, x_parts, weights, bias, gain, shift):
    slots, groups = len(mixed), len(mixed[0])
    rows, width = x_parts[0].shape
    block = min(rows, 512)
    per = rows // block
    blocks = slots * per
    order = lambda i: (i + blocks // 2) % blocks
    specs = [
        pl.BlockSpec(
            (block, part.shape[1]),
            lambda i, slot=slot: (((order(i) // per) ^ slot) * per + order(i) % per, 0),
        )
        for slot in range(slots)
        for part in mixed[slot]
    ]
    return kernel_call(
        functools.partial(post_kernel, slots=slots, groups=groups, per=per),
        (blocks,),
        specs
        + slot_specs(slots, per, block, width, order)
        + [whole(a.shape) for a in (*weights, bias, gain, shift)],
        [
            pl.BlockSpec((block, width), lambda i: (order(i), 0)),
            pl.BlockSpec((block, width), lambda i: (jnp.clip(i - blocks // 2, 0, per - 1), 0)),
        ],
        [shape_of(slots * rows, width), shape_of(rows, width, F32)],
        [*[part for parts in mixed for part in parts], *x_parts, *weights, bias, gain, shift],
        (),
        name="post_norm",
    )


def feed_kernel(*refs, count, per, extras, held):
    post_ref, act_grad_ref, up_ref, bias_ref = refs[:4]
    extra_refs = refs[4 : 4 + extras]
    active_ref, grad_ref, sum_ref = refs[4 + extras + held : 7 + extras + held]
    back_refs = refs[7 + extras + held :]
    slot = pl.program_id(0) // per

    @pl.when(pl.program_id(0) == 0)
    def _():
        sum_ref[...] = jnp.zeros_like(sum_ref)

    post = post_ref[...]
    units = active_ref.shape[1]
    chunk = min(512, units)
    scale, cubic = math.sqrt(2 / math.pi), 0.044715
    for first in range(0, units, chunk):
        cols = slice(first, first + chunk)
        hidden = dot(post, up_ref[:, cols]) + row(bias_ref)[:, cols]
        square = hidden * hidden
        curve = jnp.tanh(hidden * (scale + scale * cubic * square))
        half = 0.5 + 0.5 * curve
        active_ref[:, cols] = low(hidden * half)
        slope = half + (0.5 * hidden) * (1.0 - curve * curve) * (
            scale + 3 * scale * cubic * square
        )
        grad = low(act_grad_ref[:, cols].astype(F32) * slope)
        grad_ref[:, cols] = grad
        sum_ref[:, cols] += jnp.sum(grad.astype(F32), axis=0, keepdims=True)
    back = dot(grad_ref[...], up_ref[...], NT)
    if extras:
        back = back + choose(slot, extra_refs).astype(F32)
    back = low(back)
    for at, back_ref in enumerate(back_refs):

        @pl.when(slot == at)
        def _():
            back_ref[...] = back


def feed(post_all, act_grad, up, up_bias, slots, chosen, extras, held):
    count = len(chosen)
    total, width = post_all.shape
    rows, units = total // slots, up.shape[1]
    block = min(rows, 512)
    per = rows // block
    tall = lambda cols: tall_spec(chosen, per, block, cols)
    active, grad, sums, *backs = kernel_call(
        functools.partial(
            feed_kernel, count=count, per=per, extras=len(extras), held=len(held)
        ),
        (count * per,),
        [tall(width), tall(units), whole(up.shape), whole(up_bias.shape)]
        + slot_specs(len(extras), per, block, width),
        [tall(units), tall(units), whole((1, units))] + slot_specs(count, per, block, width),
        [shape_of(total, units), shape_of(total, units), shape_of(1, units, F32)]
        + [shape_of(rows, width)] * count,
        [post_all, act_grad, up, up_bias, *extras],
        held,
        name="feed",
    )
    return (active, grad), sums, backs


def split_rows(total, me, keep_ref, send_ref, streams):
    rows = total.shape[0] // streams
    for slot in range(streams):
        part = low(total[pl.ds(pl.multiple_of((me ^ slot) * rows, rows), rows), :])
        ref = send_ref if slot % 2 else keep_ref
        ref[slot // 2 * rows : (slot // 2 + 1) * rows, :] = part


def outer_kernel(me_ref, left_ref, right_ref, keep_ref, send_ref, total, *, streams):
    step = pl.program_id(0)

    @pl.when(step == 0)
    def _():
        total[...] = dot(left_ref[...], right_ref[...], TN)

    @pl.when(step > 0)
    def _():
        total[...] += dot(left_ref[...], right_ref[...], TN)

    @pl.when(step == pl.num_programs(0) - 1)
    def _():
        split_rows(total, me_ref[0], keep_ref, send_ref, streams)


def outer_step(left, right, me, streams):
    total = left.shape[0]
    block = min(total, 1024)
    shape = (left.shape[1], right.shape[1])
    half = (shape[0] // 2, shape[1])
    return kernel_call(
        functools.partial(outer_kernel, streams=streams),
        (total // block,),
        [pl.BlockSpec(memory_space=pltpu.SMEM)]
        + [pl.BlockSpec((block, cols), lambda i: (i, 0)) for cols in shape],
        [whole(half)] * 2,
        [shape_of(*half)] * 2,
        [me, left, right],
        scratch_shapes=[pltpu.VMEM(shape, F32)],
        name="outer_step",
    )


def join_kernel(me_ref, *refs, early, streams):
    parts, (keep_ref, send_ref) = refs[:-2], refs[-2:]
    rows = parts[0].shape[0] // streams
    for slot in range(streams):
        home = pl.ds(pl.multiple_of((me_ref[0] ^ slot) * rows, rows), rows)
        out = send_ref if slot % 2 else keep_ref
        here = slice(slot // 2 * rows, (slot // 2 + 1) * rows)
        at = 0
        for part in parts[:early]:
            out[here, at : at + part.shape[1]] = part[home, :]
            at += part.shape[1]
        total = parts[early][home, :].astype(F32)
        for part in parts[early + 1 :]:
            total = total + part[home, :].astype(F32)
        out[here, at:] = low(total)


def join_step(early, terms, me, streams):
    inputs = [*early, *terms]
    cols = sum(part.shape[1] for part in early) + terms[0].shape[1]
    half = (terms[0].shape[0] // 2, cols)
    return kernel_call(
        functools.partial(join_kernel, early=len(early), streams=streams),
        (1,),
        [pl.BlockSpec(memory_space=pltpu.SMEM)] + [whole(a.shape) for a in inputs],
        [whole(half)] * 2,
        [shape_of(*half)] * 2,
        [me, *inputs],
        name="join_step",
    )


def late_kernel(*refs):
    (keep, come, keep_late, come_late), outs = refs[:4], refs[4:]
    rows, cols = outs[0].shape[0], keep.shape[1]
    for slot, out in enumerate(outs):
        here = slice(slot * rows, (slot + 1) * rows)
        out[:, :cols] = low(keep[here, :].astype(F32) + come[here, :].astype(F32))
        out[:, cols:] = low(keep_late[here, :].astype(F32) + come_late[here, :].astype(F32))


def late_step(pairs, slots):
    inputs = [array for pair in pairs for array in pair]
    shape = (inputs[0].shape[0] // slots, inputs[0].shape[1] + inputs[2].shape[1])
    return kernel_call(
        late_kernel,
        (1,),
        [whole(a.shape) for a in inputs],
        [whole(shape)] * slots,
        [shape_of(*shape)] * slots,
        inputs,
        name="late_step",
    )


def pair_kernel(*refs, count):
    parts, outs = refs[: 2 * count], refs[2 * count :]
    rows = outs[0].shape[0] // count
    for at in range(count):
        keep, come = parts[2 * at : 2 * at + 2]
        for slot, out in enumerate(outs):
            here = slice(slot * rows, (slot + 1) * rows)
            out[at * rows : (at + 1) * rows, :] = low(
                keep[here, :].astype(F32) + come[here, :].astype(F32)
            )


def pair_step(pairs, slots):
    inputs = [array for pair in pairs for array in pair]
    rows, cols = inputs[0].shape
    shape = (rows // slots * len(pairs), cols)
    return kernel_call(
        functools.partial(pair_kernel, count=len(pairs)),
        (1,),
        [whole(a.shape) for a in inputs],
        [whole(shape)] * slots,
        [shape_of(*shape)] * slots,
        inputs,
        name="pair_step",
    )


def stack_kernel(*refs):
    rows = refs[0].shape[0]
    for at, ref in enumerate(refs[:-1]):
        refs[-1][at * rows : (at + 1) * rows, :] = ref[...]


def stack_step(parts):
    rows, cols = parts[0].shape
    return kernel_call(
        stack_kernel,
        (1,),
        [whole((rows, cols))] * len(parts),
        [whole((rows * len(parts), cols))],
        [shape_of(rows * len(parts), cols)],
        list(parts),
        name="stack_step",
    )[0]


def shard_views(even_ref, odd_ref, streams):
    rows = even_ref.shape[0] // (streams // 2)
    return [
        (slot, ref.at[slot // 2 * rows : (slot // 2 + 1) * rows])
        for slot, ref in enumerate([even_ref, odd_ref] * (streams // 2))
    ]


def feed_grads_kernel(me_ref, even_ref, odd_ref, up_ref, down_ref, up_rows, *, streams):
    rows = even_ref.shape[0] // streams
    for slot, part in shard_views(even_ref, odd_ref, streams):
        home = pl.ds(pl.multiple_of((me_ref[0] ^ slot) * rows, rows), rows)
        up_rows[home, :] = part[:rows, :].astype(F32)
        down_ref[home, :] = part[rows:, :].astype(F32)
    up_ref[...] = up_rows[...].T


def feed_grads(even, odd, me, streams):
    units, width = even.shape
    return kernel_call(
        functools.partial(feed_grads_kernel, streams=streams),
        (1,),
        [pl.BlockSpec(memory_space=pltpu.SMEM)] + [whole(even.shape)] * 2,
        [whole((width, units)), whole((units, width))],
        [shape_of(width, units, F32), shape_of(units, width, F32)],
        [me, even, odd],
        scratch_shapes=[pltpu.VMEM((units, width), F32)],
        name="feed_grads",
    )


def pack_kernel(*refs, groups):
    sums_ref, gain_ref, shift_ref = refs[:3]
    row_refs, count_refs = refs[3 : 3 + groups], refs[3 + groups : 3 + 2 * groups]
    unit_refs, out_ref = refs[3 + 2 * groups : -1], refs[-1]
    out_ref[...] = jnp.zeros_like(out_ref)
    out_ref[:4, : sums_ref.shape[1]] = sums_ref[:4, :]
    rows = row_refs[0][...]
    for ref in row_refs[1:]:
        rows = rows + ref[...]
    out_ref[4:5, : rows.shape[1]] = (rows[0:1] - row(shift_ref) * rows[1:2]) / row(gain_ref)
    out_ref[5:6, : rows.shape[1]] = rows[1:2]
    units = unit_refs[0][...]
    for ref in unit_refs[1:]:
        units = units + ref[...]
    out_ref[8:9, : units.shape[1]] = units
    for at, ref in enumerate(count_refs):
        out_ref[9 + at : 10 + at, : ref.shape[1]] = ref[...]


def pack(row_sums, gain, shift, group_rows, group_counts, unit_sums):
    inputs = [row_sums, gain, shift, *group_rows, *group_counts, *unit_sums]
    wide = max(a.shape[1] for a in (row_sums, *group_counts, *unit_sums))
    return kernel_call(
        functools.partial(pack_kernel, groups=len(group_rows)),
        (1,),
        [whole(a.shape) for a in inputs],
        [whole((16, wide))],
        [shape_of(16, wide, F32)],
        inputs,
        name="pack",
    )[0]


def resid_kernel(*refs, terms, slots):
    term_refs = refs[:terms]
    residual_ref, cot_ref, gain_ref = refs[terms : terms + 3]
    weight_refs = refs[terms + 3 : terms + 3 + slots]
    grad_ref, low_ref, sums_ref = refs[terms + 3 + slots : terms + 6 + slots]
    part_refs = refs[terms + 6 + slots :]

    @pl.when(pl.program_id(0) == 0)
    def _():
        sums_ref[...] = jnp.zeros_like(sums_ref)

    post_grad = term_refs[0][...].astype(F32)
    for ref in term_refs[1:]:
        post_grad = post_grad + ref[...].astype(F32)
    cot = cot_ref[...].astype(F32)
    normal, inverse = norm_stats(residual_ref[...])
    grad = cot + norm_pull(post_grad * row(gain_ref), normal, inverse)
    grad_ref[...] = grad
    grad_low = low(grad)
    low_ref[...] = grad_low
    for weight_ref, part_ref in zip(weight_refs, part_refs):
        part_ref[...] = low(dot(grad_low, weight_ref[...], NT))
    for at, value in enumerate((cot, grad, post_grad * normal, post_grad)):
        sums_ref[at : at + 1, :] += jnp.sum(value, axis=0, keepdims=True)


def resid_step(terms, residual, cotangent, gain, weights):
    rows, width = residual.shape
    block = min(rows, 256)
    tall = lambda cols: pl.BlockSpec((block, cols), lambda i: (i, 0))
    cols = weights[0].shape[0]
    return kernel_call(
        functools.partial(resid_kernel, terms=len(terms), slots=len(weights)),
        (rows // block,),
        [tall(width)] * (len(terms) + 2) + [whole(a.shape) for a in (gain, *weights)],
        [tall(width), tall(width), whole((8, width))] + [tall(cols)] * len(weights),
        [shape_of(rows, width, F32), shape_of(rows, width), shape_of(8, width, F32)]
        + [shape_of(rows, cols)] * len(weights),
        [*terms, residual, cotangent, gain, *weights],
        (),
        name="resid_step",
    )


def dense_grad_kernel(*refs, slots, groups):
    mixed_refs, grad_ref = refs[: slots * groups], refs[slots * groups]
    even_ref, odd_ref, *sum_refs = refs[slots * groups + 1 :]
    step = pl.program_id(0)
    grad = grad_ref[...]
    for slot in range(slots):
        mixed = [ref[...] for ref in mixed_refs[slot * groups : (slot + 1) * groups]]
        part = dot(grad, jnp.concatenate(mixed, axis=1), TN)
        sum_refs[slot][...] = jnp.where(step == 0, 0.0, sum_refs[slot][...]) + part

    @pl.when(step == pl.num_programs(0) - 1)
    def _():
        rows = sum_refs[0].shape[0]
        for slot, sum_ref in enumerate(sum_refs):
            out_ref = odd_ref if slot % 2 else even_ref
            out_ref[slot // 2 * rows : (slot // 2 + 1) * rows, :] = low(sum_ref[...])


def dense_grad(mixed, grad):
    slots, groups = len(mixed), len(mixed[0])
    rows, width = grad.shape
    block = min(rows, 512)
    per = rows // block
    cols = sum(part.shape[1] for part in mixed[0])
    return kernel_call(
        functools.partial(dense_grad_kernel, slots=slots, groups=groups),
        (per,),
        [
            pl.BlockSpec((block, part.shape[1]), lambda i, slot=slot: (slot * per + i, 0))
            for slot in range(slots)
            for part in mixed[slot]
        ]
        + [pl.BlockSpec((block, width), lambda i: (i, 0))],
        [whole((width * slots // 2, cols))] * 2,
        [shape_of(width * slots // 2, cols)] * 2,
        [*[part for parts in mixed for part in parts], grad],
        (),
        scratch_shapes=[pltpu.VMEM((width, cols), F32)] * slots,
        name="dense_grad",
    )


def weight_kernel(me_ref, normed_ref, grad_ref, wq_ref, wk_ref, wv_ref, *refs, streams):
    *out_refs, sums_ref, count_ref, total, count = refs
    step = pl.program_id(0)

    @pl.when(step == 0)
    def _():
        total[...] = jnp.zeros_like(total)
        count[...] = jnp.zeros_like(count)

    grad = grad_ref[...]
    total[...] += dot(normed_ref[...], grad, TN)
    count[...] += jnp.sum(grad.astype(F32), axis=0, keepdims=True)

    @pl.when(step == pl.num_programs(0) - 1)
    def _():
        weight = jnp.concatenate([wq_ref[...], wk_ref[...], wv_ref[...]], axis=1).astype(F32)
        if streams:
            split_rows(total, me_ref[0], *out_refs, streams)
        else:
            out_refs[0][...] = low(total[...])
        count_ref[...] = count[...]
        lane = lanes(weight.shape[0])
        cross = jnp.sum(weight * total[...], axis=1, keepdims=True)
        plain = jnp.sum(weight * count[...], axis=1, keepdims=True)
        both = jnp.where(lane == 0, cross, jnp.where(lane == 1, plain, 0.0))
        sums_ref[...] = both.T[:8]


def weight_step(normed, grad, weights, group, me, streams):
    total, width = normed.shape
    cols = grad.shape[1]
    block = min(total, 1024)
    outs = [(width // 2, cols)] * 2 if streams else [(width, cols)]
    *parts, sums, count = kernel_call(
        functools.partial(weight_kernel, streams=streams),
        (total // block,),
        [pl.BlockSpec(memory_space=pltpu.SMEM)]
        + [pl.BlockSpec((block, count), lambda i: (i, 0)) for count in (width, cols)]
        + [pl.BlockSpec((width, cols // 3), lambda i: (0, group))] * 3,
        [whole(shape) for shape in outs] + [whole((8, width)), whole((1, cols))],
        [shape_of(*shape) for shape in outs] + [shape_of(8, width, F32), shape_of(1, cols, F32)],
        [me, normed, grad, *weights],
        scratch_shapes=[pltpu.VMEM((width, cols), F32), pltpu.VMEM((1, cols), F32)],
        name="weight_step",
    )
    return parts, sums, count


def unproject_kernel(*refs, groups, per, extras):
    grad_refs, weight_refs = refs[:groups], refs[groups : 4 * groups]
    extra_refs = refs[4 * groups : 4 * groups + extras]
    out_refs = refs[4 * groups + extras : -1]
    joined = refs[-1]
    slot = pl.program_id(0) // per

    @pl.when(pl.program_id(0) == 0)
    def _():
        joined[...] = jnp.concatenate([ref[...] for ref in weight_refs], axis=1)

    total = dot(jnp.concatenate([ref[...] for ref in grad_refs], axis=1), joined[...], NT)
    if extras:
        total = total + choose(slot, extra_refs).astype(F32)
    total = low(total)
    for at, ref in enumerate(out_refs):

        @pl.when(slot == at)
        def _():
            ref[...] = total


def unproject(grads, weights, slots, chosen, extras):
    width = weights[0].shape[0]
    count, groups = len(chosen), len(grads)
    total, cols = grads[0].shape
    rows = total // slots
    block = min(rows, 512)
    per = rows // block
    return kernel_call(
        functools.partial(unproject_kernel, groups=groups, per=per, extras=len(extras)),
        (count * per,),
        [tall_spec(chosen, per, block, cols)] * groups
        + [
            pl.BlockSpec((width, cols // 3), lambda i, group=group: (0, group))
            for group in range(groups)
            for _ in weights
        ]
        + slot_specs(len(extras), per, block, width),
        slot_specs(count, per, block, width),
        [shape_of(rows, width)] * count,
        [*grads, *[weight for _ in grads for weight in weights], *extras],
        (),
        scratch_shapes=[pltpu.VMEM((width, cols * groups), BF16)],
        name="unproject",
    )


def ffn_kernel(active_ref, weight_ref, even_ref, odd_ref, *, per):
    total = low(dot(active_ref[...], weight_ref[...]))
    odd = pl.program_id(0) // per % 2

    @pl.when(odd == 0)
    def _():
        even_ref[...] = total

    @pl.when(odd == 1)
    def _():
        odd_ref[...] = total


def ffn_step(active, weight, slots):
    total, units = active.shape
    width = weight.shape[1]
    rows = total // slots
    block = min(rows, 1024)
    per = rows // block
    half = (total // 2, width)

    def half_spec(odd):
        def place(i):
            slot, step = i // per, i % per
            now = slot // 2 * per
            if odd:
                return (jnp.where(slot % 2 == 1, now + step, jnp.maximum(now - 1, 0)), 0)
            return (jnp.where(slot % 2 == 0, now + step, now + per - 1), 0)

        return pl.BlockSpec((block, width), place)

    return kernel_call(
        functools.partial(ffn_kernel, per=per),
        (slots * per,),
        [pl.BlockSpec((block, units), lambda i: (i, 0)), whole(weight.shape)],
        [half_spec(0), half_spec(1)],
        [shape_of(*half)] * 2,
        [active, weight],
        name="ffn_step",
    )


def spread_kernel(me_ref, even_ref, odd_ref, *refs, groups, streams):
    *out_refs, dense_ref, dense_rows = refs
    cols = out_refs[0].shape[1] // groups
    heads = dense_ref.shape[0]
    rows = even_ref.shape[0] * 2 // streams
    for slot, part in shard_views(even_ref, odd_ref, streams):
        home = pl.ds(pl.multiple_of((me_ref[0] ^ slot) * rows, rows), rows)
        for group in range(groups):
            first = group * 3 * cols + (heads if group == groups - 1 else 0)
            for kind in range(3):
                at = first + kind * cols
                out_refs[kind][home, group * cols : (group + 1) * cols] = part[
                    :, at : at + cols
                ].astype(F32)
        first = (groups - 1) * 3 * cols
        dense_rows[home, :] = part[:, first : first + heads].astype(F32)
    dense_ref[...] = dense_rows[...].T


def spread(even, odd, me, streams, groups, heads):
    width = even.shape[0] * 2
    shapes = [(width, heads)] * 3 + [(heads, width)]
    return kernel_call(
        functools.partial(spread_kernel, groups=groups, streams=streams),
        (1,),
        [pl.BlockSpec(memory_space=pltpu.SMEM)] + [whole(even.shape)] * 2,
        [whole(shape) for shape in shapes],
        [shape_of(*shape, F32) for shape in shapes],
        [me, even, odd],
        scratch_shapes=[pltpu.VMEM((width, heads), F32)],
        name="spread",
    )


def input_kernel(*refs, terms):
    x_ref, resid_ref, gain_ref, out_ref = refs[terms:]
    grad = refs[0][...].astype(F32)
    for ref in refs[1:terms]:
        grad = grad + ref[...].astype(F32)
    normal, inverse = norm_stats(x_ref[...].astype(F32))
    out_ref[...] = resid_ref[...] + norm_pull(grad * row(gain_ref), normal, inverse)


def input_step(terms, layer_input, resid_grad, gain):
    rows, width = resid_grad.shape
    block = min(rows, 256)
    tall = pl.BlockSpec((block, width), lambda i: (i, 0))
    return kernel_call(
        functools.partial(input_kernel, terms=len(terms)),
        (rows // block,),
        [tall] * (len(terms) + 2) + [whole(gain.shape)],
        [tall],
        [shape_of(rows, width, F32)],
        [*terms, layer_input, resid_grad, gain],
        name="input_step",
    )[0]


def shards(
    slots,
    streams,
    layer_input,
    row_ids,
    input_gain,
    input_shift,
    query_weight,
    query_bias,
    key_weight,
    value_weight,
    value_bias,
    dense_weight,
    dense_bias,
    post_gain,
    post_shift,
    up_weight,
    up_bias,
    down_weight,
    down_bias,
    cotangent,
):
    me = lax.axis_index("tensor")
    me_word = me.astype(jnp.int32)[None]
    stream = lax.axis_index("dp").astype(jnp.int32)[None]
    rows = layer_input.shape[0]
    head_cols = query_weight.shape[1]
    head_count = head_cols // HD
    groups = max(1, head_count // 2)
    bits = [1 << level for level in range(slots.bit_length() - 1)]
    half = slots // 2
    after = lambda array, *others: lax.optimization_barrier((array, *others))[0]

    def swap(array, mask):
        return lax.ppermute(array, "tensor", [(i, i ^ mask) for i in range(slots)])

    def gather(array):
        held = {0: array}
        for bit in reversed(bits):
            held.update({slot ^ bit: swap(part, bit) for slot, part in held.items()})
        return [held[slot] for slot in range(slots)]

    def blocks(array):
        return [array[slot * rows : (slot + 1) * rows] for slot in range(slots)]

    def swap_data(array, mask):
        return lax.ppermute(array, "dp", [(i, i ^ mask) for i in range(streams)])

    def finish_terms(held, terms, levels):
        for bit in levels:
            come = {slot ^ bit: swap(part, bit) for slot, part in held.items() if slot & bit}
            if 0 in come:
                terms.append(come.pop(0))
            held = {
                slot: low(held[slot].astype(F32) + part.astype(F32)) for slot, part in come.items()
            }
        return terms

    def scatter_terms(parts):
        return finish_terms(dict(enumerate(parts)), [parts[0]], bits)

    far_odd = range(half + 1, slots, 2)
    far_even = range(half, slots, 2)
    near_odd = range(1, half, 2)
    near_even = range(0, half, 2)

    def ordered_terms(make):
        far = make(far_odd, (), None)
        far_come = [swap(part, 1) for part in far]
        near = make(near_odd, (), far[-1])
        near_come = [swap(part, 1) for part in near]
        far = make(far_even, far_come, near[-1])
        near = make(near_even, near_come, far[-1])
        held = dict(zip((*far_even, *near_even), (*far, *near)))
        return finish_terms(held, [held.pop(0)], bits[1:])

    def add_up(terms):
        return functools.reduce(
            lambda sum_now, term: sum_now + term.astype(F32), terms[1:], terms[0].astype(F32)
        )

    far_streams = range(2, streams, 2)

    def exchange(parts):
        return low(add_up([parts[0], *[swap_data(parts[k // 2], k) for k in far_streams]]))

    def collect_far(shard):
        return [shard, *[swap_data(shard, k) for k in far_streams]]

    norm_vectors = (input_gain, input_shift)
    weights = (query_weight, key_weight, value_weight)
    biases = (query_bias, value_bias)
    x_held = {0: layer_input}
    for bit in reversed(bits[1:]):
        x_held.update({slot ^ bit: swap(part, bit) for slot, part in x_held.items()})
    x_held[1] = swap(x_held[0], 1)
    near_parts = [x_held[0], x_held[1]]
    first = range(2)
    held = project(near_parts, first, slots, norm_vectors, weights, biases, ())
    rest = sorted(slot for slot in x_held if slot > 1)
    *arrived, normed = lax.optimization_barrier((*[x_held[slot] for slot in rest], held[0]))
    held = (normed, *held[1:])
    for slot, part in zip(rest, arrived):
        x_held[slot], x_held[slot ^ 1] = part, swap(part, 1)
    x_parts = [x_held[slot] for slot in range(slots)]
    dense_parts = gather(after(dense_weight, arrived[-1]))
    cot_own = after(cotangent, arrived[-1])
    cot_held = {0: cot_own}
    for bit in reversed(bits[1:]):
        cot_held.update({slot ^ bit: swap(part, bit) for slot, part in cot_held.items()})
    normed, queries, key_rows, values = project(
        x_parts[2:], range(2, slots), slots, norm_vectors, weights, biases, held
    )

    heads = me * head_count + jnp.arange(head_count)
    slopes = jnp.exp2(-8.0 * (heads + 1).astype(F32) / HEADS) * LOG2E
    apart = (row_ids[:1] != row_ids[SHORT : SHORT + 1]).astype(jnp.int32)

    mixed_own, columns, mixed_parts = [], [], []
    for group in range(groups):
        mixed, *held_columns = attend(
            me_word,
            apart,
            slopes,
            queries if not group else after(queries, cot_held[half], mixed_own[-1]),
            key_rows,
            values,
            slots,
            group,
        )
        mixed_own.append(mixed)
        columns.append(held_columns)
        if not group:
            keys = sorted(cot_held)
            held = lax.optimization_barrier((*[cot_held[key] for key in keys], mixed))[:-1]
            cot_held.update(zip(keys, held))
            cot_held.update({slot ^ 1: swap(part, 1) for slot, part in cot_held.items()})
            cot_parts = [cot_held[slot] for slot in range(slots)]
        if group < groups - 1:
            mixed_parts.append(gather(mixed))
    act_grad, cot_all = act_grad_step(
        lax.optimization_barrier((*cot_parts, mixed_own[-1], *dense_parts[2:]))[:slots], down_weight
    )
    came = {0: mixed_own[-1]}
    for bit in reversed(bits[1:]):
        came.update({slot ^ bit: swap(part, bit) for slot, part in came.items()})
    far_slots = sorted(came)[1:]
    *arrived, act_grad = lax.optimization_barrier((*[came[slot] for slot in far_slots], act_grad))
    came.update(zip(far_slots, arrived))
    came.update({slot ^ 1: swap(part, 1) for slot, part in came.items()})
    mixed_parts.append([came[slot] for slot in range(slots)])
    mixed_all = [[mixed_parts[group][slot] for group in range(groups)] for slot in range(slots)]
    post_all, residual = post_norm(
        mixed_all, x_parts, dense_parts, dense_bias, post_gain, post_shift
    )

    fed, up_bias_parts = [()], []

    def make_feed(chosen, extras, gate):
        held, sums, backs = feed(
            post_all, act_grad, up_weight, up_bias, slots, chosen, extras, fed[-1]
        )
        fed.append(held)
        up_bias_parts.append(sums)
        return backs

    post_terms = ordered_terms(make_feed)
    active, hidden_grad = fed[-1]
    up_keep, up_send = outer_step(hidden_grad, post_all, stream, streams)
    down_keep, down_send = outer_step(active, after(cot_all, up_keep), stream, streams)
    up_come, down_come = swap_data(up_send, 1), swap_data(down_send, 1)
    resid_grad, attended_grad, row_sums, *mixed_grads = resid_step(
        [after(post_terms[0], down_keep), *post_terms[1:]],
        residual,
        cotangent,
        post_gain,
        dense_parts,
    )
    mixed_grads = [swap(part, slot) if slot else part for slot, part in enumerate(mixed_grads)]
    dense_even, dense_odd = dense_grad(mixed_all, attended_grad)
    ffn_even, ffn_odd = ffn_step(after(active, dense_odd), down_weight, slots)
    feed_parts = pair_step(
        [(after(up_keep, ffn_odd), up_come), (down_keep, down_come)], streams // 2
    )
    moved = lax.optimization_barrier((*mixed_grads, dense_odd, ffn_odd, *feed_parts))
    mixed_grads, (dense_odd, ffn_odd), feed_parts = (
        moved[:slots],
        moved[slots : slots + 2],
        moved[slots + 2 :],
    )
    dense_come, ffn_come = swap(dense_odd, 1), swap(ffn_odd, 1)

    def partner_sums(even, come):
        size = even.shape[0] * 2 // slots
        cuts = [slice(at * size, (at + 1) * size) for at in range(slots // 2)]
        return [low(even[cut].astype(F32) + come[cut].astype(F32)) for cut in cuts]

    cols = head_cols // groups
    head_grads, early_parts, group_rows, group_counts = [], [], [], []

    def backward(group):
        return attend_back(
            me_word, columns[group], values, mixed_own[group], mixed_grads, group
        )

    dense_sums = partner_sums(dense_even, dense_come)
    for group in range(groups - 1):
        head_grads.append(backward(group))
        grad = head_grads[-1]
        if group == groups - 2:
            grad, *dense_sums = lax.optimization_barrier((grad, *dense_sums))
        parts, row_part, count_part = weight_step(normed, grad, weights, group, stream, 0)
        early_parts += parts
        group_rows.append(row_part)
        group_counts.append(count_part)
        mixed_grads = lax.optimization_barrier((*mixed_grads, parts[-1]))[:-1]
    even_slots = range(2, slots, 2)
    dense_terms = finish_terms(dict(zip(even_slots, dense_sums[1:])), [dense_sums[0]], bits[1:])
    early_keep, early_send = join_step(early_parts, dense_terms, stream, streams)
    moved = lax.optimization_barrier(
        (*mixed_grads, early_send, exchange(feed_parts), *partner_sums(ffn_even, ffn_come))
    )
    mixed_grads, (early_send, feed_shard), ffn_sums = (
        moved[:slots],
        moved[slots : slots + 2],
        moved[slots + 2 :],
    )
    early_come = swap_data(early_send, 1)
    feed_shards = collect_far(feed_shard)
    ffn_terms = finish_terms(dict(zip(even_slots, ffn_sums[1:])), [ffn_sums[0]], bits[1:])
    head_grads.append(backward(groups - 1))
    grad, early_come, *arrived = lax.optimization_barrier(
        (head_grads[-1], early_come, *feed_shards, *ffn_terms)
    )
    feed_shards, ffn_terms = arrived[: len(feed_shards)], arrived[len(feed_shards) :]
    (late_keep, late_send), row_part, count_part = weight_step(
        normed, grad, weights, groups - 1, stream, streams
    )
    group_rows.append(row_part)
    group_counts.append(count_part)
    late_come = swap_data(late_send, 1)
    vectors = pack(row_sums, input_gain, input_shift, group_rows, group_counts, up_bias_parts)
    feed_even = stack_step([*feed_shards[:-1], after(feed_shards[-1], vectors)])
    summed = vectors + swap_data(vectors, 1)
    feed_odd = swap_data(after(feed_even, late_come, summed), 1)
    seen = []

    def make_unproject(chosen, extras, gate):
        gates = [feed_even if gate is None else gate]
        if not seen:
            gates += [late_come, summed]
        seen.append(0)
        return unproject(
            [*head_grads[:-1], after(head_grads[-1], *gates)], weights, slots, chosen, extras
        )

    normed_terms = ordered_terms(make_unproject)
    late_parts = late_step(
        [(early_keep, early_come), (after(late_keep, normed_terms[0]), late_come)], streams // 2
    )
    layer_output = low(residual + add_up(ffn_terms) + down_bias.astype(F32))
    up_grad, down_grad = feed_grads(feed_even, feed_odd, stream, streams)
    input_grad = input_step(
        [*normed_terms[:-1], after(normed_terms[-1], up_grad)],
        layer_input,
        resid_grad,
        input_gain,
    )
    *late_shards, layer_output, input_grad = lax.optimization_barrier(
        (*collect_far(exchange(late_parts)), layer_output, input_grad)
    )
    late_even = stack_step(late_shards)
    late_odd = swap_data(late_even, 1)
    for level in range(1, streams.bit_length() - 1):
        summed = summed + swap_data(summed, 1 << level)
    own = summed[8:]
    shared = after(summed, normed_terms[-1])[:8]
    for bit in reversed(bits):
        shared = shared + swap(shared, bit)
    shared = shared[:, : resid_grad.shape[1]]
    up_bias_grad = own[0, : up_bias.shape[0]]
    counts = own[1 : 1 + groups]
    query_bias_grad = counts[:, :cols].reshape(-1)
    value_bias_grad = counts[:, 2 * cols : 3 * cols].reshape(-1)
    *weight_grads, dense_weight_grad = spread(
        late_even, late_odd, stream, streams, groups, head_cols
    )
    return (
        layer_output,
        input_grad,
        shared[4],
        shared[5],
        weight_grads[0],
        query_bias_grad,
        weight_grads[1],
        weight_grads[2],
        value_bias_grad,
        dense_weight_grad,
        shared[1],
        shared[2],
        shared[3],
        up_grad,
        up_bias_grad,
        down_grad,
        shared[0],
    )


def solution(mesh):
    in_specs = (
        P(("dp", "tensor"), None),
        P("dp"),
        P(),
        P(),
        P(None, "tensor"),
        P("tensor"),
        P(None, "tensor"),
        P(None, "tensor"),
        P("tensor"),
        P("tensor", None),
        P(),
        P(),
        P(),
        P(None, "tensor"),
        P("tensor"),
        P("tensor", None),
        P(),
        P(("dp", "tensor"), None),
    )
    out_specs = (
        P(("dp", "tensor"), None),
        P(("dp", "tensor"), None),
        P(),
        P(),
        P(None, "tensor"),
        P("tensor"),
        P(None, "tensor"),
        P(None, "tensor"),
        P("tensor"),
        P("tensor", None),
        P(),
        P(),
        P(),
        P(None, "tensor"),
        P("tensor"),
        P("tensor", None),
        P(),
    )
    return jax.shard_map(
        functools.partial(shards, mesh.shape["tensor"], mesh.shape["dp"]), mesh=mesh, in_specs=in_specs, out_specs=out_specs, check_vma=False)
```

```python
import functools
import math

import jax
import jax.numpy as jnp
from jax import lax
from jax.experimental import pallas as pl
from jax.experimental.pallas import tpu as pltpu
from jax.sharding import PartitionSpec as P

HEADS = 16
HD = 64
SHORT = 2048
EPSILON = 1e-05
LOG2E = math.log2(math.e)
F32 = jnp.float32
BF16 = jnp.bfloat16
SMALL_COST = pl.CostEstimate(flops=1, transcendentals=0, bytes_accessed=1)
NT = (((1,), (1,)), ((), ()))
NN = (((1,), (0,)), ((), ()))
TN = (((0,), (0,)), ((), ()))


def dot(lhs, rhs, dims=NN):
    return lax.dot_general(lhs, rhs, dims, preferred_element_type=F32)


def low(array):
    return array.astype(BF16)


def norm_stats(rows):
    center = jnp.mean(rows, axis=-1, keepdims=True)
    centered = rows - center
    inverse = lax.rsqrt(jnp.mean(centered * centered, axis=-1, keepdims=True) + EPSILON)
    return centered * inverse, inverse


def norm_pull(grad, normal, inverse):
    grad_mean = jnp.mean(grad, axis=-1, keepdims=True)
    dot_mean = jnp.mean(grad * normal, axis=-1, keepdims=True)
    return inverse * (grad - grad_mean - normal * dot_mean)


def lanes(count):
    return lax.broadcasted_iota(jnp.int32, (count, 128), 1)


def places(count, first):
    return lax.broadcasted_iota(jnp.int32, (count, 128), 0) + first


def widen(head):
    return jnp.concatenate([head.astype(F32), jnp.zeros((head.shape[0], HD), F32)], axis=1)


def split3(value):
    high = low(value).astype(F32)
    middle = low(value - high).astype(F32)
    return high, middle, value - high - middle


def pick3(index, parts):
    return jnp.where(index == 0, parts[0], jnp.where(index == 1, parts[1], parts[2]))


def key_columns(head, first):
    count = head.shape[0]
    lane, place = lanes(count), places(count, first)
    coarse = ((place >> 6) << 6).astype(F32)
    fine = (place & 63).astype(F32)
    wall = jnp.where(place < SHORT, -1e30, 0.0)
    extra = jnp.where(lane < 73, -1.0, jnp.where(lane == 73, wall, 0.0))
    extra = jnp.where(lane < 67, coarse, jnp.where(lane < 70, fine, extra))
    return low(jnp.where(lane < HD, widen(head), extra))


def query_columns(head, first, slope, apart):
    count = head.shape[0]
    lane, place = lanes(count), places(count, first)
    extra = pick3(jnp.where(lane < 67, lane - 64, lane - 67), split3(slope))
    extra = jnp.where(lane < 70, extra, 0.0)
    extra = jnp.where(lane == 73, jnp.where(place >= SHORT, apart, 0.0), extra)
    return low(jnp.where(lane < HD, widen(head), extra))


def ones_columns(head, count):
    lane = lanes(head.shape[0])
    return low(jnp.where(lane < HD, widen(head), jnp.where(lane < HD + count, 1.0, 0.0)))


def grad_columns(head, shift):
    lane = lanes(head.shape[0])
    extra = jnp.where(lane < 67, pick3(lane - 64, split3(shift)), 0.0)
    return low(jnp.where(lane < HD, widen(head), extra))


def each_chunk(me, slots, rows, body):
    chunk = min(rows, 512)
    for slot in range(slots):
        home = (me ^ slot) * rows

        @pl.loop(0, rows // chunk)
        def _(step):
            offset = pl.multiple_of(step * chunk, chunk)
            body(slot, pl.ds(offset, chunk), pl.ds(slot * rows + offset, chunk), home + offset)


def attend_kernel(
    me_ref, apart_ref, slope_ref, q_ref, k_ref, v_ref, o_ref, qa, ka, va, *, slots, pair, tile
):
    me = me_ref[0]
    total = q_ref.shape[0]
    rows = total // slots
    chunk = min(rows, 512)
    apart = apart_ref[0].astype(F32)

    def prepare(slot, inner, spot, place):
        place = pl.multiple_of(place, chunk)
        home = pl.ds(place, chunk)
        for s in range(pair):
            cols = slice(s * HD, (s + 1) * HD)
            qa[s, home, :] = query_columns(q_ref[spot, cols], place, slope_ref[s], apart)
            ka[s, home, :] = key_columns(k_ref[spot, cols], place)
            va[s, home, :] = ones_columns(v_ref[spot, cols], 1)

    each_chunk(me, slots, rows, prepare)
    causal = lax.broadcasted_iota(jnp.int32, (tile, tile), 1) <= lax.broadcasted_iota(
        jnp.int32, (tile, tile), 0
    )
    piece = min(rows, tile)
    lane = lanes(tile)

    def query_tile(index, _):
        first = pl.multiple_of(index * tile, tile)
        queries = [qa[s, pl.ds(first, tile), :] for s in range(pair)]

        def step(at, carry, diagonal):
            after = []
            for s in range(pair):
                top, mix = carry[s]
                scores = dot(queries[s], ka[s, pl.ds(at, tile), :], NT)
                if diagonal:
                    scores = jnp.where(causal, scores, -1e30)
                higher = jnp.maximum(top, jnp.max(scores, axis=1, keepdims=True))
                weights = low(jnp.exp2(scores - higher))
                mix = mix * jnp.exp2(top - higher) + dot(weights, va[s, pl.ds(at, tile), :])
                after.append((higher, mix))
            return tuple(after)

        carry = tuple(
            (jnp.full((tile, 1), -1e38, F32), jnp.zeros((tile, 128), F32)) for _ in range(pair)
        )
        carry = step(first, carry, True)
        carry = lax.fori_loop(
            0, index, lambda at, held: step(pl.multiple_of(at * tile, tile), held, False), carry
        )
        outs = []
        for s in range(pair):
            top, mix = carry[s]
            weight = mix[:, HD : HD + 1]
            outs.append(mix[:, :HD] * (1.0 / weight))
            log_total = pick3(lane - 70, split3(top + jnp.log2(weight)))
            qa[s, pl.ds(first, tile), :] = low(
                jnp.where((lane >= 70) & (lane < 73), log_total, queries[s].astype(F32))
            )
        out = low(jnp.concatenate(outs, axis=1))
        for part in range(tile // piece):
            block = (index * (tile // piece) + part) // (rows // piece)
            offset = first + part * piece - block * rows
            spot = pl.multiple_of((block ^ me) * rows + offset, piece)
            o_ref[pl.ds(spot, piece), :] = out[part * piece : (part + 1) * piece]
        return 0

    lax.fori_loop(0, total // tile, query_tile, 0)


def attend(me, apart, slopes, queries, key_rows, values, slots, group, tile=1024):
    total, width = queries.shape
    pair = min(2, width // HD)
    cols = pair * HD
    spec = pl.BlockSpec((total, cols), lambda g: (0, group))
    scalars = pl.BlockSpec(memory_space=pltpu.SMEM)
    return pl.pallas_call(
        functools.partial(attend_kernel, slots=slots, pair=pair, tile=tile),
        grid=(1,),
        in_specs=[scalars] * 3 + [spec] * 3,
        out_specs=[
            pl.BlockSpec((total, cols), lambda g: (0, 0)),
            pl.BlockSpec((pair, total, 128), lambda g: (0, 0, 0)),
            pl.BlockSpec((pair, total, 128), lambda g: (0, 0, 0)),
        ],
        out_shape=[
            jax.ShapeDtypeStruct((total, cols), BF16),
            jax.ShapeDtypeStruct((pair, total, 128), BF16),
            jax.ShapeDtypeStruct((pair, total, 128), BF16),
        ],
        scratch_shapes=[pltpu.VMEM((pair, total, 128), BF16)],
        compiler_params=pltpu.CompilerParams(vmem_limit_bytes=56 << 20),
        cost_estimate=pl.CostEstimate(
            flops=pair * 1200 * total * total, transcendentals=0, bytes_accessed=8 * total * cols
        ),
        name="attend",
    )(me, apart, slopes[group * pair : (group + 1) * pair], queries, key_rows, values)


def attend_back_kernel(*refs, slots, pair, tile, key_tile):
    me_ref, qa, ka, v_ref, o_ref = refs[:5]
    g_refs = refs[5 : 5 + slots]
    out_ref, va, ga, kt, dq_sum = refs[5 + slots :]
    cols = pair * HD
    me = me_ref[0]
    total = v_ref.shape[0]
    rows = total // slots
    chunk = min(rows, 512)

    def prepare(slot, inner, spot, place):
        place = pl.multiple_of(place, chunk)
        home = pl.ds(place, chunk)
        for s in range(pair):
            mine = slice(s * HD, (s + 1) * HD)
            kt[s, :, home] = low(ka[s, home, :].astype(F32).T)
            va[s, home, :] = ones_columns(v_ref[spot, mine], 3)
            grad = g_refs[slot][inner, mine]
            row_dot = jnp.sum(
                grad.astype(F32) * o_ref[spot, mine].astype(F32), axis=1, keepdims=True
            )
            ga[s, home, :] = grad_columns(grad, -row_dot)
            dq_sum[s, :, home] = jnp.zeros((128, chunk), F32)

    each_chunk(me, slots, rows, prepare)
    causal = lax.broadcasted_iota(jnp.int32, (key_tile, key_tile), 0) <= lax.broadcasted_iota(
        jnp.int32, (key_tile, key_tile), 1
    )
    piece = min(rows, key_tile)

    def place_of(place, size):
        block = place // rows
        return pl.multiple_of((block ^ me) * rows + (place - block * rows), size)

    def keys_tile(index, _):
        first = pl.multiple_of(index * key_tile, key_tile)
        here = pl.ds(first, key_tile)

        def step(at, carry, diagonal, width):
            after = []
            for s in range(pair):
                dk, dv = carry[s]
                there = pl.ds(at, width)
                queries, grads = qa[s, there, :], ga[s, there, :]
                probs = jnp.exp2(dot(ka[s, here, :], queries, NT))
                if diagonal:
                    probs = jnp.where(causal, probs, 0.0)
                dv = dv + dot(low(probs), grads)
                score_grad = low(probs * dot(va[s, here, :], grads, NT))
                dk = dk + dot(score_grad, queries)
                dq_sum[s, :, there] += dot(kt[s, :, here], score_grad)
                after.append((dk, dv))
            return tuple(after)

        zeros = jnp.zeros((key_tile, 128), F32)
        carry = step(first, tuple((zeros, zeros) for _ in range(pair)), True, key_tile)
        start = first + key_tile
        short = jnp.minimum((-start) % tile, total - start) // key_tile
        if tile > key_tile:
            carry = lax.fori_loop(
                0,
                short,
                lambda at, held: step(
                    pl.multiple_of(start + at * key_tile, key_tile), held, False, key_tile
                ),
                carry,
            )
            start = start + short * key_tile
        carry = lax.fori_loop(
            0,
            (total - start) // tile,
            lambda at, held: step(
                pl.multiple_of(start + at * tile, min(tile, key_tile)), held, False, tile
            ),
            carry,
        )
        dk = low(jnp.concatenate([held[0][:, :HD] * (1.0 / LOG2E) for held in carry], axis=1))
        dv = low(jnp.concatenate([held[1][:, :HD] for held in carry], axis=1))
        for part in range(key_tile // piece):
            spot = pl.ds(place_of(first + part * piece, piece), piece)
            out_ref[spot, cols : 2 * cols] = dk[part * piece : (part + 1) * piece]
            out_ref[spot, 2 * cols :] = dv[part * piece : (part + 1) * piece]
        return 0

    lax.fori_loop(0, total // key_tile, keys_tile, 0)

    def finish(slot, inner, spot, place):
        home = pl.ds(pl.multiple_of(place, chunk), chunk)
        joined = jnp.concatenate([dq_sum[s, :HD, home] for s in range(pair)], axis=0)
        out_ref[spot, :cols] = low(joined.T * HD**-0.5)

    each_chunk(me, slots, rows, finish)


def attend_back(me, columns, values, mixed, grads, group, tile=1024, key_tile=512):
    slots = len(grads)
    total, width = values.shape
    pair = columns[0].shape[0]
    cols = pair * HD
    out_spec = pl.BlockSpec((total, cols), lambda g: (0, 0))
    column_spec = pl.BlockSpec((pair, total, 128), lambda g: (0, 0, 0))
    return pl.pallas_call(
        functools.partial(
            attend_back_kernel, slots=slots, pair=pair, tile=tile, key_tile=key_tile
        ),
        grid=(1,),
        in_specs=[pl.BlockSpec(memory_space=pltpu.SMEM), column_spec, column_spec]
        + [pl.BlockSpec((total, cols), lambda g: (0, group)), out_spec]
        + [pl.BlockSpec((total // slots, cols), lambda g: (0, group))] * slots,
        out_specs=pl.BlockSpec((total, 3 * cols), lambda g: (0, 0)),
        out_shape=jax.ShapeDtypeStruct((total, 3 * cols), BF16),
        scratch_shapes=[pltpu.VMEM((pair, total, 128), BF16)] * 2
        + [pltpu.VMEM((pair, 128, total), BF16), pltpu.VMEM((pair, 128, total), F32)],
        compiler_params=pltpu.CompilerParams(vmem_limit_bytes=60 << 20),
        cost_estimate=pl.CostEstimate(
            flops=pair * 2400 * total * total, transcendentals=0, bytes_accessed=16 * total * cols
        ),
        name="attend_back",
    )(me, *columns, values, mixed, *grads)


def whole(shape):
    return pl.BlockSpec(shape, lambda i: (0,) * len(shape))


def row(ref):
    return ref[...].astype(F32)[None, :]


def choose(slot, refs):
    rows = refs[0][...]
    for at, ref in enumerate(refs[1:], 1):
        rows = jnp.where(slot == at, ref[...], rows)
    return rows


def slot_specs(count, per, block, width, order=lambda i: i):
    return [
        pl.BlockSpec(
            (block, width), lambda i, at=at: (jnp.clip(order(i) - at * per, 0, per - 1), 0)
        )
        for at in range(count)
    ]


def tall_spec(chosen, per, block, width):
    return pl.BlockSpec(
        (block, width),
        lambda i: ((chosen.start + chosen.step * (i // per)) * per + i % per, 0),
    )


def kernel_call(kernel, grid, in_specs, out_specs, out_shape, inputs, held=(), **more):
    return pl.pallas_call(
        kernel,
        grid=grid,
        in_specs=in_specs + [pl.BlockSpec(memory_space=pl.ANY)] * len(held),
        out_specs=out_specs,
        out_shape=out_shape,
        input_output_aliases={len(inputs) + at: at for at in range(len(held))},
        compiler_params=pltpu.CompilerParams(vmem_limit_bytes=56 << 20),
        cost_estimate=SMALL_COST,
        **more,
    )(*inputs, *held)


def shape_of(rows, cols, kind=BF16):
    return jax.ShapeDtypeStruct((rows, cols), kind)


def project_kernel(*refs, count, per):
    x_refs = refs[:count]
    gain_ref, shift_ref, wq_ref, wk_ref, wv_ref, qb_ref, vb_ref = refs[count : count + 7]
    normed_ref, q_ref, k_ref, v_ref = refs[-4:]
    x = choose(pl.program_id(0) // per, x_refs).astype(F32)
    normed = low(norm_stats(x)[0] * row(gain_ref) + row(shift_ref))
    normed_ref[...] = normed
    q_ref[...] = low((dot(normed, wq_ref[...]) + row(qb_ref)) * (LOG2E * HD**-0.5))
    k_ref[...] = low(dot(normed, wk_ref[...]))
    v_ref[...] = low(dot(normed, wv_ref[...]) + row(vb_ref))


def project(x_parts, chosen, slots, vectors, weights, biases, held):
    rows, width = x_parts[0].shape
    block = min(rows, 512)
    per = rows // block
    widths = [width] + [weight.shape[1] for weight in weights]
    return kernel_call(
        functools.partial(project_kernel, count=len(chosen), per=per),
        (len(chosen) * per,),
        slot_specs(len(chosen), per, block, width)
        + [whole(a.shape) for a in (*vectors, *weights, *biases)],
        [tall_spec(chosen, per, block, cols) for cols in widths],
        [shape_of(slots * rows, cols) for cols in widths],
        [*x_parts, *vectors, *weights, *biases],
        held,
        name="project",
    )


def act_grad_kernel(*refs, count, per):
    down_ref, grad_ref, cot_ref = refs[count:]
    cot = choose(pl.program_id(0) // per, refs[:count])
    cot_ref[...] = cot
    grad_ref[...] = low(dot(cot, down_ref[...], NT))


def act_grad_step(cot_parts, down):
    slots = len(cot_parts)
    rows, width = cot_parts[0].shape
    block = min(rows, 1024)
    per = rows // block
    units = down.shape[0]
    return kernel_call(
        functools.partial(act_grad_kernel, count=slots, per=per),
        (slots * per,),
        slot_specs(slots, per, block, width) + [whole(down.shape)],
        [pl.BlockSpec((block, cols), lambda i: (i, 0)) for cols in (units, width)],
        [shape_of(slots * rows, cols) for cols in (units, width)],
        [*cot_parts, down],
        (),
        name="act_grad",
    )


def post_kernel(*refs, slots, groups, per):
    mixed_refs = refs[: slots * groups]
    x_refs = refs[slots * groups : slots * groups + slots]
    weight_refs = refs[slots * groups + slots : slots * groups + 2 * slots]
    bias_ref, gain_ref, shift_ref, post_ref, residual_ref = refs[-5:]
    blocks = pl.num_programs(0)
    at = (pl.program_id(0) + blocks // 2) % blocks
    residual = choose(at // per, x_refs).astype(F32) + row(bias_ref)
    for slot in range(slots):
        mixed = [ref[...] for ref in mixed_refs[slot * groups : (slot + 1) * groups]]
        residual = residual + dot(jnp.concatenate(mixed, axis=1), weight_refs[slot][...])
    normal, _ = norm_stats(residual)
    post_ref[...] = low(normal * row(gain_ref) + row(shift_ref))

    @pl.when(at < per)
    def _():
        residual_ref[...] = residual


def post_norm(mixed, x_parts, weights, bias, gain, shift):
    slots, groups = len(mixed), len(mixed[0])
    rows, width = x_parts[0].shape
    block = min(rows, 1024)
    per = rows // block
    blocks = slots * per
    order = lambda i: (i + blocks // 2) % blocks
    specs = [
        pl.BlockSpec(
            (block, part.shape[1]),
            lambda i, slot=slot: (((order(i) // per) ^ slot) * per + order(i) % per, 0),
        )
        for slot in range(slots)
        for part in mixed[slot]
    ]
    return kernel_call(
        functools.partial(post_kernel, slots=slots, groups=groups, per=per),
        (blocks,),
        specs
        + slot_specs(slots, per, block, width, order)
        + [whole(a.shape) for a in (*weights, bias, gain, shift)],
        [
            pl.BlockSpec((block, width), lambda i: (order(i), 0)),
            pl.BlockSpec((block, width), lambda i: (jnp.clip(i - blocks // 2, 0, per - 1), 0)),
        ],
        [shape_of(slots * rows, width), shape_of(rows, width, F32)],
        [*[part for parts in mixed for part in parts], *x_parts, *weights, bias, gain, shift],
        (),
        name="post_norm",
    )


def feed_kernel(*refs, count, per, extras, held):
    post_ref, act_grad_ref, up_ref, bias_ref = refs[:4]
    extra_refs = refs[4 : 4 + extras]
    active_ref, grad_ref, sum_ref = refs[4 + extras + held : 7 + extras + held]
    back_refs = refs[7 + extras + held :]
    slot = pl.program_id(0) // per

    @pl.when(pl.program_id(0) == 0)
    def _():
        sum_ref[...] = jnp.zeros_like(sum_ref)

    post = post_ref[...]
    units = active_ref.shape[1]
    chunk = min(512, units)
    scale, cubic = math.sqrt(2 / math.pi), 0.044715
    for first in range(0, units, chunk):
        cols = slice(first, first + chunk)
        hidden = dot(post, up_ref[:, cols]) + row(bias_ref)[:, cols]
        square = hidden * hidden
        curve = jnp.tanh(hidden * (scale + scale * cubic * square))
        half = 0.5 + 0.5 * curve
        active_ref[:, cols] = low(hidden * half)
        slope = half + (0.5 * hidden) * (1.0 - curve * curve) * (
            scale + 3 * scale * cubic * square
        )
        grad = low(act_grad_ref[:, cols].astype(F32) * slope)
        grad_ref[:, cols] = grad
        sum_ref[:, cols] += jnp.sum(grad.astype(F32), axis=0, keepdims=True)
    back = dot(grad_ref[...], up_ref[...], NT)
    if extras:
        back = back + choose(slot, extra_refs).astype(F32)
    back = low(back)
    for at, back_ref in enumerate(back_refs):

        @pl.when(slot == at)
        def _():
            back_ref[...] = back


def feed(post_all, act_grad, up, up_bias, slots, chosen, extras, held):
    count = len(chosen)
    total, width = post_all.shape
    rows, units = total // slots, up.shape[1]
    block = min(rows, 512)
    per = rows // block
    tall = lambda cols: tall_spec(chosen, per, block, cols)
    active, grad, sums, *backs = kernel_call(
        functools.partial(
            feed_kernel, count=count, per=per, extras=len(extras), held=len(held)
        ),
        (count * per,),
        [tall(width), tall(units), whole(up.shape), whole(up_bias.shape)]
        + slot_specs(len(extras), per, block, width),
        [tall(units), tall(units), whole((1, units))] + slot_specs(count, per, block, width),
        [shape_of(total, units), shape_of(total, units), shape_of(1, units, F32)]
        + [shape_of(rows, width)] * count,
        [post_all, act_grad, up, up_bias, *extras],
        held,
        name="feed",
    )
    return (active, grad), sums, backs


def split_rows(total, me, keep_ref, send_ref, streams):
    rows = total.shape[0] // streams
    for slot in range(streams):
        part = low(total[pl.ds(pl.multiple_of((me ^ slot) * rows, rows), rows), :])
        ref = send_ref if slot % 2 else keep_ref
        ref[slot // 2 * rows : (slot // 2 + 1) * rows, :] = part


def outer_kernel(me_ref, left_ref, right_ref, keep_ref, send_ref, total, *, streams):
    step = pl.program_id(0)

    @pl.when(step == 0)
    def _():
        total[...] = dot(left_ref[...], right_ref[...], TN)

    @pl.when(step > 0)
    def _():
        total[...] += dot(left_ref[...], right_ref[...], TN)

    @pl.when(step == pl.num_programs(0) - 1)
    def _():
        split_rows(total, me_ref[0], keep_ref, send_ref, streams)


def outer_step(left, right, me, streams):
    total = left.shape[0]
    block = min(total, 1024)
    shape = (left.shape[1], right.shape[1])
    half = (shape[0] // 2, shape[1])
    return kernel_call(
        functools.partial(outer_kernel, streams=streams),
        (total // block,),
        [pl.BlockSpec(memory_space=pltpu.SMEM)]
        + [pl.BlockSpec((block, cols), lambda i: (i, 0)) for cols in shape],
        [whole(half)] * 2,
        [shape_of(*half)] * 2,
        [me, left, right],
        scratch_shapes=[pltpu.VMEM(shape, F32)],
        name="outer_step",
    )


def join_kernel(me_ref, *refs, early, streams):
    parts, (keep_ref, send_ref) = refs[:-2], refs[-2:]
    rows = parts[0].shape[0] // streams
    for slot in range(streams):
        home = pl.ds(pl.multiple_of((me_ref[0] ^ slot) * rows, rows), rows)
        out = send_ref if slot % 2 else keep_ref
        here = slice(slot // 2 * rows, (slot // 2 + 1) * rows)
        at = 0
        for part in parts[:early]:
            out[here, at : at + part.shape[1]] = part[home, :]
            at += part.shape[1]
        total = parts[early][home, :].astype(F32)
        for part in parts[early + 1 :]:
            total = total + part[home, :].astype(F32)
        out[here, at:] = low(total)


def join_step(early, terms, me, streams):
    inputs = [*early, *terms]
    cols = sum(part.shape[1] for part in early) + terms[0].shape[1]
    half = (terms[0].shape[0] // 2, cols)
    return kernel_call(
        functools.partial(join_kernel, early=len(early), streams=streams),
        (1,),
        [pl.BlockSpec(memory_space=pltpu.SMEM)] + [whole(a.shape) for a in inputs],
        [whole(half)] * 2,
        [shape_of(*half)] * 2,
        [me, *inputs],
        name="join_step",
    )


def late_kernel(*refs):
    (keep, come, keep_late, come_late), outs = refs[:4], refs[4:]
    rows, cols = outs[0].shape[0], keep.shape[1]
    for slot, out in enumerate(outs):
        here = slice(slot * rows, (slot + 1) * rows)
        out[:, :cols] = low(keep[here, :].astype(F32) + come[here, :].astype(F32))
        out[:, cols:] = low(keep_late[here, :].astype(F32) + come_late[here, :].astype(F32))


def late_step(pairs, slots):
    inputs = [array for pair in pairs for array in pair]
    shape = (inputs[0].shape[0] // slots, inputs[0].shape[1] + inputs[2].shape[1])
    return kernel_call(
        late_kernel,
        (1,),
        [whole(a.shape) for a in inputs],
        [whole(shape)] * slots,
        [shape_of(*shape)] * slots,
        inputs,
        name="late_step",
    )


def pair_kernel(*refs, count):
    parts, outs = refs[: 2 * count], refs[2 * count :]
    rows = outs[0].shape[0] // count
    for at in range(count):
        keep, come = parts[2 * at : 2 * at + 2]
        for slot, out in enumerate(outs):
            here = slice(slot * rows, (slot + 1) * rows)
            out[at * rows : (at + 1) * rows, :] = low(
                keep[here, :].astype(F32) + come[here, :].astype(F32)
            )


def pair_step(pairs, slots):
    inputs = [array for pair in pairs for array in pair]
    rows, cols = inputs[0].shape
    shape = (rows // slots * len(pairs), cols)
    return kernel_call(
        functools.partial(pair_kernel, count=len(pairs)),
        (1,),
        [whole(a.shape) for a in inputs],
        [whole(shape)] * slots,
        [shape_of(*shape)] * slots,
        inputs,
        name="pair_step",
    )


def stack_kernel(*refs):
    rows = refs[0].shape[0]
    for at, ref in enumerate(refs[:-1]):
        refs[-1][at * rows : (at + 1) * rows, :] = ref[...]


def stack_step(parts):
    rows, cols = parts[0].shape
    return kernel_call(
        stack_kernel,
        (1,),
        [whole((rows, cols))] * len(parts),
        [whole((rows * len(parts), cols))],
        [shape_of(rows * len(parts), cols)],
        list(parts),
        name="stack_step",
    )[0]


def shard_views(even_ref, odd_ref, streams):
    rows = even_ref.shape[0] // (streams // 2)
    return [
        (slot, ref.at[slot // 2 * rows : (slot // 2 + 1) * rows])
        for slot, ref in enumerate([even_ref, odd_ref] * (streams // 2))
    ]


def feed_grads_kernel(me_ref, even_ref, odd_ref, up_ref, down_ref, up_rows, *, streams):
    rows = even_ref.shape[0] // streams
    for slot, part in shard_views(even_ref, odd_ref, streams):
        home = pl.ds(pl.multiple_of((me_ref[0] ^ slot) * rows, rows), rows)
        up_rows[home, :] = part[:rows, :].astype(F32)
        down_ref[home, :] = part[rows:, :].astype(F32)
    up_ref[...] = up_rows[...].T


def feed_grads(even, odd, me, streams):
    units, width = even.shape
    return kernel_call(
        functools.partial(feed_grads_kernel, streams=streams),
        (1,),
        [pl.BlockSpec(memory_space=pltpu.SMEM)] + [whole(even.shape)] * 2,
        [whole((width, units)), whole((units, width))],
        [shape_of(width, units, F32), shape_of(units, width, F32)],
        [me, even, odd],
        scratch_shapes=[pltpu.VMEM((units, width), F32)],
        name="feed_grads",
    )


def pack_kernel(*refs, groups):
    sums_ref, gain_ref, shift_ref = refs[:3]
    row_refs, count_refs = refs[3 : 3 + groups], refs[3 + groups : 3 + 2 * groups]
    unit_refs, out_ref = refs[3 + 2 * groups : -1], refs[-1]
    out_ref[...] = jnp.zeros_like(out_ref)
    out_ref[:4, : sums_ref.shape[1]] = sums_ref[:4, :]
    rows = row_refs[0][...]
    for ref in row_refs[1:]:
        rows = rows + ref[...]
    out_ref[4:5, : rows.shape[1]] = (rows[0:1] - row(shift_ref) * rows[1:2]) / row(gain_ref)
    out_ref[5:6, : rows.shape[1]] = rows[1:2]
    units = unit_refs[0][...]
    for ref in unit_refs[1:]:
        units = units + ref[...]
    out_ref[8:9, : units.shape[1]] = units
    for at, ref in enumerate(count_refs):
        out_ref[9 + at : 10 + at, : ref.shape[1]] = ref[...]


def pack(row_sums, gain, shift, group_rows, group_counts, unit_sums):
    inputs = [row_sums, gain, shift, *group_rows, *group_counts, *unit_sums]
    wide = max(a.shape[1] for a in (row_sums, *group_counts, *unit_sums))
    return kernel_call(
        functools.partial(pack_kernel, groups=len(group_rows)),
        (1,),
        [whole(a.shape) for a in inputs],
        [whole((16, wide))],
        [shape_of(16, wide, F32)],
        inputs,
        name="pack",
    )[0]


def resid_kernel(*refs, terms, slots):
    term_refs = refs[:terms]
    residual_ref, cot_ref, gain_ref = refs[terms : terms + 3]
    weight_refs = refs[terms + 3 : terms + 3 + slots]
    grad_ref, low_ref, sums_ref = refs[terms + 3 + slots : terms + 6 + slots]
    part_refs = refs[terms + 6 + slots :]

    @pl.when(pl.program_id(0) == 0)
    def _():
        sums_ref[...] = jnp.zeros_like(sums_ref)

    post_grad = term_refs[0][...].astype(F32)
    for ref in term_refs[1:]:
        post_grad = post_grad + ref[...].astype(F32)
    cot = cot_ref[...].astype(F32)
    normal, inverse = norm_stats(residual_ref[...])
    grad = cot + norm_pull(post_grad * row(gain_ref), normal, inverse)
    grad_ref[...] = grad
    grad_low = low(grad)
    low_ref[...] = grad_low
    for weight_ref, part_ref in zip(weight_refs, part_refs):
        part_ref[...] = low(dot(grad_low, weight_ref[...], NT))
    for at, value in enumerate((cot, grad, post_grad * normal, post_grad)):
        sums_ref[at : at + 1, :] += jnp.sum(value, axis=0, keepdims=True)


def resid_step(terms, residual, cotangent, gain, weights):
    rows, width = residual.shape
    block = min(rows, 256)
    tall = lambda cols: pl.BlockSpec((block, cols), lambda i: (i, 0))
    cols = weights[0].shape[0]
    return kernel_call(
        functools.partial(resid_kernel, terms=len(terms), slots=len(weights)),
        (rows // block,),
        [tall(width)] * (len(terms) + 2) + [whole(a.shape) for a in (gain, *weights)],
        [tall(width), tall(width), whole((8, width))] + [tall(cols)] * len(weights),
        [shape_of(rows, width, F32), shape_of(rows, width), shape_of(8, width, F32)]
        + [shape_of(rows, cols)] * len(weights),
        [*terms, residual, cotangent, gain, *weights],
        (),
        name="resid_step",
    )


def dense_grad_kernel(*refs, slots, groups):
    mixed_refs, grad_ref = refs[: slots * groups], refs[slots * groups]
    even_ref, odd_ref, *sum_refs = refs[slots * groups + 1 :]
    step = pl.program_id(0)
    grad = grad_ref[...]
    for slot in range(slots):
        mixed = [ref[...] for ref in mixed_refs[slot * groups : (slot + 1) * groups]]
        part = dot(grad, jnp.concatenate(mixed, axis=1), TN)
        sum_refs[slot][...] = jnp.where(step == 0, 0.0, sum_refs[slot][...]) + part

    @pl.when(step == pl.num_programs(0) - 1)
    def _():
        rows = sum_refs[0].shape[0]
        for slot, sum_ref in enumerate(sum_refs):
            out_ref = odd_ref if slot % 2 else even_ref
            out_ref[slot // 2 * rows : (slot // 2 + 1) * rows, :] = low(sum_ref[...])


def dense_grad(mixed, grad):
    slots, groups = len(mixed), len(mixed[0])
    rows, width = grad.shape
    block = min(rows, 512)
    per = rows // block
    cols = sum(part.shape[1] for part in mixed[0])
    return kernel_call(
        functools.partial(dense_grad_kernel, slots=slots, groups=groups),
        (per,),
        [
            pl.BlockSpec((block, part.shape[1]), lambda i, slot=slot: (slot * per + i, 0))
            for slot in range(slots)
            for part in mixed[slot]
        ]
        + [pl.BlockSpec((block, width), lambda i: (i, 0))],
        [whole((width * slots // 2, cols))] * 2,
        [shape_of(width * slots // 2, cols)] * 2,
        [*[part for parts in mixed for part in parts], grad],
        (),
        scratch_shapes=[pltpu.VMEM((width, cols), F32)] * slots,
        name="dense_grad",
    )


def weight_kernel(me_ref, normed_ref, grad_ref, wq_ref, wk_ref, wv_ref, *refs, streams):
    *out_refs, sums_ref, count_ref, total, count = refs
    step = pl.program_id(0)

    @pl.when(step == 0)
    def _():
        total[...] = jnp.zeros_like(total)
        count[...] = jnp.zeros_like(count)

    grad = grad_ref[...]
    total[...] += dot(normed_ref[...], grad, TN)
    count[...] += jnp.sum(grad.astype(F32), axis=0, keepdims=True)

    @pl.when(step == pl.num_programs(0) - 1)
    def _():
        weight = jnp.concatenate([wq_ref[...], wk_ref[...], wv_ref[...]], axis=1).astype(F32)
        if streams:
            split_rows(total, me_ref[0], *out_refs, streams)
        else:
            out_refs[0][...] = low(total[...])
        count_ref[...] = count[...]
        lane = lanes(weight.shape[0])
        cross = jnp.sum(weight * total[...], axis=1, keepdims=True)
        plain = jnp.sum(weight * count[...], axis=1, keepdims=True)
        both = jnp.where(lane == 0, cross, jnp.where(lane == 1, plain, 0.0))
        sums_ref[...] = both.T[:8]


def weight_step(normed, grad, weights, group, me, streams):
    total, width = normed.shape
    cols = grad.shape[1]
    block = min(total, 1024)
    outs = [(width // 2, cols)] * 2 if streams else [(width, cols)]
    *parts, sums, count = kernel_call(
        functools.partial(weight_kernel, streams=streams),
        (total // block,),
        [pl.BlockSpec(memory_space=pltpu.SMEM)]
        + [pl.BlockSpec((block, count), lambda i: (i, 0)) for count in (width, cols)]
        + [pl.BlockSpec((width, cols // 3), lambda i: (0, group))] * 3,
        [whole(shape) for shape in outs] + [whole((8, width)), whole((1, cols))],
        [shape_of(*shape) for shape in outs] + [shape_of(8, width, F32), shape_of(1, cols, F32)],
        [me, normed, grad, *weights],
        scratch_shapes=[pltpu.VMEM((width, cols), F32), pltpu.VMEM((1, cols), F32)],
        name="weight_step",
    )
    return parts, sums, count


def unproject_kernel(*refs, groups, per, extras):
    grad_refs, weight_refs = refs[:groups], refs[groups : 4 * groups]
    extra_refs = refs[4 * groups : 4 * groups + extras]
    out_refs = refs[4 * groups + extras : -1]
    joined = refs[-1]
    slot = pl.program_id(0) // per

    @pl.when(pl.program_id(0) == 0)
    def _():
        joined[...] = jnp.concatenate([ref[...] for ref in weight_refs], axis=1)

    total = dot(jnp.concatenate([ref[...] for ref in grad_refs], axis=1), joined[...], NT)
    if extras:
        total = total + choose(slot, extra_refs).astype(F32)
    total = low(total)
    for at, ref in enumerate(out_refs):

        @pl.when(slot == at)
        def _():
            ref[...] = total


def unproject(grads, weights, slots, chosen, extras):
    width = weights[0].shape[0]
    count, groups = len(chosen), len(grads)
    total, cols = grads[0].shape
    rows = total // slots
    block = min(rows, 512)
    per = rows // block
    return kernel_call(
        functools.partial(unproject_kernel, groups=groups, per=per, extras=len(extras)),
        (count * per,),
        [tall_spec(chosen, per, block, cols)] * groups
        + [
            pl.BlockSpec((width, cols // 3), lambda i, group=group: (0, group))
            for group in range(groups)
            for _ in weights
        ]
        + slot_specs(len(extras), per, block, width),
        slot_specs(count, per, block, width),
        [shape_of(rows, width)] * count,
        [*grads, *[weight for _ in grads for weight in weights], *extras],
        (),
        scratch_shapes=[pltpu.VMEM((width, cols * groups), BF16)],
        name="unproject",
    )


def ffn_kernel(active_ref, weight_ref, even_ref, odd_ref, *, per):
    total = low(dot(active_ref[...], weight_ref[...]))
    odd = pl.program_id(0) // per % 2

    @pl.when(odd == 0)
    def _():
        even_ref[...] = total

    @pl.when(odd == 1)
    def _():
        odd_ref[...] = total


def ffn_step(active, weight, slots):
    total, units = active.shape
    width = weight.shape[1]
    rows = total // slots
    block = min(rows, 1024)
    per = rows // block
    half = (total // 2, width)

    def half_spec(odd):
        def place(i):
            slot, step = i // per, i % per
            now = slot // 2 * per
            if odd:
                return (jnp.where(slot % 2 == 1, now + step, jnp.maximum(now - 1, 0)), 0)
            return (jnp.where(slot % 2 == 0, now + step, now + per - 1), 0)

        return pl.BlockSpec((block, width), place)

    return kernel_call(
        functools.partial(ffn_kernel, per=per),
        (slots * per,),
        [pl.BlockSpec((block, units), lambda i: (i, 0)), whole(weight.shape)],
        [half_spec(0), half_spec(1)],
        [shape_of(*half)] * 2,
        [active, weight],
        name="ffn_step",
    )


def spread_kernel(me_ref, even_ref, odd_ref, *refs, groups, streams):
    *out_refs, dense_ref, dense_rows = refs
    cols = out_refs[0].shape[1] // groups
    heads = dense_ref.shape[0]
    rows = even_ref.shape[0] * 2 // streams
    for slot, part in shard_views(even_ref, odd_ref, streams):
        home = pl.ds(pl.multiple_of((me_ref[0] ^ slot) * rows, rows), rows)
        for group in range(groups):
            first = group * 3 * cols + (heads if group == groups - 1 else 0)
            for kind in range(3):
                at = first + kind * cols
                out_refs[kind][home, group * cols : (group + 1) * cols] = part[
                    :, at : at + cols
                ].astype(F32)
        first = (groups - 1) * 3 * cols
        dense_rows[home, :] = part[:, first : first + heads].astype(F32)
    dense_ref[...] = dense_rows[...].T


def spread(even, odd, me, streams, groups, heads):
    width = even.shape[0] * 2
    shapes = [(width, heads)] * 3 + [(heads, width)]
    return kernel_call(
        functools.partial(spread_kernel, groups=groups, streams=streams),
        (1,),
        [pl.BlockSpec(memory_space=pltpu.SMEM)] + [whole(even.shape)] * 2,
        [whole(shape) for shape in shapes],
        [shape_of(*shape, F32) for shape in shapes],
        [me, even, odd],
        scratch_shapes=[pltpu.VMEM((width, heads), F32)],
        name="spread",
    )


def input_kernel(*refs, terms):
    x_ref, resid_ref, gain_ref, out_ref = refs[terms:]
    grad = refs[0][...].astype(F32)
    for ref in refs[1:terms]:
        grad = grad + ref[...].astype(F32)
    normal, inverse = norm_stats(x_ref[...].astype(F32))
    out_ref[...] = resid_ref[...] + norm_pull(grad * row(gain_ref), normal, inverse)


def input_step(terms, layer_input, resid_grad, gain):
    rows, width = resid_grad.shape
    block = min(rows, 256)
    tall = pl.BlockSpec((block, width), lambda i: (i, 0))
    return kernel_call(
        functools.partial(input_kernel, terms=len(terms)),
        (rows // block,),
        [tall] * (len(terms) + 2) + [whole(gain.shape)],
        [tall],
        [shape_of(rows, width, F32)],
        [*terms, layer_input, resid_grad, gain],
        name="input_step",
    )[0]


def shards(
    slots,
    streams,
    layer_input,
    row_ids,
    input_gain,
    input_shift,
    query_weight,
    query_bias,
    key_weight,
    value_weight,
    value_bias,
    dense_weight,
    dense_bias,
    post_gain,
    post_shift,
    up_weight,
    up_bias,
    down_weight,
    down_bias,
    cotangent,
):
    me = lax.axis_index("tensor")
    me_word = me.astype(jnp.int32)[None]
    stream = lax.axis_index("dp").astype(jnp.int32)[None]
    rows = layer_input.shape[0]
    head_cols = query_weight.shape[1]
    head_count = head_cols // HD
    groups = max(1, head_count // 2)
    bits = [1 << level for level in range(slots.bit_length() - 1)]
    half = slots // 2
    after = lambda array, *others: lax.optimization_barrier((array, *others))[0]

    def swap(array, mask):
        return lax.ppermute(array, "tensor", [(i, i ^ mask) for i in range(slots)])

    def gather(array):
        held = {0: array}
        for bit in reversed(bits):
            held.update({slot ^ bit: swap(part, bit) for slot, part in held.items()})
        return [held[slot] for slot in range(slots)]

    def blocks(array):
        return [array[slot * rows : (slot + 1) * rows] for slot in range(slots)]

    def swap_data(array, mask):
        return lax.ppermute(array, "dp", [(i, i ^ mask) for i in range(streams)])

    def finish_terms(held, terms, levels):
        for bit in levels:
            come = {slot ^ bit: swap(part, bit) for slot, part in held.items() if slot & bit}
            if 0 in come:
                terms.append(come.pop(0))
            held = {
                slot: low(held[slot].astype(F32) + part.astype(F32)) for slot, part in come.items()
            }
        return terms

    def scatter_terms(parts):
        return finish_terms(dict(enumerate(parts)), [parts[0]], bits)

    far_odd = range(half + 1, slots, 2)
    far_even = range(half, slots, 2)
    near_odd = range(1, half, 2)
    near_even = range(0, half, 2)

    def ordered_terms(make):
        far = make(far_odd, (), None)
        far_come = [swap(part, 1) for part in far]
        near = make(near_odd, (), far[-1])
        near_come = [swap(part, 1) for part in near]
        far = make(far_even, far_come, near[-1])
        near = make(near_even, near_come, far[-1])
        held = dict(zip((*far_even, *near_even), (*far, *near)))
        return finish_terms(held, [held.pop(0)], bits[1:])

    def add_up(terms):
        return functools.reduce(
            lambda sum_now, term: sum_now + term.astype(F32), terms[1:], terms[0].astype(F32)
        )

    far_streams = range(2, streams, 2)

    def exchange(parts):
        return low(add_up([parts[0], *[swap_data(parts[k // 2], k) for k in far_streams]]))

    def collect_far(shard):
        return [shard, *[swap_data(shard, k) for k in far_streams]]

    norm_vectors = (input_gain, input_shift)
    weights = (query_weight, key_weight, value_weight)
    biases = (query_bias, value_bias)
    x_held = {0: layer_input}
    for bit in reversed(bits[1:]):
        x_held.update({slot ^ bit: swap(part, bit) for slot, part in x_held.items()})
    x_held[1] = swap(x_held[0], 1)
    near_parts = [x_held[0], x_held[1]]
    first = range(2)
    held = project(near_parts, first, slots, norm_vectors, weights, biases, ())
    rest = sorted(slot for slot in x_held if slot > 1)
    *arrived, normed = lax.optimization_barrier((*[x_held[slot] for slot in rest], held[0]))
    held = (normed, *held[1:])
    for slot, part in zip(rest, arrived):
        x_held[slot], x_held[slot ^ 1] = part, swap(part, 1)
    x_parts = [x_held[slot] for slot in range(slots)]
    dense_parts = gather(after(dense_weight, arrived[-1]))
    cot_own = after(cotangent, arrived[-1])
    cot_held = {0: cot_own}
    for bit in reversed(bits[1:]):
        cot_held.update({slot ^ bit: swap(part, bit) for slot, part in cot_held.items()})
    normed, queries, key_rows, values = project(
        x_parts[2:], range(2, slots), slots, norm_vectors, weights, biases, held
    )

    heads = me * head_count + jnp.arange(head_count)
    slopes = jnp.exp2(-8.0 * (heads + 1).astype(F32) / HEADS) * LOG2E
    apart = (row_ids[:1] != row_ids[SHORT : SHORT + 1]).astype(jnp.int32)

    mixed_own, columns, mixed_parts = [], [], []
    for group in range(groups):
        mixed, *held_columns = attend(
            me_word,
            apart,
            slopes,
            queries if not group else after(queries, cot_held[half], mixed_own[-1]),
            key_rows,
            values,
            slots,
            group,
        )
        mixed_own.append(mixed)
        columns.append(held_columns)
        if not group:
            keys = sorted(cot_held)
            held = lax.optimization_barrier((*[cot_held[key] for key in keys], mixed))[:-1]
            cot_held.update(zip(keys, held))
            cot_held.update({slot ^ 1: swap(part, 1) for slot, part in cot_held.items()})
            cot_parts = [cot_held[slot] for slot in range(slots)]
        if group < groups - 1:
            mixed_parts.append(gather(mixed))
    act_grad, cot_all = act_grad_step(
        lax.optimization_barrier((*cot_parts, mixed_own[-1], *dense_parts[2:]))[:slots], down_weight
    )
    came = {0: mixed_own[-1]}
    for bit in reversed(bits[1:]):
        came.update({slot ^ bit: swap(part, bit) for slot, part in came.items()})
    far_slots = sorted(came)[1:]
    *arrived, act_grad = lax.optimization_barrier((*[came[slot] for slot in far_slots], act_grad))
    came.update(zip(far_slots, arrived))
    came.update({slot ^ 1: swap(part, 1) for slot, part in came.items()})
    mixed_parts.append([came[slot] for slot in range(slots)])
    mixed_all = [[mixed_parts[group][slot] for group in range(groups)] for slot in range(slots)]
    post_all, residual = post_norm(
        mixed_all, x_parts, dense_parts, dense_bias, post_gain, post_shift
    )

    fed, up_bias_parts = [()], []

    def make_feed(chosen, extras, gate):
        held, sums, backs = feed(
            post_all, act_grad, up_weight, up_bias, slots, chosen, extras, fed[-1]
        )
        fed.append(held)
        up_bias_parts.append(sums)
        return backs

    post_terms = ordered_terms(make_feed)
    active, hidden_grad = fed[-1]
    up_keep, up_send = outer_step(hidden_grad, post_all, stream, streams)
    down_keep, down_send = outer_step(active, after(cot_all, up_keep), stream, streams)
    up_come, down_come = swap_data(up_send, 1), swap_data(down_send, 1)
    resid_grad, attended_grad, row_sums, *mixed_grads = resid_step(
        [after(post_terms[0], down_keep), *post_terms[1:]],
        residual,
        cotangent,
        post_gain,
        dense_parts,
    )
    mixed_grads = [swap(part, slot) if slot else part for slot, part in enumerate(mixed_grads)]
    dense_even, dense_odd = dense_grad(mixed_all, attended_grad)
    ffn_even, ffn_odd = ffn_step(after(active, dense_odd), down_weight, slots)
    feed_parts = pair_step(
        [(after(up_keep, ffn_odd), up_come), (down_keep, down_come)], streams // 2
    )
    moved = lax.optimization_barrier((*mixed_grads, dense_odd, ffn_odd, *feed_parts))
    mixed_grads, (dense_odd, ffn_odd), feed_parts = (
        moved[:slots],
        moved[slots : slots + 2],
        moved[slots + 2 :],
    )
    dense_come, ffn_come = swap(dense_odd, 1), swap(ffn_odd, 1)

    def partner_sums(even, come):
        size = even.shape[0] * 2 // slots
        cuts = [slice(at * size, (at + 1) * size) for at in range(slots // 2)]
        return [low(even[cut].astype(F32) + come[cut].astype(F32)) for cut in cuts]

    cols = head_cols // groups
    head_grads, early_parts, group_rows, group_counts = [], [], [], []

    def backward(group):
        return attend_back(
            me_word, columns[group], values, mixed_own[group], mixed_grads, group
        )

    dense_sums = partner_sums(dense_even, dense_come)
    for group in range(groups - 1):
        head_grads.append(backward(group))
        grad = head_grads[-1]
        if group == groups - 2:
            grad, *dense_sums = lax.optimization_barrier((grad, *dense_sums))
        parts, row_part, count_part = weight_step(normed, grad, weights, group, stream, 0)
        early_parts += parts
        group_rows.append(row_part)
        group_counts.append(count_part)
        mixed_grads = lax.optimization_barrier((*mixed_grads, parts[-1]))[:-1]
    even_slots = range(2, slots, 2)
    dense_terms = finish_terms(dict(zip(even_slots, dense_sums[1:])), [dense_sums[0]], bits[1:])
    early_keep, early_send = join_step(early_parts, dense_terms, stream, streams)
    moved = lax.optimization_barrier(
        (*mixed_grads, early_send, exchange(feed_parts), *partner_sums(ffn_even, ffn_come))
    )
    mixed_grads, (early_send, feed_shard), ffn_sums = (
        moved[:slots],
        moved[slots : slots + 2],
        moved[slots + 2 :],
    )
    early_come = swap_data(early_send, 1)
    feed_shards = collect_far(feed_shard)
    ffn_terms = finish_terms(dict(zip(even_slots, ffn_sums[1:])), [ffn_sums[0]], bits[1:])
    head_grads.append(backward(groups - 1))
    grad, early_come, *arrived = lax.optimization_barrier(
        (head_grads[-1], early_come, *feed_shards, *ffn_terms)
    )
    feed_shards, ffn_terms = arrived[: len(feed_shards)], arrived[len(feed_shards) :]
    (late_keep, late_send), row_part, count_part = weight_step(
        normed, grad, weights, groups - 1, stream, streams
    )
    group_rows.append(row_part)
    group_counts.append(count_part)
    late_come = swap_data(late_send, 1)
    vectors = pack(row_sums, input_gain, input_shift, group_rows, group_counts, up_bias_parts)
    feed_even = stack_step([*feed_shards[:-1], after(feed_shards[-1], vectors)])
    summed = vectors + swap_data(vectors, 1)
    feed_odd = swap_data(after(feed_even, late_come, summed), 1)
    seen = []

    def make_unproject(chosen, extras, gate):
        gates = [feed_even if gate is None else gate]
        if not seen:
            gates += [late_come, summed]
        seen.append(0)
        return unproject(
            [*head_grads[:-1], after(head_grads[-1], *gates)], weights, slots, chosen, extras
        )

    normed_terms = ordered_terms(make_unproject)
    late_parts = late_step(
        [(early_keep, early_come), (after(late_keep, normed_terms[0]), late_come)], streams // 2
    )
    layer_output = low(residual + add_up(ffn_terms) + down_bias.astype(F32))
    up_grad, down_grad = feed_grads(feed_even, feed_odd, stream, streams)
    input_grad = input_step(
        [*normed_terms[:-1], after(normed_terms[-1], up_grad)],
        layer_input,
        resid_grad,
        input_gain,
    )
    *late_shards, layer_output, input_grad = lax.optimization_barrier(
        (*collect_far(exchange(late_parts)), layer_output, input_grad)
    )
    late_even = stack_step(late_shards)
    late_odd = swap_data(late_even, 1)
    for level in range(1, streams.bit_length() - 1):
        summed = summed + swap_data(summed, 1 << level)
    own = summed[8:]
    shared = after(summed, normed_terms[-1])[:8]
    for bit in reversed(bits):
        shared = shared + swap(shared, bit)
    shared = shared[:, : resid_grad.shape[1]]
    up_bias_grad = own[0, : up_bias.shape[0]]
    counts = own[1 : 1 + groups]
    query_bias_grad = counts[:, :cols].reshape(-1)
    value_bias_grad = counts[:, 2 * cols : 3 * cols].reshape(-1)
    *weight_grads, dense_weight_grad = spread(
        late_even, late_odd, stream, streams, groups, head_cols
    )
    return (
        layer_output,
        input_grad,
        shared[4],
        shared[5],
        weight_grads[0],
        query_bias_grad,
        weight_grads[1],
        weight_grads[2],
        value_bias_grad,
        dense_weight_grad,
        shared[1],
        shared[2],
        shared[3],
        up_grad,
        up_bias_grad,
        down_grad,
        shared[0],
    )


def solution(mesh):
    in_specs = (
        P(("dp", "tensor"), None),
        P("dp"),
        P(),
        P(),
        P(None, "tensor"),
        P("tensor"),
        P(None, "tensor"),
        P(None, "tensor"),
        P("tensor"),
        P("tensor", None),
        P(),
        P(),
        P(),
        P(None, "tensor"),
        P("tensor"),
        P("tensor", None),
        P(),
        P(("dp", "tensor"), None),
    )
    out_specs = (
        P(("dp", "tensor"), None),
        P(("dp", "tensor"), None),
        P(),
        P(),
        P(None, "tensor"),
        P("tensor"),
        P(None, "tensor"),
        P(None, "tensor"),
        P("tensor"),
        P("tensor", None),
        P(),
        P(),
        P(),
        P(None, "tensor"),
        P("tensor"),
        P("tensor", None),
        P(),
    )
    return jax.shard_map(
        functools.partial(shards, mesh.shape["tensor"], mesh.shape["dp"]), mesh=mesh, in_specs=in_specs, out_specs=out_specs, check_vma=False)
```
